32 devices in a mesh: dp: 2 (over y), row: 4 (over z), col: 4 (over x, core).
Axes of the slice: x: 2, y: 2, z: 4, core: 2. Of those that a mesh axis runs over, the one named last changes fastest.
Arguments:
- tokens: bfloat16 [6144, 2048], P(('dp', 'row'), 'col'), may hold values from -6 to 6
- seq_lengths: int32 [2], P('dp'), may hold values from 1024 to 3072, as said below
- w_query: bfloat16 [2048, 2048], P('row', 'col')
- w_key: bfloat16 [2048, 2048], P('row', 'col')
- w_value: bfloat16 [2048, 2048], P('row', 'col'), may hold values from -0.125 to 0.125
- w_out: bfloat16 [2048, 2048], P('col', 'row')
- w_gate: bfloat16 [2048, 8192], P('row', 'col'), may hold values from -0.125 to 0.125
- w_up: bfloat16 [2048, 8192], P('row', 'col'), may hold values from -0.125 to 0.125
- w_down: bfloat16 [8192, 2048], P('col', 'row')
- q_gain: float32 [2048], P('col')
- k_gain: float32 [2048], P('col')
- attn_gain: float32 [2048], P('col'), may hold values from 0.25 to 1.75
- mlp_gain: float32 [2048], P('col'), may hold values from 0.25 to 1.75
- cotangent: bfloat16 [6144, 2048], P(('dp', 'row'), 'col'), may hold values from -6 to 6
Outputs:
- block_output: bfloat16 [6144, 2048], P(('dp', 'row'), 'col')
- input_grad: float32 [6144, 2048], P(('dp', 'row'), 'col')
- w_query_grad: float32 [2048, 2048], P('row', 'col')
- w_key_grad: float32 [2048, 2048], P('row', 'col')
- w_value_grad: float32 [2048, 2048], P('row', 'col')
- w_out_grad: float32 [2048, 2048], P('col', 'row')
- w_gate_grad: float32 [2048, 8192], P('row', 'col')
- w_up_grad: float32 [2048, 8192], P('row', 'col')
- w_down_grad: float32 [8192, 2048], P('col', 'row')
- q_gain_grad: float32 [2048], P('col')
- k_gain_grad: float32 [2048], P('col')
- attn_gain_grad: float32 [2048], P('col')
- mlp_gain_grad: float32 [2048], P('col')
The draws below stay inside these ranges and needn't reach their ends.
Inputs may be any that keep to these rules, and one draw needn't show every extreme that they name: `seq_lengths`: the valid tokens of a sequence fill its first slots; some sequence is full.
All inputs are finite; a program needn't handle non-finite values.
Results may differ from the reference program's by a relative error of at most 0.022.
Values may be sent and summed in bfloat16 or wider, within the bound.
A program may use at most 256 MiB of HBM per device.

```python
import math
import jax
import jax.numpy as jnp
from jax import lax

D = 2048
FF = 8192
HEAD_DIM = 128
SEQ = 3072
SEQS = 2
TOKENS = 6144


def rising_columns(key, height, columns):
    first, second = jax.random.split(key)
    base = jax.random.normal(first, (height, columns), jnp.float32)
    place = jnp.arange(columns, dtype=jnp.float32) / (columns - 1)
    spread = jnp.exp(jax.random.uniform(second, (columns,), jnp.float32, -0.25, 0.25))
    factor = jnp.exp(place * math.log(3.0)) * spread / 1.9
    return base * factor[None, :] / math.sqrt(height)


def falling_gain(key, columns):
    place = jnp.arange(columns, dtype=jnp.float32) / (columns - 1)
    spread = jnp.exp(jax.random.uniform(key, (columns,), jnp.float32, -0.3, 0.3))
    return 2.7 * spread * jnp.exp(-place * math.log(3.0))


def draw_w_query(key, part):
    return rising_columns(jax.random.fold_in(key, 11), D, D).astype(jnp.bfloat16)


def draw_w_key(key, part):
    return rising_columns(jax.random.fold_in(key, 12), D, D).astype(jnp.bfloat16)


def draw_w_out(key, part):
    return rising_columns(jax.random.fold_in(key, 13), D, D).astype(jnp.bfloat16)


def draw_w_down(key, part):
    return rising_columns(jax.random.fold_in(key, 14), FF, D).astype(jnp.bfloat16)


def draw_q_gain(key, part):
    return falling_gain(jax.random.fold_in(key, 21), D)


def draw_k_gain(key, part):
    return falling_gain(jax.random.fold_in(key, 22), D)


def draw_seq_lengths(key, part):
    first, second = jax.random.split(jax.random.fold_in(key, 5))
    values = jax.random.randint(first, (SEQS,), SEQ // 3, SEQ)
    chosen = jax.random.randint(second, (), 0, SEQS)
    return jnp.where(jnp.arange(SEQS) == chosen, SEQ, values).astype(jnp.int32)


def block_scale(own_key, extent, pieces, low, top_value):
    def one(position, shards_of):
        heights = jax.random.uniform(jax.random.fold_in(jax.random.fold_in(own_key, 6), position), (shards_of,), jnp.float32, low / len(pieces), top_value / len(pieces))
        return jnp.repeat(jnp.exp(heights), extent[position] // shards_of).reshape((-1,) + (1,) * (len(extent) - position - 1))

    gain = one(*pieces[0])
    for cut in pieces[1:]:
        gain = gain * one(*cut)
    return gain


def gaussian(key, extent, deviation, most, cuts=(), kind=jnp.bfloat16):
    factor_of = block_scale(key, extent, cuts, -0.22, 0.18) if cuts else 1.0
    drawn = jax.random.normal(key, extent, jnp.float32) * deviation * factor_of
    return jnp.minimum(jnp.maximum(drawn, -most), most).astype(kind)


def setup_inputs(seed: int = 0) -> dict:
    key_of = jax.random.split(jax.random.key(seed), 15)
    tokens = gaussian(key_of[0], (TOKENS, D), 1.0, 6.0, ((0, 8), (1, 4)))
    seq_lengths = draw_seq_lengths(jax.random.fold_in(key_of[14], 71), 0)
    w_query = draw_w_query(jax.random.fold_in(key_of[14], 71), 0)
    w_key = draw_w_key(jax.random.fold_in(key_of[14], 71), 0)
    w_value = gaussian(key_of[4], (D, D), D ** -0.5, 0.125, ((0, 4), (1, 4)))
    w_out = draw_w_out(jax.random.fold_in(key_of[14], 71), 0)
    w_gate = gaussian(key_of[6], (D, FF), D ** -0.5, 0.125, ((0, 4), (1, 4)))
    w_up = gaussian(key_of[7], (D, FF), D ** -0.5, 0.125, ((0, 4), (1, 4)))
    w_down = draw_w_down(jax.random.fold_in(key_of[14], 71), 0)
    q_gain = draw_q_gain(jax.random.fold_in(key_of[14], 71), 0)
    k_gain = draw_k_gain(jax.random.fold_in(key_of[14], 71), 0)
    attn_gain = jnp.clip(1.0 + 0.15 * jax.random.normal(key_of[11], (D,), jnp.float32), 0.25, 1.75)
    mlp_gain = jnp.clip(1.0 + 0.15 * jax.random.normal(key_of[12], (D,), jnp.float32), 0.25, 1.75)
    cotangent = gaussian(key_of[13], (TOKENS, D), 1.0, 6.0, ((0, 8), (1, 4)))
    return dict(tokens=tokens, seq_lengths=seq_lengths, w_query=w_query, w_key=w_key, w_value=w_value, w_out=w_out, w_gate=w_gate, w_up=w_up, w_down=w_down, q_gain=q_gain, k_gain=k_gain, attn_gain=attn_gain, mlp_gain=mlp_gain, cotangent=cotangent)


rope_base = 500000.0
norm_eps = 1e-06

@jax.custom_vjp
def low(v):
    return lax.optimization_barrier(v.astype(jnp.bfloat16)).astype(jnp.float32)

@jax.custom_vjp
def low_back(v):
    return v

def low_keep(v):
    return (low(v), None)

def low_pass(kept, grad):
    return (grad,)

def back_keep(v):
    return (v, None)

def back_low(kept, grad):
    return (low(grad),)
low.defvjp(low_keep, low_pass)
low_back.defvjp(back_keep, back_low)

def matmul(left, right):
    return jnp.dot(left, right, precision=lax.Precision.HIGHEST, preferred_element_type=jnp.float32)

def inverse_rms(values):
    return lax.rsqrt(lax.optimization_barrier(jnp.mean(values * values, axis=-1, keepdims=True)) + norm_eps)

def rope_tables(positions):
    half = HEAD_DIM // 2
    freq = 1.0 / rope_base ** (jnp.arange(half, dtype=jnp.float32) / half)
    angle = positions.astype(jnp.float32)[:, None] * freq[None, :]
    angle = jnp.concatenate([angle, angle], axis=1)
    return (jnp.cos(angle), jnp.sin(angle))

def rotate(values, cosine, sine):
    count = values.shape[0]
    heads = values.reshape(count, -1, HEAD_DIM)
    half = HEAD_DIM // 2
    turned = jnp.concatenate([-heads[..., half:], heads[..., :half]], axis=-1)
    return (heads * cosine[:, None, :] + turned * sine[:, None, :]).reshape(count, -1)

def one_head(triple, allowed):
    query, keys, values = triple
    scores = low_back(matmul(query, keys.T) * HEAD_DIM ** (-0.5))
    scores = jnp.where(allowed, scores, -1e+30)
    top = lax.optimization_barrier(jnp.max(scores, axis=-1, keepdims=True))
    weights = jnp.exp(scores - top)
    probs = weights / lax.optimization_barrier(jnp.sum(weights, axis=-1, keepdims=True))
    return matmul(low(probs), values)

def split_heads(block):
    return block.reshape(SEQ, -1, HEAD_DIM).transpose(1, 0, 2)

def one_sequence(operands):
    query, keys, values, length = operands
    positions = jnp.arange(SEQ)
    allowed = (positions[None, :] <= positions[:, None]) & (positions[None, :] < length)
    checked = jax.checkpoint(one_head)
    outputs = lax.map(lambda triple: checked(triple, allowed), (split_heads(query), split_heads(keys), split_heads(values)))
    return outputs.transpose(1, 0, 2).reshape(SEQ, -1)

def forward(tokens, w_query, w_key, w_value, w_out, w_gate, w_up, w_down, q_gain, k_gain, attn_gain, mlp_gain, seq_lengths):
    positions = jnp.arange(TOKENS) % SEQ
    valid = (positions < jnp.repeat(seq_lengths, SEQ)).astype(jnp.float32)[:, None]
    cosine, sine = rope_tables(positions)
    query_pre = low_back(matmul(tokens, w_query))
    key_pre = low_back(matmul(tokens, w_key))
    value_low = low(low_back(matmul(tokens, w_value)))
    query_rot = low(rotate(query_pre * inverse_rms(query_pre) * q_gain, cosine, sine))
    key_rot = low(rotate(key_pre * inverse_rms(key_pre) * k_gain, cosine, sine))
    attended = lax.map(one_sequence, (query_rot.reshape(SEQS, SEQ, D), key_rot.reshape(SEQS, SEQ, D), value_low.reshape(SEQS, SEQ, D), seq_lengths))
    attn_low = low(low_back(attended.reshape(TOKENS, D)))
    branch = low_back(matmul(attn_low, w_out))
    resid = tokens + branch * inverse_rms(branch) * attn_gain
    resid_low = low(resid)
    gate = low_back(matmul(resid_low, w_gate))
    upper = low_back(matmul(resid_low, w_up))
    hidden = low(gate * jax.nn.sigmoid(gate) * upper)
    mixed = low_back(matmul(hidden, w_down))
    return (resid + mixed * inverse_rms(mixed) * mlp_gain) * valid

def reference(tokens, seq_lengths, w_query, w_key, w_value, w_out, w_gate, w_up, w_down, q_gain, k_gain, attn_gain, mlp_gain, cotangent):
    floats = tuple((operand.astype(jnp.float32) for operand in (tokens, w_query, w_key, w_value, w_out, w_gate, w_up, w_down, q_gain, k_gain, attn_gain, mlp_gain)))

    def wrapped(*operands):
        return forward(*operands, seq_lengths)
    output, pull = jax.vjp(wrapped, *floats)
    grads = pull(cotangent.astype(jnp.float32))
    factor = 1.0 / math.sqrt(TOKENS)
    return (output.astype(jnp.bfloat16), grads[0], grads[1] * factor, grads[2] * factor, grads[3] * factor, grads[4] * factor, grads[5] * factor, grads[6] * factor, grads[7] * factor, grads[8] * factor, grads[9] * factor, grads[10] * factor, grads[11] * factor)
```

```python
import functools
import math

import jax
import jax.numpy as jnp
from jax import lax
from jax.experimental import pallas as pl
from jax.experimental.pallas import tpu as pltpu
from jax.sharding import PartitionSpec as P

HEAD_DIM = 128
rope_base = 500000.0
norm_eps = 1e-06
masked_score = -1e30

MESH = pl.DeviceIdType.MESH
bf16 = jnp.bfloat16
f32 = jnp.float32


def rope_tables(positions, head_dim):
    half = head_dim // 2
    freq = 1.0 / rope_base ** (jnp.arange(half, dtype=f32) / half)
    angle = positions.astype(f32)[:, None] * freq[None, :]
    angle = jnp.concatenate([angle, angle], axis=1)
    return (jnp.cos(angle), jnp.sin(angle))


def rotate(values, cosine, sine, head_dim):
    count = values.shape[0]
    heads = values.reshape(count, -1, head_dim)
    half = head_dim // 2
    turned = jnp.concatenate([-heads[..., half:], heads[..., :half]], axis=-1)
    return (heads * cosine[:, None, :] + turned * sine[:, None, :]).reshape(count, -1)


def unrotate(values, cosine, sine, head_dim):
    count = values.shape[0]
    heads = values.reshape(count, -1, head_dim)
    half = head_dim // 2
    turned = heads * sine[:, None, :]
    back = jnp.concatenate([turned[..., half:], -turned[..., :half]], axis=-1)
    return (heads * cosine[:, None, :] + back).reshape(count, -1)


def matmul(left, right):
    return jnp.dot(left, right, preferred_element_type=f32)


def contract_first(left, right):
    return lax.dot_general(left, right, (((0,), (0,)), ((), ())), preferred_element_type=f32)


def contract_last(left, right):
    return lax.dot_general(left, right, (((1,), (1,)), ((), ())), preferred_element_type=f32)


def flip(axis, bit):
    return lax.axis_index(axis) ^ bit


def side(axis):
    return lax.axis_index(axis) & 1


def greet(peers):
    barrier = pltpu.get_barrier_semaphore()
    for peer in peers:
        pl.semaphore_signal(barrier, inc=1, device_id=peer, device_id_type=MESH)
    pl.semaphore_wait(barrier, len(peers))


def gather_kernel(x_ref, out_ref, local_sem, send_sem, recv_sem):
    rows, width = x_ref.shape
    half = rows // 2
    y, b = side("dp"), lax.axis_index("col")
    to_x, to_y, to_c = {"col": flip("col", 2)}, {"dp": flip("dp", 1)}, {"col": flip("col", 1)}
    greet([to_x, to_y, to_c])

    def slot(yy, h, bb, n=half):
        return out_ref.at[
            pl.ds(pl.multiple_of(yy * rows + h * half, half), n),
            pl.ds(pl.multiple_of(bb * width, width), width),
        ]

    started = []

    def send(src, dst, number, peer):
        copy = pltpu.make_async_remote_copy(
            src_ref=src,
            dst_ref=dst,
            send_sem=send_sem.at[number],
            recv_sem=recv_sem.at[number],
            device_id=peer,
            device_id_type=MESH,
        )
        copy.start()
        started.append(copy)
        return copy

    low, high = x_ref.at[pl.ds(0, half)], x_ref.at[pl.ds(half, half)]
    own = pltpu.make_async_copy(x_ref, slot(y, 0, b, rows), local_sem)
    xa = send(low, slot(y, 0, b), 0, to_x)
    ya = send(high, slot(y, 1, b), 1, to_y)
    c0 = send(x_ref, slot(y, 0, b, rows), 6, to_c)
    yb = send(low, slot(y, 0, b), 2, to_y)
    xb = send(high, slot(y, 1, b), 3, to_x)
    own.start()
    xa.wait_recv()
    piece = slot(y, 0, b ^ 2)
    yc = send(piece, piece, 4, to_y)
    c1 = send(piece, piece, 7, to_c)
    ya.wait_recv()
    piece = slot(y ^ 1, 1, b)
    xc = send(piece, piece, 5, to_x)
    c2 = send(piece, piece, 8, to_c)
    yb.wait_recv()
    piece = slot(y ^ 1, 0, b)
    c3 = send(piece, piece, 9, to_c)
    xb.wait_recv()
    piece = slot(y, 1, b ^ 2)
    c4 = send(piece, piece, 10, to_c)
    yc.wait_recv()
    piece = slot(y ^ 1, 0, b ^ 2)
    c5 = send(piece, piece, 11, to_c)
    xc.wait_recv()
    piece = slot(y ^ 1, 1, b ^ 2)
    c6 = send(piece, piece, 12, to_c)
    for copy in (c0, c1, c2, c3, c4, c5, c6):
        copy.wait_recv()
    for copy in started:
        copy.wait_send()
    own.wait()


def gather_wide(values, number, name):
    rows, width = values.shape
    return pl.pallas_call(
        gather_kernel,
        name=name,
        out_shape=jax.ShapeDtypeStruct((2 * rows, 4 * width), values.dtype),
        in_specs=[pl.BlockSpec(memory_space=pltpu.VMEM)],
        out_specs=pl.BlockSpec(memory_space=pl.ANY),
        scratch_shapes=[
            pltpu.SemaphoreType.DMA,
            pltpu.SemaphoreType.DMA((13,)),
            pltpu.SemaphoreType.DMA((13,)),
        ],
        compiler_params=pltpu.CompilerParams(collective_id=number, has_side_effects=True),
        cost_estimate=pl.CostEstimate(flops=0, bytes_accessed=60_000_000, transcendentals=0),
    )(values)


def scatter_kernel(p_ref, out_ref, rc, s1, ry, rx, s2, fy, fx, send_sem, recv_sem):
    rows, width = out_ref.shape
    half = rows // 2
    y, b = side("dp"), lax.axis_index("col")
    x, c = b >> 1, b & 1
    to_x, to_y, to_c = {"col": flip("col", 2)}, {"dp": flip("dp", 1)}, {"col": flip("col", 1)}
    greet([to_x, to_y, to_c])
    started = []

    def send(src, dst, number, peer):
        copy = pltpu.make_async_remote_copy(
            src_ref=src,
            dst_ref=dst,
            send_sem=send_sem.at[number],
            recv_sem=recv_sem.at[number],
            device_id=peer,
            device_id_type=MESH,
        )
        copy.start()
        started.append(copy)
        return copy

    def place(yy, h):
        return pl.ds(pl.multiple_of(yy * rows + h * half, half), half)

    def column(bb):
        return pl.ds(pl.multiple_of(bb * width, width), width)

    order = [(0, y ^ 1, 0), (1, y ^ 1, 0), (x ^ 1, 0, 1), (x ^ 1, 1, 1)]
    order += [(0, y, 0), (1, y, 0), (x, 0, 1), (x, 1, 1)]
    core = []
    for number, (xx, yy, h) in enumerate(order):
        core.append(
            send(
                p_ref.at[place(yy, h), column(2 * xx + (c ^ 1))],
                rc.at[xx, place(yy, h)],
                number,
                to_c,
            )
        )

    def settle(number):
        core[number].wait_recv()
        xx, yy, h = order[number]
        s1[xx, place(yy, h), :] = (
            p_ref[place(yy, h), column(2 * xx + c)].astype(f32)
            + rc[xx, place(yy, h), :].astype(f32)
        ).astype(s1.dtype)

    settle(0)
    settle(1)
    ya = send(s1.at[:, place(y ^ 1, 0), :], ry, 8, to_y)
    settle(2)
    settle(3)
    lower = s1.at[x ^ 1, pl.ds(half, half), :]
    upper = s1.at[x ^ 1, pl.ds(rows + half, half), :]
    xa0 = send(lower, rx.at[0], 9, to_x)
    xa1 = send(upper, rx.at[1], 10, to_x)
    settle(4)
    settle(5)
    settle(6)
    settle(7)
    ya.wait_recv()
    s2[0] = (s1[x ^ 1, place(y, 0), :].astype(f32) + ry[x ^ 1].astype(f32)).astype(s2.dtype)
    xb = send(s2.at[0], fx, 11, to_x)
    xa0.wait_recv()
    xa1.wait_recv()
    s2[1] = (s1[x, place(y ^ 1, 1), :].astype(f32) + rx[y ^ 1].astype(f32)).astype(s2.dtype)
    yb = send(s2.at[1], fy, 12, to_y)
    keep0 = s1[x, place(y, 0), :].astype(f32) + ry[x].astype(f32)
    xb.wait_recv()
    out_ref[pl.ds(0, half), :] = keep0 + fx[...].astype(f32)
    keep1 = s1[x, place(y, 1), :].astype(f32) + rx[y].astype(f32)
    yb.wait_recv()
    out_ref[pl.ds(half, half), :] = keep1 + fy[...].astype(f32)
    for copy in started:
        copy.wait_send()


def scatter_wide(partial, number, name):
    rows, width = partial.shape[0] // 2, partial.shape[1] // 4
    half = rows // 2
    return pl.pallas_call(
        scatter_kernel,
        name=name,
        out_shape=jax.ShapeDtypeStruct((rows, width), f32),
        in_specs=[pl.BlockSpec(memory_space=pltpu.VMEM)],
        out_specs=pl.BlockSpec(memory_space=pltpu.VMEM),
        scratch_shapes=[
            pltpu.VMEM((2, 2 * rows, width), bf16),
            pltpu.VMEM((2, 2 * rows, width), bf16),
            pltpu.VMEM((2, half, width), bf16),
            pltpu.VMEM((2, half, width), bf16),
            pltpu.VMEM((2, half, width), bf16),
            pltpu.VMEM((half, width), bf16),
            pltpu.VMEM((half, width), bf16),
            pltpu.SemaphoreType.DMA((13,)),
            pltpu.SemaphoreType.DMA((13,)),
        ],
        compiler_params=pltpu.CompilerParams(
            collective_id=number, has_side_effects=True, vmem_limit_bytes=40 * 2**20
        ),
        cost_estimate=pl.CostEstimate(flops=0, bytes_accessed=80_000_000, transcendentals=0),
    )(partial)


def total_kernel(wide, v_ref, out_ref, slots, send_sem, recv_sem):
    b = lax.axis_index("col")
    y = side("dp")
    me = y * 4 + b if wide else b
    count = 8 if wide else 4
    peers = []
    for d in range(1, count):
        peer = {"col": flip("col", d & 3)}
        if wide and d >> 2:
            peer["dp"] = flip("dp", 1)
        peers.append(peer)
    greet(peers)
    copies = []
    for d, peer in enumerate(peers):
        copy = pltpu.make_async_remote_copy(
            src_ref=v_ref,
            dst_ref=slots.at[me],
            send_sem=send_sem.at[d],
            recv_sem=recv_sem.at[d],
            device_id=peer,
            device_id_type=MESH,
        )
        copy.start()
        copies.append(copy)
    slots[me] = v_ref[...]
    for copy in copies:
        copy.wait_recv()
    total = slots[0]
    for i in range(1, count):
        total = total + slots[i]
    out_ref[...] = total
    for copy in copies:
        copy.wait_send()


def feature_total(values, wide, number, name):
    k, t = values.shape
    count = 8 if wide else 4
    flat = values.reshape(k * t // 128, 128)
    total = pl.pallas_call(
        functools.partial(total_kernel, wide),
        name=name,
        out_shape=jax.ShapeDtypeStruct(flat.shape, f32),
        in_specs=[pl.BlockSpec(memory_space=pltpu.VMEM)],
        out_specs=pl.BlockSpec(memory_space=pltpu.VMEM),
        scratch_shapes=[
            pltpu.VMEM((count,) + flat.shape, f32),
            pltpu.SemaphoreType.DMA((count - 1,)),
            pltpu.SemaphoreType.DMA((count - 1,)),
        ],
        compiler_params=pltpu.CompilerParams(collective_id=number, has_side_effects=True),
    )(flat)
    return total.reshape(k, t)


def turn_kernel(x_ref, out_ref, local_sem, send_sem, recv_sem):
    z = lax.axis_index("row")
    peers = [{"row": flip("row", d)} for d in (1, 2, 3)]
    greet(peers)
    copies = []
    for d in (3, 2, 1):
        copy = pltpu.make_async_remote_copy(
            src_ref=x_ref.at[z ^ d],
            dst_ref=out_ref.at[z],
            send_sem=send_sem.at[d - 1],
            recv_sem=recv_sem.at[d - 1],
            device_id={"row": flip("row", d)},
            device_id_type=MESH,
        )
        copy.start()
        copies.append(copy)
    own = pltpu.make_async_copy(x_ref.at[z], out_ref.at[z], local_sem)
    own.start()
    for copy in copies:
        copy.wait()
    own.wait()


def turn(values, number, name):
    return pl.pallas_call(
        turn_kernel,
        name=name,
        out_shape=jax.ShapeDtypeStruct(values.shape, values.dtype),
        in_specs=[pl.BlockSpec(memory_space=pltpu.VMEM)],
        out_specs=pl.BlockSpec(memory_space=pl.ANY),
        scratch_shapes=[
            pltpu.SemaphoreType.DMA,
            pltpu.SemaphoreType.DMA((3,)),
            pltpu.SemaphoreType.DMA((3,)),
        ],
        compiler_params=pltpu.CompilerParams(collective_id=number, has_side_effects=True),
        cost_estimate=pl.CostEstimate(flops=0, bytes_accessed=100_000_000, transcendentals=0),
    )(values)


def swap_kernel(x_ref, out_ref, send_sem, recv_sem):
    peer = {"dp": flip("dp", 1)}
    greet([peer])
    copy = pltpu.make_async_remote_copy(
        src_ref=x_ref,
        dst_ref=out_ref,
        send_sem=send_sem,
        recv_sem=recv_sem,
        device_id=peer,
        device_id_type=MESH,
    )
    copy.start()
    copy.wait()


BLOCK = 512


def allow(i0, j0, length, bq, bk):
    rows = i0 + lax.broadcasted_iota(jnp.int32, (bk, bq), 1)
    cols = j0 + lax.broadcasted_iota(jnp.int32, (bk, bq), 0)
    return (cols <= rows) & (cols < length)


def attend_kernel(len_ref, q_ref, k_ref, v_ref, o_ref, o32_ref, lse_ref):
    i = pl.program_id(0)
    bq, bk = q_ref.shape[0], BLOCK
    length = len_ref[0]
    scale = HEAD_DIM ** (-0.5)
    q = q_ref[...]
    rows = i * bq + lax.broadcasted_iota(jnp.int32, (bq, bk), 0)
    cols0 = lax.broadcasted_iota(jnp.int32, (bq, bk), 1)

    def step(j, carry, masked):
        top, total, acc = carry
        j0 = pl.multiple_of(j * bk, bk)
        scores = contract_last(q, k_ref[pl.ds(j0, bk), :]) * scale
        if masked:
            cols = j0 + cols0
            scores = jnp.where((cols <= rows) & (cols < length), scores, masked_score)
        new = jnp.maximum(top, jnp.max(scores, axis=1, keepdims=True))
        weights = jnp.exp(scores - new)
        fix = jnp.exp(top - new)
        total = total * fix + jnp.sum(weights, axis=1, keepdims=True)
        acc = acc * fix + matmul(weights.astype(bf16), v_ref[pl.ds(j0, bk), :])
        return new, total, acc

    carry = (
        jnp.full((bq, 1), -jnp.inf, f32),
        jnp.zeros((bq, 1), f32),
        jnp.zeros((bq, HEAD_DIM), f32),
    )
    whole = jnp.minimum(i, length // bk)
    last = jnp.minimum(i + 1, (length + bk - 1) // bk)
    carry = lax.fori_loop(0, whole, lambda j, s: step(j, s, False), carry)
    top, total, acc = lax.fori_loop(whole, last, lambda j, s: step(j, s, True), carry)
    out = acc / total
    o_ref[...] = out.astype(bf16)
    o32_ref[...] = out
    lse_ref[...] = jnp.broadcast_to((top + jnp.log(total)).T, lse_ref.shape)


def attend(length, q, k, v):
    slots = q.shape[0]
    whole = pl.BlockSpec((slots, HEAD_DIM), lambda i: (0, 0))
    part = pl.BlockSpec((BLOCK, HEAD_DIM), lambda i: (i, 0))
    return pl.pallas_call(
        attend_kernel,
        name="attend",
        grid=(slots // BLOCK,),
        out_shape=(
            jax.ShapeDtypeStruct((slots, HEAD_DIM), bf16),
            jax.ShapeDtypeStruct((slots, HEAD_DIM), f32),
            jax.ShapeDtypeStruct((8, slots), f32),
        ),
        in_specs=[pl.BlockSpec(memory_space=pltpu.SMEM), part, whole, whole],
        out_specs=(part, part, pl.BlockSpec((8, BLOCK), lambda i: (0, i))),
        cost_estimate=pl.CostEstimate(
            flops=2 * slots * slots * HEAD_DIM,
            bytes_accessed=8 * slots * HEAD_DIM,
            transcendentals=slots * slots // 2,
        ),
    )(length, q, k, v)


def attend_back_kernel(
    len_ref, q_ref, k_ref, v_ref, do_ref, lse_ref, delta_ref, dq_ref, dk_ref, dv_ref, dq_acc
):
    j = pl.program_id(0)
    bk, bq = k_ref.shape[0], BLOCK
    slots = q_ref.shape[0]
    length = len_ref[0]
    scale = HEAD_DIM ** (-0.5)

    @pl.when(j == 0)
    def _():
        dq_acc[...] = jnp.zeros_like(dq_acc)

    k, v = k_ref[...], v_ref[...]
    j0 = j * bk
    cols = j0 + lax.broadcasted_iota(jnp.int32, (bk, bq), 0)
    rows0 = lax.broadcasted_iota(jnp.int32, (bk, bq), 1)

    def step(i, carry, masked):
        dk, dv = carry
        i0 = pl.multiple_of(i * bq, bq)
        here = pl.ds(i0, bq)
        q, do = q_ref[here, :], do_ref[here, :]
        scores = contract_last(k, q) * scale
        probs = jnp.exp(scores - lse_ref[0:1, here])
        if masked:
            probs = jnp.where((cols <= i0 + rows0) & (cols < length), probs, 0.0)
        dv = dv + matmul(probs.astype(bf16), do)
        d_probs = contract_last(v, do)
        d_scores = (probs * (d_probs - delta_ref[0:1, here])).astype(bf16)
        dk = dk + matmul(d_scores, q)
        dq_acc[here, :] += contract_first(d_scores, k)
        return dk, dv

    zero = jnp.zeros((bk, HEAD_DIM), f32)
    top = slots // bq
    inside = j0 + bk <= length
    first = jnp.where(inside, j + 1, top)
    first = jnp.where(j0 < length, first, j)
    carry = lax.fori_loop(j, first, lambda i, s: step(i, s, True), (zero, zero))
    stop = jnp.where(j0 < length, top, j)
    dk, dv = lax.fori_loop(first, stop, lambda i, s: step(i, s, False), carry)
    dk_ref[...] = (dk * scale).astype(bf16)
    dv_ref[...] = dv.astype(bf16)

    @pl.when(j == pl.num_programs(0) - 1)
    def _():
        dq_ref[...] = (dq_acc[...] * scale).astype(bf16)


def attend_back(length, q, k, v, do, lse, delta):
    slots = q.shape[0]
    whole = pl.BlockSpec((slots, HEAD_DIM), lambda j: (0, 0))
    part = pl.BlockSpec((BLOCK, HEAD_DIM), lambda j: (j, 0))
    line = pl.BlockSpec((8, slots), lambda j: (0, 0))
    shape = jax.ShapeDtypeStruct((slots, HEAD_DIM), bf16)
    return pl.pallas_call(
        attend_back_kernel,
        name="attend_back",
        grid=(slots // BLOCK,),
        out_shape=(shape, shape, shape),
        in_specs=[pl.BlockSpec(memory_space=pltpu.SMEM), whole, part, part, whole, line, line],
        out_specs=(whole, part, part),
        scratch_shapes=[pltpu.VMEM((slots, HEAD_DIM), f32)],
        cost_estimate=pl.CostEstimate(
            flops=5 * slots * slots * HEAD_DIM,
            bytes_accessed=14 * slots * HEAD_DIM,
            transcendentals=slots * slots // 2,
        ),
    )(length, q, k, v, do, lse, delta)


def per_device(
    tokens,
    seq_lengths,
    w_query,
    w_key,
    w_value,
    w_out,
    w_gate,
    w_up,
    w_down,
    q_gain,
    k_gain,
    attn_gain,
    mlp_gain,
    cotangent,
):
    tok_rows, feat_part = tokens.shape
    row_count, data_count = lax.axis_size("row"), lax.axis_size("dp")
    width = feat_part * lax.axis_size("col")
    slots = tok_rows * row_count
    half_feat = feat_part // 2
    y, z = side("dp"), lax.axis_index("row")
    heads = half_feat // HEAD_DIM
    units = 2 * heads
    pairs = [(i, i ^ 1) for i in range(data_count)]

    def y_half(values, axis):
        size = values.shape[axis] // 2
        return lax.dynamic_slice_in_dim(values, y * size, size, axis)

    qkv_weight = lax.all_gather(
        jnp.concatenate([y_half(w_query, 1), y_half(w_key, 1), y_half(w_value, 1)], axis=1),
        "row",
        axis=0,
        tiled=True,
    )
    out_weight = lax.all_gather(y_half(w_out, 0), "row", axis=1, tiled=True)
    gate_weight = lax.all_gather(y_half(w_gate, 1), "row", axis=0, tiled=True)
    up_weight = lax.all_gather(y_half(w_up, 1), "row", axis=0, tiled=True)
    down_weight = lax.all_gather(y_half(w_down, 0), "row", axis=1, tiled=True)

    positions = z * tok_rows + jnp.arange(tok_rows)
    length = seq_lengths[0]
    valid = (positions < length).astype(f32)[:, None]
    cosine, sine = rope_tables(positions, HEAD_DIM)
    cosine, sine = jnp.concatenate([cosine, cosine]), jnp.concatenate([sine, sine])
    other_length = lax.ppermute(seq_lengths, "dp", pairs)
    pair_lengths = jnp.where(
        y == 0,
        jnp.concatenate([seq_lengths, other_length]),
        jnp.concatenate([other_length, seq_lengths]),
    )
    unit_length = lax.dynamic_slice_in_dim(pair_lengths, z // heads, 1)

    def to_units(*arrays):
        parts = [
            a.reshape(2, tok_rows, heads, HEAD_DIM).transpose(0, 2, 1, 3).reshape(
                units, 1, tok_rows, HEAD_DIM
            )
            for a in arrays
        ]
        return jnp.concatenate(parts, axis=1)

    def from_units(values):
        return [
            values[:, i]
            .reshape(2, heads, tok_rows, HEAD_DIM)
            .transpose(0, 2, 1, 3)
            .reshape(2 * tok_rows, heads * HEAD_DIM)
            for i in range(values.shape[1])
        ]

    def as_slots(values, i):
        return values[:, i].reshape(slots, HEAD_DIM)

    tokens_wide = gather_wide(tokens, 0, "gather_tokens")
    qkv = matmul(tokens_wide, qkv_weight)
    query_pre, key_pre, value_pre = (
        qkv[:, :half_feat],
        qkv[:, half_feat : 2 * half_feat],
        qkv[:, 2 * half_feat :],
    )
    squares = feature_total(
        jnp.stack([jnp.sum(query_pre * query_pre, axis=1), jnp.sum(key_pre * key_pre, axis=1)]),
        True,
        1,
        "total_qk",
    )
    inverse = lax.rsqrt(squares / width + norm_eps)
    query_inv, key_inv = inverse[0][:, None], inverse[1][:, None]
    q_gain_half, k_gain_half = y_half(q_gain, 0), y_half(k_gain, 0)
    query_rot = rotate(query_pre * query_inv * q_gain_half, cosine, sine, HEAD_DIM).astype(bf16)
    key_rot = rotate(key_pre * key_inv * k_gain_half, cosine, sine, HEAD_DIM).astype(bf16)
    turned = turn(to_units(query_rot, key_rot, value_pre.astype(bf16)), 2, "turn_qkv")
    q_unit, k_unit, v_unit = (as_slots(turned, i) for i in range(3))
    attn_unit, attn_exact, log_total = attend(unit_length, q_unit, k_unit, v_unit)
    (attn_low,) = from_units(
        turn(attn_unit.reshape(row_count, 1, tok_rows, HEAD_DIM), 3, "turn_attn")
    )
    branch = scatter_wide(matmul(attn_low, out_weight).astype(bf16), 4, "scatter_branch")
    branch_inv = lax.rsqrt(
        feature_total(jnp.sum(branch * branch, axis=1)[None, :], False, 5, "total_branch")[0]
        / width
        + norm_eps
    )[:, None]
    resid = tokens.astype(f32) + branch * branch_inv * attn_gain
    resid_wide = gather_wide(resid.astype(bf16), 6, "gather_resid")
    gate = matmul(resid_wide, gate_weight)
    upper = matmul(resid_wide, up_weight)
    sigma = jax.nn.sigmoid(gate)
    hidden = (gate * sigma * upper).astype(bf16)
    mixed = scatter_wide(matmul(hidden, down_weight).astype(bf16), 7, "scatter_mixed")
    incoming = cotangent.astype(f32) * valid
    gained = incoming * mlp_gain
    sums = feature_total(
        jnp.stack([jnp.sum(mixed * mixed, axis=1), jnp.sum(gained * mixed, axis=1)]),
        False,
        8,
        "total_mixed",
    )
    mixed_inv = lax.rsqrt(sums[0] / width + norm_eps)[:, None]
    inner = (sums[1] / width)[:, None]
    block_output = ((resid + mixed * mixed_inv * mlp_gain) * valid).astype(bf16)
    mlp_gain_raw = jnp.sum(incoming * mixed * mixed_inv, axis=0)
    d_mixed = (mixed_inv * gained - mixed * mixed_inv**3 * inner).astype(bf16)
    d_mixed_wide = gather_wide(d_mixed, 9, "gather_d_mixed")

    factor = 1.0 / math.sqrt(slots * data_count)

    def reduce_rows(raw, axis):
        return lax.psum_scatter(
            (raw * factor).astype(bf16), "row", scatter_dimension=axis, tiled=True
        )

    down_piece = reduce_rows(contract_first(hidden, d_mixed_wide), 1)
    d_hidden = contract_last(d_mixed_wide, down_weight)
    d_gate = (d_hidden * upper * sigma * (1.0 + gate * (1.0 - sigma))).astype(bf16)
    d_upper = (d_hidden * gate * sigma).astype(bf16)
    gate_piece = reduce_rows(contract_first(resid_wide, d_gate), 0)
    up_piece = reduce_rows(contract_first(resid_wide, d_upper), 0)
    d_resid = incoming + scatter_wide(
        (contract_last(d_gate, gate_weight) + contract_last(d_upper, up_weight)).astype(bf16),
        10,
        "scatter_d_resid",
    )
    attn_gain_raw = jnp.sum(d_resid * branch * branch_inv, axis=0)
    gained = d_resid * attn_gain
    inner = (
        feature_total(jnp.sum(gained * branch, axis=1)[None, :], False, 11, "total_d_resid")[0][
            :, None
        ]
        / width
    )
    d_branch = (branch_inv * gained - branch * branch_inv**3 * inner).astype(bf16)
    d_branch_wide = gather_wide(d_branch, 12, "gather_d_branch")
    d_attn = contract_last(d_branch_wide, out_weight).astype(bf16)
    d_attn_unit = as_slots(turn(to_units(d_attn), 13, "turn_d_attn"), 0)
    out_piece = reduce_rows(contract_first(attn_low, d_branch_wide), 1)
    delta = jnp.sum(d_attn_unit.astype(f32) * attn_exact, axis=1)
    delta = jnp.broadcast_to(delta[None, :], (8, slots))
    d_units = attend_back(unit_length, q_unit, k_unit, v_unit, d_attn_unit, log_total, delta)
    d_units = jnp.stack([d.reshape(row_count, tok_rows, HEAD_DIM) for d in d_units], axis=1)
    d_query_rot, d_key_rot, d_value = from_units(turn(d_units, 14, "turn_d_qkv"))
    d_query_norm = unrotate(d_query_rot.astype(f32), cosine, sine, HEAD_DIM)
    d_key_norm = unrotate(d_key_rot.astype(f32), cosine, sine, HEAD_DIM)
    q_gain_raw = jnp.sum(d_query_norm * query_pre * query_inv, axis=0)
    k_gain_raw = jnp.sum(d_key_norm * key_pre * key_inv, axis=0)
    query_scaled = d_query_norm * q_gain_half
    key_scaled = d_key_norm * k_gain_half
    inner = (
        feature_total(
            jnp.stack(
                [jnp.sum(query_scaled * query_pre, axis=1), jnp.sum(key_scaled * key_pre, axis=1)]
            ),
            True,
            15,
            "total_d_qk",
        )
        / width
    )
    d_query = (query_inv * query_scaled - query_pre * query_inv**3 * inner[0][:, None]).astype(
        bf16
    )
    d_key = (key_inv * key_scaled - key_pre * key_inv**3 * inner[1][:, None]).astype(bf16)
    d_qkv = jnp.concatenate([d_query, d_key, d_value], axis=1)
    qkv_piece = reduce_rows(contract_first(tokens_wide, d_qkv), 0)
    projected = contract_last(d_qkv, qkv_weight).astype(bf16)
    d_resid_total = scatter_wide(projected, 16, "scatter_projected")
    input_grad = d_resid + d_resid_total

    def spread(half):
        return lax.dynamic_update_slice_in_dim(jnp.zeros((feat_part,), f32), half, y * half_feat, 0)

    gains = lax.psum(
        jnp.stack([spread(q_gain_raw), spread(k_gain_raw), attn_gain_raw, mlp_gain_raw]) * factor,
        ("dp", "row"),
    )

    def finish(piece, axis):
        if data_count > 2:
            groups = [list(range(s, data_count, 2)) for s in (0, 1)]
            piece = lax.psum(piece, "dp", axis_index_groups=groups)
        other = lax.ppermute(piece, "dp", pairs)
        low = jnp.where(y == 0, piece, other).astype(f32)
        high = jnp.where(y == 0, other, piece).astype(f32)
        return jnp.concatenate([low, high], axis=axis)

    def columns(i):
        return qkv_piece[:, i * half_feat : (i + 1) * half_feat]

    return (
        block_output,
        input_grad,
        finish(columns(0), 1),
        finish(columns(1), 1),
        finish(columns(2), 1),
        finish(out_piece, 0),
        finish(gate_piece, 1),
        finish(up_piece, 1),
        finish(down_piece, 0),
        gains[0],
        gains[1],
        gains[2],
        gains[3],
    )


def solution(mesh):
    tok, row_col, col_row, gain = P(("dp", "row"), "col"), P("row", "col"), P("col", "row"), P("col")
    weights = (row_col, row_col, row_col, col_row, row_col, row_col, col_row)
    gains = (gain, gain, gain, gain)
    return jax.shard_map(
        per_device,
        mesh=mesh,
        in_specs=(tok, P("dp")) + weights + gains + (tok,),
        out_specs=(tok, tok) + weights + gains,
        check_vma=False,
    )
```

```python
import functools
import math

import jax
import jax.numpy as jnp
from jax import lax
from jax.experimental import pallas as pl
from jax.experimental.pallas import tpu as pltpu
from jax.sharding import PartitionSpec as P

HEAD_DIM = 128
rope_base = 500000.0
norm_eps = 1e-06
masked_score = -1e30

MESH = pl.DeviceIdType.MESH
bf16 = jnp.bfloat16
f32 = jnp.float32


def rope_tables(positions, head_dim):
    half = head_dim // 2
    freq = 1.0 / rope_base ** (jnp.arange(half, dtype=f32) / half)
    angle = positions.astype(f32)[:, None] * freq[None, :]
    angle = jnp.concatenate([angle, angle], axis=1)
    return (jnp.cos(angle), jnp.sin(angle))


def matmul(left, right):
    return jnp.dot(left, right, preferred_element_type=f32)


def contract_first(left, right):
    return lax.dot_general(left, right, (((0,), (0,)), ((), ())), preferred_element_type=f32)


def contract_last(left, right):
    return lax.dot_general(left, right, (((1,), (1,)), ((), ())), preferred_element_type=f32)


def flip(axis, bit):
    return lax.axis_index(axis) ^ bit


def side(axis):
    return lax.axis_index(axis) & 1


def greet(peers):
    barrier = pltpu.get_barrier_semaphore()
    for peer in peers:
        pl.semaphore_signal(barrier, inc=1, device_id=peer, device_id_type=MESH)
    pl.semaphore_wait(barrier, len(peers))


def sender(send_sem, recv_sem, started):
    def send(src, dst, number, peer):
        copy = pltpu.make_async_remote_copy(
            src_ref=src,
            dst_ref=dst,
            send_sem=send_sem.at[number],
            recv_sem=recv_sem.at[number],
            device_id=peer,
            device_id_type=MESH,
        )
        copy.start()
        started.append(copy)
        return copy

    return send


def neighbours():
    return {"col": flip("col", 2)}, {"dp": flip("dp", 1)}, {"col": flip("col", 1)}


def gather_kernel(pair, x_ref, out_ref, local_sem, send_sem, recv_sem):
    rows, width = x_ref.shape
    half = rows // 2
    y, b, p = side("dp"), lax.axis_index("col"), side("row") if pair else 0
    to_x, to_y, to_c = neighbours()
    to_z = {"row": flip("row", 1)}
    greet([to_x, to_y, to_c] + ([to_z] if pair else []))
    started = []
    send = sender(send_sem, recv_sem, started)

    def slot(pp, yy, h, bb, n=half):
        return out_ref.at[
            pl.ds(pl.multiple_of((pp * 2 + yy) * rows + h * half, half), n),
            pl.ds(pl.multiple_of(bb * width, width), width),
        ]

    def open_flow(pp, low, high, base):
        xa = send(low, slot(pp, y, 0, b), base + 0, to_x)
        ya = send(high, slot(pp, y, 1, b), base + 1, to_y)
        c0 = send(low, slot(pp, y, 0, b), base + 6, to_c)
        yb = send(low, slot(pp, y, 0, b), base + 2, to_y)
        xb = send(high, slot(pp, y, 1, b), base + 3, to_x)
        c1 = send(high, slot(pp, y, 1, b), base + 7, to_c)
        return xa, ya, xb, yb, [c0, c1]

    def relay(pp, flow, base):
        xa, ya, xb, yb, core = flow
        xa.wait_recv()
        piece = slot(pp, y, 0, b ^ 2)
        yc = send(piece, piece, base + 4, to_y)
        core.append(send(piece, piece, base + 8, to_c))
        ya.wait_recv()
        piece = slot(pp, y ^ 1, 1, b)
        xc = send(piece, piece, base + 5, to_x)
        core.append(send(piece, piece, base + 9, to_c))
        yb.wait_recv()
        piece = slot(pp, y ^ 1, 0, b)
        core.append(send(piece, piece, base + 10, to_c))
        xb.wait_recv()
        piece = slot(pp, y, 1, b ^ 2)
        core.append(send(piece, piece, base + 11, to_c))
        return yc, xc, core

    def close_flow(pp, state, base):
        yc, xc, core = state
        yc.wait_recv()
        piece = slot(pp, y ^ 1, 0, b ^ 2)
        core.append(send(piece, piece, base + 12, to_c))
        xc.wait_recv()
        piece = slot(pp, y ^ 1, 1, b ^ 2)
        core.append(send(piece, piece, base + 13, to_c))
        for copy in core:
            copy.wait_recv()

    low, high = x_ref.at[pl.ds(0, half)], x_ref.at[pl.ds(half, half)]
    own = pltpu.make_async_copy(x_ref, slot(p, y, 0, b, rows), local_sem)
    if pair:
        z0 = send(low, slot(p, y, 0, b), 28, to_z)
        z1 = send(high, slot(p, y, 1, b), 29, to_z)
    first = open_flow(p, low, high, 0)
    own.start()
    state = relay(p, first, 0)
    if pair:
        z0.wait_recv()
        z1.wait_recv()
        second = open_flow(p ^ 1, slot(p ^ 1, y, 0, b), slot(p ^ 1, y, 1, b), 14)
    close_flow(p, state, 0)
    if pair:
        close_flow(p ^ 1, relay(p ^ 1, second, 14), 14)
    for copy in started:
        copy.wait_send()
    own.wait()


def gather_wide(values, pair, number, name):
    rows, width = values.shape
    copies = 30 if pair else 14
    return pl.pallas_call(
        functools.partial(gather_kernel, pair),
        name=name,
        out_shape=jax.ShapeDtypeStruct(((4 if pair else 2) * rows, 4 * width), values.dtype),
        in_specs=[pl.BlockSpec(memory_space=pltpu.VMEM)],
        out_specs=pl.BlockSpec(memory_space=pl.ANY),
        scratch_shapes=[
            pltpu.SemaphoreType.DMA,
            pltpu.SemaphoreType.DMA((copies,)),
            pltpu.SemaphoreType.DMA((copies,)),
        ],
        compiler_params=pltpu.CompilerParams(collective_id=number, has_side_effects=True),
        cost_estimate=pl.CostEstimate(flops=0, bytes_accessed=60_000_000, transcendentals=0),
    )(values)


def scatter_kernel(pair, p_ref, out_ref, rc, s1, ry, rx, s2, fy, fx, sz, fz, send_sem, recv_sem):
    rows, width = out_ref.shape
    half = rows // 2
    y, b, p = side("dp"), lax.axis_index("col"), side("row") if pair else 0
    x, c = b >> 1, b & 1
    to_x, to_y, to_c = neighbours()
    to_z = {"row": flip("row", 1)}
    greet([to_x, to_y, to_c] + ([to_z] if pair else []))
    started = []
    send = sender(send_sem, recv_sem, started)

    def place(yy, h):
        return pl.ds(pl.multiple_of(yy * rows + h * half, half), half)

    def column(bb):
        return pl.ds(pl.multiple_of(bb * width, width), width)

    order = [(0, y ^ 1, 0), (1, y ^ 1, 0), (x ^ 1, 0, 1), (x ^ 1, 1, 1)]
    order += [(0, y, 0), (1, y, 0), (x, 0, 1), (x, 1, 1)]

    class Flow:
        def __init__(self, f, pp):
            self.f, self.base = f, 14 * f
            self.rows = lambda yy, h: pl.ds(
                pl.multiple_of((pp * 2 + yy) * rows + h * half, half), half
            )
            self.core = [
                send(
                    p_ref.at[self.rows(yy, h), column(2 * xx + (c ^ 1))],
                    rc.at[f, xx, place(yy, h)],
                    self.base + number,
                    to_c,
                )
                for number, (xx, yy, h) in enumerate(order)
            ]

        def settle(self, *numbers):
            for number in numbers:
                self.core[number].wait_recv()
                xx, yy, h = order[number]
                s1[self.f, xx, place(yy, h), :] = (
                    p_ref[self.rows(yy, h), column(2 * xx + c)].astype(f32)
                    + rc[self.f, xx, place(yy, h), :].astype(f32)
                ).astype(s1.dtype)

        def first(self, i):
            f = self.f
            ya = send(s1.at[f, i, place(y ^ 1, 0), :], ry.at[f, i], self.base + 8 + i, to_y)
            part = s1.at[f, x ^ 1, pl.ds(i * rows + half, half), :]
            xa = send(part, rx.at[f, i], self.base + 10 + i, to_x)
            return ya, xa

        def second(self, copies):
            f = self.f
            for ya, _ in copies:
                ya.wait_recv()
            s2[f, 0] = (
                s1[f, x ^ 1, place(y, 0), :].astype(f32) + ry[f, x ^ 1].astype(f32)
            ).astype(s2.dtype)
            xb = send(s2.at[f, 0], fx.at[f], self.base + 12, to_x)
            for _, xa in copies:
                xa.wait_recv()
            s2[f, 1] = (
                s1[f, x, place(y ^ 1, 1), :].astype(f32) + rx[f, y ^ 1].astype(f32)
            ).astype(s2.dtype)
            yb = send(s2.at[f, 1], fy.at[f], self.base + 13, to_y)
            return xb, yb

        def last(self, copies):
            f = self.f
            xb, yb = copies
            keep = s1[f, x, place(y, 0), :].astype(f32) + ry[f, x].astype(f32)
            xb.wait_recv()
            low = keep + fx[f].astype(f32)
            keep = s1[f, x, place(y, 1), :].astype(f32) + rx[f, y].astype(f32)
            yb.wait_recv()
            return low, keep + fy[f].astype(f32)

    if pair:
        far = Flow(0, p ^ 1)
        near = Flow(1, p)
        far.settle(0, 1, 2, 3)
        far_first = [far.first(0), far.first(1)]
        far.settle(4, 5, 6, 7)
        near.settle(0, 1, 2, 3)
        near_first = [near.first(0)]
        near.settle(4, 5, 6, 7)
        far_second = far.second(far_first)
        near_first.append(near.first(1))
        low, high = far.last(far_second)
        sz[pl.ds(0, half), :] = low.astype(bf16)
        z0 = send(sz.at[pl.ds(0, half)], fz.at[pl.ds(0, half)], 28, to_z)
        sz[pl.ds(half, half), :] = high.astype(bf16)
        z1 = send(sz.at[pl.ds(half, half)], fz.at[pl.ds(half, half)], 29, to_z)
        low, high = near.last(near.second(near_first))
        z0.wait_recv()
        out_ref[pl.ds(0, half), :] = low + fz[pl.ds(0, half), :].astype(f32)
        z1.wait_recv()
        out_ref[pl.ds(half, half), :] = high + fz[pl.ds(half, half), :].astype(f32)
    else:
        near = Flow(0, 0)
        near.settle(0, 1, 2, 3)
        near_first = [near.first(0), near.first(1)]
        near.settle(4, 5, 6, 7)
        low, high = near.last(near.second(near_first))
        out_ref[pl.ds(0, half), :] = low
        out_ref[pl.ds(half, half), :] = high
    for copy in started:
        copy.wait_send()


def scatter_wide(partial, pair, number, name):
    flows = 2 if pair else 1
    rows, width = partial.shape[0] // (2 * flows), partial.shape[1] // 4
    half = rows // 2
    copies = 30 if pair else 14
    last = (rows, width) if pair else (16, 128)
    return pl.pallas_call(
        functools.partial(scatter_kernel, pair),
        name=name,
        out_shape=jax.ShapeDtypeStruct((rows, width), f32),
        in_specs=[pl.BlockSpec(memory_space=pltpu.VMEM)],
        out_specs=pl.BlockSpec(memory_space=pltpu.VMEM),
        scratch_shapes=[
            pltpu.VMEM((flows, 2, 2 * rows, width), bf16),
            pltpu.VMEM((flows, 2, 2 * rows, width), bf16),
            pltpu.VMEM((flows, 2, half, width), bf16),
            pltpu.VMEM((flows, 2, half, width), bf16),
            pltpu.VMEM((flows, 2, half, width), bf16),
            pltpu.VMEM((flows, half, width), bf16),
            pltpu.VMEM((flows, half, width), bf16),
            pltpu.VMEM(last, bf16),
            pltpu.VMEM(last, bf16),
            pltpu.SemaphoreType.DMA((copies,)),
            pltpu.SemaphoreType.DMA((copies,)),
        ],
        compiler_params=pltpu.CompilerParams(
            collective_id=number, has_side_effects=True, vmem_limit_bytes=48 * 2**20
        ),
        cost_estimate=pl.CostEstimate(flops=0, bytes_accessed=80_000_000, transcendentals=0),
    )(partial)


def feature_peers(wide):
    peers = []
    for d in range(1, 8 if wide else 4):
        peer = {"col": flip("col", d & 3)}
        if d >> 2:
            peer["dp"] = flip("dp", 1)
        peers.append(peer)
    return peers


def total_kernel(v_ref, out_ref, slots, send_sem, recv_sem):
    me = lax.axis_index("col")
    peers = feature_peers(False)
    greet(peers)
    started = []
    send = sender(send_sem, recv_sem, started)
    for d, peer in enumerate(peers):
        send(v_ref, slots.at[me], d, peer)
    slots[me] = v_ref[...]
    for copy in started:
        copy.wait_recv()
    total = slots[0]
    for i in range(1, 4):
        total = total + slots[i]
    out_ref[...] = total
    for copy in started:
        copy.wait_send()


def feature_total(values, number, name):
    k, t = values.shape
    flat = values.reshape(k * t // 128, 128)
    total = pl.pallas_call(
        total_kernel,
        name=name,
        out_shape=jax.ShapeDtypeStruct(flat.shape, f32),
        in_specs=[pl.BlockSpec(memory_space=pltpu.VMEM)],
        out_specs=pl.BlockSpec(memory_space=pltpu.VMEM),
        scratch_shapes=[
            pltpu.VMEM((4,) + flat.shape, f32),
            pltpu.SemaphoreType.DMA((3,)),
            pltpu.SemaphoreType.DMA((3,)),
        ],
        compiler_params=pltpu.CompilerParams(collective_id=number, has_side_effects=True),
    )(flat)
    return total.reshape(k, t)


def row_peers():
    return [(d, {"row": flip("row", d)}) for d in (3, 2, 1)]


def unit_view(ref, unit, tok, heads):
    rows = pl.ds(pl.multiple_of((unit // heads) * tok, tok), tok)
    cols = pl.ds(pl.multiple_of((unit % heads) * HEAD_DIM, HEAD_DIM), HEAD_DIM)
    return ref.at[rows, cols]


def turn_kernel(back, tok, heads, x_ref, out_ref, local_sem, send_sem, recv_sem):
    z = lax.axis_index("row")
    greet([peer for _, peer in row_peers()])
    started = []
    send = sender(send_sem, recv_sem, started)

    def line(ref, i):
        return ref.at[pl.ds(pl.multiple_of(i * tok, tok), tok)]

    def ends(i):
        if back:
            return line(x_ref, i), unit_view(out_ref, z, tok, heads)
        return unit_view(x_ref, i, tok, heads), line(out_ref, z)

    for d, peer in row_peers():
        send(*ends(z ^ d), d - 1, peer)
    own = pltpu.make_async_copy(*ends(z), local_sem)
    own.start()
    for copy in started:
        copy.wait()
    own.wait()


def turn(values, back, tok, heads, number, name):
    shape = (2 * tok, heads * HEAD_DIM) if back else (2 * heads * tok, HEAD_DIM)
    return pl.pallas_call(
        functools.partial(turn_kernel, back, tok, heads),
        name=name,
        out_shape=jax.ShapeDtypeStruct(shape, values.dtype),
        in_specs=[pl.BlockSpec(memory_space=pltpu.VMEM)],
        out_specs=pl.BlockSpec(memory_space=pl.ANY),
        scratch_shapes=[
            pltpu.SemaphoreType.DMA,
            pltpu.SemaphoreType.DMA((3,)),
            pltpu.SemaphoreType.DMA((3,)),
        ],
        compiler_params=pltpu.CompilerParams(collective_id=number, has_side_effects=True),
        cost_estimate=pl.CostEstimate(flops=0, bytes_accessed=60_000_000, transcendentals=0),
    )(values)


def totals(stat, slots, started):
    for copy in started:
        copy.wait_recv()
    total = slots[0]
    for i in range(1, 8):
        total = total + slots[i]
    return total


def front_kernel(
    width,
    qkv_ref,
    cos_ref,
    sin_ref,
    gain_ref,
    out_ref,
    inv_ref,
    turned,
    packed,
    stat,
    slots,
    local_sem,
    stat_send,
    stat_recv,
    send_sem,
    recv_sem,
):
    count, tok = qkv_ref.shape[0], cos_ref.shape[0]
    part = qkv_ref.shape[1] // 3
    heads = part // HEAD_DIM
    z = lax.axis_index("row")
    me = side("dp") * 4 + lax.axis_index("col")
    peers = feature_peers(True)
    greet(peers + [peer for _, peer in row_peers()])
    for i in range(2):
        values = qkv_ref[:, i * part : (i + 1) * part]
        stat[i : i + 1, :] = jnp.sum(values * values, axis=1, keepdims=True).T
    started, moved, local = [], [], []
    send = sender(stat_send, stat_recv, started)
    for d, peer in enumerate(peers):
        send(stat, slots.at[me], d, peer)
    slots[me] = stat[...]
    move = sender(send_sem, recv_sem, moved)

    def ship(i):
        for d, peer in row_peers():
            move(packed.at[z ^ d, i], out_ref.at[z, i], 3 * i + d - 1, peer)
        copy = pltpu.make_async_copy(packed.at[z, i], out_ref.at[z, i], local_sem.at[i])
        copy.start()
        local.append(copy)

    def spots():
        return [(s, h, s * heads + h) for s in range(2) for h in range(heads)]

    for s, h, unit in spots():
        packed[unit, 2] = qkv_ref[
            s * tok : (s + 1) * tok, 2 * part + h * HEAD_DIM : 2 * part + (h + 1) * HEAD_DIM
        ].astype(bf16)
    ship(2)
    for i in (1, 0):
        for s, h, unit in spots():
            values = (
                qkv_ref[s * tok : (s + 1) * tok, i * part + h * HEAD_DIM : i * part + (h + 1) * HEAD_DIM]
                * gain_ref[i : i + 1, h * HEAD_DIM : (h + 1) * HEAD_DIM]
            )
            turned[i, unit] = values * cos_ref[...] + pltpu.roll(values, HEAD_DIM // 2, 1) * sin_ref[...]
    inverse = lax.rsqrt(totals(stat, slots, started) / width + norm_eps)
    inv_ref[...] = inverse
    for i in (1, 0):
        column = inverse[i : i + 1, :].T
        for s, h, unit in spots():
            packed[unit, i] = (turned[i, unit] * column[s * tok : (s + 1) * tok]).astype(bf16)
        ship(i)
    for copy in moved:
        copy.wait()
    for copy in local:
        copy.wait()
    for copy in started:
        copy.wait_send()


def front(qkv, cosine, sine_signed, gains, width, units, number):
    count, tok = qkv.shape[0], cosine.shape[0]
    return pl.pallas_call(
        functools.partial(front_kernel, width),
        name="front",
        out_shape=(
            jax.ShapeDtypeStruct((units, 3, tok, HEAD_DIM), bf16),
            jax.ShapeDtypeStruct((2, count), f32),
        ),
        in_specs=[pl.BlockSpec(memory_space=pltpu.VMEM)] * 4,
        out_specs=(pl.BlockSpec(memory_space=pl.ANY), pl.BlockSpec(memory_space=pltpu.VMEM)),
        scratch_shapes=[
            pltpu.VMEM((2, units, tok, HEAD_DIM), f32),
            pltpu.VMEM((units, 3, tok, HEAD_DIM), bf16),
            pltpu.VMEM((2, count), f32),
            pltpu.VMEM((8, 2, count), f32),
            pltpu.SemaphoreType.DMA((3,)),
            pltpu.SemaphoreType.DMA((7,)),
            pltpu.SemaphoreType.DMA((7,)),
            pltpu.SemaphoreType.DMA((9,)),
            pltpu.SemaphoreType.DMA((9,)),
        ],
        compiler_params=pltpu.CompilerParams(
            collective_id=number, has_side_effects=True, vmem_limit_bytes=40 * 2**20
        ),
        cost_estimate=pl.CostEstimate(flops=0, bytes_accessed=120_000_000, transcendentals=0),
    )(qkv, cosine, sine_signed, gains)


def rear_kernel(
    width,
    d_ref,
    qkv_ref,
    cos_ref,
    sin_ref,
    gain_ref,
    inv_ref,
    out_ref,
    sums_ref,
    landed,
    normed,
    stat,
    slots,
    stat_send,
    stat_recv,
    send_sem,
    recv_sem,
):
    count, tok = qkv_ref.shape[0], cos_ref.shape[0]
    part = qkv_ref.shape[1] // 2
    heads = part // HEAD_DIM
    z = lax.axis_index("row")
    me = side("dp") * 4 + lax.axis_index("col")
    peers = feature_peers(True)
    greet(peers + [peer for _, peer in row_peers()])
    started, moved = [], []
    move = sender(send_sem, recv_sem, moved)
    for i in (0, 1, 2):
        for d, peer in row_peers():
            there = pl.ds(pl.multiple_of((z ^ d) * tok, tok), tok)
            move(d_ref.at[i, there], landed.at[z, i], 3 * i + d - 1, peer)
    here = pl.ds(pl.multiple_of(z * tok, tok), tok)
    for i in (0, 1, 2):
        landed[z, i] = d_ref[i, here, :]
    spots = [(s, h, s * heads + h) for s in range(2) for h in range(heads)]
    for i in (0, 1):
        for copy in moved[3 * i : 3 * i + 3]:
            copy.wait_recv()
        for h in range(heads):
            cols = slice(i * part + h * HEAD_DIM, i * part + (h + 1) * HEAD_DIM)
            gain = gain_ref[i : i + 1, h * HEAD_DIM : (h + 1) * HEAD_DIM]
            raw = jnp.zeros((1, HEAD_DIM), f32)
            for s in range(2):
                rows = slice(s * tok, (s + 1) * tok)
                values = landed[s * heads + h, i].astype(f32)
                back = values * cos_ref[...] - pltpu.roll(values, HEAD_DIM // 2, 1) * sin_ref[...]
                pre = qkv_ref[rows, cols]
                inverse = inv_ref[i : i + 1, rows].T
                crossed = back * pre
                raw = raw + jnp.sum(crossed * inverse, axis=0, keepdims=True)
                partial = jnp.sum(crossed * gain, axis=1, keepdims=True).T
                if h == 0:
                    stat[i : i + 1, rows] = partial
                else:
                    stat[i : i + 1, rows] = stat[i : i + 1, rows] + partial
                normed[rows, cols] = back * gain
            sums_ref[i : i + 1, h * HEAD_DIM : (h + 1) * HEAD_DIM] = raw
    send = sender(stat_send, stat_recv, started)
    for d, peer in enumerate(peers):
        send(stat, slots.at[me], d, peer)
    slots[me] = stat[...]
    for copy in moved[6:]:
        copy.wait_recv()
    for s, h, unit in spots:
        cols = slice(2 * part + h * HEAD_DIM, 2 * part + (h + 1) * HEAD_DIM)
        out_ref[s * tok : (s + 1) * tok, cols] = landed[unit, 2]
    inner = totals(stat, slots, started) / width
    for i in (0, 1):
        inverse = inv_ref[i : i + 1, :]
        first = inverse.T
        second = (inverse * inverse * inverse * inner[i : i + 1, :]).T
        cols = slice(i * part, (i + 1) * part)
        out_ref[:, cols] = (first * normed[:, cols] - qkv_ref[:, cols] * second).astype(bf16)
    for copy in moved + started:
        copy.wait_send()


def rear(d_units, qkv, cosine, sine_signed, gains, inverse, width, number):
    count, tok = qkv.shape[0], cosine.shape[0]
    part = qkv.shape[1] // 2
    units = d_units.shape[1] // tok
    return pl.pallas_call(
        functools.partial(rear_kernel, width),
        name="rear",
        out_shape=(
            jax.ShapeDtypeStruct((count, 3 * part), bf16),
            jax.ShapeDtypeStruct((2, part), f32),
        ),
        in_specs=[pl.BlockSpec(memory_space=pltpu.VMEM)] * 6,
        out_specs=[pl.BlockSpec(memory_space=pltpu.VMEM)] * 2,
        scratch_shapes=[
            pltpu.VMEM((units, 3, tok, HEAD_DIM), bf16),
            pltpu.VMEM((count, 2 * part), f32),
            pltpu.VMEM((2, count), f32),
            pltpu.VMEM((8, 2, count), f32),
            pltpu.SemaphoreType.DMA((7,)),
            pltpu.SemaphoreType.DMA((7,)),
            pltpu.SemaphoreType.DMA((9,)),
            pltpu.SemaphoreType.DMA((9,)),
        ],
        compiler_params=pltpu.CompilerParams(
            collective_id=number, has_side_effects=True, vmem_limit_bytes=40 * 2**20
        ),
        cost_estimate=pl.CostEstimate(flops=0, bytes_accessed=120_000_000, transcendentals=0),
    )(d_units, qkv, cosine, sine_signed, gains, inverse)


BLOCK = 512


def attend_kernel(len_ref, q_ref, k_ref, v_ref, o_ref, o32_ref, lse_ref):
    i = pl.program_id(0)
    bq, bk = q_ref.shape[0], BLOCK
    length = len_ref[0]
    scale = HEAD_DIM ** (-0.5)
    q = q_ref[...]
    rows = i * bq + lax.broadcasted_iota(jnp.int32, (bq, bk), 0)
    cols0 = lax.broadcasted_iota(jnp.int32, (bq, bk), 1)

    def step(j, carry, masked):
        top, total, acc = carry
        j0 = pl.multiple_of(j * bk, bk)
        scores = contract_last(q, k_ref[pl.ds(j0, bk), :]) * scale
        if masked:
            cols = j0 + cols0
            scores = jnp.where((cols <= rows) & (cols < length), scores, masked_score)
        new = jnp.maximum(top, jnp.max(scores, axis=1, keepdims=True))
        weights = jnp.exp(scores - new)
        fix = jnp.exp(top - new)
        total = total * fix + jnp.sum(weights, axis=1, keepdims=True)
        acc = acc * fix + matmul(weights.astype(bf16), v_ref[pl.ds(j0, bk), :])
        return new, total, acc

    carry = (
        jnp.full((bq, 1), -jnp.inf, f32),
        jnp.zeros((bq, 1), f32),
        jnp.zeros((bq, HEAD_DIM), f32),
    )
    whole = jnp.minimum(i, length // bk)
    last = jnp.minimum(i + 1, (length + bk - 1) // bk)
    carry = lax.fori_loop(0, whole, lambda j, s: step(j, s, False), carry)
    top, total, acc = lax.fori_loop(whole, last, lambda j, s: step(j, s, True), carry)
    out = acc / total
    o_ref[...] = out.astype(bf16)
    o32_ref[...] = out
    lse_ref[...] = jnp.broadcast_to((top + jnp.log(total)).T, lse_ref.shape)


def attend(length, q, k, v):
    slots = q.shape[0]
    whole = pl.BlockSpec((slots, HEAD_DIM), lambda i: (0, 0))
    part = pl.BlockSpec((BLOCK, HEAD_DIM), lambda i: (i, 0))
    return pl.pallas_call(
        attend_kernel,
        name="attend",
        grid=(slots // BLOCK,),
        out_shape=(
            jax.ShapeDtypeStruct((slots, HEAD_DIM), bf16),
            jax.ShapeDtypeStruct((slots, HEAD_DIM), f32),
            jax.ShapeDtypeStruct((8, slots), f32),
        ),
        in_specs=[pl.BlockSpec(memory_space=pltpu.SMEM), part, whole, whole],
        out_specs=(part, part, pl.BlockSpec((8, BLOCK), lambda i: (0, i))),
        cost_estimate=pl.CostEstimate(
            flops=2 * slots * slots * HEAD_DIM,
            bytes_accessed=8 * slots * HEAD_DIM,
            transcendentals=slots * slots // 2,
        ),
    )(length, q, k, v)


def attend_back_kernel(
    len_ref, q_ref, k_ref, v_ref, do_ref, o_ref, lse_ref, out_ref, dq_acc, delta_ref
):
    j = pl.program_id(0)
    bk, bq = k_ref.shape[0], BLOCK
    slots = q_ref.shape[0]
    length = len_ref[0]
    scale = HEAD_DIM ** (-0.5)

    @pl.when(j == 0)
    def _():
        dq_acc[...] = jnp.zeros_like(dq_acc)
        for i in range(slots // bq):
            here = slice(i * bq, (i + 1) * bq)
            product = do_ref[here, :].astype(f32) * o_ref[here, :]
            delta_ref[0:1, here] = jnp.sum(product, axis=1, keepdims=True).T

    k, v = k_ref[...], v_ref[...]
    j0 = j * bk
    cols = j0 + lax.broadcasted_iota(jnp.int32, (bk, bq), 0)
    rows0 = lax.broadcasted_iota(jnp.int32, (bk, bq), 1)

    def step(i, carry, masked):
        dk, dv = carry
        i0 = pl.multiple_of(i * bq, bq)
        here = pl.ds(i0, bq)
        q, do = q_ref[here, :], do_ref[here, :]
        scores = contract_last(k, q) * scale
        if masked:
            scores = jnp.where((cols <= i0 + rows0) & (cols < length), scores, masked_score)
        probs = jnp.exp(scores - lse_ref[0:1, here])
        dv = dv + matmul(probs.astype(bf16), do)
        d_probs = contract_last(v, do)
        d_scores = (probs * (d_probs - delta_ref[0:1, here])).astype(bf16)
        dk = dk + matmul(d_scores, q)
        dq_acc[here, :] += contract_first(d_scores, k)
        return dk, dv

    zero = jnp.zeros((bk, HEAD_DIM), f32)
    top = slots // bq
    first = jnp.where(j0 + bk <= length, j + 1, top)
    first = jnp.where(j0 < length, first, j)
    stop = jnp.where(j0 < length, top, j)
    carry = lax.fori_loop(j, first, lambda i, s: step(i, s, True), (zero, zero))
    dk, dv = lax.fori_loop(first, stop, lambda i, s: step(i, s, False), carry)
    there = pl.ds(pl.multiple_of(j0, bk), bk)
    out_ref[1, there, :] = (dk * scale).astype(bf16)
    out_ref[2, there, :] = dv.astype(bf16)

    @pl.when(j == pl.num_programs(0) - 1)
    def _():
        out_ref[0] = (dq_acc[...] * scale).astype(bf16)


def attend_back(length, q, k, v, do, o, lse):
    slots = q.shape[0]
    whole = pl.BlockSpec((slots, HEAD_DIM), lambda j: (0, 0))
    part = pl.BlockSpec((BLOCK, HEAD_DIM), lambda j: (j, 0))
    line = pl.BlockSpec((8, slots), lambda j: (0, 0))
    return pl.pallas_call(
        attend_back_kernel,
        name="attend_back",
        grid=(slots // BLOCK,),
        out_shape=jax.ShapeDtypeStruct((3, slots, HEAD_DIM), bf16),
        in_specs=[pl.BlockSpec(memory_space=pltpu.SMEM), whole, part, part, whole, whole, line],
        out_specs=pl.BlockSpec((3, slots, HEAD_DIM), lambda j: (0, 0, 0)),
        scratch_shapes=[pltpu.VMEM((slots, HEAD_DIM), f32), pltpu.VMEM((8, slots), f32)],
        cost_estimate=pl.CostEstimate(
            flops=5 * slots * slots * HEAD_DIM,
            bytes_accessed=14 * slots * HEAD_DIM,
            transcendentals=slots * slots // 2,
        ),
    )(length, q, k, v, do, o, lse)


def per_device(
    tokens,
    seq_lengths,
    w_query,
    w_key,
    w_value,
    w_out,
    w_gate,
    w_up,
    w_down,
    q_gain,
    k_gain,
    attn_gain,
    mlp_gain,
    cotangent,
):
    tok_rows, feat_part = tokens.shape
    row_count, data_count = lax.axis_size("row"), lax.axis_size("dp")
    width = feat_part * lax.axis_size("col")
    slots = tok_rows * row_count
    half_feat = feat_part // 2
    y, z = side("dp"), lax.axis_index("row")
    p = z & 1
    heads = half_feat // HEAD_DIM
    hid = w_gate.shape[1] // 4
    pairs = [(i, i ^ 1) for i in range(data_count)]
    after = lambda values, *done: lax.optimization_barrier((values,) + done)[0]

    def y_half(values, axis):
        size = values.shape[axis] // 2
        return lax.dynamic_slice_in_dim(values, y * size, size, axis)

    def row_swap(values, d):
        return lax.ppermute(values, "row", [(i, i ^ d) for i in range(row_count)])

    def hidden_part(weight, axis):
        def quarter(d):
            return lax.dynamic_slice_in_dim(weight, (y * 2 + (p ^ (d & 1))) * hid, hid, axis)

        parts = [quarter(0)] + [row_swap(quarter(d), d) for d in (1, 2, 3)]
        stacked = jnp.stack(parts)
        return [lax.dynamic_index_in_dim(stacked, z ^ i, 0, keepdims=False) for i in range(row_count)]

    qkv_weight = lax.all_gather(
        jnp.concatenate([y_half(w_query, 1), y_half(w_key, 1), y_half(w_value, 1)], axis=1),
        "row",
        axis=0,
        tiled=True,
    )
    out_weight = lax.all_gather(y_half(after(w_out, qkv_weight), 0), "row", axis=1, tiled=True)

    positions = z * tok_rows + jnp.arange(tok_rows)
    length = seq_lengths[0]
    valid = (positions < length).astype(f32)[:, None]
    cosine, sine = rope_tables(positions, HEAD_DIM)
    sine_signed = jnp.where(jnp.arange(HEAD_DIM)[None, :] < HEAD_DIM // 2, -sine, sine)
    other_length = lax.ppermute(seq_lengths, "dp", pairs)
    pair_lengths = jnp.where(
        y == 0,
        jnp.concatenate([seq_lengths, other_length]),
        jnp.concatenate([other_length, seq_lengths]),
    )
    unit_length = lax.dynamic_slice_in_dim(pair_lengths, z // heads, 1)
    qk_gain = jnp.stack([y_half(q_gain, 0), y_half(k_gain, 0)])

    tokens_wide = gather_wide(tokens, False, 0, "gather_tokens")
    qkv = matmul(tokens_wide, qkv_weight)
    units, inverse = front(qkv, cosine, sine_signed, qk_gain, width, 2 * heads, 2)
    q_unit, k_unit, v_unit = (units[:, i].reshape(slots, HEAD_DIM) for i in range(3))
    gate_weight = jnp.concatenate(hidden_part(after(w_gate, units), 1), axis=0)
    up_weight = jnp.concatenate(hidden_part(after(w_up, units), 1), axis=0)
    attn_unit, attn_exact, log_total = attend(unit_length, q_unit, k_unit, v_unit)
    attn_low = turn(attn_unit, True, tok_rows, heads, 3, "turn_attn")
    down_weight = jnp.concatenate(hidden_part(after(w_down, attn_low), 0), axis=1)
    branch = scatter_wide(matmul(attn_low, out_weight).astype(bf16), False, 4, "scatter_branch")
    branch_inv = lax.rsqrt(
        feature_total(jnp.sum(branch * branch, axis=1)[None, :], 5, "total_branch")[0] / width
        + norm_eps
    )[:, None]
    resid = tokens.astype(f32) + branch * branch_inv * attn_gain
    resid_wide = gather_wide(resid.astype(bf16), True, 6, "gather_resid")
    gate = matmul(resid_wide, gate_weight)
    upper = matmul(resid_wide, up_weight)
    sigma = jax.nn.sigmoid(gate)
    hidden = (gate * sigma * upper).astype(bf16)
    mixed = scatter_wide(matmul(hidden, down_weight).astype(bf16), True, 7, "scatter_mixed")
    incoming = cotangent.astype(f32) * valid
    gained = incoming * mlp_gain
    sums = feature_total(
        jnp.stack([jnp.sum(mixed * mixed, axis=1), jnp.sum(gained * mixed, axis=1)]),
        8,
        "total_mixed",
    )
    mixed_inv = lax.rsqrt(sums[0] / width + norm_eps)[:, None]
    inner = (sums[1] / width)[:, None]
    block_output = ((resid + mixed * mixed_inv * mlp_gain) * valid).astype(bf16)
    mlp_gain_raw = jnp.sum(incoming * mixed * mixed_inv, axis=0)
    d_mixed = (mixed_inv * gained - mixed * mixed_inv**3 * inner).astype(bf16)
    d_mixed_wide = gather_wide(d_mixed, True, 9, "gather_d_mixed")

    factor = 1.0 / math.sqrt(slots * data_count)

    def cut(values, index, count, axis):
        size = values.shape[axis] // count
        return lax.dynamic_slice_in_dim(values, index * size, size, axis)

    def over_dp(piece):
        if data_count > 2:
            groups = [list(range(s, data_count, 2)) for s in (0, 1)]
            piece = lax.psum(piece, "dp", axis_index_groups=groups)
        return piece

    def two_sides(piece, other, bit, axis):
        low = jnp.where(bit == 0, piece, other)
        high = jnp.where(bit == 0, other, piece)
        return jnp.concatenate([low, high], axis=axis)

    def hidden_grad(raw, axis):
        far = row_swap(cut(raw, 1 - (z >> 1), 2, axis), 2)
        near = cut(raw, z >> 1, 2, axis)
        near = (near.astype(f32) + far.astype(f32)).astype(bf16)
        near = over_dp(near)
        own, away = cut(near, p, 2, axis), row_swap(cut(near, 1 - p, 2, axis), 1)
        block = two_sides(own, away, p, 1 - axis)
        return two_sides(block, lax.ppermute(block, "dp", pairs), y, 1 - axis).astype(f32)

    def reduce_rows(raw, axis):
        return lax.psum_scatter(raw, "row", scatter_dimension=axis, tiled=True)

    d_hidden = contract_last(d_mixed_wide, down_weight)
    down_raw = (contract_first(hidden, d_mixed_wide) * factor).astype(bf16)
    d_gate = (d_hidden * upper * sigma * (1.0 + gate * (1.0 - sigma))).astype(bf16)
    d_upper = (d_hidden * gate * sigma).astype(bf16)
    gate_raw = (contract_first(resid_wide, d_gate) * factor).astype(bf16)
    up_raw = (contract_first(resid_wide, d_upper) * factor).astype(bf16)
    d_resid_wide = (
        contract_last(d_gate, gate_weight) + contract_last(d_upper, up_weight)
    ).astype(bf16)
    d_resid_wide, down_raw, gate_raw, up_raw = lax.optimization_barrier(
        (d_resid_wide, down_raw, gate_raw, up_raw)
    )
    d_resid = incoming + scatter_wide(d_resid_wide, True, 10, "scatter_d_resid")
    attn_gain_raw = jnp.sum(d_resid * branch * branch_inv, axis=0)
    gained = d_resid * attn_gain
    inner = (
        feature_total(jnp.sum(gained * branch, axis=1)[None, :], 11, "total_d_resid")[0][:, None]
        / width
    )
    d_branch = (branch_inv * gained - branch * branch_inv**3 * inner).astype(bf16)
    d_branch_wide = gather_wide(d_branch, False, 12, "gather_d_branch")
    d_attn = contract_last(d_branch_wide, out_weight).astype(bf16)
    d_attn_unit = turn(d_attn, False, tok_rows, heads, 13, "turn_d_attn")
    out_raw = (contract_first(attn_low, after(d_branch_wide, d_attn_unit)) * factor).astype(bf16)
    d_attn_unit, out_raw = lax.optimization_barrier((d_attn_unit, out_raw))
    out_piece = reduce_rows(out_raw, 1)
    d_units = attend_back(unit_length, q_unit, k_unit, v_unit, d_attn_unit, attn_exact, log_total)
    d_qkv, gain_sums = rear(
        d_units, qkv[:, : 2 * half_feat], cosine, sine_signed, qk_gain, inverse, width, 14
    )
    qkv_raw = (contract_first(tokens_wide, d_qkv) * factor).astype(bf16)
    projected = contract_last(d_qkv, qkv_weight).astype(bf16)
    projected, qkv_raw = lax.optimization_barrier((projected, qkv_raw))
    qkv_piece = over_dp(reduce_rows(qkv_raw, 0))
    input_grad = d_resid + scatter_wide(projected, False, 16, "scatter_projected")

    def spread(half):
        return lax.dynamic_update_slice_in_dim(jnp.zeros((feat_part,), f32), half, y * half_feat, 0)

    gains = lax.psum(
        jnp.stack([spread(gain_sums[0]), spread(gain_sums[1]), attn_gain_raw, mlp_gain_raw])
        * factor,
        ("dp", "row"),
    )
    qkv_other = lax.ppermute(qkv_piece, "dp", pairs)
    q_grad, k_grad, v_grad = (
        two_sides(cut(qkv_piece, i, 3, 1), cut(qkv_other, i, 3, 1), y, 1).astype(f32)
        for i in range(3)
    )
    out_piece = over_dp(out_piece)
    out_grad = two_sides(out_piece, lax.ppermute(out_piece, "dp", pairs), y, 0).astype(f32)
    return (
        block_output,
        input_grad,
        q_grad,
        k_grad,
        v_grad,
        out_grad,
        hidden_grad(gate_raw, 0),
        hidden_grad(up_raw, 0),
        hidden_grad(down_raw, 1),
        gains[0],
        gains[1],
        gains[2],
        gains[3],
    )


def solution(mesh):
    tok, row_col, col_row, gain = P(("dp", "row"), "col"), P("row", "col"), P("col", "row"), P("col")
    weights = (row_col, row_col, row_col, col_row, row_col, row_col, col_row)
    gains = (gain, gain, gain, gain)
    return jax.shard_map(
        per_device,
        mesh=mesh,
        in_specs=(tok, P("dp")) + weights + gains + (tok,),
        out_specs=(tok, tok) + weights + gains,
        check_vma=False,
    )
```

```python
import functools
import math

import jax
import jax.numpy as jnp
from jax import lax
from jax.experimental import pallas as pl
from jax.experimental.pallas import tpu as pltpu
from jax.sharding import PartitionSpec as P

HEAD_DIM = 128
rope_base = 500000.0
norm_eps = 1e-06
masked_score = -1e30

MESH = pl.DeviceIdType.MESH
bf16 = jnp.bfloat16
f32 = jnp.float32
COST = pl.CostEstimate(flops=0, bytes_accessed=1000, transcendentals=0)


def rope_tables(positions, head_dim):
    half = head_dim // 2
    freq = 1.0 / rope_base ** (jnp.arange(half, dtype=f32) / half)
    angle = positions.astype(f32)[:, None] * freq[None, :]
    angle = jnp.concatenate([angle, angle], axis=1)
    return (jnp.cos(angle), jnp.sin(angle))


def matmul(left, right):
    return jnp.dot(left, right, preferred_element_type=f32)


def contract_first(left, right):
    return lax.dot_general(left, right, (((0,), (0,)), ((), ())), preferred_element_type=f32)


def contract_last(left, right):
    return lax.dot_general(left, right, (((1,), (1,)), ((), ())), preferred_element_type=f32)


def flip(axis, bit):
    return lax.axis_index(axis) ^ bit


def side(axis):
    return lax.axis_index(axis) & 1


def greet(peers):
    barrier = pltpu.get_barrier_semaphore()
    for peer in peers:
        pl.semaphore_signal(barrier, inc=1, device_id=peer, device_id_type=MESH)
    pl.semaphore_wait(barrier, len(peers))


def sender(send_sem, recv_sem, started):
    def send(src, dst, number, peer):
        copy = pltpu.make_async_remote_copy(
            src_ref=src,
            dst_ref=dst,
            send_sem=send_sem.at[number],
            recv_sem=recv_sem.at[number],
            device_id=peer,
            device_id_type=MESH,
        )
        copy.start()
        started.append(copy)
        return copy

    return send


def neighbours():
    return {"col": flip("col", 2)}, {"dp": flip("dp", 1)}, {"col": flip("col", 1)}


def gather_kernel(pair, x_ref, out_ref, local_sem, send_sem, recv_sem):
    rows, width = x_ref.shape
    half = rows // 2
    y, b, p = side("dp"), lax.axis_index("col"), side("row") if pair else 0
    to_x, to_y, to_c = neighbours()
    to_z = {"row": flip("row", 1)}
    greet([to_x, to_y, to_c] + ([to_z] if pair else []))
    started = []
    send = sender(send_sem, recv_sem, started)

    def slot(pp, yy, h, bb, n=half):
        return out_ref.at[
            pl.ds(pl.multiple_of((pp * 2 + yy) * rows + h * half, half), n),
            pl.ds(pl.multiple_of(bb * width, width), width),
        ]

    def open_flow(pp, low, high, base):
        xa = send(low, slot(pp, y, 0, b), base + 0, to_x)
        ya = send(high, slot(pp, y, 1, b), base + 1, to_y)
        c0 = send(low, slot(pp, y, 0, b), base + 6, to_c)
        yb = send(low, slot(pp, y, 0, b), base + 2, to_y)
        xb = send(high, slot(pp, y, 1, b), base + 3, to_x)
        c1 = send(high, slot(pp, y, 1, b), base + 7, to_c)
        return xa, ya, xb, yb, [c0, c1]

    def relay(pp, flow, base):
        xa, ya, xb, yb, core = flow
        xa.wait_recv()
        piece = slot(pp, y, 0, b ^ 2)
        yc = send(piece, piece, base + 4, to_y)
        core.append(send(piece, piece, base + 8, to_c))
        ya.wait_recv()
        piece = slot(pp, y ^ 1, 1, b)
        xc = send(piece, piece, base + 5, to_x)
        core.append(send(piece, piece, base + 9, to_c))
        yb.wait_recv()
        piece = slot(pp, y ^ 1, 0, b)
        core.append(send(piece, piece, base + 10, to_c))
        xb.wait_recv()
        piece = slot(pp, y, 1, b ^ 2)
        core.append(send(piece, piece, base + 11, to_c))
        return yc, xc, core

    def close_flow(pp, state, base):
        yc, xc, core = state
        yc.wait_recv()
        piece = slot(pp, y ^ 1, 0, b ^ 2)
        core.append(send(piece, piece, base + 12, to_c))
        xc.wait_recv()
        piece = slot(pp, y ^ 1, 1, b ^ 2)
        core.append(send(piece, piece, base + 13, to_c))
        for copy in core:
            copy.wait_recv()

    low, high = x_ref.at[pl.ds(0, half)], x_ref.at[pl.ds(half, half)]
    own = pltpu.make_async_copy(x_ref, slot(p, y, 0, b, rows), local_sem)
    if pair:
        z0 = send(low, slot(p, y, 0, b), 28, to_z)
        z1 = send(high, slot(p, y, 1, b), 29, to_z)
    first = open_flow(p, low, high, 0)
    own.start()
    state = relay(p, first, 0)
    if pair:
        z0.wait_recv()
        z1.wait_recv()
        second = open_flow(p ^ 1, slot(p ^ 1, y, 0, b), slot(p ^ 1, y, 1, b), 14)
    close_flow(p, state, 0)
    if pair:
        close_flow(p ^ 1, relay(p ^ 1, second, 14), 14)
    for copy in started:
        copy.wait_send()
    own.wait()


def gather_wide(values, pair, number, name):
    rows, width = values.shape
    copies = 30 if pair else 14
    return pl.pallas_call(
        functools.partial(gather_kernel, pair),
        name=name,
        out_shape=jax.ShapeDtypeStruct(((4 if pair else 2) * rows, 4 * width), values.dtype),
        in_specs=[pl.BlockSpec(memory_space=pltpu.VMEM)],
        out_specs=pl.BlockSpec(memory_space=pl.ANY),
        scratch_shapes=[
            pltpu.SemaphoreType.DMA,
            pltpu.SemaphoreType.DMA((copies,)),
            pltpu.SemaphoreType.DMA((copies,)),
        ],
        compiler_params=pltpu.CompilerParams(collective_id=number, has_side_effects=True),
        cost_estimate=COST,
    )(values)


def scatter_kernel(pair, rider, p_ref, *refs):
    if rider:
        cargo_ref, out_ref, far_ref = refs[:3]
    else:
        out_ref = refs[0]
    rc, s1, ry, rx, s2, fy, fx, sz, fz, send_sem, recv_sem = refs[3 if rider else 1 :]
    rows, width = out_ref.shape
    half = rows // 2
    y, b, p = side("dp"), lax.axis_index("col"), side("row") if pair else 0
    x, c = b >> 1, b & 1
    to_x, to_y, to_c = neighbours()
    to_z = {"row": flip("row", 1)}
    to_far = {"row": flip("row", 2)}
    greet([to_x, to_y, to_c] + ([to_z] if pair else []) + ([to_far] if rider else []))
    started = []
    send = sender(send_sem, recv_sem, started)
    if rider:
        size = far_ref.shape[1]
        start = pl.multiple_of((1 - (lax.axis_index("row") >> 1)) * size, size)
        cargo = send(cargo_ref.at[:, pl.ds(start, size)], far_ref, 30, to_far)

    def place(yy, h):
        return pl.ds(pl.multiple_of(yy * rows + h * half, half), half)

    def column(bb):
        return pl.ds(pl.multiple_of(bb * width, width), width)

    order = [(0, y ^ 1, 0), (1, y ^ 1, 0), (x ^ 1, 0, 1), (x ^ 1, 1, 1)]
    order += [(0, y, 0), (1, y, 0), (x, 0, 1), (x, 1, 1)]

    class Flow:
        def __init__(self, f, pp):
            self.f, self.base = f, 14 * f
            self.rows = lambda yy, h: pl.ds(
                pl.multiple_of((pp * 2 + yy) * rows + h * half, half), half
            )
            self.core = [
                send(
                    p_ref.at[self.rows(yy, h), column(2 * xx + (c ^ 1))],
                    rc.at[f, xx, place(yy, h)],
                    self.base + number,
                    to_c,
                )
                for number, (xx, yy, h) in enumerate(order)
            ]

        def settle(self, *numbers):
            for number in numbers:
                self.core[number].wait_recv()
                xx, yy, h = order[number]
                s1[self.f, xx, place(yy, h), :] = (
                    p_ref[self.rows(yy, h), column(2 * xx + c)].astype(f32)
                    + rc[self.f, xx, place(yy, h), :].astype(f32)
                ).astype(s1.dtype)

        def first(self, i):
            f = self.f
            ya = send(s1.at[f, i, place(y ^ 1, 0), :], ry.at[f, i], self.base + 8 + i, to_y)
            part = s1.at[f, x ^ 1, pl.ds(i * rows + half, half), :]
            xa = send(part, rx.at[f, i], self.base + 10 + i, to_x)
            return ya, xa

        def second(self, copies):
            f = self.f
            for ya, _ in copies:
                ya.wait_recv()
            s2[f, 0] = (
                s1[f, x ^ 1, place(y, 0), :].astype(f32) + ry[f, x ^ 1].astype(f32)
            ).astype(s2.dtype)
            xb = send(s2.at[f, 0], fx.at[f], self.base + 12, to_x)
            for _, xa in copies:
                xa.wait_recv()
            s2[f, 1] = (
                s1[f, x, place(y ^ 1, 1), :].astype(f32) + rx[f, y ^ 1].astype(f32)
            ).astype(s2.dtype)
            yb = send(s2.at[f, 1], fy.at[f], self.base + 13, to_y)
            return xb, yb

        def last(self, copies):
            f = self.f
            xb, yb = copies
            keep = s1[f, x, place(y, 0), :].astype(f32) + ry[f, x].astype(f32)
            xb.wait_recv()
            low = keep + fx[f].astype(f32)
            keep = s1[f, x, place(y, 1), :].astype(f32) + rx[f, y].astype(f32)
            yb.wait_recv()
            return low, keep + fy[f].astype(f32)

    if pair:
        far = Flow(0, p ^ 1)
        near = Flow(1, p)
        far.settle(0, 1, 2, 3)
        far_first = [far.first(0), far.first(1)]
        far.settle(4, 5, 6, 7)
        near.settle(0, 1, 2, 3)
        near_first = [near.first(0)]
        near.settle(4, 5, 6, 7)
        far_second = far.second(far_first)
        near_first.append(near.first(1))
        low, high = far.last(far_second)
        sz[pl.ds(0, half), :] = low.astype(bf16)
        z0 = send(sz.at[pl.ds(0, half)], fz.at[pl.ds(0, half)], 28, to_z)
        sz[pl.ds(half, half), :] = high.astype(bf16)
        z1 = send(sz.at[pl.ds(half, half)], fz.at[pl.ds(half, half)], 29, to_z)
        low, high = near.last(near.second(near_first))
        z0.wait_recv()
        out_ref[pl.ds(0, half), :] = low + fz[pl.ds(0, half), :].astype(f32)
        z1.wait_recv()
        out_ref[pl.ds(half, half), :] = high + fz[pl.ds(half, half), :].astype(f32)
    else:
        near = Flow(0, 0)
        near.settle(0, 1, 2, 3)
        near_first = [near.first(0), near.first(1)]
        near.settle(4, 5, 6, 7)
        low, high = near.last(near.second(near_first))
        out_ref[pl.ds(0, half), :] = low
        out_ref[pl.ds(half, half), :] = high
    if rider:
        cargo.wait_recv()
    for copy in started:
        copy.wait_send()


def scatter_wide(partial, pair, number, name, cargo=None):
    flows = 2 if pair else 1
    rows, width = partial.shape[0] // (2 * flows), partial.shape[1] // 4
    half = rows // 2
    rider = cargo is not None
    copies = 31 if pair else 14
    out_shape, out_spec = [jax.ShapeDtypeStruct((rows, width), f32)], [pl.BlockSpec(memory_space=pltpu.VMEM)]
    anywhere = [pl.BlockSpec(memory_space=pl.ANY)] * rider
    if rider:
        out_shape.append(jax.ShapeDtypeStruct((cargo.shape[0], cargo.shape[1] // 2), cargo.dtype))
    last = (rows, width) if pair else (16, 128)
    out = pl.pallas_call(
        functools.partial(scatter_kernel, pair, rider),
        name=name,
        out_shape=out_shape,
        in_specs=[pl.BlockSpec(memory_space=pltpu.VMEM)] + anywhere,
        out_specs=out_spec + anywhere,
        scratch_shapes=[
            pltpu.VMEM((flows, 2, 2 * rows, width), bf16),
            pltpu.VMEM((flows, 2, 2 * rows, width), bf16),
            pltpu.VMEM((flows, 2, half, width), bf16),
            pltpu.VMEM((flows, 2, half, width), bf16),
            pltpu.VMEM((flows, 2, half, width), bf16),
            pltpu.VMEM((flows, half, width), bf16),
            pltpu.VMEM((flows, half, width), bf16),
            pltpu.VMEM(last, bf16),
            pltpu.VMEM(last, bf16),
            pltpu.SemaphoreType.DMA((copies,)),
            pltpu.SemaphoreType.DMA((copies,)),
        ],
        compiler_params=pltpu.CompilerParams(
            collective_id=number, has_side_effects=True, vmem_limit_bytes=48 * 2**20
        ),
        cost_estimate=COST,
    )(partial, *([cargo] * rider))
    return out if rider else out[0]


def feature_peers(wide):
    peers = []
    for d in range(1, 8 if wide else 4):
        peer = {"col": flip("col", d & 3)}
        if d >> 2:
            peer["dp"] = flip("dp", 1)
        peers.append(peer)
    return peers


def total_kernel(v_ref, out_ref, slots, send_sem, recv_sem):
    me = lax.axis_index("col")
    peers = feature_peers(False)
    greet(peers)
    started = []
    send = sender(send_sem, recv_sem, started)
    for d, peer in enumerate(peers):
        send(v_ref, slots.at[me], d, peer)
    slots[me] = v_ref[...]
    for copy in started:
        copy.wait_recv()
    total = slots[0]
    for i in range(1, 4):
        total = total + slots[i]
    out_ref[...] = total
    for copy in started:
        copy.wait_send()


def feature_total(values, number, name):
    k, t = values.shape
    flat = values.reshape(k * t // 128, 128)
    total = pl.pallas_call(
        total_kernel,
        name=name,
        out_shape=jax.ShapeDtypeStruct(flat.shape, f32),
        in_specs=[pl.BlockSpec(memory_space=pltpu.VMEM)],
        out_specs=pl.BlockSpec(memory_space=pltpu.VMEM),
        scratch_shapes=[
            pltpu.VMEM((4,) + flat.shape, f32),
            pltpu.SemaphoreType.DMA((3,)),
            pltpu.SemaphoreType.DMA((3,)),
        ],
        compiler_params=pltpu.CompilerParams(collective_id=number, has_side_effects=True),
    )(flat)
    return total.reshape(k, t)


def gain_peers():
    peers = []
    for d in range(1, 8):
        peers.append({"row": flip("row", d & 3), "dp": flip("dp", d >> 2)})
    return peers


def gain_kernel(v_ref, out_ref, slots, send_sem, recv_sem):
    me = side("dp") * 4 + lax.axis_index("row")
    peers = gain_peers()
    greet(peers)
    started = []
    send = sender(send_sem, recv_sem, started)
    for d, peer in enumerate(peers):
        send(v_ref, slots.at[me], d, peer)
    slots[me] = v_ref[...]
    for copy in started:
        copy.wait_recv()
    total = slots[0]
    for i in range(1, 8):
        total = total + slots[i]
    out_ref[...] = total
    for copy in started:
        copy.wait_send()


def gain_total(values, number):
    flat = values.reshape(-1, 128)
    total = pl.pallas_call(
        gain_kernel,
        name="total_gains",
        out_shape=jax.ShapeDtypeStruct(flat.shape, f32),
        in_specs=[pl.BlockSpec(memory_space=pltpu.VMEM)],
        out_specs=pl.BlockSpec(memory_space=pltpu.VMEM),
        scratch_shapes=[
            pltpu.VMEM((8,) + flat.shape, f32),
            pltpu.SemaphoreType.DMA((7,)),
            pltpu.SemaphoreType.DMA((7,)),
        ],
        compiler_params=pltpu.CompilerParams(collective_id=number, has_side_effects=True),
    )(flat)
    return total.reshape(values.shape)


def row_peers():
    return [(d, {"row": flip("row", d)}) for d in (3, 2, 1)]


def unit_view(ref, unit, tok, heads):
    rows = pl.ds(pl.multiple_of((unit // heads) * tok, tok), tok)
    cols = pl.ds(pl.multiple_of((unit % heads) * HEAD_DIM, HEAD_DIM), HEAD_DIM)
    return ref.at[rows, cols]


def turn_kernel(back, tok, heads, x_ref, out_ref, local_sem, send_sem, recv_sem):
    z = lax.axis_index("row")
    greet([peer for _, peer in row_peers()])
    started = []
    send = sender(send_sem, recv_sem, started)

    def line(ref, i):
        return ref.at[pl.ds(pl.multiple_of(i * tok, tok), tok)]

    def ends(i):
        if back:
            return line(x_ref, i), unit_view(out_ref, z, tok, heads)
        return unit_view(x_ref, i, tok, heads), line(out_ref, z)

    for d, peer in row_peers():
        send(*ends(z ^ d), d - 1, peer)
    own = pltpu.make_async_copy(*ends(z), local_sem)
    own.start()
    for copy in started:
        copy.wait()
    own.wait()


def turn(values, back, tok, heads, number, name):
    shape = (2 * tok, heads * HEAD_DIM) if back else (2 * heads * tok, HEAD_DIM)
    return pl.pallas_call(
        functools.partial(turn_kernel, back, tok, heads),
        name=name,
        out_shape=jax.ShapeDtypeStruct(shape, values.dtype),
        in_specs=[pl.BlockSpec(memory_space=pltpu.VMEM)],
        out_specs=pl.BlockSpec(memory_space=pl.ANY),
        scratch_shapes=[
            pltpu.SemaphoreType.DMA,
            pltpu.SemaphoreType.DMA((3,)),
            pltpu.SemaphoreType.DMA((3,)),
        ],
        compiler_params=pltpu.CompilerParams(collective_id=number, has_side_effects=True),
        cost_estimate=COST,
    )(values)


def totals(stat, slots, started):
    for copy in started:
        copy.wait_recv()
    total = slots[0]
    for i in range(1, 8):
        total = total + slots[i]
    return total


def front_kernel(
    width,
    qkv_ref,
    cos_ref,
    sin_ref,
    gain_ref,
    out_ref,
    inv_ref,
    turned,
    packed,
    stat,
    slots,
    local_sem,
    stat_send,
    stat_recv,
    send_sem,
    recv_sem,
):
    count, tok = qkv_ref.shape[0], cos_ref.shape[0]
    part = qkv_ref.shape[1] // 3
    heads = part // HEAD_DIM
    z = lax.axis_index("row")
    me = side("dp") * 4 + lax.axis_index("col")
    peers = feature_peers(True)
    greet(peers + [peer for _, peer in row_peers()])
    for i in range(2):
        values = qkv_ref[:, i * part : (i + 1) * part]
        stat[i : i + 1, :] = jnp.sum(values * values, axis=1, keepdims=True).T
    started, moved, local = [], [], []
    send = sender(stat_send, stat_recv, started)
    for d, peer in enumerate(peers):
        send(stat, slots.at[me], d, peer)
    slots[me] = stat[...]
    move = sender(send_sem, recv_sem, moved)

    def ship(i):
        for d, peer in row_peers():
            move(packed.at[z ^ d, i], out_ref.at[z, i], 3 * i + d - 1, peer)
        copy = pltpu.make_async_copy(packed.at[z, i], out_ref.at[z, i], local_sem.at[i])
        copy.start()
        local.append(copy)

    def spots():
        return [(s, h, s * heads + h) for s in range(2) for h in range(heads)]

    for s, h, unit in spots():
        packed[unit, 2] = qkv_ref[
            s * tok : (s + 1) * tok, 2 * part + h * HEAD_DIM : 2 * part + (h + 1) * HEAD_DIM
        ].astype(bf16)
    ship(2)
    for i in (1, 0):
        for s, h, unit in spots():
            values = (
                qkv_ref[s * tok : (s + 1) * tok, i * part + h * HEAD_DIM : i * part + (h + 1) * HEAD_DIM]
                * gain_ref[i : i + 1, h * HEAD_DIM : (h + 1) * HEAD_DIM]
            )
            turned[i, unit] = values * cos_ref[...] + pltpu.roll(values, HEAD_DIM // 2, 1) * sin_ref[...]
    inverse = lax.rsqrt(totals(stat, slots, started) / width + norm_eps)
    inv_ref[...] = inverse
    for i in (1, 0):
        column = inverse[i : i + 1, :].T
        for s, h, unit in spots():
            packed[unit, i] = (turned[i, unit] * column[s * tok : (s + 1) * tok]).astype(bf16)
        ship(i)
    for copy in moved:
        copy.wait()
    for copy in local:
        copy.wait()
    for copy in started:
        copy.wait_send()


def front(qkv, cosine, sine_signed, gains, width, units, number):
    count, tok = qkv.shape[0], cosine.shape[0]
    return pl.pallas_call(
        functools.partial(front_kernel, width),
        name="front",
        out_shape=(
            jax.ShapeDtypeStruct((units, 3, tok, HEAD_DIM), bf16),
            jax.ShapeDtypeStruct((2, count), f32),
        ),
        in_specs=[pl.BlockSpec(memory_space=pltpu.VMEM)] * 4,
        out_specs=(pl.BlockSpec(memory_space=pl.ANY), pl.BlockSpec(memory_space=pltpu.VMEM)),
        scratch_shapes=[
            pltpu.VMEM((2, units, tok, HEAD_DIM), f32),
            pltpu.VMEM((units, 3, tok, HEAD_DIM), bf16),
            pltpu.VMEM((2, count), f32),
            pltpu.VMEM((8, 2, count), f32),
            pltpu.SemaphoreType.DMA((3,)),
            pltpu.SemaphoreType.DMA((7,)),
            pltpu.SemaphoreType.DMA((7,)),
            pltpu.SemaphoreType.DMA((9,)),
            pltpu.SemaphoreType.DMA((9,)),
        ],
        compiler_params=pltpu.CompilerParams(
            collective_id=number, has_side_effects=True, vmem_limit_bytes=40 * 2**20
        ),
        cost_estimate=COST,
    )(qkv, cosine, sine_signed, gains)


def rear_kernel(
    width,
    d_ref,
    qkv_ref,
    cos_ref,
    sin_ref,
    gain_ref,
    inv_ref,
    out_ref,
    sums_ref,
    landed,
    normed,
    stat,
    slots,
    stat_send,
    stat_recv,
    send_sem,
    recv_sem,
):
    count, tok = qkv_ref.shape[0], cos_ref.shape[0]
    part = qkv_ref.shape[1] // 2
    heads = part // HEAD_DIM
    z = lax.axis_index("row")
    me = side("dp") * 4 + lax.axis_index("col")
    peers = feature_peers(True)
    greet(peers + [peer for _, peer in row_peers()])
    started, moved = [], []
    move = sender(send_sem, recv_sem, moved)
    for i in (0, 1, 2):
        for d, peer in row_peers():
            there = pl.ds(pl.multiple_of((z ^ d) * tok, tok), tok)
            move(d_ref.at[i, there], landed.at[z, i], 3 * i + d - 1, peer)
    here = pl.ds(pl.multiple_of(z * tok, tok), tok)
    for i in (0, 1, 2):
        landed[z, i] = d_ref[i, here, :]
    spots = [(s, h, s * heads + h) for s in range(2) for h in range(heads)]
    for i in (0, 1):
        for copy in moved[3 * i : 3 * i + 3]:
            copy.wait_recv()
        for h in range(heads):
            cols = slice(i * part + h * HEAD_DIM, i * part + (h + 1) * HEAD_DIM)
            gain = gain_ref[i : i + 1, h * HEAD_DIM : (h + 1) * HEAD_DIM]
            raw = jnp.zeros((1, HEAD_DIM), f32)
            for s in range(2):
                rows = slice(s * tok, (s + 1) * tok)
                values = landed[s * heads + h, i].astype(f32)
                back = values * cos_ref[...] - pltpu.roll(values, HEAD_DIM // 2, 1) * sin_ref[...]
                pre = qkv_ref[rows, cols]
                inverse = inv_ref[i : i + 1, rows].T
                crossed = back * pre
                raw = raw + jnp.sum(crossed * inverse, axis=0, keepdims=True)
                partial = jnp.sum(crossed * gain, axis=1, keepdims=True).T
                if h == 0:
                    stat[i : i + 1, rows] = partial
                else:
                    stat[i : i + 1, rows] = stat[i : i + 1, rows] + partial
                normed[rows, cols] = back * gain
            sums_ref[i : i + 1, h * HEAD_DIM : (h + 1) * HEAD_DIM] = raw
    send = sender(stat_send, stat_recv, started)
    for d, peer in enumerate(peers):
        send(stat, slots.at[me], d, peer)
    slots[me] = stat[...]
    for copy in moved[6:]:
        copy.wait_recv()
    for s, h, unit in spots:
        cols = slice(2 * part + h * HEAD_DIM, 2 * part + (h + 1) * HEAD_DIM)
        out_ref[s * tok : (s + 1) * tok, cols] = landed[unit, 2]
    inner = totals(stat, slots, started) / width
    for i in (0, 1):
        inverse = inv_ref[i : i + 1, :]
        first = inverse.T
        second = (inverse * inverse * inverse * inner[i : i + 1, :]).T
        cols = slice(i * part, (i + 1) * part)
        out_ref[:, cols] = (first * normed[:, cols] - qkv_ref[:, cols] * second).astype(bf16)
    for copy in moved + started:
        copy.wait_send()


def rear(d_units, qkv, cosine, sine_signed, gains, inverse, width, number):
    count, tok = qkv.shape[0], cosine.shape[0]
    part = qkv.shape[1] // 2
    units = d_units.shape[1] // tok
    return pl.pallas_call(
        functools.partial(rear_kernel, width),
        name="rear",
        out_shape=(
            jax.ShapeDtypeStruct((count, 3 * part), bf16),
            jax.ShapeDtypeStruct((2, part), f32),
        ),
        in_specs=[pl.BlockSpec(memory_space=pltpu.VMEM)] * 6,
        out_specs=[pl.BlockSpec(memory_space=pltpu.VMEM)] * 2,
        scratch_shapes=[
            pltpu.VMEM((units, 3, tok, HEAD_DIM), bf16),
            pltpu.VMEM((count, 2 * part), f32),
            pltpu.VMEM((2, count), f32),
            pltpu.VMEM((8, 2, count), f32),
            pltpu.SemaphoreType.DMA((7,)),
            pltpu.SemaphoreType.DMA((7,)),
            pltpu.SemaphoreType.DMA((9,)),
            pltpu.SemaphoreType.DMA((9,)),
        ],
        compiler_params=pltpu.CompilerParams(
            collective_id=number, has_side_effects=True, vmem_limit_bytes=40 * 2**20
        ),
        cost_estimate=COST,
    )(d_units, qkv, cosine, sine_signed, gains, inverse)


BLOCK = 512


def attend_kernel(len_ref, q_ref, k_ref, v_ref, o_ref, o32_ref, lse_ref):
    i = pl.program_id(0)
    bq, bk = q_ref.shape[0], BLOCK
    length = len_ref[0]
    scale = HEAD_DIM ** (-0.5)
    q = q_ref[...]
    rows = i * bq + lax.broadcasted_iota(jnp.int32, (bq, bk), 0)
    cols0 = lax.broadcasted_iota(jnp.int32, (bq, bk), 1)

    def step(j, carry, masked):
        top, total, acc = carry
        j0 = pl.multiple_of(j * bk, bk)
        scores = contract_last(q, k_ref[pl.ds(j0, bk), :]) * scale
        if masked:
            cols = j0 + cols0
            scores = jnp.where((cols <= rows) & (cols < length), scores, masked_score)
        new = jnp.maximum(top, jnp.max(scores, axis=1, keepdims=True))
        weights = jnp.exp(scores - new)
        fix = jnp.exp(top - new)
        total = total * fix + jnp.sum(weights, axis=1, keepdims=True)
        acc = acc * fix + matmul(weights.astype(bf16), v_ref[pl.ds(j0, bk), :])
        return new, total, acc

    carry = (
        jnp.full((bq, 1), -jnp.inf, f32),
        jnp.zeros((bq, 1), f32),
        jnp.zeros((bq, HEAD_DIM), f32),
    )
    whole = jnp.minimum(i, length // bk)
    last = jnp.minimum(i + 1, (length + bk - 1) // bk)
    carry = lax.fori_loop(0, whole, lambda j, s: step(j, s, False), carry)
    top, total, acc = lax.fori_loop(whole, last, lambda j, s: step(j, s, True), carry)
    out = acc / total
    o_ref[...] = out.astype(bf16)
    o32_ref[...] = out
    lse_ref[...] = jnp.broadcast_to((top + jnp.log(total)).T, lse_ref.shape)


def attend(length, q, k, v):
    slots = q.shape[0]
    whole = pl.BlockSpec((slots, HEAD_DIM), lambda i: (0, 0))
    part = pl.BlockSpec((BLOCK, HEAD_DIM), lambda i: (i, 0))
    return pl.pallas_call(
        attend_kernel,
        name="attend",
        grid=(slots // BLOCK,),
        out_shape=(
            jax.ShapeDtypeStruct((slots, HEAD_DIM), bf16),
            jax.ShapeDtypeStruct((slots, HEAD_DIM), f32),
            jax.ShapeDtypeStruct((8, slots), f32),
        ),
        in_specs=[pl.BlockSpec(memory_space=pltpu.SMEM), part, whole, whole],
        out_specs=(part, part, pl.BlockSpec((8, BLOCK), lambda i: (0, i))),
        cost_estimate=COST,
    )(length, q, k, v)


def attend_back_kernel(
    len_ref, q_ref, k_ref, v_ref, do_ref, o_ref, lse_ref, out_ref, dq_acc, delta_ref
):
    j = pl.program_id(0)
    bk, bq = k_ref.shape[0], BLOCK
    slots = q_ref.shape[0]
    length = len_ref[0]
    scale = HEAD_DIM ** (-0.5)

    @pl.when(j == 0)
    def _():
        dq_acc[...] = jnp.zeros_like(dq_acc)
        for i in range(slots // bq):
            here = slice(i * bq, (i + 1) * bq)
            product = do_ref[here, :].astype(f32) * o_ref[here, :]
            delta_ref[0:1, here] = jnp.sum(product, axis=1, keepdims=True).T

    k, v = k_ref[...], v_ref[...]
    j0 = j * bk
    cols = j0 + lax.broadcasted_iota(jnp.int32, (bk, bq), 0)
    rows0 = lax.broadcasted_iota(jnp.int32, (bk, bq), 1)

    def step(i, carry, masked):
        dk, dv = carry
        i0 = pl.multiple_of(i * bq, bq)
        here = pl.ds(i0, bq)
        q, do = q_ref[here, :], do_ref[here, :]
        scores = contract_last(k, q) * scale
        if masked:
            scores = jnp.where((cols <= i0 + rows0) & (cols < length), scores, masked_score)
        probs = jnp.exp(scores - lse_ref[0:1, here])
        dv = dv + matmul(probs.astype(bf16), do)
        d_probs = contract_last(v, do)
        d_scores = (probs * (d_probs - delta_ref[0:1, here])).astype(bf16)
        dk = dk + matmul(d_scores, q)
        dq_acc[here, :] += contract_first(d_scores, k)
        return dk, dv

    zero = jnp.zeros((bk, HEAD_DIM), f32)
    top = slots // bq
    first = jnp.where(j0 + bk <= length, j + 1, top)
    first = jnp.where(j0 < length, first, j)
    stop = jnp.where(j0 < length, top, j)
    carry = lax.fori_loop(j, first, lambda i, s: step(i, s, True), (zero, zero))
    dk, dv = lax.fori_loop(first, stop, lambda i, s: step(i, s, False), carry)
    there = pl.ds(pl.multiple_of(j0, bk), bk)
    out_ref[1, there, :] = (dk * scale).astype(bf16)
    out_ref[2, there, :] = dv.astype(bf16)

    @pl.when(j == pl.num_programs(0) - 1)
    def _():
        out_ref[0] = (dq_acc[...] * scale).astype(bf16)


def attend_back(length, q, k, v, do, o, lse):
    slots = q.shape[0]
    whole = pl.BlockSpec((slots, HEAD_DIM), lambda j: (0, 0))
    part = pl.BlockSpec((BLOCK, HEAD_DIM), lambda j: (j, 0))
    line = pl.BlockSpec((8, slots), lambda j: (0, 0))
    return pl.pallas_call(
        attend_back_kernel,
        name="attend_back",
        grid=(slots // BLOCK,),
        out_shape=jax.ShapeDtypeStruct((3, slots, HEAD_DIM), bf16),
        in_specs=[pl.BlockSpec(memory_space=pltpu.SMEM), whole, part, part, whole, whole, line],
        out_specs=pl.BlockSpec((3, slots, HEAD_DIM), lambda j: (0, 0, 0)),
        scratch_shapes=[pltpu.VMEM((slots, HEAD_DIM), f32), pltpu.VMEM((8, slots), f32)],
        cost_estimate=COST,
    )(length, q, k, v, do, o, lse)


def per_device(
    tokens,
    seq_lengths,
    w_query,
    w_key,
    w_value,
    w_out,
    w_gate,
    w_up,
    w_down,
    q_gain,
    k_gain,
    attn_gain,
    mlp_gain,
    cotangent,
):
    tok_rows, feat_part = tokens.shape
    row_count, data_count = lax.axis_size("row"), lax.axis_size("dp")
    width = feat_part * lax.axis_size("col")
    slots = tok_rows * row_count
    half_feat = feat_part // 2
    y, z = side("dp"), lax.axis_index("row")
    p = z & 1
    heads = half_feat // HEAD_DIM
    hid = w_gate.shape[1] // 4
    pairs = [(i, i ^ 1) for i in range(data_count)]
    after = lambda values, *done: lax.optimization_barrier((values,) + done)[0]

    def y_half(values, axis):
        size = values.shape[axis] // 2
        return lax.dynamic_slice_in_dim(values, y * size, size, axis)

    def row_swap(values, d):
        return lax.ppermute(values, "row", [(i, i ^ d) for i in range(row_count)])

    def hidden_parts(*done):
        def quarters(d):
            start = (y * 2 + (p ^ (d & 1))) * hid
            return jnp.stack(
                [
                    lax.dynamic_slice_in_dim(w_gate, start, hid, 1),
                    lax.dynamic_slice_in_dim(w_up, start, hid, 1),
                    lax.dynamic_slice_in_dim(w_down, start, hid, 0),
                ]
            )

        parts = [quarters(0)] + [row_swap(after(quarters(d), *done), d) for d in (1, 2, 3)]
        depth = w_gate.shape[0]
        gate_up = jnp.zeros((width, 2 * hid), bf16)
        down = jnp.zeros((hid, width), bf16)
        for d, part in enumerate(parts):
            spot = (z ^ d) * depth
            gate_up = lax.dynamic_update_slice(gate_up, part[0], (spot, 0))
            gate_up = lax.dynamic_update_slice(gate_up, part[1], (spot, hid))
            down = lax.dynamic_update_slice(down, part[2], (0, spot))
        return gate_up, down

    qkv_weight = lax.all_gather(
        jnp.concatenate([y_half(w_query, 1), y_half(w_key, 1), y_half(w_value, 1)], axis=1),
        "row",
        axis=0,
        tiled=True,
    )
    out_weight = lax.all_gather(y_half(after(w_out, qkv_weight), 0), "row", axis=1, tiled=True)

    positions = z * tok_rows + jnp.arange(tok_rows)
    length = seq_lengths[0]
    valid = (positions < length).astype(f32)[:, None]
    cosine, sine = rope_tables(positions, HEAD_DIM)
    sine_signed = jnp.where(jnp.arange(HEAD_DIM)[None, :] < HEAD_DIM // 2, -sine, sine)
    other_length = lax.ppermute(seq_lengths, "dp", pairs)
    pair_lengths = jnp.where(
        y == 0,
        jnp.concatenate([seq_lengths, other_length]),
        jnp.concatenate([other_length, seq_lengths]),
    )
    unit_length = lax.dynamic_slice_in_dim(pair_lengths, z // heads, 1)
    qk_gain = jnp.stack([y_half(q_gain, 0), y_half(k_gain, 0)])

    tokens_wide = gather_wide(tokens, False, 0, "gather_tokens")
    qkv = matmul(tokens_wide, qkv_weight)
    units, inverse = front(qkv, cosine, sine_signed, qk_gain, width, 2 * heads, 2)
    q_unit, k_unit, v_unit = (units[:, i].reshape(slots, HEAD_DIM) for i in range(3))
    gate_up_weight, down_weight = hidden_parts(units)
    attn_unit, attn_exact, log_total = attend(unit_length, q_unit, k_unit, v_unit)
    attn_low = turn(attn_unit, True, tok_rows, heads, 3, "turn_attn")
    branch = scatter_wide(matmul(attn_low, out_weight).astype(bf16), False, 4, "scatter_branch")
    branch_inv = lax.rsqrt(
        feature_total(jnp.sum(branch * branch, axis=1)[None, :], 5, "total_branch")[0] / width
        + norm_eps
    )[:, None]
    resid = tokens.astype(f32) + branch * branch_inv * attn_gain
    resid_wide = gather_wide(resid.astype(bf16), True, 6, "gather_resid")
    gate = matmul(resid_wide, gate_up_weight[:, :hid])
    upper = matmul(resid_wide, gate_up_weight[:, hid:])
    sigma = jax.nn.sigmoid(gate)
    hidden = (gate * sigma * upper).astype(bf16)
    mixed = scatter_wide(matmul(hidden, down_weight).astype(bf16), True, 7, "scatter_mixed")
    incoming = cotangent.astype(f32) * valid
    gained = incoming * mlp_gain
    sums = feature_total(
        jnp.stack([jnp.sum(mixed * mixed, axis=1), jnp.sum(gained * mixed, axis=1)]),
        8,
        "total_mixed",
    )
    mixed_inv = lax.rsqrt(sums[0] / width + norm_eps)[:, None]
    inner = (sums[1] / width)[:, None]
    block_output = ((resid + mixed * mixed_inv * mlp_gain) * valid).astype(bf16)
    mlp_gain_raw = jnp.sum(incoming * mixed * mixed_inv, axis=0)
    d_mixed = (mixed_inv * gained - mixed * mixed_inv**3 * inner).astype(bf16)
    d_mixed_wide = gather_wide(d_mixed, True, 9, "gather_d_mixed")

    factor = 1.0 / math.sqrt(slots * data_count)

    def cut(values, index, count, axis):
        size = values.shape[axis] // count
        return lax.dynamic_slice_in_dim(values, index * size, size, axis)

    def over_dp(piece):
        if data_count > 2:
            groups = [list(range(s, data_count, 2)) for s in (0, 1)]
            piece = lax.psum(piece, "dp", axis_index_groups=groups)
        return piece

    def two_sides(piece, other, bit, axis):
        low = jnp.where(bit == 0, piece, other)
        high = jnp.where(bit == 0, other, piece)
        return jnp.concatenate([low, high], axis=axis)


    def from_far(raw, axis):
        return row_swap(cut(raw, 1 - (z >> 1), 2, axis), 2)

    def with_far(raw, far, axis):
        near = cut(raw, z >> 1, 2, axis)
        return over_dp((near.astype(f32) + far.astype(f32)).astype(bf16))

    def from_near(near, axis):
        own, away = cut(near, p, 2, axis), row_swap(cut(near, 1 - p, 2, axis), 1)
        return own, away

    def from_twin(own, away):
        return lax.ppermute(jnp.stack([own, away]), "dp", pairs)

    def blocks(own, away, other, axis, count):
        def block(i):
            mine = two_sides(cut(own, i, count, 1 - axis), cut(away, i, count, 1 - axis), p, 1 - axis)
            theirs = two_sides(
                cut(other[0], i, count, 1 - axis), cut(other[1], i, count, 1 - axis), p, 1 - axis
            )
            return two_sides(mine, theirs, y, 1 - axis).astype(f32)

        return [block(i) for i in range(count)]

    def reduce_rows(raw, axis):
        return lax.psum_scatter(raw, "row", scatter_dimension=axis, tiled=True)

    d_hidden = contract_last(d_mixed_wide, down_weight)
    down_raw = (contract_first(hidden, d_mixed_wide) * factor).astype(bf16)
    d_gate = (d_hidden * upper * sigma * (1.0 + gate * (1.0 - sigma))).astype(bf16)
    d_upper = (d_hidden * gate * sigma).astype(bf16)
    d_gate_up = jnp.concatenate([d_gate, d_upper], axis=1)
    gate_up_raw = (contract_first(resid_wide, d_gate_up) * factor).astype(bf16)
    d_resid_wide = contract_last(d_gate_up, gate_up_weight).astype(bf16)
    d_resid_wide, down_raw, gate_up_raw = lax.optimization_barrier(
        (d_resid_wide, down_raw, gate_up_raw)
    )
    d_resid, far_down = scatter_wide(d_resid_wide, True, 10, "scatter_d_resid", down_raw)
    d_resid = incoming + d_resid
    far_gate_up = from_far(gate_up_raw, 0)
    attn_gain_raw = jnp.sum(d_resid * branch * branch_inv, axis=0)
    gained = d_resid * attn_gain
    inner = (
        feature_total(jnp.sum(gained * branch, axis=1)[None, :], 11, "total_d_resid")[0][:, None]
        / width
    )
    d_branch = (branch_inv * gained - branch * branch_inv**3 * inner).astype(bf16)
    d_branch_wide, far_down = lax.optimization_barrier(
        (gather_wide(d_branch, False, 12, "gather_d_branch"), far_down)
    )
    own_down, away_down = from_near(with_far(down_raw, far_down, 1), 1)
    d_attn = contract_last(d_branch_wide, out_weight).astype(bf16)
    d_attn_unit = turn(d_attn, False, tok_rows, heads, 13, "turn_d_attn")
    out_raw = (contract_first(attn_low, after(d_branch_wide, d_attn_unit)) * factor).astype(bf16)
    d_attn_unit, out_raw = lax.optimization_barrier((d_attn_unit, out_raw))
    out_piece = reduce_rows(out_raw, 1)
    d_units = attend_back(unit_length, q_unit, k_unit, v_unit, d_attn_unit, attn_exact, log_total)
    d_units, far_gate_up, away_down = lax.optimization_barrier((d_units, far_gate_up, away_down))
    own_gate_up, away_gate_up = from_near(with_far(gate_up_raw, far_gate_up, 0), 0)
    other_down = from_twin(own_down, away_down)
    d_qkv, gain_sums = rear(
        d_units, qkv[:, : 2 * half_feat], cosine, sine_signed, qk_gain, inverse, width, 14
    )
    d_qkv, away_gate_up, other_down = lax.optimization_barrier((d_qkv, away_gate_up, other_down))
    other_gate_up = from_twin(own_gate_up, away_gate_up)
    qkv_raw = (contract_first(tokens_wide, d_qkv) * factor).astype(bf16)
    projected = contract_last(d_qkv, qkv_weight).astype(bf16)
    projected, qkv_raw = lax.optimization_barrier((projected, qkv_raw))
    qkv_piece = over_dp(reduce_rows(qkv_raw, 0))
    input_grad = d_resid + scatter_wide(projected, False, 16, "scatter_projected")

    def spread(half):
        return lax.dynamic_update_slice_in_dim(jnp.zeros((feat_part,), f32), half, y * half_feat, 0)

    gains = over_dp(
        gain_total(
            jnp.stack([spread(gain_sums[0]), spread(gain_sums[1]), attn_gain_raw, mlp_gain_raw])
            * factor,
            15,
        )
    )
    (down_grad,) = blocks(own_down, away_down, other_down, 1, 1)
    gate_grad, up_grad = blocks(own_gate_up, away_gate_up, other_gate_up, 0, 2)
    qkv_other = lax.ppermute(qkv_piece, "dp", pairs)
    q_grad, k_grad, v_grad = (
        two_sides(cut(qkv_piece, i, 3, 1), cut(qkv_other, i, 3, 1), y, 1).astype(f32)
        for i in range(3)
    )
    out_piece = over_dp(out_piece)
    out_grad = two_sides(out_piece, lax.ppermute(out_piece, "dp", pairs), y, 0).astype(f32)
    return (
        block_output,
        input_grad,
        q_grad,
        k_grad,
        v_grad,
        out_grad,
        gate_grad,
        up_grad,
        down_grad,
        gains[0],
        gains[1],
        gains[2],
        gains[3],
    )


def solution(mesh):
    tok, row_col, col_row, gain = P(("dp", "row"), "col"), P("row", "col"), P("col", "row"), P("col")
    weights = (row_col, row_col, row_col, col_row, row_col, row_col, col_row)
    gains = (gain, gain, gain, gain)
    return jax.shard_map(
        per_device,
        mesh=mesh,
        in_specs=(tok, P("dp")) + weights + gains + (tok,),
        out_specs=(tok, tok) + weights + gains,
        check_vma=False,
    )
```

```python
import functools
import math

import jax
import jax.numpy as jnp
from jax import lax
from jax.experimental import pallas as pl
from jax.experimental.pallas import tpu as pltpu
from jax.sharding import PartitionSpec as P

HEAD_DIM = 128
rope_base = 500000.0
norm_eps = 1e-06
masked_score = -1e30

MESH = pl.DeviceIdType.MESH
bf16 = jnp.bfloat16
f32 = jnp.float32
COST = pl.CostEstimate(flops=0, bytes_accessed=1000, transcendentals=0)


def rope_tables(positions, head_dim):
    half = head_dim // 2
    freq = 1.0 / rope_base ** (jnp.arange(half, dtype=f32) / half)
    angle = positions.astype(f32)[:, None] * freq[None, :]
    angle = jnp.concatenate([angle, angle], axis=1)
    return (jnp.cos(angle), jnp.sin(angle))


def matmul(left, right):
    return jnp.dot(left, right, preferred_element_type=f32)


def contract_first(left, right):
    return lax.dot_general(left, right, (((0,), (0,)), ((), ())), preferred_element_type=f32)


def contract_last(left, right):
    return lax.dot_general(left, right, (((1,), (1,)), ((), ())), preferred_element_type=f32)


def flip(axis, bit):
    return lax.axis_index(axis) ^ bit


def side(axis):
    return lax.axis_index(axis) & 1


def greet(peers):
    barrier = pltpu.get_barrier_semaphore()
    for peer in peers:
        pl.semaphore_signal(barrier, inc=1, device_id=peer, device_id_type=MESH)
    pl.semaphore_wait(barrier, len(peers))


def sender(send_sem, recv_sem, started):
    def send(src, dst, number, peer):
        copy = pltpu.make_async_remote_copy(
            src_ref=src,
            dst_ref=dst,
            send_sem=send_sem.at[number],
            recv_sem=recv_sem.at[number],
            device_id=peer,
            device_id_type=MESH,
        )
        copy.start()
        started.append(copy)
        return copy

    return send


def neighbours():
    return {"col": flip("col", 2)}, {"dp": flip("dp", 1)}, {"col": flip("col", 1)}


def gather_kernel(pair, x_ref, out_ref, local_sem, send_sem, recv_sem):
    rows, width = x_ref.shape
    half = rows // 2
    y, b, p = side("dp"), lax.axis_index("col"), side("row") if pair else 0
    to_x, to_y, to_c = neighbours()
    to_z = {"row": flip("row", 1)}
    greet([to_x, to_y, to_c] + ([to_z] if pair else []))
    started = []
    send = sender(send_sem, recv_sem, started)

    def slot(pp, yy, h, bb, n=half):
        return out_ref.at[
            pl.ds(pl.multiple_of((pp * 2 + yy) * rows + h * half, half), n),
            pl.ds(pl.multiple_of(bb * width, width), width),
        ]

    def open_flow(pp, low, high, base):
        xa = send(low, slot(pp, y, 0, b), base + 0, to_x)
        ya = send(high, slot(pp, y, 1, b), base + 1, to_y)
        c0 = send(low, slot(pp, y, 0, b), base + 6, to_c)
        yb = send(low, slot(pp, y, 0, b), base + 2, to_y)
        xb = send(high, slot(pp, y, 1, b), base + 3, to_x)
        c1 = send(high, slot(pp, y, 1, b), base + 7, to_c)
        return xa, ya, xb, yb, [c0, c1]

    def relay(pp, flow, base):
        xa, ya, xb, yb, core = flow
        xa.wait_recv()
        piece = slot(pp, y, 0, b ^ 2)
        yc = send(piece, piece, base + 4, to_y)
        core.append(send(piece, piece, base + 8, to_c))
        ya.wait_recv()
        piece = slot(pp, y ^ 1, 1, b)
        xc = send(piece, piece, base + 5, to_x)
        core.append(send(piece, piece, base + 9, to_c))
        yb.wait_recv()
        piece = slot(pp, y ^ 1, 0, b)
        core.append(send(piece, piece, base + 10, to_c))
        xb.wait_recv()
        piece = slot(pp, y, 1, b ^ 2)
        core.append(send(piece, piece, base + 11, to_c))
        return yc, xc, core

    def close_flow(pp, state, base):
        yc, xc, core = state
        yc.wait_recv()
        piece = slot(pp, y ^ 1, 0, b ^ 2)
        core.append(send(piece, piece, base + 12, to_c))
        xc.wait_recv()
        piece = slot(pp, y ^ 1, 1, b ^ 2)
        core.append(send(piece, piece, base + 13, to_c))
        for copy in core:
            copy.wait_recv()

    low, high = x_ref.at[pl.ds(0, half)], x_ref.at[pl.ds(half, half)]
    own = pltpu.make_async_copy(x_ref, slot(p, y, 0, b, rows), local_sem)
    if pair:
        z0 = send(low, slot(p, y, 0, b), 28, to_z)
        z1 = send(high, slot(p, y, 1, b), 29, to_z)
    first = open_flow(p, low, high, 0)
    own.start()
    state = relay(p, first, 0)
    if pair:
        z0.wait_recv()
        z1.wait_recv()
        second = open_flow(p ^ 1, slot(p ^ 1, y, 0, b), slot(p ^ 1, y, 1, b), 14)
    close_flow(p, state, 0)
    if pair:
        close_flow(p ^ 1, relay(p ^ 1, second, 14), 14)
    for copy in started:
        copy.wait_send()
    own.wait()


def gather_wide(values, pair, number, name):
    rows, width = values.shape
    copies = 30 if pair else 14
    return pl.pallas_call(
        functools.partial(gather_kernel, pair),
        name=name,
        out_shape=jax.ShapeDtypeStruct(((4 if pair else 2) * rows, 4 * width), values.dtype),
        in_specs=[pl.BlockSpec(memory_space=pltpu.VMEM)],
        out_specs=pl.BlockSpec(memory_space=pl.ANY),
        scratch_shapes=[
            pltpu.SemaphoreType.DMA,
            pltpu.SemaphoreType.DMA((copies,)),
            pltpu.SemaphoreType.DMA((copies,)),
        ],
        compiler_params=pltpu.CompilerParams(collective_id=number, has_side_effects=True),
        cost_estimate=COST,
    )(values)


def scatter_kernel(pair, rider, p_ref, *refs):
    if rider:
        cargo_ref, out_ref, far_ref = refs[:3]
    else:
        out_ref = refs[0]
    rc, s1, ry, rx, s2, fy, fx, sz, fz, send_sem, recv_sem = refs[3 if rider else 1 :]
    rows, width = out_ref.shape
    half = rows // 2
    y, b, p = side("dp"), lax.axis_index("col"), side("row") if pair else 0
    x, c = b >> 1, b & 1
    to_x, to_y, to_c = neighbours()
    to_z = {"row": flip("row", 1)}
    to_far = {"row": flip("row", 2)}
    greet([to_x, to_y, to_c] + ([to_z] if pair else []) + ([to_far] if rider else []))
    started = []
    send = sender(send_sem, recv_sem, started)
    if rider:
        size = far_ref.shape[1]
        start = pl.multiple_of((1 - (lax.axis_index("row") >> 1)) * size, size)
        cargo = send(cargo_ref.at[:, pl.ds(start, size)], far_ref, 30, to_far)

    def place(yy, h):
        return pl.ds(pl.multiple_of(yy * rows + h * half, half), half)

    def column(bb):
        return pl.ds(pl.multiple_of(bb * width, width), width)

    order = [(0, y ^ 1, 0), (1, y ^ 1, 0), (x ^ 1, 0, 1), (x ^ 1, 1, 1)]
    order += [(0, y, 0), (1, y, 0), (x, 0, 1), (x, 1, 1)]

    class Flow:
        def __init__(self, f, pp):
            self.f, self.base = f, 14 * f
            self.rows = lambda yy, h: pl.ds(
                pl.multiple_of((pp * 2 + yy) * rows + h * half, half), half
            )
            self.core = [
                send(
                    p_ref.at[self.rows(yy, h), column(2 * xx + (c ^ 1))],
                    rc.at[f, xx, place(yy, h)],
                    self.base + number,
                    to_c,
                )
                for number, (xx, yy, h) in enumerate(order)
            ]

        def settle(self, *numbers):
            for number in numbers:
                self.core[number].wait_recv()
                xx, yy, h = order[number]
                s1[self.f, xx, place(yy, h), :] = (
                    p_ref[self.rows(yy, h), column(2 * xx + c)].astype(f32)
                    + rc[self.f, xx, place(yy, h), :].astype(f32)
                ).astype(s1.dtype)

        def first(self, i):
            f = self.f
            ya = send(s1.at[f, i, place(y ^ 1, 0), :], ry.at[f, i], self.base + 8 + i, to_y)
            part = s1.at[f, x ^ 1, pl.ds(i * rows + half, half), :]
            xa = send(part, rx.at[f, i], self.base + 10 + i, to_x)
            return ya, xa

        def second(self, copies):
            f = self.f
            for ya, _ in copies:
                ya.wait_recv()
            s2[f, 0] = (
                s1[f, x ^ 1, place(y, 0), :].astype(f32) + ry[f, x ^ 1].astype(f32)
            ).astype(s2.dtype)
            xb = send(s2.at[f, 0], fx.at[f], self.base + 12, to_x)
            for _, xa in copies:
                xa.wait_recv()
            s2[f, 1] = (
                s1[f, x, place(y ^ 1, 1), :].astype(f32) + rx[f, y ^ 1].astype(f32)
            ).astype(s2.dtype)
            yb = send(s2.at[f, 1], fy.at[f], self.base + 13, to_y)
            return xb, yb

        def last(self, copies):
            f = self.f
            xb, yb = copies
            keep = s1[f, x, place(y, 0), :].astype(f32) + ry[f, x].astype(f32)
            xb.wait_recv()
            low = keep + fx[f].astype(f32)
            keep = s1[f, x, place(y, 1), :].astype(f32) + rx[f, y].astype(f32)
            yb.wait_recv()
            return low, keep + fy[f].astype(f32)

    if pair:
        far = Flow(0, p ^ 1)
        near = Flow(1, p)
        far.settle(0, 1, 2, 3)
        far_first = [far.first(0), far.first(1)]
        far.settle(4, 5, 6, 7)
        near.settle(0, 1, 2, 3)
        near_first = [near.first(0)]
        near.settle(4, 5, 6, 7)
        far_second = far.second(far_first)
        near_first.append(near.first(1))
        low, high = far.last(far_second)
        sz[pl.ds(0, half), :] = low.astype(bf16)
        z0 = send(sz.at[pl.ds(0, half)], fz.at[pl.ds(0, half)], 28, to_z)
        sz[pl.ds(half, half), :] = high.astype(bf16)
        z1 = send(sz.at[pl.ds(half, half)], fz.at[pl.ds(half, half)], 29, to_z)
        low, high = near.last(near.second(near_first))
        z0.wait_recv()
        out_ref[pl.ds(0, half), :] = low + fz[pl.ds(0, half), :].astype(f32)
        z1.wait_recv()
        out_ref[pl.ds(half, half), :] = high + fz[pl.ds(half, half), :].astype(f32)
    else:
        near = Flow(0, 0)
        near.settle(0, 1, 2, 3)
        near_first = [near.first(0), near.first(1)]
        near.settle(4, 5, 6, 7)
        low, high = near.last(near.second(near_first))
        out_ref[pl.ds(0, half), :] = low
        out_ref[pl.ds(half, half), :] = high
    if rider:
        cargo.wait_recv()
    for copy in started:
        copy.wait_send()


def scatter_wide(partial, pair, number, name, cargo=None):
    flows = 2 if pair else 1
    rows, width = partial.shape[0] // (2 * flows), partial.shape[1] // 4
    half = rows // 2
    rider = cargo is not None
    copies = 31 if pair else 14
    out_shape, out_spec = [jax.ShapeDtypeStruct((rows, width), f32)], [pl.BlockSpec(memory_space=pltpu.VMEM)]
    anywhere = [pl.BlockSpec(memory_space=pl.ANY)] * rider
    if rider:
        out_shape.append(jax.ShapeDtypeStruct((cargo.shape[0], cargo.shape[1] // 2), cargo.dtype))
    last = (rows, width) if pair else (16, 128)
    out = pl.pallas_call(
        functools.partial(scatter_kernel, pair, rider),
        name=name,
        out_shape=out_shape,
        in_specs=[pl.BlockSpec(memory_space=pltpu.VMEM)] + anywhere,
        out_specs=out_spec + anywhere,
        scratch_shapes=[
            pltpu.VMEM((flows, 2, 2 * rows, width), bf16),
            pltpu.VMEM((flows, 2, 2 * rows, width), bf16),
            pltpu.VMEM((flows, 2, half, width), bf16),
            pltpu.VMEM((flows, 2, half, width), bf16),
            pltpu.VMEM((flows, 2, half, width), bf16),
            pltpu.VMEM((flows, half, width), bf16),
            pltpu.VMEM((flows, half, width), bf16),
            pltpu.VMEM(last, bf16),
            pltpu.VMEM(last, bf16),
            pltpu.SemaphoreType.DMA((copies,)),
            pltpu.SemaphoreType.DMA((copies,)),
        ],
        compiler_params=pltpu.CompilerParams(
            collective_id=number, has_side_effects=True, vmem_limit_bytes=48 * 2**20
        ),
        cost_estimate=COST,
    )(partial, *([cargo] * rider))
    return out if rider else out[0]


def feature_peers(wide):
    peers = []
    for d in range(1, 8 if wide else 4):
        peer = {"col": flip("col", d & 3)}
        if d >> 2:
            peer["dp"] = flip("dp", 1)
        peers.append(peer)
    return peers


def total_kernel(v_ref, out_ref, slots, send_sem, recv_sem):
    me = lax.axis_index("col")
    peers = feature_peers(False)
    greet(peers)
    started = []
    send = sender(send_sem, recv_sem, started)
    for d, peer in enumerate(peers):
        send(v_ref, slots.at[me], d, peer)
    slots[me] = v_ref[...]
    for copy in started:
        copy.wait_recv()
    total = slots[0]
    for i in range(1, 4):
        total = total + slots[i]
    out_ref[...] = total
    for copy in started:
        copy.wait_send()


def feature_total(values, number, name):
    k, t = values.shape
    flat = values.reshape(k * t // 128, 128)
    total = pl.pallas_call(
        total_kernel,
        name=name,
        out_shape=jax.ShapeDtypeStruct(flat.shape, f32),
        in_specs=[pl.BlockSpec(memory_space=pltpu.VMEM)],
        out_specs=pl.BlockSpec(memory_space=pltpu.VMEM),
        scratch_shapes=[
            pltpu.VMEM((4,) + flat.shape, f32),
            pltpu.SemaphoreType.DMA((3,)),
            pltpu.SemaphoreType.DMA((3,)),
        ],
        compiler_params=pltpu.CompilerParams(collective_id=number, has_side_effects=True),
    )(flat)
    return total.reshape(k, t)


def gain_peers():
    peers = []
    for d in range(1, 8):
        peers.append({"row": flip("row", d & 3), "dp": flip("dp", d >> 2)})
    return peers


def gain_kernel(v_ref, out_ref, slots, send_sem, recv_sem):
    me = side("dp") * 4 + lax.axis_index("row")
    peers = gain_peers()
    greet(peers)
    started = []
    send = sender(send_sem, recv_sem, started)
    for d, peer in enumerate(peers):
        send(v_ref, slots.at[me], d, peer)
    slots[me] = v_ref[...]
    for copy in started:
        copy.wait_recv()
    total = slots[0]
    for i in range(1, 8):
        total = total + slots[i]
    out_ref[...] = total
    for copy in started:
        copy.wait_send()


def gain_total(values, number):
    flat = values.reshape(-1, 128)
    total = pl.pallas_call(
        gain_kernel,
        name="total_gains",
        out_shape=jax.ShapeDtypeStruct(flat.shape, f32),
        in_specs=[pl.BlockSpec(memory_space=pltpu.VMEM)],
        out_specs=pl.BlockSpec(memory_space=pltpu.VMEM),
        scratch_shapes=[
            pltpu.VMEM((8,) + flat.shape, f32),
            pltpu.SemaphoreType.DMA((7,)),
            pltpu.SemaphoreType.DMA((7,)),
        ],
        compiler_params=pltpu.CompilerParams(collective_id=number, has_side_effects=True),
    )(flat)
    return total.reshape(values.shape)


def row_peers():
    return [(d, {"row": flip("row", d)}) for d in (3, 2, 1)]


def unit_view(ref, unit, tok, heads):
    rows = pl.ds(pl.multiple_of((unit // heads) * tok, tok), tok)
    cols = pl.ds(pl.multiple_of((unit % heads) * HEAD_DIM, HEAD_DIM), HEAD_DIM)
    return ref.at[rows, cols]


def turn_kernel(back, tok, heads, x_ref, out_ref, local_sem, send_sem, recv_sem):
    z = lax.axis_index("row")
    greet([peer for _, peer in row_peers()])
    started = []
    send = sender(send_sem, recv_sem, started)

    def line(ref, i):
        return ref.at[pl.ds(pl.multiple_of(i * tok, tok), tok)]

    def ends(i):
        if back:
            return line(x_ref, i), unit_view(out_ref, z, tok, heads)
        return unit_view(x_ref, i, tok, heads), line(out_ref, z)

    for d, peer in row_peers():
        send(*ends(z ^ d), d - 1, peer)
    own = pltpu.make_async_copy(*ends(z), local_sem)
    own.start()
    for copy in started:
        copy.wait()
    own.wait()


def turn(values, back, tok, heads, number, name):
    shape = (2 * tok, heads * HEAD_DIM) if back else (2 * heads * tok, HEAD_DIM)
    return pl.pallas_call(
        functools.partial(turn_kernel, back, tok, heads),
        name=name,
        out_shape=jax.ShapeDtypeStruct(shape, values.dtype),
        in_specs=[pl.BlockSpec(memory_space=pltpu.VMEM)],
        out_specs=pl.BlockSpec(memory_space=pl.ANY),
        scratch_shapes=[
            pltpu.SemaphoreType.DMA,
            pltpu.SemaphoreType.DMA((3,)),
            pltpu.SemaphoreType.DMA((3,)),
        ],
        compiler_params=pltpu.CompilerParams(collective_id=number, has_side_effects=True),
        cost_estimate=COST,
    )(values)


def totals(stat, slots, started):
    for copy in started:
        copy.wait_recv()
    total = slots[0]
    for i in range(1, 8):
        total = total + slots[i]
    return total


def front_kernel(
    width,
    qkv_ref,
    cos_ref,
    sin_ref,
    gain_ref,
    out_ref,
    inv_ref,
    turned,
    packed,
    stat,
    slots,
    local_sem,
    stat_send,
    stat_recv,
    send_sem,
    recv_sem,
):
    count, tok = qkv_ref.shape[0], cos_ref.shape[0]
    part = qkv_ref.shape[1] // 3
    heads = part // HEAD_DIM
    z = lax.axis_index("row")
    me = side("dp") * 4 + lax.axis_index("col")
    peers = feature_peers(True)
    greet(peers + [peer for _, peer in row_peers()])
    for i in range(2):
        values = qkv_ref[:, i * part : (i + 1) * part]
        stat[i : i + 1, :] = jnp.sum(values * values, axis=1, keepdims=True).T
    started, moved, local = [], [], []
    send = sender(stat_send, stat_recv, started)
    for d, peer in enumerate(peers):
        send(stat, slots.at[me], d, peer)
    slots[me] = stat[...]
    move = sender(send_sem, recv_sem, moved)

    def ship(i):
        for d, peer in row_peers():
            move(packed.at[z ^ d, i], out_ref.at[z, i], 3 * i + d - 1, peer)
        copy = pltpu.make_async_copy(packed.at[z, i], out_ref.at[z, i], local_sem.at[i])
        copy.start()
        local.append(copy)

    def spots():
        return [(s, h, s * heads + h) for s in range(2) for h in range(heads)]

    for s, h, unit in spots():
        packed[unit, 2] = qkv_ref[
            s * tok : (s + 1) * tok, 2 * part + h * HEAD_DIM : 2 * part + (h + 1) * HEAD_DIM
        ].astype(bf16)
    ship(2)
    for i in (1, 0):
        for s, h, unit in spots():
            values = (
                qkv_ref[s * tok : (s + 1) * tok, i * part + h * HEAD_DIM : i * part + (h + 1) * HEAD_DIM]
                * gain_ref[i : i + 1, h * HEAD_DIM : (h + 1) * HEAD_DIM]
            )
            turned[i, unit] = values * cos_ref[...] + pltpu.roll(values, HEAD_DIM // 2, 1) * sin_ref[...]
    inverse = lax.rsqrt(totals(stat, slots, started) / width + norm_eps)
    inv_ref[...] = inverse
    for i in (1, 0):
        column = inverse[i : i + 1, :].T
        for s, h, unit in spots():
            packed[unit, i] = (turned[i, unit] * column[s * tok : (s + 1) * tok]).astype(bf16)
        ship(i)
    for copy in moved:
        copy.wait()
    for copy in local:
        copy.wait()
    for copy in started:
        copy.wait_send()


def front(qkv, cosine, sine_signed, gains, width, units, number):
    count, tok = qkv.shape[0], cosine.shape[0]
    return pl.pallas_call(
        functools.partial(front_kernel, width),
        name="front",
        out_shape=(
            jax.ShapeDtypeStruct((units, 3, tok, HEAD_DIM), bf16),
            jax.ShapeDtypeStruct((2, count), f32),
        ),
        in_specs=[pl.BlockSpec(memory_space=pltpu.VMEM)] * 4,
        out_specs=(pl.BlockSpec(memory_space=pl.ANY), pl.BlockSpec(memory_space=pltpu.VMEM)),
        scratch_shapes=[
            pltpu.VMEM((2, units, tok, HEAD_DIM), f32),
            pltpu.VMEM((units, 3, tok, HEAD_DIM), bf16),
            pltpu.VMEM((2, count), f32),
            pltpu.VMEM((8, 2, count), f32),
            pltpu.SemaphoreType.DMA((3,)),
            pltpu.SemaphoreType.DMA((7,)),
            pltpu.SemaphoreType.DMA((7,)),
            pltpu.SemaphoreType.DMA((9,)),
            pltpu.SemaphoreType.DMA((9,)),
        ],
        compiler_params=pltpu.CompilerParams(
            collective_id=number, has_side_effects=True, vmem_limit_bytes=40 * 2**20
        ),
        cost_estimate=COST,
    )(qkv, cosine, sine_signed, gains)


def rear_kernel(
    width,
    d_ref,
    qkv_ref,
    cos_ref,
    sin_ref,
    gain_ref,
    inv_ref,
    out_ref,
    sums_ref,
    landed,
    normed,
    stat,
    slots,
    stat_send,
    stat_recv,
    send_sem,
    recv_sem,
):
    count, tok = qkv_ref.shape[0], cos_ref.shape[0]
    part = qkv_ref.shape[1] // 2
    heads = part // HEAD_DIM
    z = lax.axis_index("row")
    me = side("dp") * 4 + lax.axis_index("col")
    peers = feature_peers(True)
    greet(peers + [peer for _, peer in row_peers()])
    started, moved = [], []
    move = sender(send_sem, recv_sem, moved)
    for i in (0, 1, 2):
        for d, peer in row_peers():
            there = pl.ds(pl.multiple_of((z ^ d) * tok, tok), tok)
            move(d_ref.at[i, there], landed.at[z, i], 3 * i + d - 1, peer)
    here = pl.ds(pl.multiple_of(z * tok, tok), tok)
    for i in (0, 1, 2):
        landed[z, i] = d_ref[i, here, :]
    spots = [(s, h, s * heads + h) for s in range(2) for h in range(heads)]
    for i in (0, 1):
        for copy in moved[3 * i : 3 * i + 3]:
            copy.wait_recv()
        for h in range(heads):
            cols = slice(i * part + h * HEAD_DIM, i * part + (h + 1) * HEAD_DIM)
            gain = gain_ref[i : i + 1, h * HEAD_DIM : (h + 1) * HEAD_DIM]
            raw = jnp.zeros((1, HEAD_DIM), f32)
            for s in range(2):
                rows = slice(s * tok, (s + 1) * tok)
                values = landed[s * heads + h, i].astype(f32)
                back = values * cos_ref[...] - pltpu.roll(values, HEAD_DIM // 2, 1) * sin_ref[...]
                pre = qkv_ref[rows, cols]
                inverse = inv_ref[i : i + 1, rows].T
                crossed = back * pre
                raw = raw + jnp.sum(crossed * inverse, axis=0, keepdims=True)
                partial = jnp.sum(crossed * gain, axis=1, keepdims=True).T
                if h == 0:
                    stat[i : i + 1, rows] = partial
                else:
                    stat[i : i + 1, rows] = stat[i : i + 1, rows] + partial
                normed[rows, cols] = back * gain
            sums_ref[i : i + 1, h * HEAD_DIM : (h + 1) * HEAD_DIM] = raw
    send = sender(stat_send, stat_recv, started)
    for d, peer in enumerate(peers):
        send(stat, slots.at[me], d, peer)
    slots[me] = stat[...]
    for copy in moved[6:]:
        copy.wait_recv()
    for s, h, unit in spots:
        cols = slice(2 * part + h * HEAD_DIM, 2 * part + (h + 1) * HEAD_DIM)
        out_ref[s * tok : (s + 1) * tok, cols] = landed[unit, 2]
    inner = totals(stat, slots, started) / width
    for i in (0, 1):
        inverse = inv_ref[i : i + 1, :]
        first = inverse.T
        second = (inverse * inverse * inverse * inner[i : i + 1, :]).T
        cols = slice(i * part, (i + 1) * part)
        out_ref[:, cols] = (first * normed[:, cols] - qkv_ref[:, cols] * second).astype(bf16)
    for copy in moved + started:
        copy.wait_send()


def rear(d_units, qkv, cosine, sine_signed, gains, inverse, width, number):
    count, tok = qkv.shape[0], cosine.shape[0]
    part = qkv.shape[1] // 2
    units = d_units.shape[1] // tok
    return pl.pallas_call(
        functools.partial(rear_kernel, width),
        name="rear",
        out_shape=(
            jax.ShapeDtypeStruct((count, 3 * part), bf16),
            jax.ShapeDtypeStruct((2, part), f32),
        ),
        in_specs=[pl.BlockSpec(memory_space=pltpu.VMEM)] * 6,
        out_specs=[pl.BlockSpec(memory_space=pltpu.VMEM)] * 2,
        scratch_shapes=[
            pltpu.VMEM((units, 3, tok, HEAD_DIM), bf16),
            pltpu.VMEM((count, 2 * part), f32),
            pltpu.VMEM((2, count), f32),
            pltpu.VMEM((8, 2, count), f32),
            pltpu.SemaphoreType.DMA((7,)),
            pltpu.SemaphoreType.DMA((7,)),
            pltpu.SemaphoreType.DMA((9,)),
            pltpu.SemaphoreType.DMA((9,)),
        ],
        compiler_params=pltpu.CompilerParams(
            collective_id=number, has_side_effects=True, vmem_limit_bytes=40 * 2**20
        ),
        cost_estimate=COST,
    )(d_units, qkv, cosine, sine_signed, gains, inverse)


BLOCK = 512


def attend_kernel(len_ref, q_ref, k_ref, v_ref, o_ref, o32_ref, lse_ref):
    i = pl.program_id(0)
    bq, bk = q_ref.shape[0], BLOCK
    length = len_ref[0]
    scale = HEAD_DIM ** (-0.5)
    q = q_ref[...]
    rows = i * bq + lax.broadcasted_iota(jnp.int32, (bq, bk), 0)
    cols0 = lax.broadcasted_iota(jnp.int32, (bq, bk), 1)

    def step(j, carry, masked):
        top, total, acc = carry
        j0 = pl.multiple_of(j * bk, bk)
        scores = contract_last(q, k_ref[pl.ds(j0, bk), :]) * scale
        if masked:
            cols = j0 + cols0
            scores = jnp.where((cols <= rows) & (cols < length), scores, masked_score)
        new = jnp.maximum(top, jnp.max(scores, axis=1, keepdims=True))
        weights = jnp.exp(scores - new)
        fix = jnp.exp(top - new)
        total = total * fix + jnp.sum(weights, axis=1, keepdims=True)
        acc = acc * fix + matmul(weights.astype(bf16), v_ref[pl.ds(j0, bk), :])
        return new, total, acc

    carry = (
        jnp.full((bq, 1), -jnp.inf, f32),
        jnp.zeros((bq, 1), f32),
        jnp.zeros((bq, HEAD_DIM), f32),
    )
    whole = jnp.minimum(i, length // bk)
    last = jnp.minimum(i + 1, (length + bk - 1) // bk)
    carry = lax.fori_loop(0, whole, lambda j, s: step(j, s, False), carry)
    top, total, acc = lax.fori_loop(whole, last, lambda j, s: step(j, s, True), carry)
    out = acc / total
    o_ref[...] = out.astype(bf16)
    o32_ref[...] = out
    lse_ref[...] = jnp.broadcast_to((top + jnp.log(total)).T, lse_ref.shape)


def attend(length, q, k, v):
    slots = q.shape[0]
    whole = pl.BlockSpec((slots, HEAD_DIM), lambda i: (0, 0))
    part = pl.BlockSpec((BLOCK, HEAD_DIM), lambda i: (i, 0))
    return pl.pallas_call(
        attend_kernel,
        name="attend",
        grid=(slots // BLOCK,),
        out_shape=(
            jax.ShapeDtypeStruct((slots, HEAD_DIM), bf16),
            jax.ShapeDtypeStruct((slots, HEAD_DIM), f32),
            jax.ShapeDtypeStruct((8, slots), f32),
        ),
        in_specs=[pl.BlockSpec(memory_space=pltpu.SMEM), part, whole, whole],
        out_specs=(part, part, pl.BlockSpec((8, BLOCK), lambda i: (0, i))),
        cost_estimate=COST,
    )(length, q, k, v)


def attend_back_kernel(
    len_ref, q_ref, k_ref, v_ref, do_ref, o_ref, lse_ref, out_ref, dq_acc, delta_ref
):
    j = pl.program_id(0)
    bk, bq = k_ref.shape[0], BLOCK
    slots = q_ref.shape[0]
    length = len_ref[0]
    scale = HEAD_DIM ** (-0.5)

    @pl.when(j == 0)
    def _():
        dq_acc[...] = jnp.zeros_like(dq_acc)
        for i in range(slots // bq):
            here = slice(i * bq, (i + 1) * bq)
            product = do_ref[here, :].astype(f32) * o_ref[here, :]
            delta_ref[0:1, here] = jnp.sum(product, axis=1, keepdims=True).T

    k, v = k_ref[...], v_ref[...]
    j0 = j * bk
    cols = j0 + lax.broadcasted_iota(jnp.int32, (bk, bq), 0)
    rows0 = lax.broadcasted_iota(jnp.int32, (bk, bq), 1)

    def step(i, carry, masked):
        dk, dv = carry
        i0 = pl.multiple_of(i * bq, bq)
        here = pl.ds(i0, bq)
        q, do = q_ref[here, :], do_ref[here, :]
        scores = contract_last(k, q) * scale
        if masked:
            scores = jnp.where((cols <= i0 + rows0) & (cols < length), scores, masked_score)
        probs = jnp.exp(scores - lse_ref[0:1, here])
        dv = dv + matmul(probs.astype(bf16), do)
        d_probs = contract_last(v, do)
        d_scores = (probs * (d_probs - delta_ref[0:1, here])).astype(bf16)
        dk = dk + matmul(d_scores, q)
        dq_acc[here, :] += contract_first(d_scores, k)
        return dk, dv

    zero = jnp.zeros((bk, HEAD_DIM), f32)
    top = slots // bq
    first = jnp.where(j0 + bk <= length, j + 1, top)
    first = jnp.where(j0 < length, first, j)
    stop = jnp.where(j0 < length, top, j)
    carry = lax.fori_loop(j, first, lambda i, s: step(i, s, True), (zero, zero))
    dk, dv = lax.fori_loop(first, stop, lambda i, s: step(i, s, False), carry)
    there = pl.ds(pl.multiple_of(j0, bk), bk)
    out_ref[1, there, :] = (dk * scale).astype(bf16)
    out_ref[2, there, :] = dv.astype(bf16)

    @pl.when(j == pl.num_programs(0) - 1)
    def _():
        out_ref[0] = (dq_acc[...] * scale).astype(bf16)


def attend_back(length, q, k, v, do, o, lse):
    slots = q.shape[0]
    whole = pl.BlockSpec((slots, HEAD_DIM), lambda j: (0, 0))
    part = pl.BlockSpec((BLOCK, HEAD_DIM), lambda j: (j, 0))
    line = pl.BlockSpec((8, slots), lambda j: (0, 0))
    return pl.pallas_call(
        attend_back_kernel,
        name="attend_back",
        grid=(slots // BLOCK,),
        out_shape=jax.ShapeDtypeStruct((3, slots, HEAD_DIM), bf16),
        in_specs=[pl.BlockSpec(memory_space=pltpu.SMEM), whole, part, part, whole, whole, line],
        out_specs=pl.BlockSpec((3, slots, HEAD_DIM), lambda j: (0, 0, 0)),
        scratch_shapes=[pltpu.VMEM((slots, HEAD_DIM), f32), pltpu.VMEM((8, slots), f32)],
        cost_estimate=COST,
    )(length, q, k, v, do, o, lse)


def per_device(
    tokens,
    seq_lengths,
    w_query,
    w_key,
    w_value,
    w_out,
    w_gate,
    w_up,
    w_down,
    q_gain,
    k_gain,
    attn_gain,
    mlp_gain,
    cotangent,
):
    tok_rows, feat_part = tokens.shape
    row_count, data_count = lax.axis_size("row"), lax.axis_size("dp")
    width = feat_part * lax.axis_size("col")
    slots = tok_rows * row_count
    half_feat = feat_part // 2
    y, z = side("dp"), lax.axis_index("row")
    heads = half_feat // HEAD_DIM
    pairs = [(i, i ^ 1) for i in range(data_count)]
    after = lambda values, *done: lax.optimization_barrier((values,) + done)[0]

    def y_half(values, axis):
        size = values.shape[axis] // 2
        return lax.dynamic_slice_in_dim(values, y * size, size, axis)

    qkv_weight = lax.all_gather(
        jnp.concatenate([y_half(w_query, 1), y_half(w_key, 1), y_half(w_value, 1)], axis=1),
        "row",
        axis=0,
        tiled=True,
    )
    out_weight = lax.all_gather(y_half(w_out, 0), "row", axis=1, tiled=True)
    gate_weight = lax.all_gather(y_half(w_gate, 1), "row", axis=0, tiled=True)
    up_weight = lax.all_gather(y_half(w_up, 1), "row", axis=0, tiled=True)
    down_weight = lax.all_gather(y_half(w_down, 0), "row", axis=1, tiled=True)

    positions = z * tok_rows + jnp.arange(tok_rows)
    length = seq_lengths[0]
    valid = (positions < length).astype(f32)[:, None]
    cosine, sine = rope_tables(positions, HEAD_DIM)
    sine_signed = jnp.where(jnp.arange(HEAD_DIM)[None, :] < HEAD_DIM // 2, -sine, sine)
    other_length = lax.ppermute(seq_lengths, "dp", pairs)
    pair_lengths = jnp.where(
        y == 0,
        jnp.concatenate([seq_lengths, other_length]),
        jnp.concatenate([other_length, seq_lengths]),
    )
    unit_length = lax.dynamic_slice_in_dim(pair_lengths, z // heads, 1)
    qk_gain = jnp.stack([y_half(q_gain, 0), y_half(k_gain, 0)])

    tokens_wide = gather_wide(tokens, False, 0, "gather_tokens")
    qkv = matmul(tokens_wide, qkv_weight)
    units, inverse = front(qkv, cosine, sine_signed, qk_gain, width, 2 * heads, 2)
    q_unit, k_unit, v_unit = (units[:, i].reshape(slots, HEAD_DIM) for i in range(3))
    attn_unit, attn_exact, log_total = attend(unit_length, q_unit, k_unit, v_unit)
    attn_low = turn(attn_unit, True, tok_rows, heads, 3, "turn_attn")
    branch = scatter_wide(matmul(attn_low, out_weight).astype(bf16), False, 4, "scatter_branch")
    branch_inv = lax.rsqrt(
        feature_total(jnp.sum(branch * branch, axis=1)[None, :], 5, "total_branch")[0] / width
        + norm_eps
    )[:, None]
    resid = tokens.astype(f32) + branch * branch_inv * attn_gain
    resid_wide = gather_wide(resid.astype(bf16), False, 6, "gather_resid")
    gate = matmul(resid_wide, gate_weight)
    upper = matmul(resid_wide, up_weight)
    sigma = jax.nn.sigmoid(gate)
    hidden = (gate * sigma * upper).astype(bf16)
    mixed = scatter_wide(matmul(hidden, down_weight).astype(bf16), False, 7, "scatter_mixed")
    incoming = cotangent.astype(f32) * valid
    gained = incoming * mlp_gain
    sums = feature_total(
        jnp.stack([jnp.sum(mixed * mixed, axis=1), jnp.sum(gained * mixed, axis=1)]),
        8,
        "total_mixed",
    )
    mixed_inv = lax.rsqrt(sums[0] / width + norm_eps)[:, None]
    inner = (sums[1] / width)[:, None]
    block_output = ((resid + mixed * mixed_inv * mlp_gain) * valid).astype(bf16)
    mlp_gain_raw = jnp.sum(incoming * mixed * mixed_inv, axis=0)
    d_mixed = (mixed_inv * gained - mixed * mixed_inv**3 * inner).astype(bf16)
    d_mixed_wide = gather_wide(d_mixed, False, 9, "gather_d_mixed")

    factor = 1.0 / math.sqrt(slots * data_count)

    def cut(values, index, count, axis):
        size = values.shape[axis] // count
        return lax.dynamic_slice_in_dim(values, index * size, size, axis)

    def over_dp(piece):
        if data_count > 2:
            groups = [list(range(s, data_count, 2)) for s in (0, 1)]
            piece = lax.psum(piece, "dp", axis_index_groups=groups)
        return piece

    def two_sides(piece, other, bit, axis):
        low = jnp.where(bit == 0, piece, other)
        high = jnp.where(bit == 0, other, piece)
        return jnp.concatenate([low, high], axis=axis)

    def reduce_rows(raw, axis):
        return lax.psum_scatter(raw, "row", scatter_dimension=axis, tiled=True)

    d_hidden = contract_last(d_mixed_wide, down_weight)
    down_raw = (contract_first(hidden, d_mixed_wide) * factor).astype(bf16)
    d_gate = (d_hidden * upper * sigma * (1.0 + gate * (1.0 - sigma))).astype(bf16)
    d_upper = (d_hidden * gate * sigma).astype(bf16)
    gate_raw = (contract_first(resid_wide, d_gate) * factor).astype(bf16)
    up_raw = (contract_first(resid_wide, d_upper) * factor).astype(bf16)
    d_resid_wide = (
        contract_last(d_gate, gate_weight) + contract_last(d_upper, up_weight)
    ).astype(bf16)
    d_resid_wide = after(d_resid_wide, down_raw, gate_raw, up_raw)
    down_piece = reduce_rows(down_raw, 1)
    gate_piece, up_piece = reduce_rows(gate_raw, 0), reduce_rows(up_raw, 0)
    d_resid = scatter_wide(d_resid_wide, False, 10, "scatter_d_resid")
    d_resid = incoming + d_resid
    attn_gain_raw = jnp.sum(d_resid * branch * branch_inv, axis=0)
    gained = d_resid * attn_gain
    inner = (
        feature_total(jnp.sum(gained * branch, axis=1)[None, :], 11, "total_d_resid")[0][:, None]
        / width
    )
    d_branch = (branch_inv * gained - branch * branch_inv**3 * inner).astype(bf16)
    d_branch_wide, down_piece = lax.optimization_barrier(
        (gather_wide(d_branch, False, 12, "gather_d_branch"), down_piece)
    )
    d_attn = contract_last(d_branch_wide, out_weight).astype(bf16)
    d_attn_unit = turn(d_attn, False, tok_rows, heads, 13, "turn_d_attn")
    out_raw = (contract_first(attn_low, after(d_branch_wide, d_attn_unit)) * factor).astype(bf16)
    d_attn_unit = after(d_attn_unit, out_raw)
    out_piece = reduce_rows(out_raw, 1)
    d_units = attend_back(unit_length, q_unit, k_unit, v_unit, d_attn_unit, attn_exact, log_total)
    d_units, gate_piece = lax.optimization_barrier((d_units, gate_piece))
    d_qkv, gain_sums = rear(
        d_units, qkv[:, : 2 * half_feat], cosine, sine_signed, qk_gain, inverse, width, 14
    )
    qkv_raw = (contract_first(tokens_wide, d_qkv) * factor).astype(bf16)
    projected = contract_last(d_qkv, qkv_weight).astype(bf16)
    projected, qkv_raw = lax.optimization_barrier((projected, qkv_raw))
    qkv_piece = over_dp(reduce_rows(qkv_raw, 0))
    scattered, up_piece, out_piece = lax.optimization_barrier(
        (scatter_wide(projected, False, 16, "scatter_projected"), up_piece, out_piece)
    )
    input_grad = d_resid + scattered

    def spread(half):
        return lax.dynamic_update_slice_in_dim(jnp.zeros((feat_part,), f32), half, y * half_feat, 0)

    gains = over_dp(
        gain_total(
            jnp.stack([spread(gain_sums[0]), spread(gain_sums[1]), attn_gain_raw, mlp_gain_raw])
            * factor,
            15,
        )
    )
    def whole(piece, axis):
        piece = over_dp(piece)
        return two_sides(piece, lax.ppermute(piece, "dp", pairs), y, axis).astype(f32)

    qkv_other = lax.ppermute(qkv_piece, "dp", pairs)
    q_grad, k_grad, v_grad = (
        two_sides(cut(qkv_piece, i, 3, 1), cut(qkv_other, i, 3, 1), y, 1).astype(f32)
        for i in range(3)
    )
    return (
        block_output,
        input_grad,
        q_grad,
        k_grad,
        v_grad,
        whole(out_piece, 0),
        whole(gate_piece, 1),
        whole(up_piece, 1),
        whole(down_piece, 0),
        gains[0],
        gains[1],
        gains[2],
        gains[3],
    )


def solution(mesh):
    tok, row_col, col_row, gain = P(("dp", "row"), "col"), P("row", "col"), P("col", "row"), P("col")
    weights = (row_col, row_col, row_col, col_row, row_col, row_col, col_row)
    gains = (gain, gain, gain, gain)
    return jax.shard_map(
        per_device,
        mesh=mesh,
        in_specs=(tok, P("dp")) + weights + gains + (tok,),
        out_specs=(tok, tok) + weights + gains,
        check_vma=False,
    )
```

```python
import functools
import math

import jax
import jax.numpy as jnp
from jax import lax
from jax.experimental import pallas as pl
from jax.experimental.pallas import tpu as pltpu
from jax.sharding import PartitionSpec as P

HEAD_DIM = 128
rope_base = 500000.0
norm_eps = 1e-06
masked_score = -1e30

MESH = pl.DeviceIdType.MESH
bf16 = jnp.bfloat16
f32 = jnp.float32
COST = pl.CostEstimate(flops=0, bytes_accessed=1000, transcendentals=0)


def rope_tables(positions, head_dim):
    half = head_dim // 2
    freq = 1.0 / rope_base ** (jnp.arange(half, dtype=f32) / half)
    angle = positions.astype(f32)[:, None] * freq[None, :]
    angle = jnp.concatenate([angle, angle], axis=1)
    return (jnp.cos(angle), jnp.sin(angle))


def matmul(left, right):
    return jnp.dot(left, right, preferred_element_type=f32)


def contract_first(left, right):
    return lax.dot_general(left, right, (((0,), (0,)), ((), ())), preferred_element_type=f32)


def contract_last(left, right):
    return lax.dot_general(left, right, (((1,), (1,)), ((), ())), preferred_element_type=f32)


def flip(axis, bit):
    return lax.axis_index(axis) ^ bit


def side(axis):
    return lax.axis_index(axis) & 1


def greet(peers):
    barrier = pltpu.get_barrier_semaphore()
    for peer in peers:
        pl.semaphore_signal(barrier, inc=1, device_id=peer, device_id_type=MESH)
    pl.semaphore_wait(barrier, len(peers))


def sender(send_sem, recv_sem, started):
    def send(src, dst, number, peer):
        copy = pltpu.make_async_remote_copy(
            src_ref=src,
            dst_ref=dst,
            send_sem=send_sem.at[number],
            recv_sem=recv_sem.at[number],
            device_id=peer,
            device_id_type=MESH,
        )
        copy.start()
        started.append(copy)
        return copy

    return send


def neighbours():
    return {"col": flip("col", 2)}, {"dp": flip("dp", 1)}, {"col": flip("col", 1)}


def gather_kernel(pair, x_ref, out_ref, local_sem, send_sem, recv_sem):
    rows, width = x_ref.shape
    half = rows // 2
    y, b, p = side("dp"), lax.axis_index("col"), side("row") if pair else 0
    to_x, to_y, to_c = neighbours()
    to_z = {"row": flip("row", 1)}
    greet([to_x, to_y, to_c] + ([to_z] if pair else []))
    started = []
    send = sender(send_sem, recv_sem, started)

    def slot(pp, yy, h, bb, n=half):
        return out_ref.at[
            pl.ds(pl.multiple_of((pp * 2 + yy) * rows + h * half, half), n),
            pl.ds(pl.multiple_of(bb * width, width), width),
        ]

    def open_flow(pp, low, high, base):
        xa = send(low, slot(pp, y, 0, b), base + 0, to_x)
        ya = send(high, slot(pp, y, 1, b), base + 1, to_y)
        c0 = send(low, slot(pp, y, 0, b), base + 6, to_c)
        yb = send(low, slot(pp, y, 0, b), base + 2, to_y)
        xb = send(high, slot(pp, y, 1, b), base + 3, to_x)
        c1 = send(high, slot(pp, y, 1, b), base + 7, to_c)
        return xa, ya, xb, yb, [c0, c1]

    def relay(pp, flow, base):
        xa, ya, xb, yb, core = flow
        xa.wait_recv()
        piece = slot(pp, y, 0, b ^ 2)
        yc = send(piece, piece, base + 4, to_y)
        core.append(send(piece, piece, base + 8, to_c))
        ya.wait_recv()
        piece = slot(pp, y ^ 1, 1, b)
        xc = send(piece, piece, base + 5, to_x)
        core.append(send(piece, piece, base + 9, to_c))
        yb.wait_recv()
        piece = slot(pp, y ^ 1, 0, b)
        core.append(send(piece, piece, base + 10, to_c))
        xb.wait_recv()
        piece = slot(pp, y, 1, b ^ 2)
        core.append(send(piece, piece, base + 11, to_c))
        return yc, xc, core

    def close_flow(pp, state, base):
        yc, xc, core = state
        yc.wait_recv()
        piece = slot(pp, y ^ 1, 0, b ^ 2)
        core.append(send(piece, piece, base + 12, to_c))
        xc.wait_recv()
        piece = slot(pp, y ^ 1, 1, b ^ 2)
        core.append(send(piece, piece, base + 13, to_c))
        for copy in core:
            copy.wait_recv()

    low, high = x_ref.at[pl.ds(0, half)], x_ref.at[pl.ds(half, half)]
    own = pltpu.make_async_copy(x_ref, slot(p, y, 0, b, rows), local_sem)
    if pair:
        z0 = send(low, slot(p, y, 0, b), 28, to_z)
        z1 = send(high, slot(p, y, 1, b), 29, to_z)
    first = open_flow(p, low, high, 0)
    own.start()
    state = relay(p, first, 0)
    if pair:
        z0.wait_recv()
        z1.wait_recv()
        second = open_flow(p ^ 1, slot(p ^ 1, y, 0, b), slot(p ^ 1, y, 1, b), 14)
    close_flow(p, state, 0)
    if pair:
        close_flow(p ^ 1, relay(p ^ 1, second, 14), 14)
    for copy in started:
        copy.wait_send()
    own.wait()


def gather_wide(values, pair, number, name):
    rows, width = values.shape
    copies = 30 if pair else 14
    return pl.pallas_call(
        functools.partial(gather_kernel, pair),
        name=name,
        out_shape=jax.ShapeDtypeStruct(((4 if pair else 2) * rows, 4 * width), values.dtype),
        in_specs=[pl.BlockSpec(memory_space=pltpu.VMEM)],
        out_specs=pl.BlockSpec(memory_space=pl.ANY),
        scratch_shapes=[
            pltpu.SemaphoreType.DMA,
            pltpu.SemaphoreType.DMA((copies,)),
            pltpu.SemaphoreType.DMA((copies,)),
        ],
        compiler_params=pltpu.CompilerParams(collective_id=number, has_side_effects=True),
        cost_estimate=COST,
    )(values)


def scatter_kernel(pair, rider, p_ref, *refs):
    if rider:
        cargo_ref, out_ref, far_ref = refs[:3]
    else:
        out_ref = refs[0]
    rc, s1, ry, rx, s2, fy, fx, sz, fz, send_sem, recv_sem = refs[3 if rider else 1 :]
    rows, width = out_ref.shape
    half = rows // 2
    y, b, p = side("dp"), lax.axis_index("col"), side("row") if pair else 0
    x, c = b >> 1, b & 1
    to_x, to_y, to_c = neighbours()
    to_z = {"row": flip("row", 1)}
    to_far = {"row": flip("row", 2)}
    greet([to_x, to_y, to_c] + ([to_z] if pair else []) + ([to_far] if rider else []))
    started = []
    send = sender(send_sem, recv_sem, started)
    if rider:
        size = far_ref.shape[1]
        start = pl.multiple_of((1 - (lax.axis_index("row") >> 1)) * size, size)
        cargo = send(cargo_ref.at[:, pl.ds(start, size)], far_ref, 30, to_far)

    def place(yy, h):
        return pl.ds(pl.multiple_of(yy * rows + h * half, half), half)

    def column(bb):
        return pl.ds(pl.multiple_of(bb * width, width), width)

    order = [(0, y ^ 1, 0), (1, y ^ 1, 0), (x ^ 1, 0, 1), (x ^ 1, 1, 1)]
    order += [(0, y, 0), (1, y, 0), (x, 0, 1), (x, 1, 1)]

    class Flow:
        def __init__(self, f, pp):
            self.f, self.base = f, 14 * f
            self.rows = lambda yy, h: pl.ds(
                pl.multiple_of((pp * 2 + yy) * rows + h * half, half), half
            )
            self.core = [
                send(
                    p_ref.at[self.rows(yy, h), column(2 * xx + (c ^ 1))],
                    rc.at[f, xx, place(yy, h)],
                    self.base + number,
                    to_c,
                )
                for number, (xx, yy, h) in enumerate(order)
            ]

        def settle(self, *numbers):
            for number in numbers:
                self.core[number].wait_recv()
                xx, yy, h = order[number]
                s1[self.f, xx, place(yy, h), :] = (
                    p_ref[self.rows(yy, h), column(2 * xx + c)].astype(f32)
                    + rc[self.f, xx, place(yy, h), :].astype(f32)
                ).astype(s1.dtype)

        def first(self, i):
            f = self.f
            ya = send(s1.at[f, i, place(y ^ 1, 0), :], ry.at[f, i], self.base + 8 + i, to_y)
            part = s1.at[f, x ^ 1, pl.ds(i * rows + half, half), :]
            xa = send(part, rx.at[f, i], self.base + 10 + i, to_x)
            return ya, xa

        def second(self, copies):
            f = self.f
            for ya, _ in copies:
                ya.wait_recv()
            s2[f, 0] = (
                s1[f, x ^ 1, place(y, 0), :].astype(f32) + ry[f, x ^ 1].astype(f32)
            ).astype(s2.dtype)
            xb = send(s2.at[f, 0], fx.at[f], self.base + 12, to_x)
            for _, xa in copies:
                xa.wait_recv()
            s2[f, 1] = (
                s1[f, x, place(y ^ 1, 1), :].astype(f32) + rx[f, y ^ 1].astype(f32)
            ).astype(s2.dtype)
            yb = send(s2.at[f, 1], fy.at[f], self.base + 13, to_y)
            return xb, yb

        def last(self, copies):
            f = self.f
            xb, yb = copies
            keep = s1[f, x, place(y, 0), :].astype(f32) + ry[f, x].astype(f32)
            xb.wait_recv()
            low = keep + fx[f].astype(f32)
            keep = s1[f, x, place(y, 1), :].astype(f32) + rx[f, y].astype(f32)
            yb.wait_recv()
            return low, keep + fy[f].astype(f32)

    if pair:
        far = Flow(0, p ^ 1)
        near = Flow(1, p)
        far.settle(0, 1, 2, 3)
        far_first = [far.first(0), far.first(1)]
        far.settle(4, 5, 6, 7)
        near.settle(0, 1, 2, 3)
        near_first = [near.first(0)]
        near.settle(4, 5, 6, 7)
        far_second = far.second(far_first)
        near_first.append(near.first(1))
        low, high = far.last(far_second)
        sz[pl.ds(0, half), :] = low.astype(bf16)
        z0 = send(sz.at[pl.ds(0, half)], fz.at[pl.ds(0, half)], 28, to_z)
        sz[pl.ds(half, half), :] = high.astype(bf16)
        z1 = send(sz.at[pl.ds(half, half)], fz.at[pl.ds(half, half)], 29, to_z)
        low, high = near.last(near.second(near_first))
        z0.wait_recv()
        out_ref[pl.ds(0, half), :] = low + fz[pl.ds(0, half), :].astype(f32)
        z1.wait_recv()
        out_ref[pl.ds(half, half), :] = high + fz[pl.ds(half, half), :].astype(f32)
    else:
        near = Flow(0, 0)
        near.settle(0, 1, 2, 3)
        near_first = [near.first(0), near.first(1)]
        near.settle(4, 5, 6, 7)
        low, high = near.last(near.second(near_first))
        out_ref[pl.ds(0, half), :] = low
        out_ref[pl.ds(half, half), :] = high
    if rider:
        cargo.wait_recv()
    for copy in started:
        copy.wait_send()


def scatter_wide(partial, pair, number, name, cargo=None):
    flows = 2 if pair else 1
    rows, width = partial.shape[0] // (2 * flows), partial.shape[1] // 4
    half = rows // 2
    rider = cargo is not None
    copies = 31 if pair else 14
    out_shape, out_spec = [jax.ShapeDtypeStruct((rows, width), f32)], [pl.BlockSpec(memory_space=pltpu.VMEM)]
    anywhere = [pl.BlockSpec(memory_space=pl.ANY)] * rider
    if rider:
        out_shape.append(jax.ShapeDtypeStruct((cargo.shape[0], cargo.shape[1] // 2), cargo.dtype))
    last = (rows, width) if pair else (16, 128)
    out = pl.pallas_call(
        functools.partial(scatter_kernel, pair, rider),
        name=name,
        out_shape=out_shape,
        in_specs=[pl.BlockSpec(memory_space=pltpu.VMEM)] + anywhere,
        out_specs=out_spec + anywhere,
        scratch_shapes=[
            pltpu.VMEM((flows, 2, 2 * rows, width), bf16),
            pltpu.VMEM((flows, 2, 2 * rows, width), bf16),
            pltpu.VMEM((flows, 2, half, width), bf16),
            pltpu.VMEM((flows, 2, half, width), bf16),
            pltpu.VMEM((flows, 2, half, width), bf16),
            pltpu.VMEM((flows, half, width), bf16),
            pltpu.VMEM((flows, half, width), bf16),
            pltpu.VMEM(last, bf16),
            pltpu.VMEM(last, bf16),
            pltpu.SemaphoreType.DMA((copies,)),
            pltpu.SemaphoreType.DMA((copies,)),
        ],
        compiler_params=pltpu.CompilerParams(
            collective_id=number, has_side_effects=True, vmem_limit_bytes=48 * 2**20
        ),
        cost_estimate=COST,
    )(partial, *([cargo] * rider))
    return out if rider else out[0]


def feature_peers(wide):
    peers = []
    for d in range(1, 8 if wide else 4):
        peer = {"col": flip("col", d & 3)}
        if d >> 2:
            peer["dp"] = flip("dp", 1)
        peers.append(peer)
    return peers


def total_kernel(v_ref, out_ref, slots, send_sem, recv_sem):
    me = lax.axis_index("col")
    peers = feature_peers(False)
    greet(peers)
    started = []
    send = sender(send_sem, recv_sem, started)
    for d, peer in enumerate(peers):
        send(v_ref, slots.at[me], d, peer)
    slots[me] = v_ref[...]
    for copy in started:
        copy.wait_recv()
    total = slots[0]
    for i in range(1, 4):
        total = total + slots[i]
    out_ref[...] = total
    for copy in started:
        copy.wait_send()


def feature_total(values, number, name):
    k, t = values.shape
    flat = values.reshape(k * t // 128, 128)
    total = pl.pallas_call(
        total_kernel,
        name=name,
        out_shape=jax.ShapeDtypeStruct(flat.shape, f32),
        in_specs=[pl.BlockSpec(memory_space=pltpu.VMEM)],
        out_specs=pl.BlockSpec(memory_space=pltpu.VMEM),
        scratch_shapes=[
            pltpu.VMEM((4,) + flat.shape, f32),
            pltpu.SemaphoreType.DMA((3,)),
            pltpu.SemaphoreType.DMA((3,)),
        ],
        compiler_params=pltpu.CompilerParams(collective_id=number, has_side_effects=True),
    )(flat)
    return total.reshape(k, t)


def gain_peers():
    peers = []
    for d in range(1, 8):
        peers.append({"row": flip("row", d & 3), "dp": flip("dp", d >> 2)})
    return peers


def gain_kernel(v_ref, out_ref, slots, send_sem, recv_sem):
    me = side("dp") * 4 + lax.axis_index("row")
    peers = gain_peers()
    greet(peers)
    started = []
    send = sender(send_sem, recv_sem, started)
    for d, peer in enumerate(peers):
        send(v_ref, slots.at[me], d, peer)
    slots[me] = v_ref[...]
    for copy in started:
        copy.wait_recv()
    total = slots[0]
    for i in range(1, 8):
        total = total + slots[i]
    out_ref[...] = total
    for copy in started:
        copy.wait_send()


def gain_total(values, number):
    flat = values.reshape(-1, 128)
    total = pl.pallas_call(
        gain_kernel,
        name="total_gains",
        out_shape=jax.ShapeDtypeStruct(flat.shape, f32),
        in_specs=[pl.BlockSpec(memory_space=pltpu.VMEM)],
        out_specs=pl.BlockSpec(memory_space=pltpu.VMEM),
        scratch_shapes=[
            pltpu.VMEM((8,) + flat.shape, f32),
            pltpu.SemaphoreType.DMA((7,)),
            pltpu.SemaphoreType.DMA((7,)),
        ],
        compiler_params=pltpu.CompilerParams(collective_id=number, has_side_effects=True),
    )(flat)
    return total.reshape(values.shape)


def row_peers():
    return [(d, {"row": flip("row", d)}) for d in (3, 2, 1)]


def unit_view(ref, unit, tok, heads):
    rows = pl.ds(pl.multiple_of((unit // heads) * tok, tok), tok)
    cols = pl.ds(pl.multiple_of((unit % heads) * HEAD_DIM, HEAD_DIM), HEAD_DIM)
    return ref.at[rows, cols]


def turn_kernel(back, tok, heads, x_ref, out_ref, local_sem, send_sem, recv_sem):
    z = lax.axis_index("row")
    greet([peer for _, peer in row_peers()])
    started = []
    send = sender(send_sem, recv_sem, started)

    def line(ref, i):
        return ref.at[pl.ds(pl.multiple_of(i * tok, tok), tok)]

    def ends(i):
        if back:
            return line(x_ref, i), unit_view(out_ref, z, tok, heads)
        return unit_view(x_ref, i, tok, heads), line(out_ref, z)

    for d, peer in row_peers():
        send(*ends(z ^ d), d - 1, peer)
    own = pltpu.make_async_copy(*ends(z), local_sem)
    own.start()
    for copy in started:
        copy.wait()
    own.wait()


def turn(values, back, tok, heads, number, name):
    shape = (2 * tok, heads * HEAD_DIM) if back else (2 * heads * tok, HEAD_DIM)
    return pl.pallas_call(
        functools.partial(turn_kernel, back, tok, heads),
        name=name,
        out_shape=jax.ShapeDtypeStruct(shape, values.dtype),
        in_specs=[pl.BlockSpec(memory_space=pltpu.VMEM)],
        out_specs=pl.BlockSpec(memory_space=pl.ANY),
        scratch_shapes=[
            pltpu.SemaphoreType.DMA,
            pltpu.SemaphoreType.DMA((3,)),
            pltpu.SemaphoreType.DMA((3,)),
        ],
        compiler_params=pltpu.CompilerParams(collective_id=number, has_side_effects=True),
        cost_estimate=COST,
    )(values)


def totals(stat, slots, started):
    for copy in started:
        copy.wait_recv()
    total = slots[0]
    for i in range(1, 8):
        total = total + slots[i]
    return total


def front_kernel(
    width,
    qkv_ref,
    cos_ref,
    sin_ref,
    gain_ref,
    out_ref,
    inv_ref,
    turned,
    packed,
    stat,
    slots,
    local_sem,
    stat_send,
    stat_recv,
    send_sem,
    recv_sem,
):
    count, tok = qkv_ref.shape[0], cos_ref.shape[0]
    part = qkv_ref.shape[1] // 3
    heads = part // HEAD_DIM
    z = lax.axis_index("row")
    me = side("dp") * 4 + lax.axis_index("col")
    peers = feature_peers(True)
    greet(peers + [peer for _, peer in row_peers()])
    for i in range(2):
        values = qkv_ref[:, i * part : (i + 1) * part]
        stat[i : i + 1, :] = jnp.sum(values * values, axis=1, keepdims=True).T
    started, moved, local = [], [], []
    send = sender(stat_send, stat_recv, started)
    for d, peer in enumerate(peers):
        send(stat, slots.at[me], d, peer)
    slots[me] = stat[...]
    move = sender(send_sem, recv_sem, moved)

    def ship(i):
        for d, peer in row_peers():
            move(packed.at[z ^ d, i], out_ref.at[z, i], 3 * i + d - 1, peer)
        copy = pltpu.make_async_copy(packed.at[z, i], out_ref.at[z, i], local_sem.at[i])
        copy.start()
        local.append(copy)

    def spots():
        return [(s, h, s * heads + h) for s in range(2) for h in range(heads)]

    for s, h, unit in spots():
        packed[unit, 2] = qkv_ref[
            s * tok : (s + 1) * tok, 2 * part + h * HEAD_DIM : 2 * part + (h + 1) * HEAD_DIM
        ].astype(bf16)
    ship(2)
    for i in (1, 0):
        for s, h, unit in spots():
            values = (
                qkv_ref[s * tok : (s + 1) * tok, i * part + h * HEAD_DIM : i * part + (h + 1) * HEAD_DIM]
                * gain_ref[i : i + 1, h * HEAD_DIM : (h + 1) * HEAD_DIM]
            )
            turned[i, unit] = values * cos_ref[...] + pltpu.roll(values, HEAD_DIM // 2, 1) * sin_ref[...]
    inverse = lax.rsqrt(totals(stat, slots, started) / width + norm_eps)
    inv_ref[...] = inverse
    for i in (1, 0):
        column = inverse[i : i + 1, :].T
        for s, h, unit in spots():
            packed[unit, i] = (turned[i, unit] * column[s * tok : (s + 1) * tok]).astype(bf16)
        ship(i)
    for copy in moved:
        copy.wait()
    for copy in local:
        copy.wait()
    for copy in started:
        copy.wait_send()


def front(qkv, cosine, sine_signed, gains, width, units, number):
    count, tok = qkv.shape[0], cosine.shape[0]
    return pl.pallas_call(
        functools.partial(front_kernel, width),
        name="front",
        out_shape=(
            jax.ShapeDtypeStruct((units, 3, tok, HEAD_DIM), bf16),
            jax.ShapeDtypeStruct((2, count), f32),
        ),
        in_specs=[pl.BlockSpec(memory_space=pltpu.VMEM)] * 4,
        out_specs=(pl.BlockSpec(memory_space=pl.ANY), pl.BlockSpec(memory_space=pltpu.VMEM)),
        scratch_shapes=[
            pltpu.VMEM((2, units, tok, HEAD_DIM), f32),
            pltpu.VMEM((units, 3, tok, HEAD_DIM), bf16),
            pltpu.VMEM((2, count), f32),
            pltpu.VMEM((8, 2, count), f32),
            pltpu.SemaphoreType.DMA((3,)),
            pltpu.SemaphoreType.DMA((7,)),
            pltpu.SemaphoreType.DMA((7,)),
            pltpu.SemaphoreType.DMA((9,)),
            pltpu.SemaphoreType.DMA((9,)),
        ],
        compiler_params=pltpu.CompilerParams(
            collective_id=number, has_side_effects=True, vmem_limit_bytes=40 * 2**20
        ),
        cost_estimate=COST,
    )(qkv, cosine, sine_signed, gains)


def rear_kernel(
    width,
    d_ref,
    qkv_ref,
    cos_ref,
    sin_ref,
    gain_ref,
    inv_ref,
    out_ref,
    sums_ref,
    landed,
    normed,
    stat,
    slots,
    stat_send,
    stat_recv,
    send_sem,
    recv_sem,
):
    count, tok = qkv_ref.shape[0], cos_ref.shape[0]
    part = qkv_ref.shape[1] // 3
    heads = part // HEAD_DIM
    z = lax.axis_index("row")
    me = side("dp") * 4 + lax.axis_index("col")
    peers = feature_peers(True)
    greet(peers + [peer for _, peer in row_peers()])
    started, moved = [], []
    move = sender(send_sem, recv_sem, moved)
    for i in (0, 1, 2):
        for d, peer in row_peers():
            there = pl.ds(pl.multiple_of((z ^ d) * tok, tok), tok)
            move(d_ref.at[i, there], landed.at[z, i], 3 * i + d - 1, peer)
    here = pl.ds(pl.multiple_of(z * tok, tok), tok)
    for i in (0, 1, 2):
        landed[z, i] = d_ref[i, here, :]
    spots = [(s, h, s * heads + h) for s in range(2) for h in range(heads)]
    for i in (0, 1):
        for copy in moved[3 * i : 3 * i + 3]:
            copy.wait_recv()
        for h in range(heads):
            cols = slice(i * part + h * HEAD_DIM, i * part + (h + 1) * HEAD_DIM)
            gain = gain_ref[i : i + 1, h * HEAD_DIM : (h + 1) * HEAD_DIM]
            raw = jnp.zeros((1, HEAD_DIM), f32)
            for s in range(2):
                rows = slice(s * tok, (s + 1) * tok)
                values = landed[s * heads + h, i].astype(f32)
                back = values * cos_ref[...] - pltpu.roll(values, HEAD_DIM // 2, 1) * sin_ref[...]
                pre = qkv_ref[rows, cols]
                inverse = inv_ref[i : i + 1, rows].T
                crossed = back * pre
                raw = raw + jnp.sum(crossed * inverse, axis=0, keepdims=True)
                partial = jnp.sum(crossed * gain, axis=1, keepdims=True).T
                if h == 0:
                    stat[i : i + 1, rows] = partial
                else:
                    stat[i : i + 1, rows] = stat[i : i + 1, rows] + partial
                normed[rows, cols] = back * gain
            sums_ref[i : i + 1, h * HEAD_DIM : (h + 1) * HEAD_DIM] = raw
    send = sender(stat_send, stat_recv, started)
    for d, peer in enumerate(peers):
        send(stat, slots.at[me], d, peer)
    slots[me] = stat[...]
    for copy in moved[6:]:
        copy.wait_recv()
    for s, h, unit in spots:
        cols = slice(2 * part + h * HEAD_DIM, 2 * part + (h + 1) * HEAD_DIM)
        out_ref[s * tok : (s + 1) * tok, cols] = landed[unit, 2]
    inner = totals(stat, slots, started) / width
    for i in (0, 1):
        inverse = inv_ref[i : i + 1, :]
        first = inverse.T
        second = (inverse * inverse * inverse * inner[i : i + 1, :]).T
        cols = slice(i * part, (i + 1) * part)
        out_ref[:, cols] = (first * normed[:, cols] - qkv_ref[:, cols] * second).astype(bf16)
    for copy in moved + started:
        copy.wait_send()


def rear(d_units, qkv, cosine, sine_signed, gains, inverse, width, number):
    count, tok = qkv.shape[0], cosine.shape[0]
    part = qkv.shape[1] // 3
    units = d_units.shape[1] // tok
    return pl.pallas_call(
        functools.partial(rear_kernel, width),
        name="rear",
        out_shape=(
            jax.ShapeDtypeStruct((count, 3 * part), bf16),
            jax.ShapeDtypeStruct((2, part), f32),
        ),
        in_specs=[pl.BlockSpec(memory_space=pltpu.VMEM)] * 6,
        out_specs=[pl.BlockSpec(memory_space=pltpu.VMEM)] * 2,
        scratch_shapes=[
            pltpu.VMEM((units, 3, tok, HEAD_DIM), bf16),
            pltpu.VMEM((count, 2 * part), f32),
            pltpu.VMEM((2, count), f32),
            pltpu.VMEM((8, 2, count), f32),
            pltpu.SemaphoreType.DMA((7,)),
            pltpu.SemaphoreType.DMA((7,)),
            pltpu.SemaphoreType.DMA((9,)),
            pltpu.SemaphoreType.DMA((9,)),
        ],
        compiler_params=pltpu.CompilerParams(
            collective_id=number, has_side_effects=True, vmem_limit_bytes=40 * 2**20
        ),
        cost_estimate=COST,
    )(d_units, qkv, cosine, sine_signed, gains, inverse)


BLOCK = 512


def attend_kernel(len_ref, q_ref, k_ref, v_ref, o_ref, o32_ref, lse_ref):
    i = pl.program_id(0)
    bq, bk = q_ref.shape[0], BLOCK
    length = len_ref[0]
    scale = HEAD_DIM ** (-0.5)
    q = q_ref[...]
    rows = i * bq + lax.broadcasted_iota(jnp.int32, (bq, bk), 0)
    cols0 = lax.broadcasted_iota(jnp.int32, (bq, bk), 1)

    def step(j, carry, masked):
        top, total, acc = carry
        j0 = pl.multiple_of(j * bk, bk)
        scores = contract_last(q, k_ref[pl.ds(j0, bk), :]) * scale
        if masked:
            cols = j0 + cols0
            scores = jnp.where((cols <= rows) & (cols < length), scores, masked_score)
        new = jnp.maximum(top, jnp.max(scores, axis=1, keepdims=True))
        weights = jnp.exp(scores - new)
        fix = jnp.exp(top - new)
        total = total * fix + jnp.sum(weights, axis=1, keepdims=True)
        acc = acc * fix + matmul(weights.astype(bf16), v_ref[pl.ds(j0, bk), :])
        return new, total, acc

    carry = (
        jnp.full((bq, 1), -jnp.inf, f32),
        jnp.zeros((bq, 1), f32),
        jnp.zeros((bq, HEAD_DIM), f32),
    )
    whole = jnp.minimum(i, length // bk)
    last = jnp.minimum(i + 1, (length + bk - 1) // bk)
    carry = lax.fori_loop(0, whole, lambda j, s: step(j, s, False), carry)
    top, total, acc = lax.fori_loop(whole, last, lambda j, s: step(j, s, True), carry)
    out = acc / total
    o_ref[...] = out.astype(bf16)
    o32_ref[...] = out
    lse_ref[...] = jnp.broadcast_to((top + jnp.log(total)).T, lse_ref.shape)


def attend(length, q, k, v):
    slots = q.shape[0]
    whole = pl.BlockSpec((slots, HEAD_DIM), lambda i: (0, 0))
    part = pl.BlockSpec((BLOCK, HEAD_DIM), lambda i: (i, 0))
    return pl.pallas_call(
        attend_kernel,
        name="attend",
        grid=(slots // BLOCK,),
        out_shape=(
            jax.ShapeDtypeStruct((slots, HEAD_DIM), bf16),
            jax.ShapeDtypeStruct((slots, HEAD_DIM), f32),
            jax.ShapeDtypeStruct((8, slots), f32),
        ),
        in_specs=[pl.BlockSpec(memory_space=pltpu.SMEM), part, whole, whole],
        out_specs=(part, part, pl.BlockSpec((8, BLOCK), lambda i: (0, i))),
        cost_estimate=COST,
    )(length, q, k, v)


def attend_back_kernel(
    len_ref, q_ref, k_ref, v_ref, do_ref, o_ref, lse_ref, out_ref, dq_acc, delta_ref
):
    j = pl.program_id(0)
    bk, bq = k_ref.shape[0], BLOCK
    slots = q_ref.shape[0]
    length = len_ref[0]
    scale = HEAD_DIM ** (-0.5)

    @pl.when(j == 0)
    def _():
        dq_acc[...] = jnp.zeros_like(dq_acc)
        for i in range(slots // bq):
            here = slice(i * bq, (i + 1) * bq)
            product = do_ref[here, :].astype(f32) * o_ref[here, :]
            delta_ref[0:1, here] = jnp.sum(product, axis=1, keepdims=True).T

    k, v = k_ref[...], v_ref[...]
    j0 = j * bk
    cols = j0 + lax.broadcasted_iota(jnp.int32, (bk, bq), 0)
    rows0 = lax.broadcasted_iota(jnp.int32, (bk, bq), 1)

    def step(i, carry, masked):
        dk, dv = carry
        i0 = pl.multiple_of(i * bq, bq)
        here = pl.ds(i0, bq)
        q, do = q_ref[here, :], do_ref[here, :]
        scores = contract_last(k, q) * scale
        if masked:
            scores = jnp.where((cols <= i0 + rows0) & (cols < length), scores, masked_score)
        probs = jnp.exp(scores - lse_ref[0:1, here])
        dv = dv + matmul(probs.astype(bf16), do)
        d_probs = contract_last(v, do)
        d_scores = (probs * (d_probs - delta_ref[0:1, here])).astype(bf16)
        dk = dk + matmul(d_scores, q)
        dq_acc[here, :] += contract_first(d_scores, k)
        return dk, dv

    zero = jnp.zeros((bk, HEAD_DIM), f32)
    top = slots // bq
    first = jnp.where(j0 + bk <= length, j + 1, top)
    first = jnp.where(j0 < length, first, j)
    stop = jnp.where(j0 < length, top, j)
    carry = lax.fori_loop(j, first, lambda i, s: step(i, s, True), (zero, zero))
    dk, dv = lax.fori_loop(first, stop, lambda i, s: step(i, s, False), carry)
    there = pl.ds(pl.multiple_of(j0, bk), bk)
    out_ref[1, there, :] = (dk * scale).astype(bf16)
    out_ref[2, there, :] = dv.astype(bf16)

    @pl.when(j == pl.num_programs(0) - 1)
    def _():
        out_ref[0] = (dq_acc[...] * scale).astype(bf16)


def attend_back(length, q, k, v, do, o, lse):
    slots = q.shape[0]
    whole = pl.BlockSpec((slots, HEAD_DIM), lambda j: (0, 0))
    part = pl.BlockSpec((BLOCK, HEAD_DIM), lambda j: (j, 0))
    line = pl.BlockSpec((8, slots), lambda j: (0, 0))
    return pl.pallas_call(
        attend_back_kernel,
        name="attend_back",
        grid=(slots // BLOCK,),
        out_shape=jax.ShapeDtypeStruct((3, slots, HEAD_DIM), bf16),
        in_specs=[pl.BlockSpec(memory_space=pltpu.SMEM), whole, part, part, whole, whole, line],
        out_specs=pl.BlockSpec((3, slots, HEAD_DIM), lambda j: (0, 0, 0)),
        scratch_shapes=[pltpu.VMEM((slots, HEAD_DIM), f32), pltpu.VMEM((8, slots), f32)],
        cost_estimate=COST,
    )(length, q, k, v, do, o, lse)


def per_device(
    tokens,
    seq_lengths,
    w_query,
    w_key,
    w_value,
    w_out,
    w_gate,
    w_up,
    w_down,
    q_gain,
    k_gain,
    attn_gain,
    mlp_gain,
    cotangent,
):
    tok_rows, feat_part = tokens.shape
    row_count, data_count = lax.axis_size("row"), lax.axis_size("dp")
    width = feat_part * lax.axis_size("col")
    slots = tok_rows * row_count
    half_feat = feat_part // 2
    y, z = side("dp"), lax.axis_index("row")
    heads = half_feat // HEAD_DIM
    pairs = [(i, i ^ 1) for i in range(data_count)]
    after = lambda values, *done: lax.optimization_barrier((values,) + done)[0]

    def y_half(values, axis):
        size = values.shape[axis] // 2
        return lax.dynamic_slice_in_dim(values, y * size, size, axis)

    qkv_weight = lax.all_gather(
        jnp.concatenate([y_half(w_query, 1), y_half(w_key, 1), y_half(w_value, 1)], axis=1),
        "row",
        axis=0,
        tiled=True,
    )
    out_weight = lax.all_gather(y_half(w_out, 0), "row", axis=1, tiled=True)
    gate_weight = lax.all_gather(y_half(w_gate, 1), "row", axis=0, tiled=True)
    up_weight = lax.all_gather(y_half(w_up, 1), "row", axis=0, tiled=True)
    down_weight = lax.all_gather(y_half(w_down, 0), "row", axis=1, tiled=True)

    positions = z * tok_rows + jnp.arange(tok_rows)
    length = seq_lengths[0]
    valid = (positions < length).astype(f32)[:, None]
    cosine, sine = rope_tables(positions, HEAD_DIM)
    sine_signed = jnp.where(jnp.arange(HEAD_DIM)[None, :] < HEAD_DIM // 2, -sine, sine)
    other_length = lax.ppermute(seq_lengths, "dp", pairs)
    pair_lengths = jnp.where(
        y == 0,
        jnp.concatenate([seq_lengths, other_length]),
        jnp.concatenate([other_length, seq_lengths]),
    )
    unit_length = lax.dynamic_slice_in_dim(pair_lengths, z // heads, 1)
    qk_gain = jnp.stack([y_half(q_gain, 0), y_half(k_gain, 0)])

    tokens_wide = gather_wide(tokens, False, 0, "gather_tokens")
    qkv = matmul(tokens_wide, qkv_weight)
    units, inverse = front(qkv, cosine, sine_signed, qk_gain, width, 2 * heads, 2)
    q_unit, k_unit, v_unit = (units[:, i].reshape(slots, HEAD_DIM) for i in range(3))
    attn_unit, attn_exact, log_total = attend(unit_length, q_unit, k_unit, v_unit)
    attn_low = turn(attn_unit, True, tok_rows, heads, 3, "turn_attn")
    branch = scatter_wide(matmul(attn_low, out_weight).astype(bf16), False, 4, "scatter_branch")
    branch_inv = lax.rsqrt(
        feature_total(jnp.sum(branch * branch, axis=1)[None, :], 5, "total_branch")[0] / width
        + norm_eps
    )[:, None]
    resid = tokens.astype(f32) + branch * branch_inv * attn_gain
    resid_wide = gather_wide(resid.astype(bf16), False, 6, "gather_resid")
    gate = matmul(resid_wide, gate_weight)
    upper = matmul(resid_wide, up_weight)
    sigma = jax.nn.sigmoid(gate)
    hidden = (gate * sigma * upper).astype(bf16)
    mixed = scatter_wide(matmul(hidden, down_weight).astype(bf16), False, 7, "scatter_mixed")
    incoming = cotangent.astype(f32) * valid
    gained = incoming * mlp_gain
    sums = feature_total(
        jnp.stack([jnp.sum(mixed * mixed, axis=1), jnp.sum(gained * mixed, axis=1)]),
        8,
        "total_mixed",
    )
    mixed_inv = lax.rsqrt(sums[0] / width + norm_eps)[:, None]
    inner = (sums[1] / width)[:, None]
    block_output = ((resid + mixed * mixed_inv * mlp_gain) * valid).astype(bf16)
    mlp_gain_raw = jnp.sum(incoming * mixed * mixed_inv, axis=0)
    d_mixed = (mixed_inv * gained - mixed * mixed_inv**3 * inner).astype(bf16)
    d_mixed_wide = gather_wide(d_mixed, False, 9, "gather_d_mixed")

    factor = 1.0 / math.sqrt(slots * data_count)

    def cut(values, index, count, axis):
        size = values.shape[axis] // count
        return lax.dynamic_slice_in_dim(values, index * size, size, axis)

    def over_dp(piece):
        if data_count > 2:
            groups = [list(range(s, data_count, 2)) for s in (0, 1)]
            piece = lax.psum(piece, "dp", axis_index_groups=groups)
        return piece

    def two_sides(piece, other, bit, axis):
        low = jnp.where(bit == 0, piece, other)
        high = jnp.where(bit == 0, other, piece)
        return jnp.concatenate([low, high], axis=axis)

    def from_twin(piece):
        return lax.ppermute(piece, "dp", pairs)

    def reduce_rows(raw, axis):
        return lax.psum_scatter(raw, "row", scatter_dimension=axis, tiled=True)

    d_hidden = contract_last(d_mixed_wide, down_weight)
    down_raw = (contract_first(hidden, d_mixed_wide) * factor).astype(bf16)
    d_gate = (d_hidden * upper * sigma * (1.0 + gate * (1.0 - sigma))).astype(bf16)
    d_upper = (d_hidden * gate * sigma).astype(bf16)
    gate_raw = (contract_first(resid_wide, d_gate) * factor).astype(bf16)
    up_raw = (contract_first(resid_wide, d_upper) * factor).astype(bf16)
    d_resid_wide = (
        contract_last(d_gate, gate_weight) + contract_last(d_upper, up_weight)
    ).astype(bf16)
    d_resid_wide = after(d_resid_wide, down_raw, gate_raw, up_raw)
    down_piece = reduce_rows(down_raw, 1)
    gate_piece, up_piece = reduce_rows(gate_raw, 0), reduce_rows(up_raw, 0)
    d_resid = scatter_wide(d_resid_wide, False, 10, "scatter_d_resid")
    d_resid = incoming + d_resid
    attn_gain_raw = jnp.sum(d_resid * branch * branch_inv, axis=0)
    gained = d_resid * attn_gain
    inner = (
        feature_total(jnp.sum(gained * branch, axis=1)[None, :], 11, "total_d_resid")[0][:, None]
        / width
    )
    d_branch = (branch_inv * gained - branch * branch_inv**3 * inner).astype(bf16)
    down_piece = over_dp(down_piece)
    d_branch_wide, down_piece = lax.optimization_barrier(
        (gather_wide(d_branch, False, 12, "gather_d_branch"), down_piece)
    )
    d_attn = contract_last(d_branch_wide, out_weight).astype(bf16)
    other_down = from_twin(down_piece)
    d_attn_unit, other_down = lax.optimization_barrier(
        (turn(d_attn, False, tok_rows, heads, 13, "turn_d_attn"), other_down)
    )
    out_raw = (contract_first(attn_low, after(d_branch_wide, d_attn_unit)) * factor).astype(bf16)
    d_attn_unit = after(d_attn_unit, out_raw)
    out_piece = reduce_rows(out_raw, 1)
    d_units = attend_back(unit_length, q_unit, k_unit, v_unit, d_attn_unit, attn_exact, log_total)
    d_units, gate_piece = lax.optimization_barrier((d_units, over_dp(gate_piece)))
    other_gate = from_twin(gate_piece)
    d_qkv, gain_sums = rear(d_units, qkv, cosine, sine_signed, qk_gain, inverse, width, 14)
    d_qkv, gain_sums, other_gate = lax.optimization_barrier((d_qkv, gain_sums, other_gate))
    qkv_raw = (contract_first(tokens_wide, d_qkv) * factor).astype(bf16)
    projected = contract_last(d_qkv, qkv_weight).astype(bf16)
    projected, qkv_raw = lax.optimization_barrier((projected, qkv_raw))
    qkv_piece = over_dp(reduce_rows(qkv_raw, 0))
    def spread(half):
        return lax.dynamic_update_slice_in_dim(jnp.zeros((feat_part,), f32), half, y * half_feat, 0)

    gains = over_dp(
        gain_total(
            jnp.stack([spread(gain_sums[0]), spread(gain_sums[1]), attn_gain_raw, mlp_gain_raw])
            * factor,
            15,
        )
    )
    projected = after(projected, gains)
    up_piece, out_piece = over_dp(up_piece), over_dp(out_piece)
    scattered, up_piece, out_piece = lax.optimization_barrier(
        (scatter_wide(projected, False, 16, "scatter_projected"), up_piece, out_piece)
    )
    input_grad = d_resid + scattered

    def whole(piece, other, axis):
        return two_sides(piece, other, y, axis).astype(f32)

    qkv_other = from_twin(qkv_piece)
    q_grad, k_grad, v_grad = (
        two_sides(cut(qkv_piece, i, 3, 1), cut(qkv_other, i, 3, 1), y, 1).astype(f32)
        for i in range(3)
    )
    return (
        block_output,
        input_grad,
        q_grad,
        k_grad,
        v_grad,
        whole(out_piece, from_twin(out_piece), 0),
        whole(gate_piece, other_gate, 1),
        whole(up_piece, from_twin(up_piece), 1),
        whole(down_piece, other_down, 0),
        gains[0],
        gains[1],
        gains[2],
        gains[3],
    )


def solution(mesh):
    tok, row_col, col_row, gain = P(("dp", "row"), "col"), P("row", "col"), P("col", "row"), P("col")
    weights = (row_col, row_col, row_col, col_row, row_col, row_col, col_row)
    gains = (gain, gain, gain, gain)
    return jax.shard_map(
        per_device,
        mesh=mesh,
        in_specs=(tok, P("dp")) + weights + gains + (tok,),
        out_specs=(tok, tok) + weights + gains,
        check_vma=False,
    )
```

```python
import functools
import math

import jax
import jax.numpy as jnp
from jax import lax
from jax.experimental import pallas as pl
from jax.experimental.pallas import tpu as pltpu
from jax.sharding import PartitionSpec as P

HEAD_DIM = 128
rope_base = 500000.0
norm_eps = 1e-06
masked_score = -1e30

MESH = pl.DeviceIdType.MESH
bf16 = jnp.bfloat16
f32 = jnp.float32
COST = pl.CostEstimate(flops=0, bytes_accessed=1000, transcendentals=0)


def rope_tables(positions, head_dim):
    half = head_dim // 2
    freq = 1.0 / rope_base ** (jnp.arange(half, dtype=f32) / half)
    angle = positions.astype(f32)[:, None] * freq[None, :]
    angle = jnp.concatenate([angle, angle], axis=1)
    return (jnp.cos(angle), jnp.sin(angle))


def matmul(left, right):
    return jnp.dot(left, right, preferred_element_type=f32)


def contract_first(left, right):
    return lax.dot_general(left, right, (((0,), (0,)), ((), ())), preferred_element_type=f32)


def contract_last(left, right):
    return lax.dot_general(left, right, (((1,), (1,)), ((), ())), preferred_element_type=f32)


def flip(axis, bit):
    return lax.axis_index(axis) ^ bit


def side(axis):
    return lax.axis_index(axis) & 1


def greet(peers):
    barrier = pltpu.get_barrier_semaphore()
    for peer in peers:
        pl.semaphore_signal(barrier, inc=1, device_id=peer, device_id_type=MESH)
    pl.semaphore_wait(barrier, len(peers))


def sender(send_sem, recv_sem, started):
    def send(src, dst, number, peer):
        copy = pltpu.make_async_remote_copy(
            src_ref=src,
            dst_ref=dst,
            send_sem=send_sem.at[number],
            recv_sem=recv_sem.at[number],
            device_id=peer,
            device_id_type=MESH,
        )
        copy.start()
        started.append(copy)
        return copy

    return send


def neighbours():
    return {"col": flip("col", 2)}, {"dp": flip("dp", 1)}, {"col": flip("col", 1)}


def gather_kernel(pair, x_ref, out_ref, local_sem, send_sem, recv_sem):
    rows, width = x_ref.shape
    half = rows // 2
    y, b, p = side("dp"), lax.axis_index("col"), side("row") if pair else 0
    to_x, to_y, to_c = neighbours()
    to_z = {"row": flip("row", 1)}
    greet([to_x, to_y, to_c] + ([to_z] if pair else []))
    started = []
    send = sender(send_sem, recv_sem, started)

    def slot(pp, yy, h, bb, n=half):
        return out_ref.at[
            pl.ds(pl.multiple_of((pp * 2 + yy) * rows + h * half, half), n),
            pl.ds(pl.multiple_of(bb * width, width), width),
        ]

    def open_flow(pp, low, high, base):
        xa = send(low, slot(pp, y, 0, b), base + 0, to_x)
        ya = send(high, slot(pp, y, 1, b), base + 1, to_y)
        c0 = send(low, slot(pp, y, 0, b), base + 6, to_c)
        yb = send(low, slot(pp, y, 0, b), base + 2, to_y)
        xb = send(high, slot(pp, y, 1, b), base + 3, to_x)
        c1 = send(high, slot(pp, y, 1, b), base + 7, to_c)
        return xa, ya, xb, yb, [c0, c1]

    def relay(pp, flow, base):
        xa, ya, xb, yb, core = flow
        xa.wait_recv()
        piece = slot(pp, y, 0, b ^ 2)
        yc = send(piece, piece, base + 4, to_y)
        core.append(send(piece, piece, base + 8, to_c))
        ya.wait_recv()
        piece = slot(pp, y ^ 1, 1, b)
        xc = send(piece, piece, base + 5, to_x)
        core.append(send(piece, piece, base + 9, to_c))
        yb.wait_recv()
        piece = slot(pp, y ^ 1, 0, b)
        core.append(send(piece, piece, base + 10, to_c))
        xb.wait_recv()
        piece = slot(pp, y, 1, b ^ 2)
        core.append(send(piece, piece, base + 11, to_c))
        return yc, xc, core

    def close_flow(pp, state, base):
        yc, xc, core = state
        yc.wait_recv()
        piece = slot(pp, y ^ 1, 0, b ^ 2)
        core.append(send(piece, piece, base + 12, to_c))
        xc.wait_recv()
        piece = slot(pp, y ^ 1, 1, b ^ 2)
        core.append(send(piece, piece, base + 13, to_c))
        for copy in core:
            copy.wait_recv()

    low, high = x_ref.at[pl.ds(0, half)], x_ref.at[pl.ds(half, half)]
    own = pltpu.make_async_copy(x_ref, slot(p, y, 0, b, rows), local_sem)
    if pair:
        z0 = send(low, slot(p, y, 0, b), 28, to_z)
        z1 = send(high, slot(p, y, 1, b), 29, to_z)
    first = open_flow(p, low, high, 0)
    own.start()
    state = relay(p, first, 0)
    if pair:
        z0.wait_recv()
        z1.wait_recv()
        second = open_flow(p ^ 1, slot(p ^ 1, y, 0, b), slot(p ^ 1, y, 1, b), 14)
    close_flow(p, state, 0)
    if pair:
        close_flow(p ^ 1, relay(p ^ 1, second, 14), 14)
    for copy in started:
        copy.wait_send()
    own.wait()


def gather_wide(values, pair, number, name):
    rows, width = values.shape
    copies = 30 if pair else 14
    return pl.pallas_call(
        functools.partial(gather_kernel, pair),
        name=name,
        out_shape=jax.ShapeDtypeStruct(((4 if pair else 2) * rows, 4 * width), values.dtype),
        in_specs=[pl.BlockSpec(memory_space=pltpu.VMEM)],
        out_specs=pl.BlockSpec(memory_space=pl.ANY),
        scratch_shapes=[
            pltpu.SemaphoreType.DMA,
            pltpu.SemaphoreType.DMA((copies,)),
            pltpu.SemaphoreType.DMA((copies,)),
        ],
        compiler_params=pltpu.CompilerParams(collective_id=number, has_side_effects=True),
        cost_estimate=COST,
    )(values)


def scatter_kernel(pair, rider, p_ref, *refs):
    if rider:
        cargo_ref, out_ref, far_ref = refs[:3]
    else:
        out_ref = refs[0]
    rc, s1, ry, rx, s2, fy, fx, sz, fz, send_sem, recv_sem = refs[3 if rider else 1 :]
    rows, width = out_ref.shape
    half = rows // 2
    y, b, p = side("dp"), lax.axis_index("col"), side("row") if pair else 0
    x, c = b >> 1, b & 1
    to_x, to_y, to_c = neighbours()
    to_z = {"row": flip("row", 1)}
    to_far = {"row": flip("row", 2)}
    greet([to_x, to_y, to_c] + ([to_z] if pair else []) + ([to_far] if rider else []))
    started = []
    send = sender(send_sem, recv_sem, started)
    if rider:
        size = far_ref.shape[1]
        start = pl.multiple_of((1 - (lax.axis_index("row") >> 1)) * size, size)
        cargo = send(cargo_ref.at[:, pl.ds(start, size)], far_ref, 30, to_far)

    def place(yy, h):
        return pl.ds(pl.multiple_of(yy * rows + h * half, half), half)

    def column(bb):
        return pl.ds(pl.multiple_of(bb * width, width), width)

    order = [(0, y ^ 1, 0), (1, y ^ 1, 0), (x ^ 1, 0, 1), (x ^ 1, 1, 1)]
    order += [(0, y, 0), (1, y, 0), (x, 0, 1), (x, 1, 1)]

    class Flow:
        def __init__(self, f, pp):
            self.f, self.base = f, 14 * f
            self.rows = lambda yy, h: pl.ds(
                pl.multiple_of((pp * 2 + yy) * rows + h * half, half), half
            )
            self.core = [
                send(
                    p_ref.at[self.rows(yy, h), column(2 * xx + (c ^ 1))],
                    rc.at[f, xx, place(yy, h)],
                    self.base + number,
                    to_c,
                )
                for number, (xx, yy, h) in enumerate(order)
            ]

        def settle(self, *numbers):
            for number in numbers:
                self.core[number].wait_recv()
                xx, yy, h = order[number]
                s1[self.f, xx, place(yy, h), :] = (
                    p_ref[self.rows(yy, h), column(2 * xx + c)].astype(f32)
                    + rc[self.f, xx, place(yy, h), :].astype(f32)
                ).astype(s1.dtype)

        def first(self, i):
            f = self.f
            ya = send(s1.at[f, i, place(y ^ 1, 0), :], ry.at[f, i], self.base + 8 + i, to_y)
            part = s1.at[f, x ^ 1, pl.ds(i * rows + half, half), :]
            xa = send(part, rx.at[f, i], self.base + 10 + i, to_x)
            return ya, xa

        def second(self, copies):
            f = self.f
            for ya, _ in copies:
                ya.wait_recv()
            s2[f, 0] = (
                s1[f, x ^ 1, place(y, 0), :].astype(f32) + ry[f, x ^ 1].astype(f32)
            ).astype(s2.dtype)
            xb = send(s2.at[f, 0], fx.at[f], self.base + 12, to_x)
            for _, xa in copies:
                xa.wait_recv()
            s2[f, 1] = (
                s1[f, x, place(y ^ 1, 1), :].astype(f32) + rx[f, y ^ 1].astype(f32)
            ).astype(s2.dtype)
            yb = send(s2.at[f, 1], fy.at[f], self.base + 13, to_y)
            return xb, yb

        def last(self, copies):
            f = self.f
            xb, yb = copies
            keep = s1[f, x, place(y, 0), :].astype(f32) + ry[f, x].astype(f32)
            xb.wait_recv()
            low = keep + fx[f].astype(f32)
            keep = s1[f, x, place(y, 1), :].astype(f32) + rx[f, y].astype(f32)
            yb.wait_recv()
            return low, keep + fy[f].astype(f32)

    if pair:
        far = Flow(0, p ^ 1)
        near = Flow(1, p)
        far.settle(0, 1, 2, 3)
        far_first = [far.first(0), far.first(1)]
        far.settle(4, 5, 6, 7)
        near.settle(0, 1, 2, 3)
        near_first = [near.first(0)]
        near.settle(4, 5, 6, 7)
        far_second = far.second(far_first)
        near_first.append(near.first(1))
        low, high = far.last(far_second)
        sz[pl.ds(0, half), :] = low.astype(bf16)
        z0 = send(sz.at[pl.ds(0, half)], fz.at[pl.ds(0, half)], 28, to_z)
        sz[pl.ds(half, half), :] = high.astype(bf16)
        z1 = send(sz.at[pl.ds(half, half)], fz.at[pl.ds(half, half)], 29, to_z)
        low, high = near.last(near.second(near_first))
        z0.wait_recv()
        out_ref[pl.ds(0, half), :] = low + fz[pl.ds(0, half), :].astype(f32)
        z1.wait_recv()
        out_ref[pl.ds(half, half), :] = high + fz[pl.ds(half, half), :].astype(f32)
    else:
        near = Flow(0, 0)
        near.settle(0, 1, 2, 3)
        near_first = [near.first(0), near.first(1)]
        near.settle(4, 5, 6, 7)
        low, high = near.last(near.second(near_first))
        out_ref[pl.ds(0, half), :] = low
        out_ref[pl.ds(half, half), :] = high
    if rider:
        cargo.wait_recv()
    for copy in started:
        copy.wait_send()


def scatter_wide(partial, pair, number, name, cargo=None):
    flows = 2 if pair else 1
    rows, width = partial.shape[0] // (2 * flows), partial.shape[1] // 4
    half = rows // 2
    rider = cargo is not None
    copies = 31 if pair else 14
    out_shape, out_spec = [jax.ShapeDtypeStruct((rows, width), f32)], [pl.BlockSpec(memory_space=pltpu.VMEM)]
    anywhere = [pl.BlockSpec(memory_space=pl.ANY)] * rider
    if rider:
        out_shape.append(jax.ShapeDtypeStruct((cargo.shape[0], cargo.shape[1] // 2), cargo.dtype))
    last = (rows, width) if pair else (16, 128)
    out = pl.pallas_call(
        functools.partial(scatter_kernel, pair, rider),
        name=name,
        out_shape=out_shape,
        in_specs=[pl.BlockSpec(memory_space=pltpu.VMEM)] + anywhere,
        out_specs=out_spec + anywhere,
        scratch_shapes=[
            pltpu.VMEM((flows, 2, 2 * rows, width), bf16),
            pltpu.VMEM((flows, 2, 2 * rows, width), bf16),
            pltpu.VMEM((flows, 2, half, width), bf16),
            pltpu.VMEM((flows, 2, half, width), bf16),
            pltpu.VMEM((flows, 2, half, width), bf16),
            pltpu.VMEM((flows, half, width), bf16),
            pltpu.VMEM((flows, half, width), bf16),
            pltpu.VMEM(last, bf16),
            pltpu.VMEM(last, bf16),
            pltpu.SemaphoreType.DMA((copies,)),
            pltpu.SemaphoreType.DMA((copies,)),
        ],
        compiler_params=pltpu.CompilerParams(
            collective_id=number, has_side_effects=True, vmem_limit_bytes=48 * 2**20
        ),
        cost_estimate=COST,
    )(partial, *([cargo] * rider))
    return out if rider else out[0]


def feature_peers(wide):
    peers = []
    for d in range(1, 8 if wide else 4):
        peer = {"col": flip("col", d & 3)}
        if d >> 2:
            peer["dp"] = flip("dp", 1)
        peers.append(peer)
    return peers


def total_kernel(v_ref, out_ref, slots, send_sem, recv_sem):
    me = lax.axis_index("col")
    peers = feature_peers(False)
    greet(peers)
    started = []
    send = sender(send_sem, recv_sem, started)
    for d, peer in enumerate(peers):
        send(v_ref, slots.at[me], d, peer)
    slots[me] = v_ref[...]
    for copy in started:
        copy.wait_recv()
    total = slots[0]
    for i in range(1, 4):
        total = total + slots[i]
    out_ref[...] = total
    for copy in started:
        copy.wait_send()


def feature_total(values, number, name):
    k, t = values.shape
    flat = values.reshape(k * t // 128, 128)
    total = pl.pallas_call(
        total_kernel,
        name=name,
        out_shape=jax.ShapeDtypeStruct(flat.shape, f32),
        in_specs=[pl.BlockSpec(memory_space=pltpu.VMEM)],
        out_specs=pl.BlockSpec(memory_space=pltpu.VMEM),
        scratch_shapes=[
            pltpu.VMEM((4,) + flat.shape, f32),
            pltpu.SemaphoreType.DMA((3,)),
            pltpu.SemaphoreType.DMA((3,)),
        ],
        compiler_params=pltpu.CompilerParams(collective_id=number, has_side_effects=True),
    )(flat)
    return total.reshape(k, t)


def gain_peers():
    peers = []
    for d in range(1, 8):
        peers.append({"row": flip("row", d & 3), "dp": flip("dp", d >> 2)})
    return peers


def gain_kernel(v_ref, out_ref, slots, send_sem, recv_sem):
    me = side("dp") * 4 + lax.axis_index("row")
    peers = gain_peers()
    greet(peers)
    started = []
    send = sender(send_sem, recv_sem, started)
    for d, peer in enumerate(peers):
        send(v_ref, slots.at[me], d, peer)
    slots[me] = v_ref[...]
    for copy in started:
        copy.wait_recv()
    total = slots[0]
    for i in range(1, 8):
        total = total + slots[i]
    out_ref[...] = total
    for copy in started:
        copy.wait_send()


def gain_total(values, number):
    flat = values.reshape(-1, 128)
    total = pl.pallas_call(
        gain_kernel,
        name="total_gains",
        out_shape=jax.ShapeDtypeStruct(flat.shape, f32),
        in_specs=[pl.BlockSpec(memory_space=pltpu.VMEM)],
        out_specs=pl.BlockSpec(memory_space=pltpu.VMEM),
        scratch_shapes=[
            pltpu.VMEM((8,) + flat.shape, f32),
            pltpu.SemaphoreType.DMA((7,)),
            pltpu.SemaphoreType.DMA((7,)),
        ],
        compiler_params=pltpu.CompilerParams(collective_id=number, has_side_effects=True),
    )(flat)
    return total.reshape(values.shape)


def row_peers():
    return [(d, {"row": flip("row", d)}) for d in (3, 2, 1)]


def unit_view(ref, unit, tok, heads):
    rows = pl.ds(pl.multiple_of((unit // heads) * tok, tok), tok)
    cols = pl.ds(pl.multiple_of((unit % heads) * HEAD_DIM, HEAD_DIM), HEAD_DIM)
    return ref.at[rows, cols]


def turn_kernel(back, tok, heads, x_ref, out_ref, local_sem, send_sem, recv_sem):
    z = lax.axis_index("row")
    greet([peer for _, peer in row_peers()])
    started = []
    send = sender(send_sem, recv_sem, started)

    def line(ref, i):
        return ref.at[pl.ds(pl.multiple_of(i * tok, tok), tok)]

    def ends(i):
        if back:
            return line(x_ref, i), unit_view(out_ref, z, tok, heads)
        return unit_view(x_ref, i, tok, heads), line(out_ref, z)

    for d, peer in row_peers():
        send(*ends(z ^ d), d - 1, peer)
    own = pltpu.make_async_copy(*ends(z), local_sem)
    own.start()
    for copy in started:
        copy.wait()
    own.wait()


def turn(values, back, tok, heads, number, name):
    shape = (2 * tok, heads * HEAD_DIM) if back else (2 * heads * tok, HEAD_DIM)
    return pl.pallas_call(
        functools.partial(turn_kernel, back, tok, heads),
        name=name,
        out_shape=jax.ShapeDtypeStruct(shape, values.dtype),
        in_specs=[pl.BlockSpec(memory_space=pltpu.VMEM)],
        out_specs=pl.BlockSpec(memory_space=pl.ANY),
        scratch_shapes=[
            pltpu.SemaphoreType.DMA,
            pltpu.SemaphoreType.DMA((3,)),
            pltpu.SemaphoreType.DMA((3,)),
        ],
        compiler_params=pltpu.CompilerParams(collective_id=number, has_side_effects=True),
        cost_estimate=COST,
    )(values)


def totals(stat, slots, started):
    for copy in started:
        copy.wait_recv()
    total = slots[0]
    for i in range(1, 8):
        total = total + slots[i]
    return total


def front_kernel(
    width,
    qkv_ref,
    cos_ref,
    sin_ref,
    gain_ref,
    out_ref,
    inv_ref,
    turned,
    packed,
    stat,
    slots,
    local_sem,
    stat_send,
    stat_recv,
    send_sem,
    recv_sem,
):
    count, tok = qkv_ref.shape[0], cos_ref.shape[0]
    part = qkv_ref.shape[1] // 3
    heads = part // HEAD_DIM
    z = lax.axis_index("row")
    me = side("dp") * 4 + lax.axis_index("col")
    peers = feature_peers(True)
    greet(peers + [peer for _, peer in row_peers()])
    for i in range(2):
        values = qkv_ref[:, i * part : (i + 1) * part]
        stat[i : i + 1, :] = jnp.sum(values * values, axis=1, keepdims=True).T
    started, moved, local = [], [], []
    send = sender(stat_send, stat_recv, started)
    for d, peer in enumerate(peers):
        send(stat, slots.at[me], d, peer)
    slots[me] = stat[...]
    move = sender(send_sem, recv_sem, moved)

    def ship(i):
        for d, peer in row_peers():
            move(packed.at[z ^ d, i], out_ref.at[z, i], 3 * i + d - 1, peer)
        copy = pltpu.make_async_copy(packed.at[z, i], out_ref.at[z, i], local_sem.at[i])
        copy.start()
        local.append(copy)

    def spots():
        return [(s, h, s * heads + h) for s in range(2) for h in range(heads)]

    for s, h, unit in spots():
        packed[unit, 2] = qkv_ref[
            s * tok : (s + 1) * tok, 2 * part + h * HEAD_DIM : 2 * part + (h + 1) * HEAD_DIM
        ].astype(bf16)
    ship(2)
    for i in (1, 0):
        for s, h, unit in spots():
            values = (
                qkv_ref[s * tok : (s + 1) * tok, i * part + h * HEAD_DIM : i * part + (h + 1) * HEAD_DIM]
                * gain_ref[i : i + 1, h * HEAD_DIM : (h + 1) * HEAD_DIM]
            )
            turned[i, unit] = values * cos_ref[...] + pltpu.roll(values, HEAD_DIM // 2, 1) * sin_ref[...]
    inverse = lax.rsqrt(totals(stat, slots, started) / width + norm_eps)
    inv_ref[...] = inverse
    for i in (1, 0):
        column = inverse[i : i + 1, :].T
        for s, h, unit in spots():
            packed[unit, i] = (turned[i, unit] * column[s * tok : (s + 1) * tok]).astype(bf16)
        ship(i)
    for copy in moved:
        copy.wait()
    for copy in local:
        copy.wait()
    for copy in started:
        copy.wait_send()


def front(qkv, cosine, sine_signed, gains, width, units, number):
    count, tok = qkv.shape[0], cosine.shape[0]
    return pl.pallas_call(
        functools.partial(front_kernel, width),
        name="front",
        out_shape=(
            jax.ShapeDtypeStruct((units, 3, tok, HEAD_DIM), bf16),
            jax.ShapeDtypeStruct((2, count), f32),
        ),
        in_specs=[pl.BlockSpec(memory_space=pltpu.VMEM)] * 4,
        out_specs=(pl.BlockSpec(memory_space=pl.ANY), pl.BlockSpec(memory_space=pltpu.VMEM)),
        scratch_shapes=[
            pltpu.VMEM((2, units, tok, HEAD_DIM), f32),
            pltpu.VMEM((units, 3, tok, HEAD_DIM), bf16),
            pltpu.VMEM((2, count), f32),
            pltpu.VMEM((8, 2, count), f32),
            pltpu.SemaphoreType.DMA((3,)),
            pltpu.SemaphoreType.DMA((7,)),
            pltpu.SemaphoreType.DMA((7,)),
            pltpu.SemaphoreType.DMA((9,)),
            pltpu.SemaphoreType.DMA((9,)),
        ],
        compiler_params=pltpu.CompilerParams(
            collective_id=number, has_side_effects=True, vmem_limit_bytes=40 * 2**20
        ),
        cost_estimate=COST,
    )(qkv, cosine, sine_signed, gains)


def rear_kernel(
    width,
    d_ref,
    qkv_ref,
    cos_ref,
    sin_ref,
    gain_ref,
    inv_ref,
    out_ref,
    sums_ref,
    landed,
    normed,
    stat,
    slots,
    stat_send,
    stat_recv,
    send_sem,
    recv_sem,
):
    count, tok = qkv_ref.shape[0], cos_ref.shape[0]
    part = qkv_ref.shape[1] // 3
    heads = part // HEAD_DIM
    z = lax.axis_index("row")
    me = side("dp") * 4 + lax.axis_index("col")
    peers = feature_peers(True)
    greet(peers + [peer for _, peer in row_peers()])
    started, moved = [], []
    move = sender(send_sem, recv_sem, moved)
    for i in (0, 1, 2):
        for d, peer in row_peers():
            there = pl.ds(pl.multiple_of((z ^ d) * tok, tok), tok)
            move(d_ref.at[i, there], landed.at[z, i], 3 * i + d - 1, peer)
    here = pl.ds(pl.multiple_of(z * tok, tok), tok)
    for i in (0, 1, 2):
        landed[z, i] = d_ref[i, here, :]
    spots = [(s, h, s * heads + h) for s in range(2) for h in range(heads)]
    for i in (0, 1):
        for copy in moved[3 * i : 3 * i + 3]:
            copy.wait_recv()
        for h in range(heads):
            cols = slice(i * part + h * HEAD_DIM, i * part + (h + 1) * HEAD_DIM)
            gain = gain_ref[i : i + 1, h * HEAD_DIM : (h + 1) * HEAD_DIM]
            raw = jnp.zeros((1, HEAD_DIM), f32)
            for s in range(2):
                rows = slice(s * tok, (s + 1) * tok)
                values = landed[s * heads + h, i].astype(f32)
                back = values * cos_ref[...] - pltpu.roll(values, HEAD_DIM // 2, 1) * sin_ref[...]
                pre = qkv_ref[rows, cols]
                inverse = inv_ref[i : i + 1, rows].T
                crossed = back * pre
                raw = raw + jnp.sum(crossed * inverse, axis=0, keepdims=True)
                partial = jnp.sum(crossed * gain, axis=1, keepdims=True).T
                if h == 0:
                    stat[i : i + 1, rows] = partial
                else:
                    stat[i : i + 1, rows] = stat[i : i + 1, rows] + partial
                normed[rows, cols] = back * gain
            sums_ref[i : i + 1, h * HEAD_DIM : (h + 1) * HEAD_DIM] = raw
    send = sender(stat_send, stat_recv, started)
    for d, peer in enumerate(peers):
        send(stat, slots.at[me], d, peer)
    slots[me] = stat[...]
    for copy in moved[6:]:
        copy.wait_recv()
    for s, h, unit in spots:
        cols = slice(2 * part + h * HEAD_DIM, 2 * part + (h + 1) * HEAD_DIM)
        out_ref[s * tok : (s + 1) * tok, cols] = landed[unit, 2]
    inner = totals(stat, slots, started) / width
    for i in (0, 1):
        inverse = inv_ref[i : i + 1, :]
        first = inverse.T
        second = (inverse * inverse * inverse * inner[i : i + 1, :]).T
        cols = slice(i * part, (i + 1) * part)
        out_ref[:, cols] = (first * normed[:, cols] - qkv_ref[:, cols] * second).astype(bf16)
    for copy in moved + started:
        copy.wait_send()


def rear(d_units, qkv, cosine, sine_signed, gains, inverse, width, number):
    count, tok = qkv.shape[0], cosine.shape[0]
    part = qkv.shape[1] // 3
    units = d_units.shape[1] // tok
    return pl.pallas_call(
        functools.partial(rear_kernel, width),
        name="rear",
        out_shape=(
            jax.ShapeDtypeStruct((count, 3 * part), bf16),
            jax.ShapeDtypeStruct((2, part), f32),
        ),
        in_specs=[pl.BlockSpec(memory_space=pltpu.VMEM)] * 6,
        out_specs=[pl.BlockSpec(memory_space=pltpu.VMEM)] * 2,
        scratch_shapes=[
            pltpu.VMEM((units, 3, tok, HEAD_DIM), bf16),
            pltpu.VMEM((count, 2 * part), f32),
            pltpu.VMEM((2, count), f32),
            pltpu.VMEM((8, 2, count), f32),
            pltpu.SemaphoreType.DMA((7,)),
            pltpu.SemaphoreType.DMA((7,)),
            pltpu.SemaphoreType.DMA((9,)),
            pltpu.SemaphoreType.DMA((9,)),
        ],
        compiler_params=pltpu.CompilerParams(
            collective_id=number, has_side_effects=True, vmem_limit_bytes=40 * 2**20
        ),
        cost_estimate=COST,
    )(d_units, qkv, cosine, sine_signed, gains, inverse)


BLOCK = 512


def attend_kernel(len_ref, q_ref, k_ref, v_ref, o_ref, o32_ref, lse_ref):
    i = pl.program_id(0)
    bq, bk = q_ref.shape[0], BLOCK
    length = len_ref[0]
    scale = HEAD_DIM ** (-0.5)
    q = q_ref[...]
    rows = i * bq + lax.broadcasted_iota(jnp.int32, (bq, bk), 0)
    cols0 = lax.broadcasted_iota(jnp.int32, (bq, bk), 1)

    def step(j, carry, masked):
        top, total, acc = carry
        j0 = pl.multiple_of(j * bk, bk)
        scores = contract_last(q, k_ref[pl.ds(j0, bk), :]) * scale
        if masked:
            cols = j0 + cols0
            scores = jnp.where((cols <= rows) & (cols < length), scores, masked_score)
        new = jnp.maximum(top, jnp.max(scores, axis=1, keepdims=True))
        weights = jnp.exp(scores - new)
        fix = jnp.exp(top - new)
        total = total * fix + jnp.sum(weights, axis=1, keepdims=True)
        acc = acc * fix + matmul(weights.astype(bf16), v_ref[pl.ds(j0, bk), :])
        return new, total, acc

    carry = (
        jnp.full((bq, 1), -jnp.inf, f32),
        jnp.zeros((bq, 1), f32),
        jnp.zeros((bq, HEAD_DIM), f32),
    )
    whole = jnp.minimum(i, length // bk)
    last = jnp.minimum(i + 1, (length + bk - 1) // bk)
    carry = lax.fori_loop(0, whole, lambda j, s: step(j, s, False), carry)
    top, total, acc = lax.fori_loop(whole, last, lambda j, s: step(j, s, True), carry)
    out = acc / total
    o_ref[...] = out.astype(bf16)
    o32_ref[...] = out
    lse_ref[...] = jnp.broadcast_to((top + jnp.log(total)).T, lse_ref.shape)


def attend(length, q, k, v):
    slots = q.shape[0]
    whole = pl.BlockSpec((slots, HEAD_DIM), lambda i: (0, 0))
    part = pl.BlockSpec((BLOCK, HEAD_DIM), lambda i: (i, 0))
    return pl.pallas_call(
        attend_kernel,
        name="attend",
        grid=(slots // BLOCK,),
        out_shape=(
            jax.ShapeDtypeStruct((slots, HEAD_DIM), bf16),
            jax.ShapeDtypeStruct((slots, HEAD_DIM), f32),
            jax.ShapeDtypeStruct((8, slots), f32),
        ),
        in_specs=[pl.BlockSpec(memory_space=pltpu.SMEM), part, whole, whole],
        out_specs=(part, part, pl.BlockSpec((8, BLOCK), lambda i: (0, i))),
        cost_estimate=COST,
    )(length, q, k, v)


def attend_back_kernel(
    len_ref, q_ref, k_ref, v_ref, do_ref, o_ref, lse_ref, out_ref, dq_acc, delta_ref
):
    j = pl.program_id(0)
    bk, bq = k_ref.shape[0], BLOCK
    slots = q_ref.shape[0]
    length = len_ref[0]
    scale = HEAD_DIM ** (-0.5)

    @pl.when(j == 0)
    def _():
        dq_acc[...] = jnp.zeros_like(dq_acc)
        for i in range(slots // bq):
            here = slice(i * bq, (i + 1) * bq)
            product = do_ref[here, :].astype(f32) * o_ref[here, :]
            delta_ref[0:1, here] = jnp.sum(product, axis=1, keepdims=True).T

    k, v = k_ref[...], v_ref[...]
    j0 = j * bk
    cols = j0 + lax.broadcasted_iota(jnp.int32, (bk, bq), 0)
    rows0 = lax.broadcasted_iota(jnp.int32, (bk, bq), 1)

    def step(i, carry, masked):
        dk, dv = carry
        i0 = pl.multiple_of(i * bq, bq)
        here = pl.ds(i0, bq)
        q, do = q_ref[here, :], do_ref[here, :]
        scores = contract_last(k, q) * scale
        if masked:
            scores = jnp.where((cols <= i0 + rows0) & (cols < length), scores, masked_score)
        probs = jnp.exp(scores - lse_ref[0:1, here])
        dv = dv + matmul(probs.astype(bf16), do)
        d_probs = contract_last(v, do)
        d_scores = (probs * (d_probs - delta_ref[0:1, here])).astype(bf16)
        dk = dk + matmul(d_scores, q)
        dq_acc[here, :] += contract_first(d_scores, k)
        return dk, dv

    zero = jnp.zeros((bk, HEAD_DIM), f32)
    top = slots // bq
    first = jnp.where(j0 + bk <= length, j + 1, top)
    first = jnp.where(j0 < length, first, j)
    stop = jnp.where(j0 < length, top, j)
    carry = lax.fori_loop(j, first, lambda i, s: step(i, s, True), (zero, zero))
    dk, dv = lax.fori_loop(first, stop, lambda i, s: step(i, s, False), carry)
    there = pl.ds(pl.multiple_of(j0, bk), bk)
    out_ref[1, there, :] = (dk * scale).astype(bf16)
    out_ref[2, there, :] = dv.astype(bf16)

    @pl.when(j == pl.num_programs(0) - 1)
    def _():
        out_ref[0] = (dq_acc[...] * scale).astype(bf16)


def attend_back(length, q, k, v, do, o, lse):
    slots = q.shape[0]
    whole = pl.BlockSpec((slots, HEAD_DIM), lambda j: (0, 0))
    part = pl.BlockSpec((BLOCK, HEAD_DIM), lambda j: (j, 0))
    line = pl.BlockSpec((8, slots), lambda j: (0, 0))
    return pl.pallas_call(
        attend_back_kernel,
        name="attend_back",
        grid=(slots // BLOCK,),
        out_shape=jax.ShapeDtypeStruct((3, slots, HEAD_DIM), bf16),
        in_specs=[pl.BlockSpec(memory_space=pltpu.SMEM), whole, part, part, whole, whole, line],
        out_specs=pl.BlockSpec((3, slots, HEAD_DIM), lambda j: (0, 0, 0)),
        scratch_shapes=[pltpu.VMEM((slots, HEAD_DIM), f32), pltpu.VMEM((8, slots), f32)],
        cost_estimate=COST,
    )(length, q, k, v, do, o, lse)


def per_device(
    tokens,
    seq_lengths,
    w_query,
    w_key,
    w_value,
    w_out,
    w_gate,
    w_up,
    w_down,
    q_gain,
    k_gain,
    attn_gain,
    mlp_gain,
    cotangent,
):
    tok_rows, feat_part = tokens.shape
    row_count, data_count = lax.axis_size("row"), lax.axis_size("dp")
    width = feat_part * lax.axis_size("col")
    slots = tok_rows * row_count
    half_feat = feat_part // 2
    y, z = side("dp"), lax.axis_index("row")
    heads = half_feat // HEAD_DIM
    pairs = [(i, i ^ 1) for i in range(data_count)]
    after = lambda values, *done: lax.optimization_barrier((values,) + done)[0]

    def y_half(values, axis):
        size = values.shape[axis] // 2
        return lax.dynamic_slice_in_dim(values, y * size, size, axis)

    qkv_weight = lax.all_gather(
        jnp.concatenate([y_half(w_query, 1), y_half(w_key, 1), y_half(w_value, 1)], axis=1),
        "row",
        axis=0,
        tiled=True,
    )
    out_weight = lax.all_gather(y_half(w_out, 0), "row", axis=1, tiled=True)
    gate_weight = lax.all_gather(y_half(w_gate, 1), "row", axis=0, tiled=True)
    up_weight = lax.all_gather(y_half(w_up, 1), "row", axis=0, tiled=True)
    down_half = y_half(w_down, 0)
    split = down_half.shape[1] // 2
    low_weight = lax.all_gather(down_half[:, :split], "row", axis=1, tiled=True)
    high_weight = lax.all_gather(down_half[:, split:], "row", axis=1, tiled=True)

    positions = z * tok_rows + jnp.arange(tok_rows)
    length = seq_lengths[0]
    valid = (positions < length).astype(f32)[:, None]
    cosine, sine = rope_tables(positions, HEAD_DIM)
    sine_signed = jnp.where(jnp.arange(HEAD_DIM)[None, :] < HEAD_DIM // 2, -sine, sine)
    other_length = lax.ppermute(seq_lengths, "dp", pairs)
    pair_lengths = jnp.where(
        y == 0,
        jnp.concatenate([seq_lengths, other_length]),
        jnp.concatenate([other_length, seq_lengths]),
    )
    unit_length = lax.dynamic_slice_in_dim(pair_lengths, z // heads, 1)
    qk_gain = jnp.stack([y_half(q_gain, 0), y_half(k_gain, 0)])

    tokens_wide = gather_wide(tokens, False, 0, "gather_tokens")
    qkv = matmul(tokens_wide, qkv_weight)
    units, inverse = front(qkv, cosine, sine_signed, qk_gain, width, 2 * heads, 2)
    q_unit, k_unit, v_unit = (units[:, i].reshape(slots, HEAD_DIM) for i in range(3))
    attn_unit, attn_exact, log_total = attend(unit_length, q_unit, k_unit, v_unit)
    attn_low = turn(attn_unit, True, tok_rows, heads, 3, "turn_attn")
    branch = scatter_wide(matmul(attn_low, out_weight).astype(bf16), False, 4, "scatter_branch")
    branch_inv = lax.rsqrt(
        feature_total(jnp.sum(branch * branch, axis=1)[None, :], 5, "total_branch")[0] / width
        + norm_eps
    )[:, None]
    resid = tokens.astype(f32) + branch * branch_inv * attn_gain
    resid_wide = gather_wide(resid.astype(bf16), False, 6, "gather_resid")
    gate = matmul(resid_wide, gate_weight)
    upper = matmul(resid_wide, up_weight)
    sigma = jax.nn.sigmoid(gate)
    hidden = (gate * sigma * upper).astype(bf16)
    mixed_low = scatter_wide(matmul(hidden, low_weight).astype(bf16), False, 7, "scatter_mixed_low")
    high_weight = after(high_weight, mixed_low)
    mixed_high = scatter_wide(matmul(hidden, high_weight).astype(bf16), False, 17, "scatter_mixed_high")
    mixed = jnp.concatenate([mixed_low, mixed_high], axis=1)
    incoming = cotangent.astype(f32) * valid
    gained = incoming * mlp_gain
    sums = feature_total(
        jnp.stack([jnp.sum(mixed * mixed, axis=1), jnp.sum(gained * mixed, axis=1)]),
        8,
        "total_mixed",
    )
    mixed_inv = lax.rsqrt(sums[0] / width + norm_eps)[:, None]
    inner = (sums[1] / width)[:, None]
    block_output = ((resid + mixed * mixed_inv * mlp_gain) * valid).astype(bf16)
    mlp_gain_raw = jnp.sum(incoming * mixed * mixed_inv, axis=0)
    d_mixed = (mixed_inv * gained - mixed * mixed_inv**3 * inner).astype(bf16)
    factor = 1.0 / math.sqrt(slots * data_count)
    d_low_wide = gather_wide(d_mixed[:, :split], False, 9, "gather_d_mixed_low")
    low_raw = (contract_first(hidden, d_low_wide) * factor).astype(bf16)
    d_high = after(d_mixed[:, split:], low_raw)
    d_high_wide = gather_wide(d_high, False, 18, "gather_d_mixed_high")
    high_raw = (contract_first(hidden, d_high_wide) * factor).astype(bf16)

    def cut(values, index, count, axis):
        size = values.shape[axis] // count
        return lax.dynamic_slice_in_dim(values, index * size, size, axis)

    def over_dp(piece):
        if data_count > 2:
            groups = [list(range(s, data_count, 2)) for s in (0, 1)]
            piece = lax.psum(piece, "dp", axis_index_groups=groups)
        return piece

    def two_sides(piece, other, bit, axis):
        low = jnp.where(bit == 0, piece, other)
        high = jnp.where(bit == 0, other, piece)
        return jnp.concatenate([low, high], axis=axis)

    def from_twin(piece):
        return lax.ppermute(piece, "dp", pairs)

    def reduce_rows(raw, axis):
        return lax.psum_scatter(raw, "row", scatter_dimension=axis, tiled=True)

    d_hidden = contract_last(d_low_wide, low_weight) + contract_last(d_high_wide, high_weight)
    d_gate = (d_hidden * upper * sigma * (1.0 + gate * (1.0 - sigma))).astype(bf16)
    d_upper = (d_hidden * gate * sigma).astype(bf16)
    gate_raw = (contract_first(resid_wide, d_gate) * factor).astype(bf16)
    up_raw = (contract_first(resid_wide, d_upper) * factor).astype(bf16)
    d_resid_wide = (
        contract_last(d_gate, gate_weight) + contract_last(d_upper, up_weight)
    ).astype(bf16)
    d_resid_wide, low_piece = lax.optimization_barrier(
        (after(d_resid_wide, high_raw, gate_raw, up_raw), reduce_rows(low_raw, 1))
    )
    down_piece = jnp.concatenate([low_piece, reduce_rows(high_raw, 1)], axis=1)
    gate_piece, up_piece = reduce_rows(gate_raw, 0), reduce_rows(up_raw, 0)
    d_resid = scatter_wide(d_resid_wide, False, 10, "scatter_d_resid")
    d_resid = incoming + d_resid
    attn_gain_raw = jnp.sum(d_resid * branch * branch_inv, axis=0)
    gained = d_resid * attn_gain
    inner = (
        feature_total(jnp.sum(gained * branch, axis=1)[None, :], 11, "total_d_resid")[0][:, None]
        / width
    )
    d_branch = (branch_inv * gained - branch * branch_inv**3 * inner).astype(bf16)
    down_piece = over_dp(down_piece)
    d_branch_wide, down_piece = lax.optimization_barrier(
        (gather_wide(d_branch, False, 12, "gather_d_branch"), down_piece)
    )
    d_attn = contract_last(d_branch_wide, out_weight).astype(bf16)
    other_down = from_twin(down_piece)
    d_attn_unit, other_down = lax.optimization_barrier(
        (turn(d_attn, False, tok_rows, heads, 13, "turn_d_attn"), other_down)
    )
    out_raw = (contract_first(attn_low, after(d_branch_wide, d_attn_unit)) * factor).astype(bf16)
    d_attn_unit = after(d_attn_unit, out_raw)
    out_piece = reduce_rows(out_raw, 1)
    d_units = attend_back(unit_length, q_unit, k_unit, v_unit, d_attn_unit, attn_exact, log_total)
    d_units, gate_piece = lax.optimization_barrier((d_units, over_dp(gate_piece)))
    other_gate = from_twin(gate_piece)
    d_qkv, gain_sums = rear(d_units, qkv, cosine, sine_signed, qk_gain, inverse, width, 14)
    d_qkv, gain_sums, other_gate, up_piece = lax.optimization_barrier(
        (d_qkv, gain_sums, other_gate, over_dp(up_piece))
    )
    other_up = from_twin(up_piece)
    qkv_raw = (contract_first(tokens_wide, d_qkv) * factor).astype(bf16)
    projected = contract_last(after(d_qkv, qkv_raw), qkv_weight).astype(bf16)
    projected, out_piece = lax.optimization_barrier((projected, over_dp(out_piece)))
    other_out = from_twin(out_piece)
    qkv_piece = over_dp(reduce_rows(qkv_raw, 0))

    def spread(half):
        return lax.dynamic_update_slice_in_dim(jnp.zeros((feat_part,), f32), half, y * half_feat, 0)

    gains = over_dp(
        gain_total(
            jnp.stack([spread(gain_sums[0]), spread(gain_sums[1]), attn_gain_raw, mlp_gain_raw])
            * factor,
            15,
        )
    )
    projected = after(projected, gains, other_up, other_out)
    scattered, qkv_piece = lax.optimization_barrier(
        (scatter_wide(projected, False, 16, "scatter_projected"), qkv_piece)
    )
    input_grad = d_resid + scattered

    def whole(piece, other, axis):
        return two_sides(piece, other, y, axis).astype(f32)

    qkv_other = from_twin(qkv_piece)
    q_grad, k_grad, v_grad = (
        two_sides(cut(qkv_piece, i, 3, 1), cut(qkv_other, i, 3, 1), y, 1).astype(f32)
        for i in range(3)
    )
    return (
        block_output,
        input_grad,
        q_grad,
        k_grad,
        v_grad,
        whole(out_piece, other_out, 0),
        whole(gate_piece, other_gate, 1),
        whole(up_piece, other_up, 1),
        whole(down_piece, other_down, 0),
        gains[0],
        gains[1],
        gains[2],
        gains[3],
    )


def solution(mesh):
    tok, row_col, col_row, gain = P(("dp", "row"), "col"), P("row", "col"), P("col", "row"), P("col")
    weights = (row_col, row_col, row_col, col_row, row_col, row_col, col_row)
    gains = (gain, gain, gain, gain)
    return jax.shard_map(
        per_device,
        mesh=mesh,
        in_specs=(tok, P("dp")) + weights + gains + (tok,),
        out_specs=(tok, tok) + weights + gains,
        check_vma=False,
    )
```

```python
import functools
import math

import jax
import jax.numpy as jnp
from jax import lax
from jax.experimental import pallas as pl
from jax.experimental.pallas import tpu as pltpu
from jax.sharding import PartitionSpec as P

HEAD_DIM = 128
rope_base = 500000.0
norm_eps = 1e-06
masked_score = -1e30

MESH = pl.DeviceIdType.MESH
bf16 = jnp.bfloat16
f32 = jnp.float32
COST = pl.CostEstimate(flops=0, bytes_accessed=1000, transcendentals=0)


def rope_tables(positions, head_dim):
    half = head_dim // 2
    freq = 1.0 / rope_base ** (jnp.arange(half, dtype=f32) / half)
    angle = positions.astype(f32)[:, None] * freq[None, :]
    angle = jnp.concatenate([angle, angle], axis=1)
    return (jnp.cos(angle), jnp.sin(angle))


def matmul(left, right):
    return jnp.dot(left, right, preferred_element_type=f32)


def contract_first(left, right):
    return lax.dot_general(left, right, (((0,), (0,)), ((), ())), preferred_element_type=f32)


def contract_last(left, right):
    return lax.dot_general(left, right, (((1,), (1,)), ((), ())), preferred_element_type=f32)


def flip(axis, bit):
    return lax.axis_index(axis) ^ bit


def side(axis):
    return lax.axis_index(axis) & 1


def greet(peers):
    barrier = pltpu.get_barrier_semaphore()
    for peer in peers:
        pl.semaphore_signal(barrier, inc=1, device_id=peer, device_id_type=MESH)
    pl.semaphore_wait(barrier, len(peers))


def sender(send_sem, recv_sem, started):
    def send(src, dst, number, peer):
        copy = pltpu.make_async_remote_copy(
            src_ref=src,
            dst_ref=dst,
            send_sem=send_sem.at[number],
            recv_sem=recv_sem.at[number],
            device_id=peer,
            device_id_type=MESH,
        )
        copy.start()
        started.append(copy)
        return copy

    return send


def neighbours():
    return {"col": flip("col", 2)}, {"dp": flip("dp", 1)}, {"col": flip("col", 1)}


def gather_kernel(pair, x_ref, out_ref, local_sem, send_sem, recv_sem):
    rows, width = x_ref.shape
    half = rows // 2
    y, b, p = side("dp"), lax.axis_index("col"), side("row") if pair else 0
    to_x, to_y, to_c = neighbours()
    to_z = {"row": flip("row", 1)}
    greet([to_x, to_y, to_c] + ([to_z] if pair else []))
    started = []
    send = sender(send_sem, recv_sem, started)

    def slot(pp, yy, h, bb, n=half):
        return out_ref.at[
            pl.ds(pl.multiple_of((pp * 2 + yy) * rows + h * half, half), n),
            pl.ds(pl.multiple_of(bb * width, width), width),
        ]

    def open_flow(pp, low, high, base):
        xa = send(low, slot(pp, y, 0, b), base + 0, to_x)
        ya = send(high, slot(pp, y, 1, b), base + 1, to_y)
        c0 = send(low, slot(pp, y, 0, b), base + 6, to_c)
        yb = send(low, slot(pp, y, 0, b), base + 2, to_y)
        xb = send(high, slot(pp, y, 1, b), base + 3, to_x)
        c1 = send(high, slot(pp, y, 1, b), base + 7, to_c)
        return xa, ya, xb, yb, [c0, c1]

    def relay(pp, flow, base):
        xa, ya, xb, yb, core = flow
        xa.wait_recv()
        piece = slot(pp, y, 0, b ^ 2)
        yc = send(piece, piece, base + 4, to_y)
        core.append(send(piece, piece, base + 8, to_c))
        ya.wait_recv()
        piece = slot(pp, y ^ 1, 1, b)
        xc = send(piece, piece, base + 5, to_x)
        core.append(send(piece, piece, base + 9, to_c))
        yb.wait_recv()
        piece = slot(pp, y ^ 1, 0, b)
        core.append(send(piece, piece, base + 10, to_c))
        xb.wait_recv()
        piece = slot(pp, y, 1, b ^ 2)
        core.append(send(piece, piece, base + 11, to_c))
        return yc, xc, core

    def close_flow(pp, state, base):
        yc, xc, core = state
        yc.wait_recv()
        piece = slot(pp, y ^ 1, 0, b ^ 2)
        core.append(send(piece, piece, base + 12, to_c))
        xc.wait_recv()
        piece = slot(pp, y ^ 1, 1, b ^ 2)
        core.append(send(piece, piece, base + 13, to_c))
        for copy in core:
            copy.wait_recv()

    low, high = x_ref.at[pl.ds(0, half)], x_ref.at[pl.ds(half, half)]
    own = pltpu.make_async_copy(x_ref, slot(p, y, 0, b, rows), local_sem)
    if pair:
        z0 = send(low, slot(p, y, 0, b), 28, to_z)
        z1 = send(high, slot(p, y, 1, b), 29, to_z)
    first = open_flow(p, low, high, 0)
    own.start()
    state = relay(p, first, 0)
    if pair:
        z0.wait_recv()
        z1.wait_recv()
        second = open_flow(p ^ 1, slot(p ^ 1, y, 0, b), slot(p ^ 1, y, 1, b), 14)
    close_flow(p, state, 0)
    if pair:
        close_flow(p ^ 1, relay(p ^ 1, second, 14), 14)
    for copy in started:
        copy.wait_send()
    own.wait()


def gather_wide(values, pair, number, name):
    rows, width = values.shape
    copies = 30 if pair else 14
    return pl.pallas_call(
        functools.partial(gather_kernel, pair),
        name=name,
        out_shape=jax.ShapeDtypeStruct(((4 if pair else 2) * rows, 4 * width), values.dtype),
        in_specs=[pl.BlockSpec(memory_space=pltpu.VMEM)],
        out_specs=pl.BlockSpec(memory_space=pl.ANY),
        scratch_shapes=[
            pltpu.SemaphoreType.DMA,
            pltpu.SemaphoreType.DMA((copies,)),
            pltpu.SemaphoreType.DMA((copies,)),
        ],
        compiler_params=pltpu.CompilerParams(collective_id=number, has_side_effects=True),
        cost_estimate=COST,
    )(values)


def scatter_kernel(pair, rider, p_ref, *refs):
    if rider:
        cargo_ref, out_ref, far_ref = refs[:3]
    else:
        out_ref = refs[0]
    rc, s1, ry, rx, s2, fy, fx, sz, fz, send_sem, recv_sem = refs[3 if rider else 1 :]
    rows, width = out_ref.shape
    half = rows // 2
    y, b, p = side("dp"), lax.axis_index("col"), side("row") if pair else 0
    x, c = b >> 1, b & 1
    to_x, to_y, to_c = neighbours()
    to_z = {"row": flip("row", 1)}
    to_far = {"row": flip("row", 2)}
    greet([to_x, to_y, to_c] + ([to_z] if pair else []) + ([to_far] if rider else []))
    started = []
    send = sender(send_sem, recv_sem, started)
    if rider:
        size = far_ref.shape[1]
        start = pl.multiple_of((1 - (lax.axis_index("row") >> 1)) * size, size)
        cargo = send(cargo_ref.at[:, pl.ds(start, size)], far_ref, 30, to_far)

    def place(yy, h):
        return pl.ds(pl.multiple_of(yy * rows + h * half, half), half)

    def column(bb):
        return pl.ds(pl.multiple_of(bb * width, width), width)

    order = [(0, y ^ 1, 0), (1, y ^ 1, 0), (x ^ 1, 0, 1), (x ^ 1, 1, 1)]
    order += [(0, y, 0), (1, y, 0), (x, 0, 1), (x, 1, 1)]

    class Flow:
        def __init__(self, f, pp):
            self.f, self.base = f, 14 * f
            self.rows = lambda yy, h: pl.ds(
                pl.multiple_of((pp * 2 + yy) * rows + h * half, half), half
            )
            self.core = [
                send(
                    p_ref.at[self.rows(yy, h), column(2 * xx + (c ^ 1))],
                    rc.at[f, xx, place(yy, h)],
                    self.base + number,
                    to_c,
                )
                for number, (xx, yy, h) in enumerate(order)
            ]

        def settle(self, *numbers):
            for number in numbers:
                self.core[number].wait_recv()
                xx, yy, h = order[number]
                s1[self.f, xx, place(yy, h), :] = (
                    p_ref[self.rows(yy, h), column(2 * xx + c)].astype(f32)
                    + rc[self.f, xx, place(yy, h), :].astype(f32)
                ).astype(s1.dtype)

        def first(self, i):
            f = self.f
            ya = send(s1.at[f, i, place(y ^ 1, 0), :], ry.at[f, i], self.base + 8 + i, to_y)
            part = s1.at[f, x ^ 1, pl.ds(i * rows + half, half), :]
            xa = send(part, rx.at[f, i], self.base + 10 + i, to_x)
            return ya, xa

        def second(self, copies):
            f = self.f
            for ya, _ in copies:
                ya.wait_recv()
            s2[f, 0] = (
                s1[f, x ^ 1, place(y, 0), :].astype(f32) + ry[f, x ^ 1].astype(f32)
            ).astype(s2.dtype)
            xb = send(s2.at[f, 0], fx.at[f], self.base + 12, to_x)
            for _, xa in copies:
                xa.wait_recv()
            s2[f, 1] = (
                s1[f, x, place(y ^ 1, 1), :].astype(f32) + rx[f, y ^ 1].astype(f32)
            ).astype(s2.dtype)
            yb = send(s2.at[f, 1], fy.at[f], self.base + 13, to_y)
            return xb, yb

        def last(self, copies):
            f = self.f
            xb, yb = copies
            keep = s1[f, x, place(y, 0), :].astype(f32) + ry[f, x].astype(f32)
            xb.wait_recv()
            low = keep + fx[f].astype(f32)
            keep = s1[f, x, place(y, 1), :].astype(f32) + rx[f, y].astype(f32)
            yb.wait_recv()
            return low, keep + fy[f].astype(f32)

    if pair:
        far = Flow(0, p ^ 1)
        near = Flow(1, p)
        far.settle(0, 1, 2, 3)
        far_first = [far.first(0), far.first(1)]
        far.settle(4, 5, 6, 7)
        near.settle(0, 1, 2, 3)
        near_first = [near.first(0)]
        near.settle(4, 5, 6, 7)
        far_second = far.second(far_first)
        near_first.append(near.first(1))
        low, high = far.last(far_second)
        sz[pl.ds(0, half), :] = low.astype(bf16)
        z0 = send(sz.at[pl.ds(0, half)], fz.at[pl.ds(0, half)], 28, to_z)
        sz[pl.ds(half, half), :] = high.astype(bf16)
        z1 = send(sz.at[pl.ds(half, half)], fz.at[pl.ds(half, half)], 29, to_z)
        low, high = near.last(near.second(near_first))
        z0.wait_recv()
        out_ref[pl.ds(0, half), :] = low + fz[pl.ds(0, half), :].astype(f32)
        z1.wait_recv()
        out_ref[pl.ds(half, half), :] = high + fz[pl.ds(half, half), :].astype(f32)
    else:
        near = Flow(0, 0)
        near.settle(0, 1, 2, 3)
        near_first = [near.first(0), near.first(1)]
        near.settle(4, 5, 6, 7)
        low, high = near.last(near.second(near_first))
        out_ref[pl.ds(0, half), :] = low
        out_ref[pl.ds(half, half), :] = high
    if rider:
        cargo.wait_recv()
    for copy in started:
        copy.wait_send()


def scatter_wide(partial, pair, number, name, cargo=None):
    flows = 2 if pair else 1
    rows, width = partial.shape[0] // (2 * flows), partial.shape[1] // 4
    half = rows // 2
    rider = cargo is not None
    copies = 31 if pair else 14
    out_shape, out_spec = [jax.ShapeDtypeStruct((rows, width), f32)], [pl.BlockSpec(memory_space=pltpu.VMEM)]
    anywhere = [pl.BlockSpec(memory_space=pl.ANY)] * rider
    if rider:
        out_shape.append(jax.ShapeDtypeStruct((cargo.shape[0], cargo.shape[1] // 2), cargo.dtype))
    last = (rows, width) if pair else (16, 128)
    out = pl.pallas_call(
        functools.partial(scatter_kernel, pair, rider),
        name=name,
        out_shape=out_shape,
        in_specs=[pl.BlockSpec(memory_space=pltpu.VMEM)] + anywhere,
        out_specs=out_spec + anywhere,
        scratch_shapes=[
            pltpu.VMEM((flows, 2, 2 * rows, width), bf16),
            pltpu.VMEM((flows, 2, 2 * rows, width), bf16),
            pltpu.VMEM((flows, 2, half, width), bf16),
            pltpu.VMEM((flows, 2, half, width), bf16),
            pltpu.VMEM((flows, 2, half, width), bf16),
            pltpu.VMEM((flows, half, width), bf16),
            pltpu.VMEM((flows, half, width), bf16),
            pltpu.VMEM(last, bf16),
            pltpu.VMEM(last, bf16),
            pltpu.SemaphoreType.DMA((copies,)),
            pltpu.SemaphoreType.DMA((copies,)),
        ],
        compiler_params=pltpu.CompilerParams(
            collective_id=number, has_side_effects=True, vmem_limit_bytes=48 * 2**20
        ),
        cost_estimate=COST,
    )(partial, *([cargo] * rider))
    return out if rider else out[0]


def feature_peers(wide):
    peers = []
    for d in range(1, 8 if wide else 4):
        peer = {"col": flip("col", d & 3)}
        if d >> 2:
            peer["dp"] = flip("dp", 1)
        peers.append(peer)
    return peers


def total_kernel(v_ref, out_ref, slots, send_sem, recv_sem):
    me = lax.axis_index("col")
    peers = feature_peers(False)
    greet(peers)
    started = []
    send = sender(send_sem, recv_sem, started)
    for d, peer in enumerate(peers):
        send(v_ref, slots.at[me], d, peer)
    slots[me] = v_ref[...]
    for copy in started:
        copy.wait_recv()
    total = slots[0]
    for i in range(1, 4):
        total = total + slots[i]
    out_ref[...] = total
    for copy in started:
        copy.wait_send()


def feature_total(values, number, name):
    k, t = values.shape
    flat = values.reshape(k * t // 128, 128)
    total = pl.pallas_call(
        total_kernel,
        name=name,
        out_shape=jax.ShapeDtypeStruct(flat.shape, f32),
        in_specs=[pl.BlockSpec(memory_space=pltpu.VMEM)],
        out_specs=pl.BlockSpec(memory_space=pltpu.VMEM),
        scratch_shapes=[
            pltpu.VMEM((4,) + flat.shape, f32),
            pltpu.SemaphoreType.DMA((3,)),
            pltpu.SemaphoreType.DMA((3,)),
        ],
        compiler_params=pltpu.CompilerParams(collective_id=number, has_side_effects=True),
    )(flat)
    return total.reshape(k, t)


def gain_peers():
    peers = []
    for d in range(1, 8):
        peers.append({"row": flip("row", d & 3), "dp": flip("dp", d >> 2)})
    return peers


def gain_kernel(v_ref, out_ref, slots, send_sem, recv_sem):
    me = side("dp") * 4 + lax.axis_index("row")
    peers = gain_peers()
    greet(peers)
    started = []
    send = sender(send_sem, recv_sem, started)
    for d, peer in enumerate(peers):
        send(v_ref, slots.at[me], d, peer)
    slots[me] = v_ref[...]
    for copy in started:
        copy.wait_recv()
    total = slots[0]
    for i in range(1, 8):
        total = total + slots[i]
    out_ref[...] = total
    for copy in started:
        copy.wait_send()


def gain_total(values, number):
    flat = values.reshape(-1, 128)
    total = pl.pallas_call(
        gain_kernel,
        name="total_gains",
        out_shape=jax.ShapeDtypeStruct(flat.shape, f32),
        in_specs=[pl.BlockSpec(memory_space=pltpu.VMEM)],
        out_specs=pl.BlockSpec(memory_space=pltpu.VMEM),
        scratch_shapes=[
            pltpu.VMEM((8,) + flat.shape, f32),
            pltpu.SemaphoreType.DMA((7,)),
            pltpu.SemaphoreType.DMA((7,)),
        ],
        compiler_params=pltpu.CompilerParams(collective_id=number, has_side_effects=True),
    )(flat)
    return total.reshape(values.shape)


def row_peers():
    return [(d, {"row": flip("row", d)}) for d in (3, 2, 1)]


def unit_view(ref, unit, tok, heads):
    rows = pl.ds(pl.multiple_of((unit // heads) * tok, tok), tok)
    cols = pl.ds(pl.multiple_of((unit % heads) * HEAD_DIM, HEAD_DIM), HEAD_DIM)
    return ref.at[rows, cols]


def turn_kernel(back, tok, heads, x_ref, out_ref, local_sem, send_sem, recv_sem):
    z = lax.axis_index("row")
    greet([peer for _, peer in row_peers()])
    started = []
    send = sender(send_sem, recv_sem, started)

    def line(ref, i):
        return ref.at[pl.ds(pl.multiple_of(i * tok, tok), tok)]

    def ends(i):
        if back:
            return line(x_ref, i), unit_view(out_ref, z, tok, heads)
        return unit_view(x_ref, i, tok, heads), line(out_ref, z)

    for d, peer in row_peers():
        send(*ends(z ^ d), d - 1, peer)
    own = pltpu.make_async_copy(*ends(z), local_sem)
    own.start()
    for copy in started:
        copy.wait()
    own.wait()


def turn(values, back, tok, heads, number, name):
    shape = (2 * tok, heads * HEAD_DIM) if back else (2 * heads * tok, HEAD_DIM)
    return pl.pallas_call(
        functools.partial(turn_kernel, back, tok, heads),
        name=name,
        out_shape=jax.ShapeDtypeStruct(shape, values.dtype),
        in_specs=[pl.BlockSpec(memory_space=pltpu.VMEM)],
        out_specs=pl.BlockSpec(memory_space=pl.ANY),
        scratch_shapes=[
            pltpu.SemaphoreType.DMA,
            pltpu.SemaphoreType.DMA((3,)),
            pltpu.SemaphoreType.DMA((3,)),
        ],
        compiler_params=pltpu.CompilerParams(collective_id=number, has_side_effects=True),
        cost_estimate=COST,
    )(values)


def totals(stat, slots, started):
    for copy in started:
        copy.wait_recv()
    total = slots[0]
    for i in range(1, 8):
        total = total + slots[i]
    return total


def front_kernel(
    width,
    qkv_ref,
    cos_ref,
    sin_ref,
    gain_ref,
    out_ref,
    inv_ref,
    turned,
    packed,
    stat,
    slots,
    local_sem,
    stat_send,
    stat_recv,
    send_sem,
    recv_sem,
):
    count, tok = qkv_ref.shape[0], cos_ref.shape[0]
    part = qkv_ref.shape[1] // 3
    heads = part // HEAD_DIM
    z = lax.axis_index("row")
    me = side("dp") * 4 + lax.axis_index("col")
    peers = feature_peers(True)
    greet(peers + [peer for _, peer in row_peers()])
    for i in range(2):
        values = qkv_ref[:, i * part : (i + 1) * part]
        stat[i : i + 1, :] = jnp.sum(values * values, axis=1, keepdims=True).T
    started, moved, local = [], [], []
    send = sender(stat_send, stat_recv, started)
    for d, peer in enumerate(peers):
        send(stat, slots.at[me], d, peer)
    slots[me] = stat[...]
    move = sender(send_sem, recv_sem, moved)

    def ship(i):
        for d, peer in row_peers():
            move(packed.at[z ^ d, i], out_ref.at[z, i], 3 * i + d - 1, peer)
        copy = pltpu.make_async_copy(packed.at[z, i], out_ref.at[z, i], local_sem.at[i])
        copy.start()
        local.append(copy)

    def spots():
        return [(s, h, s * heads + h) for s in range(2) for h in range(heads)]

    for s, h, unit in spots():
        packed[unit, 2] = qkv_ref[
            s * tok : (s + 1) * tok, 2 * part + h * HEAD_DIM : 2 * part + (h + 1) * HEAD_DIM
        ].astype(bf16)
    ship(2)
    for i in (1, 0):
        for s, h, unit in spots():
            values = (
                qkv_ref[s * tok : (s + 1) * tok, i * part + h * HEAD_DIM : i * part + (h + 1) * HEAD_DIM]
                * gain_ref[i : i + 1, h * HEAD_DIM : (h + 1) * HEAD_DIM]
            )
            turned[i, unit] = values * cos_ref[...] + pltpu.roll(values, HEAD_DIM // 2, 1) * sin_ref[...]
    inverse = lax.rsqrt(totals(stat, slots, started) / width + norm_eps)
    inv_ref[...] = inverse
    for i in (1, 0):
        column = inverse[i : i + 1, :].T
        for s, h, unit in spots():
            packed[unit, i] = (turned[i, unit] * column[s * tok : (s + 1) * tok]).astype(bf16)
        ship(i)
    for copy in moved:
        copy.wait()
    for copy in local:
        copy.wait()
    for copy in started:
        copy.wait_send()


def front(qkv, cosine, sine_signed, gains, width, units, number):
    count, tok = qkv.shape[0], cosine.shape[0]
    return pl.pallas_call(
        functools.partial(front_kernel, width),
        name="front",
        out_shape=(
            jax.ShapeDtypeStruct((units, 3, tok, HEAD_DIM), bf16),
            jax.ShapeDtypeStruct((2, count), f32),
        ),
        in_specs=[pl.BlockSpec(memory_space=pltpu.VMEM)] * 4,
        out_specs=(pl.BlockSpec(memory_space=pl.ANY), pl.BlockSpec(memory_space=pltpu.VMEM)),
        scratch_shapes=[
            pltpu.VMEM((2, units, tok, HEAD_DIM), f32),
            pltpu.VMEM((units, 3, tok, HEAD_DIM), bf16),
            pltpu.VMEM((2, count), f32),
            pltpu.VMEM((8, 2, count), f32),
            pltpu.SemaphoreType.DMA((3,)),
            pltpu.SemaphoreType.DMA((7,)),
            pltpu.SemaphoreType.DMA((7,)),
            pltpu.SemaphoreType.DMA((9,)),
            pltpu.SemaphoreType.DMA((9,)),
        ],
        compiler_params=pltpu.CompilerParams(
            collective_id=number, has_side_effects=True, vmem_limit_bytes=40 * 2**20
        ),
        cost_estimate=COST,
    )(qkv, cosine, sine_signed, gains)


def rear_kernel(
    width,
    d_ref,
    qkv_ref,
    cos_ref,
    sin_ref,
    gain_ref,
    inv_ref,
    out_ref,
    sums_ref,
    landed,
    normed,
    stat,
    slots,
    stat_send,
    stat_recv,
    send_sem,
    recv_sem,
):
    count, tok = qkv_ref.shape[0], cos_ref.shape[0]
    part = qkv_ref.shape[1] // 3
    heads = part // HEAD_DIM
    z = lax.axis_index("row")
    me = side("dp") * 4 + lax.axis_index("col")
    peers = feature_peers(True)
    greet(peers + [peer for _, peer in row_peers()])
    started, moved = [], []
    move = sender(send_sem, recv_sem, moved)
    for i in (0, 1, 2):
        for d, peer in row_peers():
            there = pl.ds(pl.multiple_of((z ^ d) * tok, tok), tok)
            move(d_ref.at[i, there], landed.at[z, i], 3 * i + d - 1, peer)
    here = pl.ds(pl.multiple_of(z * tok, tok), tok)
    for i in (0, 1, 2):
        landed[z, i] = d_ref[i, here, :]
    spots = [(s, h, s * heads + h) for s in range(2) for h in range(heads)]
    for i in (0, 1):
        for copy in moved[3 * i : 3 * i + 3]:
            copy.wait_recv()
        for h in range(heads):
            cols = slice(i * part + h * HEAD_DIM, i * part + (h + 1) * HEAD_DIM)
            gain = gain_ref[i : i + 1, h * HEAD_DIM : (h + 1) * HEAD_DIM]
            raw = jnp.zeros((1, HEAD_DIM), f32)
            for s in range(2):
                rows = slice(s * tok, (s + 1) * tok)
                values = landed[s * heads + h, i].astype(f32)
                back = values * cos_ref[...] - pltpu.roll(values, HEAD_DIM // 2, 1) * sin_ref[...]
                pre = qkv_ref[rows, cols]
                inverse = inv_ref[i : i + 1, rows].T
                crossed = back * pre
                raw = raw + jnp.sum(crossed * inverse, axis=0, keepdims=True)
                partial = jnp.sum(crossed * gain, axis=1, keepdims=True).T
                if h == 0:
                    stat[i : i + 1, rows] = partial
                else:
                    stat[i : i + 1, rows] = stat[i : i + 1, rows] + partial
                normed[rows, cols] = back * gain
            sums_ref[i : i + 1, h * HEAD_DIM : (h + 1) * HEAD_DIM] = raw
    send = sender(stat_send, stat_recv, started)
    for d, peer in enumerate(peers):
        send(stat, slots.at[me], d, peer)
    slots[me] = stat[...]
    for copy in moved[6:]:
        copy.wait_recv()
    for s, h, unit in spots:
        cols = slice(2 * part + h * HEAD_DIM, 2 * part + (h + 1) * HEAD_DIM)
        out_ref[s * tok : (s + 1) * tok, cols] = landed[unit, 2]
    inner = totals(stat, slots, started) / width
    for i in (0, 1):
        inverse = inv_ref[i : i + 1, :]
        first = inverse.T
        second = (inverse * inverse * inverse * inner[i : i + 1, :]).T
        cols = slice(i * part, (i + 1) * part)
        out_ref[:, cols] = (first * normed[:, cols] - qkv_ref[:, cols] * second).astype(bf16)
    for copy in moved + started:
        copy.wait_send()


def rear(d_units, qkv, cosine, sine_signed, gains, inverse, width, number):
    count, tok = qkv.shape[0], cosine.shape[0]
    part = qkv.shape[1] // 3
    units = d_units.shape[1] // tok
    return pl.pallas_call(
        functools.partial(rear_kernel, width),
        name="rear",
        out_shape=(
            jax.ShapeDtypeStruct((count, 3 * part), bf16),
            jax.ShapeDtypeStruct((2, part), f32),
        ),
        in_specs=[pl.BlockSpec(memory_space=pltpu.VMEM)] * 6,
        out_specs=[pl.BlockSpec(memory_space=pltpu.VMEM)] * 2,
        scratch_shapes=[
            pltpu.VMEM((units, 3, tok, HEAD_DIM), bf16),
            pltpu.VMEM((count, 2 * part), f32),
            pltpu.VMEM((2, count), f32),
            pltpu.VMEM((8, 2, count), f32),
            pltpu.SemaphoreType.DMA((7,)),
            pltpu.SemaphoreType.DMA((7,)),
            pltpu.SemaphoreType.DMA((9,)),
            pltpu.SemaphoreType.DMA((9,)),
        ],
        compiler_params=pltpu.CompilerParams(
            collective_id=number, has_side_effects=True, vmem_limit_bytes=40 * 2**20
        ),
        cost_estimate=COST,
    )(d_units, qkv, cosine, sine_signed, gains, inverse)


BLOCK = 512


def attend_kernel(len_ref, q_ref, k_ref, v_ref, o_ref, o32_ref, lse_ref):
    i = pl.program_id(0)
    bq, bk = q_ref.shape[0], BLOCK
    length = len_ref[0]
    scale = HEAD_DIM ** (-0.5)
    q = q_ref[...]
    rows = i * bq + lax.broadcasted_iota(jnp.int32, (bq, bk), 0)
    cols0 = lax.broadcasted_iota(jnp.int32, (bq, bk), 1)

    def step(j, carry, masked):
        top, total, acc = carry
        j0 = pl.multiple_of(j * bk, bk)
        scores = contract_last(q, k_ref[pl.ds(j0, bk), :]) * scale
        if masked:
            cols = j0 + cols0
            scores = jnp.where((cols <= rows) & (cols < length), scores, masked_score)
        new = jnp.maximum(top, jnp.max(scores, axis=1, keepdims=True))
        weights = jnp.exp(scores - new)
        fix = jnp.exp(top - new)
        total = total * fix + jnp.sum(weights, axis=1, keepdims=True)
        acc = acc * fix + matmul(weights.astype(bf16), v_ref[pl.ds(j0, bk), :])
        return new, total, acc

    carry = (
        jnp.full((bq, 1), -jnp.inf, f32),
        jnp.zeros((bq, 1), f32),
        jnp.zeros((bq, HEAD_DIM), f32),
    )
    whole = jnp.minimum(i, length // bk)
    last = jnp.minimum(i + 1, (length + bk - 1) // bk)
    carry = lax.fori_loop(0, whole, lambda j, s: step(j, s, False), carry)
    top, total, acc = lax.fori_loop(whole, last, lambda j, s: step(j, s, True), carry)
    out = acc / total
    o_ref[...] = out.astype(bf16)
    o32_ref[...] = out
    lse_ref[...] = jnp.broadcast_to((top + jnp.log(total)).T, lse_ref.shape)


def attend(length, q, k, v):
    slots = q.shape[0]
    whole = pl.BlockSpec((slots, HEAD_DIM), lambda i: (0, 0))
    part = pl.BlockSpec((BLOCK, HEAD_DIM), lambda i: (i, 0))
    return pl.pallas_call(
        attend_kernel,
        name="attend",
        grid=(slots // BLOCK,),
        out_shape=(
            jax.ShapeDtypeStruct((slots, HEAD_DIM), bf16),
            jax.ShapeDtypeStruct((slots, HEAD_DIM), f32),
            jax.ShapeDtypeStruct((8, slots), f32),
        ),
        in_specs=[pl.BlockSpec(memory_space=pltpu.SMEM), part, whole, whole],
        out_specs=(part, part, pl.BlockSpec((8, BLOCK), lambda i: (0, i))),
        cost_estimate=COST,
    )(length, q, k, v)


def attend_back_kernel(
    len_ref, q_ref, k_ref, v_ref, do_ref, o_ref, lse_ref, out_ref, dq_acc, delta_ref
):
    j = pl.program_id(0)
    bk, bq = k_ref.shape[0], BLOCK
    slots = q_ref.shape[0]
    length = len_ref[0]
    scale = HEAD_DIM ** (-0.5)

    @pl.when(j == 0)
    def _():
        dq_acc[...] = jnp.zeros_like(dq_acc)
        for i in range(slots // bq):
            here = slice(i * bq, (i + 1) * bq)
            product = do_ref[here, :].astype(f32) * o_ref[here, :]
            delta_ref[0:1, here] = jnp.sum(product, axis=1, keepdims=True).T

    k, v = k_ref[...], v_ref[...]
    j0 = j * bk
    cols = j0 + lax.broadcasted_iota(jnp.int32, (bk, bq), 0)
    rows0 = lax.broadcasted_iota(jnp.int32, (bk, bq), 1)

    def step(i, carry, masked):
        dk, dv = carry
        i0 = pl.multiple_of(i * bq, bq)
        here = pl.ds(i0, bq)
        q, do = q_ref[here, :], do_ref[here, :]
        scores = contract_last(k, q) * scale
        if masked:
            scores = jnp.where((cols <= i0 + rows0) & (cols < length), scores, masked_score)
        probs = jnp.exp(scores - lse_ref[0:1, here])
        dv = dv + matmul(probs.astype(bf16), do)
        d_probs = contract_last(v, do)
        d_scores = (probs * (d_probs - delta_ref[0:1, here])).astype(bf16)
        dk = dk + matmul(d_scores, q)
        dq_acc[here, :] += contract_first(d_scores, k)
        return dk, dv

    zero = jnp.zeros((bk, HEAD_DIM), f32)
    top = slots // bq
    first = jnp.where(j0 + bk <= length, j + 1, top)
    first = jnp.where(j0 < length, first, j)
    stop = jnp.where(j0 < length, top, j)
    carry = lax.fori_loop(j, first, lambda i, s: step(i, s, True), (zero, zero))
    dk, dv = lax.fori_loop(first, stop, lambda i, s: step(i, s, False), carry)
    there = pl.ds(pl.multiple_of(j0, bk), bk)
    out_ref[1, there, :] = (dk * scale).astype(bf16)
    out_ref[2, there, :] = dv.astype(bf16)

    @pl.when(j == pl.num_programs(0) - 1)
    def _():
        out_ref[0] = (dq_acc[...] * scale).astype(bf16)


def attend_back(length, q, k, v, do, o, lse):
    slots = q.shape[0]
    whole = pl.BlockSpec((slots, HEAD_DIM), lambda j: (0, 0))
    part = pl.BlockSpec((BLOCK, HEAD_DIM), lambda j: (j, 0))
    line = pl.BlockSpec((8, slots), lambda j: (0, 0))
    return pl.pallas_call(
        attend_back_kernel,
        name="attend_back",
        grid=(slots // BLOCK,),
        out_shape=jax.ShapeDtypeStruct((3, slots, HEAD_DIM), bf16),
        in_specs=[pl.BlockSpec(memory_space=pltpu.SMEM), whole, part, part, whole, whole, line],
        out_specs=pl.BlockSpec((3, slots, HEAD_DIM), lambda j: (0, 0, 0)),
        scratch_shapes=[pltpu.VMEM((slots, HEAD_DIM), f32), pltpu.VMEM((8, slots), f32)],
        cost_estimate=COST,
    )(length, q, k, v, do, o, lse)


def per_device(
    tokens,
    seq_lengths,
    w_query,
    w_key,
    w_value,
    w_out,
    w_gate,
    w_up,
    w_down,
    q_gain,
    k_gain,
    attn_gain,
    mlp_gain,
    cotangent,
):
    tok_rows, feat_part = tokens.shape
    row_count, data_count = lax.axis_size("row"), lax.axis_size("dp")
    width = feat_part * lax.axis_size("col")
    slots = tok_rows * row_count
    half_feat = feat_part // 2
    y, z = side("dp"), lax.axis_index("row")
    heads = half_feat // HEAD_DIM
    pairs = [(i, i ^ 1) for i in range(data_count)]
    after = lambda values, *done: lax.optimization_barrier((values,) + done)[0]

    def y_half(values, axis):
        size = values.shape[axis] // 2
        return lax.dynamic_slice_in_dim(values, y * size, size, axis)

    qkv_weight = lax.all_gather(
        jnp.concatenate([y_half(w_query, 1), y_half(w_key, 1), y_half(w_value, 1)], axis=1),
        "row",
        axis=0,
        tiled=True,
    )
    out_weight = lax.all_gather(y_half(w_out, 0), "row", axis=1, tiled=True)
    gate_up_weight = lax.all_gather(
        jnp.concatenate([y_half(w_gate, 1), y_half(w_up, 1)], axis=1), "row", axis=0, tiled=True
    )
    hidden_part = gate_up_weight.shape[1] // 2
    gate_weight, up_weight = gate_up_weight[:, :hidden_part], gate_up_weight[:, hidden_part:]
    down_half = y_half(w_down, 0)
    split = down_half.shape[1] // 2
    low_weight = lax.all_gather(down_half[:, :split], "row", axis=1, tiled=True)
    high_weight = lax.all_gather(down_half[:, split:], "row", axis=1, tiled=True)

    positions = z * tok_rows + jnp.arange(tok_rows)
    length = seq_lengths[0]
    valid = (positions < length).astype(f32)[:, None]
    cosine, sine = rope_tables(positions, HEAD_DIM)
    sine_signed = jnp.where(jnp.arange(HEAD_DIM)[None, :] < HEAD_DIM // 2, -sine, sine)
    other_length = lax.ppermute(seq_lengths, "dp", pairs)
    pair_lengths = jnp.where(
        y == 0,
        jnp.concatenate([seq_lengths, other_length]),
        jnp.concatenate([other_length, seq_lengths]),
    )
    unit_length = lax.dynamic_slice_in_dim(pair_lengths, z // heads, 1)
    qk_gain = jnp.stack([y_half(q_gain, 0), y_half(k_gain, 0)])

    tokens_wide = gather_wide(tokens, False, 0, "gather_tokens")
    qkv = matmul(tokens_wide, qkv_weight)
    units, inverse = front(qkv, cosine, sine_signed, qk_gain, width, 2 * heads, 2)
    q_unit, k_unit, v_unit = (units[:, i].reshape(slots, HEAD_DIM) for i in range(3))
    attn_unit, attn_exact, log_total = attend(unit_length, q_unit, k_unit, v_unit)
    attn_low = turn(attn_unit, True, tok_rows, heads, 3, "turn_attn")
    branch = scatter_wide(matmul(attn_low, out_weight).astype(bf16), False, 4, "scatter_branch")
    branch_inv = lax.rsqrt(
        feature_total(jnp.sum(branch * branch, axis=1)[None, :], 5, "total_branch")[0] / width
        + norm_eps
    )[:, None]
    resid = tokens.astype(f32) + branch * branch_inv * attn_gain
    resid_wide = gather_wide(resid.astype(bf16), False, 6, "gather_resid")
    gate = matmul(resid_wide, gate_weight)
    upper = matmul(resid_wide, up_weight)
    sigma = jax.nn.sigmoid(gate)
    hidden = (gate * sigma * upper).astype(bf16)
    mixed_low = scatter_wide(matmul(hidden, low_weight).astype(bf16), False, 7, "scatter_mixed_low")
    high_weight = after(high_weight, mixed_low)
    mixed_high = scatter_wide(matmul(hidden, high_weight).astype(bf16), False, 17, "scatter_mixed_high")
    mixed = jnp.concatenate([mixed_low, mixed_high], axis=1)
    incoming = cotangent.astype(f32) * valid
    gained = incoming * mlp_gain
    sums = feature_total(
        jnp.stack([jnp.sum(mixed * mixed, axis=1), jnp.sum(gained * mixed, axis=1)]),
        8,
        "total_mixed",
    )
    mixed_inv = lax.rsqrt(sums[0] / width + norm_eps)[:, None]
    inner = (sums[1] / width)[:, None]
    block_output = ((resid + mixed * mixed_inv * mlp_gain) * valid).astype(bf16)
    mlp_gain_raw = jnp.sum(incoming * mixed * mixed_inv, axis=0)
    d_mixed = (mixed_inv * gained - mixed * mixed_inv**3 * inner).astype(bf16)
    factor = 1.0 / math.sqrt(slots * data_count)
    d_low_wide = gather_wide(d_mixed[:, :split], False, 9, "gather_d_mixed_low")
    low_raw = (contract_first(hidden, d_low_wide) * factor).astype(bf16)
    d_high = after(d_mixed[:, split:], low_raw)
    d_high_wide = gather_wide(d_high, False, 18, "gather_d_mixed_high")
    high_raw = (contract_first(hidden, d_high_wide) * factor).astype(bf16)

    def cut(values, index, count, axis):
        size = values.shape[axis] // count
        return lax.dynamic_slice_in_dim(values, index * size, size, axis)

    def over_dp(piece):
        if data_count > 2:
            groups = [list(range(s, data_count, 2)) for s in (0, 1)]
            piece = lax.psum(piece, "dp", axis_index_groups=groups)
        return piece

    def two_sides(piece, other, bit, axis):
        low = jnp.where(bit == 0, piece, other)
        high = jnp.where(bit == 0, other, piece)
        return jnp.concatenate([low, high], axis=axis)

    def from_twin(piece):
        return lax.ppermute(piece, "dp", pairs)

    def reduce_rows(raw, axis):
        return lax.psum_scatter(raw, "row", scatter_dimension=axis, tiled=True)

    d_hidden = contract_last(d_low_wide, low_weight) + contract_last(d_high_wide, high_weight)
    d_gate = (d_hidden * upper * sigma * (1.0 + gate * (1.0 - sigma))).astype(bf16)
    d_upper = (d_hidden * gate * sigma).astype(bf16)
    gate_raw = (contract_first(resid_wide, d_gate) * factor).astype(bf16)
    up_raw = (contract_first(resid_wide, d_upper) * factor).astype(bf16)
    d_resid_wide = (
        contract_last(d_gate, gate_weight) + contract_last(d_upper, up_weight)
    ).astype(bf16)
    d_resid_wide, low_piece = lax.optimization_barrier(
        (after(d_resid_wide, high_raw, gate_raw, up_raw), reduce_rows(low_raw, 1))
    )
    down_piece = jnp.concatenate([low_piece, reduce_rows(high_raw, 1)], axis=1)
    gate_piece, up_piece = reduce_rows(gate_raw, 0), reduce_rows(up_raw, 0)
    d_resid = scatter_wide(d_resid_wide, False, 10, "scatter_d_resid")
    d_resid = incoming + d_resid
    attn_gain_raw = jnp.sum(d_resid * branch * branch_inv, axis=0)
    gained = d_resid * attn_gain
    inner = (
        feature_total(jnp.sum(gained * branch, axis=1)[None, :], 11, "total_d_resid")[0][:, None]
        / width
    )
    d_branch = (branch_inv * gained - branch * branch_inv**3 * inner).astype(bf16)
    down_piece = over_dp(down_piece)
    d_branch_wide, down_piece = lax.optimization_barrier(
        (gather_wide(d_branch, False, 12, "gather_d_branch"), down_piece)
    )
    d_attn = contract_last(d_branch_wide, out_weight).astype(bf16)
    other_down = from_twin(down_piece)
    d_attn_unit, other_down = lax.optimization_barrier(
        (turn(d_attn, False, tok_rows, heads, 13, "turn_d_attn"), other_down)
    )
    out_raw = (contract_first(attn_low, after(d_branch_wide, d_attn_unit)) * factor).astype(bf16)
    d_attn_unit = after(d_attn_unit, out_raw)
    out_piece = reduce_rows(out_raw, 1)
    d_units = attend_back(unit_length, q_unit, k_unit, v_unit, d_attn_unit, attn_exact, log_total)
    d_units, gate_piece = lax.optimization_barrier((d_units, over_dp(gate_piece)))
    other_gate = from_twin(gate_piece)
    d_qkv, gain_sums = rear(d_units, qkv, cosine, sine_signed, qk_gain, inverse, width, 14)
    d_qkv, gain_sums, other_gate, up_piece = lax.optimization_barrier(
        (d_qkv, gain_sums, other_gate, over_dp(up_piece))
    )
    other_up = from_twin(up_piece)
    qkv_raw = (contract_first(tokens_wide, d_qkv) * factor).astype(bf16)
    projected = contract_last(after(d_qkv, qkv_raw), qkv_weight).astype(bf16)
    qkv_piece = over_dp(reduce_rows(qkv_raw, 0))
    scattered, other_down, other_gate, other_up, out_piece, gain_sums = lax.optimization_barrier(
        (
            scatter_wide(projected, False, 16, "scatter_projected"),
            other_down,
            other_gate,
            other_up,
            over_dp(out_piece),
            gain_sums,
        )
    )
    other_out = from_twin(out_piece)
    input_grad = d_resid + scattered

    def spread(half):
        return lax.dynamic_update_slice_in_dim(jnp.zeros((feat_part,), f32), half, y * half_feat, 0)

    gains = over_dp(
        gain_total(
            jnp.stack([spread(gain_sums[0]), spread(gain_sums[1]), attn_gain_raw, mlp_gain_raw])
            * factor,
            15,
        )
    )

    gains, qkv_piece = lax.optimization_barrier((gains, qkv_piece))

    def whole(piece, other, axis):
        return two_sides(piece, other, y, axis).astype(f32)

    qkv_other = from_twin(qkv_piece)
    q_grad, k_grad, v_grad = (
        two_sides(cut(qkv_piece, i, 3, 1), cut(qkv_other, i, 3, 1), y, 1).astype(f32)
        for i in range(3)
    )
    return (
        block_output,
        input_grad,
        q_grad,
        k_grad,
        v_grad,
        whole(out_piece, other_out, 0),
        whole(gate_piece, other_gate, 1),
        whole(up_piece, other_up, 1),
        whole(down_piece, other_down, 0),
        gains[0],
        gains[1],
        gains[2],
        gains[3],
    )


def solution(mesh):
    tok, row_col, col_row, gain = P(("dp", "row"), "col"), P("row", "col"), P("col", "row"), P("col")
    weights = (row_col, row_col, row_col, col_row, row_col, row_col, col_row)
    gains = (gain, gain, gain, gain)
    return jax.shard_map(
        per_device,
        mesh=mesh,
        in_specs=(tok, P("dp")) + weights + gains + (tok,),
        out_specs=(tok, tok) + weights + gains,
        check_vma=False,
    )
```

```python
import functools
import math

import jax
import jax.numpy as jnp
from jax import lax
from jax.experimental import pallas as pl
from jax.experimental.pallas import tpu as pltpu
from jax.sharding import PartitionSpec as P

HEAD_DIM = 128
rope_base = 500000.0
norm_eps = 1e-06
masked_score = -1e30

MESH = pl.DeviceIdType.MESH
bf16 = jnp.bfloat16
f32 = jnp.float32
COST = pl.CostEstimate(flops=0, bytes_accessed=1000, transcendentals=0)


def rope_tables(positions, head_dim):
    half = head_dim // 2
    freq = 1.0 / rope_base ** (jnp.arange(half, dtype=f32) / half)
    angle = positions.astype(f32)[:, None] * freq[None, :]
    angle = jnp.concatenate([angle, angle], axis=1)
    return (jnp.cos(angle), jnp.sin(angle))


def matmul(left, right):
    return jnp.dot(left, right, preferred_element_type=f32)


def contract_first(left, right):
    return lax.dot_general(left, right, (((0,), (0,)), ((), ())), preferred_element_type=f32)


def contract_last(left, right):
    return lax.dot_general(left, right, (((1,), (1,)), ((), ())), preferred_element_type=f32)


def flip(axis, bit):
    return lax.axis_index(axis) ^ bit


def side(axis):
    return lax.axis_index(axis) & 1


def greet(peers):
    barrier = pltpu.get_barrier_semaphore()
    for peer in peers:
        pl.semaphore_signal(barrier, inc=1, device_id=peer, device_id_type=MESH)
    pl.semaphore_wait(barrier, len(peers))


def sender(send_sem, recv_sem, started):
    def send(src, dst, number, peer):
        copy = pltpu.make_async_remote_copy(
            src_ref=src,
            dst_ref=dst,
            send_sem=send_sem.at[number],
            recv_sem=recv_sem.at[number],
            device_id=peer,
            device_id_type=MESH,
        )
        copy.start()
        started.append(copy)
        return copy

    return send


def neighbours():
    return {"col": flip("col", 2)}, {"dp": flip("dp", 1)}, {"col": flip("col", 1)}


def gather_flow(x_ref, out_ref, local_sem, send, base, meanwhile=None):
    rows, width = x_ref.shape
    half = rows // 2
    y, b = side("dp"), lax.axis_index("col")
    to_x, to_y, to_c = neighbours()

    def slot(yy, h, bb, n=half):
        return out_ref.at[
            pl.ds(pl.multiple_of(yy * rows + h * half, half), n),
            pl.ds(pl.multiple_of(bb * width, width), width),
        ]

    low, high = x_ref.at[pl.ds(0, half)], x_ref.at[pl.ds(half, half)]
    own = pltpu.make_async_copy(x_ref, slot(y, 0, b, rows), local_sem)
    xa = send(low, slot(y, 0, b), base + 0, to_x)
    ya = send(high, slot(y, 1, b), base + 1, to_y)
    core = [send(low, slot(y, 0, b), base + 6, to_c)]
    yb = send(low, slot(y, 0, b), base + 2, to_y)
    xb = send(high, slot(y, 1, b), base + 3, to_x)
    core.append(send(high, slot(y, 1, b), base + 7, to_c))
    own.start()
    if meanwhile is not None:
        meanwhile()
    xa.wait_recv()
    piece = slot(y, 0, b ^ 2)
    yc = send(piece, piece, base + 4, to_y)
    core.append(send(piece, piece, base + 8, to_c))
    ya.wait_recv()
    piece = slot(y ^ 1, 1, b)
    xc = send(piece, piece, base + 5, to_x)
    core.append(send(piece, piece, base + 9, to_c))
    yb.wait_recv()
    piece = slot(y ^ 1, 0, b)
    core.append(send(piece, piece, base + 10, to_c))
    xb.wait_recv()
    piece = slot(y, 1, b ^ 2)
    core.append(send(piece, piece, base + 11, to_c))
    yc.wait_recv()
    piece = slot(y ^ 1, 0, b ^ 2)
    core.append(send(piece, piece, base + 12, to_c))
    xc.wait_recv()
    piece = slot(y ^ 1, 1, b ^ 2)
    core.append(send(piece, piece, base + 13, to_c))
    for copy in core:
        copy.wait_recv()
    own.wait()


def gather_kernel(x_ref, out_ref, local_sem, send_sem, recv_sem):
    greet(neighbours())
    started = []
    gather_flow(x_ref, out_ref, local_sem, sender(send_sem, recv_sem, started), 0)
    for copy in started:
        copy.wait_send()


def gather_wide(values, number, name):
    rows, width = values.shape
    return pl.pallas_call(
        gather_kernel,
        name=name,
        out_shape=jax.ShapeDtypeStruct((2 * rows, 4 * width), values.dtype),
        in_specs=[pl.BlockSpec(memory_space=pltpu.VMEM)],
        out_specs=pl.BlockSpec(memory_space=pl.ANY),
        scratch_shapes=[
            pltpu.SemaphoreType.DMA,
            pltpu.SemaphoreType.DMA((14,)),
            pltpu.SemaphoreType.DMA((14,)),
        ],
        compiler_params=pltpu.CompilerParams(collective_id=number, has_side_effects=True),
        cost_estimate=COST,
    )(values)


def scatter_flow(p_ref, buffers, send):
    rc, s1, ry, rx, s2, fy, fx = buffers
    rows, width = p_ref.shape[0] // 2, p_ref.shape[1] // 4
    half = rows // 2
    y, b = side("dp"), lax.axis_index("col")
    x, c = b >> 1, b & 1
    to_x, to_y, to_c = neighbours()

    def place(yy, h):
        return pl.ds(pl.multiple_of(yy * rows + h * half, half), half)

    def column(bb):
        return pl.ds(pl.multiple_of(bb * width, width), width)

    order = [(0, y ^ 1, 0), (1, y ^ 1, 0), (x ^ 1, 0, 1), (x ^ 1, 1, 1)]
    order += [(0, y, 0), (1, y, 0), (x, 0, 1), (x, 1, 1)]
    core = [
        send(
            p_ref.at[place(yy, h), column(2 * xx + (c ^ 1))],
            rc.at[xx, place(yy, h)],
            number,
            to_c,
        )
        for number, (xx, yy, h) in enumerate(order)
    ]

    def settle(*numbers):
        for number in numbers:
            core[number].wait_recv()
            xx, yy, h = order[number]
            s1[xx, place(yy, h), :] = (
                p_ref[place(yy, h), column(2 * xx + c)].astype(f32)
                + rc[xx, place(yy, h), :].astype(f32)
            ).astype(s1.dtype)

    settle(0, 1, 2, 3)
    ya, xa = [], []
    for i in range(2):
        ya.append(send(s1.at[i, place(y ^ 1, 0), :], ry.at[i], 8 + i, to_y))
        xa.append(send(s1.at[x ^ 1, pl.ds(i * rows + half, half), :], rx.at[i], 10 + i, to_x))
    settle(4, 5, 6, 7)
    for copy in ya:
        copy.wait_recv()
    s2[0] = (s1[x ^ 1, place(y, 0), :].astype(f32) + ry[x ^ 1].astype(f32)).astype(s2.dtype)
    xb = send(s2.at[0], fx, 12, to_x)
    for copy in xa:
        copy.wait_recv()
    s2[1] = (s1[x, place(y ^ 1, 1), :].astype(f32) + rx[y ^ 1].astype(f32)).astype(s2.dtype)
    yb = send(s2.at[1], fy, 13, to_y)
    keep = s1[x, place(y, 0), :].astype(f32) + ry[x].astype(f32)
    xb.wait_recv()
    low = keep + fx[...].astype(f32)
    keep = s1[x, place(y, 1), :].astype(f32) + rx[y].astype(f32)
    yb.wait_recv()
    return low, keep + fy[...].astype(f32)


def scatter_buffers(rows, width):
    half = rows // 2
    return [
        pltpu.VMEM((2, 2 * rows, width), bf16),
        pltpu.VMEM((2, 2 * rows, width), bf16),
        pltpu.VMEM((2, half, width), bf16),
        pltpu.VMEM((2, half, width), bf16),
        pltpu.VMEM((2, half, width), bf16),
        pltpu.VMEM((half, width), bf16),
        pltpu.VMEM((half, width), bf16),
    ]


def scatter_kernel(p_ref, out_ref, *refs):
    buffers, (send_sem, recv_sem) = refs[:7], refs[7:]
    half = out_ref.shape[0] // 2
    greet(neighbours())
    started = []
    low, high = scatter_flow(p_ref, buffers, sender(send_sem, recv_sem, started))
    out_ref[:half, :] = low
    out_ref[half:, :] = high
    for copy in started:
        copy.wait_send()


def scatter_wide(partial, number, name):
    rows, width = partial.shape[0] // 2, partial.shape[1] // 4
    return pl.pallas_call(
        scatter_kernel,
        name=name,
        out_shape=jax.ShapeDtypeStruct((rows, width), f32),
        in_specs=[pl.BlockSpec(memory_space=pltpu.VMEM)],
        out_specs=pl.BlockSpec(memory_space=pltpu.VMEM),
        scratch_shapes=scatter_buffers(rows, width)
        + [pltpu.SemaphoreType.DMA((14,)), pltpu.SemaphoreType.DMA((14,))],
        compiler_params=pltpu.CompilerParams(
            collective_id=number, has_side_effects=True, vmem_limit_bytes=48 * 2**20
        ),
        cost_estimate=COST,
    )(partial)


def exchange(stat, slots, send, base):
    me = lax.axis_index("col")
    copies = [send(stat, slots.at[me], base + d, peer) for d, peer in enumerate(feature_peers(False))]
    slots[me] = stat[...]
    return copies


def column_total(slots, copies):
    for copy in copies:
        copy.wait_recv()
    return (slots[0] + slots[1]) + (slots[2] + slots[3])


def junction_peers():
    to_x, to_y, to_c = neighbours()
    return [to_x, to_y, to_c, {"col": flip("col", 3)}]


def mixed_kernel(
    width,
    p_ref,
    low_ref,
    incoming_ref,
    resid_ref,
    valid_ref,
    gain_ref,
    block_ref,
    raw_ref,
    rest_ref,
    wide_ref,
    mixed,
    x_ref,
    stat,
    slots,
    *refs,
):
    buffers, (local_sem, send_sem, recv_sem) = refs[:7], refs[7:]
    rows, split = low_ref.shape
    half = rows // 2
    greet(junction_peers())
    started = []
    send = sender(send_sem, recv_sem, started)
    mixed[:, :split] = low_ref[...]
    low, high = scatter_flow(p_ref, buffers, send)
    mixed[:half, split:] = low
    mixed[half:, split:] = high
    stat[0:1, :] = jnp.sum(mixed[...] * mixed[...], axis=1, keepdims=True).T
    stat[1:2, :] = jnp.sum(incoming_ref[...] * gain_ref[...] * mixed[...], axis=1, keepdims=True).T
    total = column_total(slots, exchange(stat, slots, send, 14)) / width
    inverse = lax.rsqrt(total[0:1, :] + norm_eps)
    first = inverse.T
    second = (inverse * inverse * inverse * total[1:2, :]).T

    def slope(cols):
        return (
            first * (incoming_ref[:, cols] * gain_ref[:, cols]) - mixed[:, cols] * second
        ).astype(bf16)

    x_ref[...] = slope(slice(0, split))

    def meanwhile():
        rest_ref[...] = slope(slice(split, 2 * split))
        normed = mixed[...] * first
        block_ref[...] = ((resid_ref[...] + normed * gain_ref[...]) * valid_ref[...].T).astype(bf16)
        raw_ref[...] = jnp.sum(incoming_ref[...] * normed, axis=0, keepdims=True)

    gather_flow(x_ref, wide_ref, local_sem, send, 17, meanwhile)
    for copy in started:
        copy.wait_send()


def mixed_junction(partial, mixed_low, incoming, resid, valid, gain, width, number):
    rows, part = incoming.shape
    split = mixed_low.shape[1]
    vmem = pl.BlockSpec(memory_space=pltpu.VMEM)
    return pl.pallas_call(
        functools.partial(mixed_kernel, width),
        name="mixed_junction",
        out_shape=(
            jax.ShapeDtypeStruct((rows, part), bf16),
            jax.ShapeDtypeStruct((1, part), f32),
            jax.ShapeDtypeStruct((rows, part - split), bf16),
            jax.ShapeDtypeStruct((2 * rows, 4 * split), bf16),
        ),
        in_specs=[vmem] * 6,
        out_specs=(vmem, vmem, vmem, pl.BlockSpec(memory_space=pl.ANY)),
        scratch_shapes=[
            pltpu.VMEM((rows, part), f32),
            pltpu.VMEM((rows, split), bf16),
            pltpu.VMEM((2, rows), f32),
            pltpu.VMEM((4, 2, rows), f32),
        ]
        + scatter_buffers(rows, split)
        + [
            pltpu.SemaphoreType.DMA,
            pltpu.SemaphoreType.DMA((31,)),
            pltpu.SemaphoreType.DMA((31,)),
        ],
        compiler_params=pltpu.CompilerParams(
            collective_id=number, has_side_effects=True, vmem_limit_bytes=48 * 2**20
        ),
        cost_estimate=COST,
    )(partial, mixed_low, incoming, resid, valid, gain)


def d_resid_kernel(
    width,
    p_ref,
    incoming_ref,
    branch_ref,
    inv_ref,
    gain_ref,
    resid_ref,
    raw_ref,
    wide_ref,
    x_ref,
    stat,
    slots,
    *refs,
):
    buffers, (local_sem, send_sem, recv_sem) = refs[:7], refs[7:]
    half = x_ref.shape[0] // 2
    greet(junction_peers())
    started = []
    send = sender(send_sem, recv_sem, started)
    low, high = scatter_flow(p_ref, buffers, send)
    resid_ref[:half, :] = low + incoming_ref[:half, :]
    resid_ref[half:, :] = high + incoming_ref[half:, :]
    stat[...] = jnp.sum(resid_ref[...] * gain_ref[...] * branch_ref[...], axis=1, keepdims=True).T
    inner = column_total(slots, exchange(stat, slots, send, 14)) / width
    inverse = inv_ref[...]
    first = inverse.T
    second = (inverse * inverse * inverse * inner).T
    x_ref[...] = (first * (resid_ref[...] * gain_ref[...]) - branch_ref[...] * second).astype(bf16)

    def meanwhile():
        raw_ref[...] = jnp.sum(resid_ref[...] * branch_ref[...] * first, axis=0, keepdims=True)

    gather_flow(x_ref, wide_ref, local_sem, send, 17, meanwhile)
    for copy in started:
        copy.wait_send()


def d_resid_junction(partial, incoming, branch, inverse, gain, width, number):
    rows, part = incoming.shape
    vmem = pl.BlockSpec(memory_space=pltpu.VMEM)
    return pl.pallas_call(
        functools.partial(d_resid_kernel, width),
        name="d_resid_junction",
        out_shape=(
            jax.ShapeDtypeStruct((rows, part), f32),
            jax.ShapeDtypeStruct((1, part), f32),
            jax.ShapeDtypeStruct((2 * rows, 4 * part), bf16),
        ),
        in_specs=[vmem] * 5,
        out_specs=(vmem, vmem, pl.BlockSpec(memory_space=pl.ANY)),
        scratch_shapes=[
            pltpu.VMEM((rows, part), bf16),
            pltpu.VMEM((1, rows), f32),
            pltpu.VMEM((4, 1, rows), f32),
        ]
        + scatter_buffers(rows, part)
        + [
            pltpu.SemaphoreType.DMA,
            pltpu.SemaphoreType.DMA((31,)),
            pltpu.SemaphoreType.DMA((31,)),
        ],
        compiler_params=pltpu.CompilerParams(
            collective_id=number, has_side_effects=True, vmem_limit_bytes=48 * 2**20
        ),
        cost_estimate=COST,
    )(partial, incoming, branch, inverse, gain)


def feature_peers(wide):
    peers = []
    for d in range(1, 8 if wide else 4):
        peer = {"col": flip("col", d & 3)}
        if d >> 2:
            peer["dp"] = flip("dp", 1)
        peers.append(peer)
    return peers


def total_kernel(v_ref, out_ref, slots, send_sem, recv_sem):
    me = lax.axis_index("col")
    peers = feature_peers(False)
    greet(peers)
    started = []
    send = sender(send_sem, recv_sem, started)
    for d, peer in enumerate(peers):
        send(v_ref, slots.at[me], d, peer)
    slots[me] = v_ref[...]
    for copy in started:
        copy.wait_recv()
    total = slots[0]
    for i in range(1, 4):
        total = total + slots[i]
    out_ref[...] = total
    for copy in started:
        copy.wait_send()


def feature_total(values, number, name):
    k, t = values.shape
    flat = values.reshape(k * t // 128, 128)
    total = pl.pallas_call(
        total_kernel,
        name=name,
        out_shape=jax.ShapeDtypeStruct(flat.shape, f32),
        in_specs=[pl.BlockSpec(memory_space=pltpu.VMEM)],
        out_specs=pl.BlockSpec(memory_space=pltpu.VMEM),
        scratch_shapes=[
            pltpu.VMEM((4,) + flat.shape, f32),
            pltpu.SemaphoreType.DMA((3,)),
            pltpu.SemaphoreType.DMA((3,)),
        ],
        compiler_params=pltpu.CompilerParams(collective_id=number, has_side_effects=True),
    )(flat)
    return total.reshape(k, t)


def gain_peers():
    peers = []
    for d in range(1, 8):
        peers.append({"row": flip("row", d & 3), "dp": flip("dp", d >> 2)})
    return peers


def gain_kernel(v_ref, out_ref, slots, send_sem, recv_sem):
    me = side("dp") * 4 + lax.axis_index("row")
    peers = gain_peers()
    greet(peers)
    started = []
    send = sender(send_sem, recv_sem, started)
    for d, peer in enumerate(peers):
        send(v_ref, slots.at[me], d, peer)
    slots[me] = v_ref[...]
    for copy in started:
        copy.wait_recv()
    total = slots[0]
    for i in range(1, 8):
        total = total + slots[i]
    out_ref[...] = total
    for copy in started:
        copy.wait_send()


def gain_total(values, number):
    flat = values.reshape(-1, 128)
    total = pl.pallas_call(
        gain_kernel,
        name="total_gains",
        out_shape=jax.ShapeDtypeStruct(flat.shape, f32),
        in_specs=[pl.BlockSpec(memory_space=pltpu.VMEM)],
        out_specs=pl.BlockSpec(memory_space=pltpu.VMEM),
        scratch_shapes=[
            pltpu.VMEM((8,) + flat.shape, f32),
            pltpu.SemaphoreType.DMA((7,)),
            pltpu.SemaphoreType.DMA((7,)),
        ],
        compiler_params=pltpu.CompilerParams(collective_id=number, has_side_effects=True),
    )(flat)
    return total.reshape(values.shape)


def row_peers():
    return [(d, {"row": flip("row", d)}) for d in (3, 2, 1)]


def unit_view(ref, unit, tok, heads):
    rows = pl.ds(pl.multiple_of((unit // heads) * tok, tok), tok)
    cols = pl.ds(pl.multiple_of((unit % heads) * HEAD_DIM, HEAD_DIM), HEAD_DIM)
    return ref.at[rows, cols]


def turn_kernel(back, tok, heads, x_ref, out_ref, local_sem, send_sem, recv_sem):
    z = lax.axis_index("row")
    greet([peer for _, peer in row_peers()])
    started = []
    send = sender(send_sem, recv_sem, started)

    def line(ref, i):
        return ref.at[pl.ds(pl.multiple_of(i * tok, tok), tok)]

    def ends(i):
        if back:
            return line(x_ref, i), unit_view(out_ref, z, tok, heads)
        return unit_view(x_ref, i, tok, heads), line(out_ref, z)

    for d, peer in row_peers():
        send(*ends(z ^ d), d - 1, peer)
    own = pltpu.make_async_copy(*ends(z), local_sem)
    own.start()
    for copy in started:
        copy.wait()
    own.wait()


def turn(values, back, tok, heads, number, name):
    shape = (2 * tok, heads * HEAD_DIM) if back else (2 * heads * tok, HEAD_DIM)
    return pl.pallas_call(
        functools.partial(turn_kernel, back, tok, heads),
        name=name,
        out_shape=jax.ShapeDtypeStruct(shape, values.dtype),
        in_specs=[pl.BlockSpec(memory_space=pltpu.VMEM)],
        out_specs=pl.BlockSpec(memory_space=pl.ANY),
        scratch_shapes=[
            pltpu.SemaphoreType.DMA,
            pltpu.SemaphoreType.DMA((3,)),
            pltpu.SemaphoreType.DMA((3,)),
        ],
        compiler_params=pltpu.CompilerParams(collective_id=number, has_side_effects=True),
        cost_estimate=COST,
    )(values)


def totals(stat, slots, started):
    for copy in started:
        copy.wait_recv()
    total = slots[0]
    for i in range(1, 8):
        total = total + slots[i]
    return total


def front_kernel(
    width,
    qkv_ref,
    cos_ref,
    sin_ref,
    gain_ref,
    out_ref,
    inv_ref,
    turned,
    packed,
    stat,
    slots,
    local_sem,
    stat_send,
    stat_recv,
    send_sem,
    recv_sem,
):
    count, tok = qkv_ref.shape[0], cos_ref.shape[0]
    part = qkv_ref.shape[1] // 3
    heads = part // HEAD_DIM
    z = lax.axis_index("row")
    me = side("dp") * 4 + lax.axis_index("col")
    peers = feature_peers(True)
    greet(peers + [peer for _, peer in row_peers()])
    for i in range(2):
        values = qkv_ref[:, i * part : (i + 1) * part]
        stat[i : i + 1, :] = jnp.sum(values * values, axis=1, keepdims=True).T
    started, moved, local = [], [], []
    send = sender(stat_send, stat_recv, started)
    for d, peer in enumerate(peers):
        send(stat, slots.at[me], d, peer)
    slots[me] = stat[...]
    move = sender(send_sem, recv_sem, moved)

    def ship(i):
        for d, peer in row_peers():
            move(packed.at[z ^ d, i], out_ref.at[z, i], 3 * i + d - 1, peer)
        copy = pltpu.make_async_copy(packed.at[z, i], out_ref.at[z, i], local_sem.at[i])
        copy.start()
        local.append(copy)

    def spots():
        return [(s, h, s * heads + h) for s in range(2) for h in range(heads)]

    for s, h, unit in spots():
        packed[unit, 2] = qkv_ref[
            s * tok : (s + 1) * tok, 2 * part + h * HEAD_DIM : 2 * part + (h + 1) * HEAD_DIM
        ].astype(bf16)
    ship(2)
    for i in (1, 0):
        for s, h, unit in spots():
            values = (
                qkv_ref[s * tok : (s + 1) * tok, i * part + h * HEAD_DIM : i * part + (h + 1) * HEAD_DIM]
                * gain_ref[i : i + 1, h * HEAD_DIM : (h + 1) * HEAD_DIM]
            )
            turned[i, unit] = values * cos_ref[...] + pltpu.roll(values, HEAD_DIM // 2, 1) * sin_ref[...]
    inverse = lax.rsqrt(totals(stat, slots, started) / width + norm_eps)
    inv_ref[...] = inverse
    for i in (1, 0):
        column = inverse[i : i + 1, :].T
        for s, h, unit in spots():
            packed[unit, i] = (turned[i, unit] * column[s * tok : (s + 1) * tok]).astype(bf16)
        ship(i)
    for copy in moved:
        copy.wait()
    for copy in local:
        copy.wait()
    for copy in started:
        copy.wait_send()


def front(qkv, cosine, sine_signed, gains, width, units, number):
    count, tok = qkv.shape[0], cosine.shape[0]
    return pl.pallas_call(
        functools.partial(front_kernel, width),
        name="front",
        out_shape=(
            jax.ShapeDtypeStruct((units, 3, tok, HEAD_DIM), bf16),
            jax.ShapeDtypeStruct((2, count), f32),
        ),
        in_specs=[pl.BlockSpec(memory_space=pltpu.VMEM)] * 4,
        out_specs=(pl.BlockSpec(memory_space=pl.ANY), pl.BlockSpec(memory_space=pltpu.VMEM)),
        scratch_shapes=[
            pltpu.VMEM((2, units, tok, HEAD_DIM), f32),
            pltpu.VMEM((units, 3, tok, HEAD_DIM), bf16),
            pltpu.VMEM((2, count), f32),
            pltpu.VMEM((8, 2, count), f32),
            pltpu.SemaphoreType.DMA((3,)),
            pltpu.SemaphoreType.DMA((7,)),
            pltpu.SemaphoreType.DMA((7,)),
            pltpu.SemaphoreType.DMA((9,)),
            pltpu.SemaphoreType.DMA((9,)),
        ],
        compiler_params=pltpu.CompilerParams(
            collective_id=number, has_side_effects=True, vmem_limit_bytes=40 * 2**20
        ),
        cost_estimate=COST,
    )(qkv, cosine, sine_signed, gains)


def rear_kernel(
    width,
    d_ref,
    qkv_ref,
    cos_ref,
    sin_ref,
    gain_ref,
    inv_ref,
    out_ref,
    sums_ref,
    landed,
    normed,
    stat,
    slots,
    stat_send,
    stat_recv,
    send_sem,
    recv_sem,
):
    count, tok = qkv_ref.shape[0], cos_ref.shape[0]
    part = qkv_ref.shape[1] // 3
    heads = part // HEAD_DIM
    z = lax.axis_index("row")
    me = side("dp") * 4 + lax.axis_index("col")
    peers = feature_peers(True)
    greet(peers + [peer for _, peer in row_peers()])
    started, moved = [], []
    move = sender(send_sem, recv_sem, moved)
    for i in (0, 1, 2):
        for d, peer in row_peers():
            there = pl.ds(pl.multiple_of((z ^ d) * tok, tok), tok)
            move(d_ref.at[i, there], landed.at[z, i], 3 * i + d - 1, peer)
    here = pl.ds(pl.multiple_of(z * tok, tok), tok)
    for i in (0, 1, 2):
        landed[z, i] = d_ref[i, here, :]
    spots = [(s, h, s * heads + h) for s in range(2) for h in range(heads)]
    for i in (0, 1):
        for copy in moved[3 * i : 3 * i + 3]:
            copy.wait_recv()
        for h in range(heads):
            cols = slice(i * part + h * HEAD_DIM, i * part + (h + 1) * HEAD_DIM)
            gain = gain_ref[i : i + 1, h * HEAD_DIM : (h + 1) * HEAD_DIM]
            raw = jnp.zeros((1, HEAD_DIM), f32)
            for s in range(2):
                rows = slice(s * tok, (s + 1) * tok)
                values = landed[s * heads + h, i].astype(f32)
                back = values * cos_ref[...] - pltpu.roll(values, HEAD_DIM // 2, 1) * sin_ref[...]
                pre = qkv_ref[rows, cols]
                inverse = inv_ref[i : i + 1, rows].T
                crossed = back * pre
                raw = raw + jnp.sum(crossed * inverse, axis=0, keepdims=True)
                partial = jnp.sum(crossed * gain, axis=1, keepdims=True).T
                if h == 0:
                    stat[i : i + 1, rows] = partial
                else:
                    stat[i : i + 1, rows] = stat[i : i + 1, rows] + partial
                normed[rows, cols] = back * gain
            sums_ref[i : i + 1, h * HEAD_DIM : (h + 1) * HEAD_DIM] = raw
    send = sender(stat_send, stat_recv, started)
    for d, peer in enumerate(peers):
        send(stat, slots.at[me], d, peer)
    slots[me] = stat[...]
    for copy in moved[6:]:
        copy.wait_recv()
    for s, h, unit in spots:
        cols = slice(2 * part + h * HEAD_DIM, 2 * part + (h + 1) * HEAD_DIM)
        out_ref[s * tok : (s + 1) * tok, cols] = landed[unit, 2]
    inner = totals(stat, slots, started) / width
    for i in (0, 1):
        inverse = inv_ref[i : i + 1, :]
        first = inverse.T
        second = (inverse * inverse * inverse * inner[i : i + 1, :]).T
        cols = slice(i * part, (i + 1) * part)
        out_ref[:, cols] = (first * normed[:, cols] - qkv_ref[:, cols] * second).astype(bf16)
    for copy in moved + started:
        copy.wait_send()


def rear(d_units, qkv, cosine, sine_signed, gains, inverse, width, number):
    count, tok = qkv.shape[0], cosine.shape[0]
    part = qkv.shape[1] // 3
    units = d_units.shape[1] // tok
    return pl.pallas_call(
        functools.partial(rear_kernel, width),
        name="rear",
        out_shape=(
            jax.ShapeDtypeStruct((count, 3 * part), bf16),
            jax.ShapeDtypeStruct((2, part), f32),
        ),
        in_specs=[pl.BlockSpec(memory_space=pltpu.VMEM)] * 6,
        out_specs=[pl.BlockSpec(memory_space=pltpu.VMEM)] * 2,
        scratch_shapes=[
            pltpu.VMEM((units, 3, tok, HEAD_DIM), bf16),
            pltpu.VMEM((count, 2 * part), f32),
            pltpu.VMEM((2, count), f32),
            pltpu.VMEM((8, 2, count), f32),
            pltpu.SemaphoreType.DMA((7,)),
            pltpu.SemaphoreType.DMA((7,)),
            pltpu.SemaphoreType.DMA((9,)),
            pltpu.SemaphoreType.DMA((9,)),
        ],
        compiler_params=pltpu.CompilerParams(
            collective_id=number, has_side_effects=True, vmem_limit_bytes=40 * 2**20
        ),
        cost_estimate=COST,
    )(d_units, qkv, cosine, sine_signed, gains, inverse)


BLOCK = 512


def attend_kernel(len_ref, q_ref, k_ref, v_ref, o_ref, o32_ref, lse_ref):
    i = pl.program_id(0)
    bq, bk = q_ref.shape[0], BLOCK
    length = len_ref[0]
    scale = HEAD_DIM ** (-0.5)
    q = q_ref[...]
    rows = i * bq + lax.broadcasted_iota(jnp.int32, (bq, bk), 0)
    cols0 = lax.broadcasted_iota(jnp.int32, (bq, bk), 1)

    def step(j, carry, masked):
        top, total, acc = carry
        j0 = pl.multiple_of(j * bk, bk)
        scores = contract_last(q, k_ref[pl.ds(j0, bk), :]) * scale
        if masked:
            cols = j0 + cols0
            scores = jnp.where((cols <= rows) & (cols < length), scores, masked_score)
        new = jnp.maximum(top, jnp.max(scores, axis=1, keepdims=True))
        weights = jnp.exp(scores - new)
        fix = jnp.exp(top - new)
        total = total * fix + jnp.sum(weights, axis=1, keepdims=True)
        acc = acc * fix + matmul(weights.astype(bf16), v_ref[pl.ds(j0, bk), :])
        return new, total, acc

    carry = (
        jnp.full((bq, 1), -jnp.inf, f32),
        jnp.zeros((bq, 1), f32),
        jnp.zeros((bq, HEAD_DIM), f32),
    )
    whole = jnp.minimum(i, length // bk)
    last = jnp.minimum(i + 1, (length + bk - 1) // bk)
    carry = lax.fori_loop(0, whole, lambda j, s: step(j, s, False), carry)
    top, total, acc = lax.fori_loop(whole, last, lambda j, s: step(j, s, True), carry)
    out = acc / total
    o_ref[...] = out.astype(bf16)
    o32_ref[...] = out
    lse_ref[...] = jnp.broadcast_to((top + jnp.log(total)).T, lse_ref.shape)


def attend(length, q, k, v):
    slots = q.shape[0]
    whole = pl.BlockSpec((slots, HEAD_DIM), lambda i: (0, 0))
    part = pl.BlockSpec((BLOCK, HEAD_DIM), lambda i: (i, 0))
    return pl.pallas_call(
        attend_kernel,
        name="attend",
        grid=(slots // BLOCK,),
        out_shape=(
            jax.ShapeDtypeStruct((slots, HEAD_DIM), bf16),
            jax.ShapeDtypeStruct((slots, HEAD_DIM), f32),
            jax.ShapeDtypeStruct((8, slots), f32),
        ),
        in_specs=[pl.BlockSpec(memory_space=pltpu.SMEM), part, whole, whole],
        out_specs=(part, part, pl.BlockSpec((8, BLOCK), lambda i: (0, i))),
        cost_estimate=COST,
    )(length, q, k, v)


def attend_back_kernel(
    len_ref, q_ref, k_ref, v_ref, do_ref, o_ref, lse_ref, out_ref, dq_acc, delta_ref
):
    j = pl.program_id(0)
    bk, bq = k_ref.shape[0], BLOCK
    slots = q_ref.shape[0]
    length = len_ref[0]
    scale = HEAD_DIM ** (-0.5)

    @pl.when(j == 0)
    def _():
        dq_acc[...] = jnp.zeros_like(dq_acc)
        for i in range(slots // bq):
            here = slice(i * bq, (i + 1) * bq)
            product = do_ref[here, :].astype(f32) * o_ref[here, :]
            delta_ref[0:1, here] = jnp.sum(product, axis=1, keepdims=True).T

    k, v = k_ref[...], v_ref[...]
    j0 = j * bk
    cols = j0 + lax.broadcasted_iota(jnp.int32, (bk, bq), 0)
    rows0 = lax.broadcasted_iota(jnp.int32, (bk, bq), 1)

    def step(i, carry, masked):
        dk, dv = carry
        i0 = pl.multiple_of(i * bq, bq)
        here = pl.ds(i0, bq)
        q, do = q_ref[here, :], do_ref[here, :]
        scores = contract_last(k, q) * scale
        if masked:
            scores = jnp.where((cols <= i0 + rows0) & (cols < length), scores, masked_score)
        probs = jnp.exp(scores - lse_ref[0:1, here])
        dv = dv + matmul(probs.astype(bf16), do)
        d_probs = contract_last(v, do)
        d_scores = (probs * (d_probs - delta_ref[0:1, here])).astype(bf16)
        dk = dk + matmul(d_scores, q)
        dq_acc[here, :] += contract_first(d_scores, k)
        return dk, dv

    zero = jnp.zeros((bk, HEAD_DIM), f32)
    top = slots // bq
    first = jnp.where(j0 + bk <= length, j + 1, top)
    first = jnp.where(j0 < length, first, j)
    stop = jnp.where(j0 < length, top, j)
    carry = lax.fori_loop(j, first, lambda i, s: step(i, s, True), (zero, zero))
    dk, dv = lax.fori_loop(first, stop, lambda i, s: step(i, s, False), carry)
    there = pl.ds(pl.multiple_of(j0, bk), bk)
    out_ref[1, there, :] = (dk * scale).astype(bf16)
    out_ref[2, there, :] = dv.astype(bf16)

    @pl.when(j == pl.num_programs(0) - 1)
    def _():
        out_ref[0] = (dq_acc[...] * scale).astype(bf16)


def attend_back(length, q, k, v, do, o, lse):
    slots = q.shape[0]
    whole = pl.BlockSpec((slots, HEAD_DIM), lambda j: (0, 0))
    part = pl.BlockSpec((BLOCK, HEAD_DIM), lambda j: (j, 0))
    line = pl.BlockSpec((8, slots), lambda j: (0, 0))
    return pl.pallas_call(
        attend_back_kernel,
        name="attend_back",
        grid=(slots // BLOCK,),
        out_shape=jax.ShapeDtypeStruct((3, slots, HEAD_DIM), bf16),
        in_specs=[pl.BlockSpec(memory_space=pltpu.SMEM), whole, part, part, whole, whole, line],
        out_specs=pl.BlockSpec((3, slots, HEAD_DIM), lambda j: (0, 0, 0)),
        scratch_shapes=[pltpu.VMEM((slots, HEAD_DIM), f32), pltpu.VMEM((8, slots), f32)],
        cost_estimate=COST,
    )(length, q, k, v, do, o, lse)


def per_device(
    tokens,
    seq_lengths,
    w_query,
    w_key,
    w_value,
    w_out,
    w_gate,
    w_up,
    w_down,
    q_gain,
    k_gain,
    attn_gain,
    mlp_gain,
    cotangent,
):
    tok_rows, feat_part = tokens.shape
    row_count, data_count = lax.axis_size("row"), lax.axis_size("dp")
    width = feat_part * lax.axis_size("col")
    slots = tok_rows * row_count
    half_feat = feat_part // 2
    y, z = side("dp"), lax.axis_index("row")
    heads = half_feat // HEAD_DIM
    pairs = [(i, i ^ 1) for i in range(data_count)]
    after = lambda values, *done: lax.optimization_barrier((values,) + done)[0]

    def y_half(values, axis):
        size = values.shape[axis] // 2
        return lax.dynamic_slice_in_dim(values, y * size, size, axis)

    qkv_weight = lax.all_gather(
        jnp.concatenate([y_half(w_query, 1), y_half(w_key, 1), y_half(w_value, 1)], axis=1),
        "row",
        axis=0,
        tiled=True,
    )
    out_weight = lax.all_gather(y_half(w_out, 0), "row", axis=1, tiled=True)
    gate_up_weight = lax.all_gather(
        jnp.concatenate([y_half(w_gate, 1), y_half(w_up, 1)], axis=1), "row", axis=0, tiled=True
    )
    hidden_part = gate_up_weight.shape[1] // 2
    gate_weight, up_weight = gate_up_weight[:, :hidden_part], gate_up_weight[:, hidden_part:]
    down_half = y_half(w_down, 0)
    split = down_half.shape[1] // 2
    low_weight = lax.all_gather(down_half[:, :split], "row", axis=1, tiled=True)

    positions = z * tok_rows + jnp.arange(tok_rows)
    length = seq_lengths[0]
    valid = (positions < length).astype(f32)[:, None]
    cosine, sine = rope_tables(positions, HEAD_DIM)
    sine_signed = jnp.where(jnp.arange(HEAD_DIM)[None, :] < HEAD_DIM // 2, -sine, sine)
    other_length = lax.ppermute(seq_lengths, "dp", pairs)
    pair_lengths = jnp.where(
        y == 0,
        jnp.concatenate([seq_lengths, other_length]),
        jnp.concatenate([other_length, seq_lengths]),
    )
    unit_length = lax.dynamic_slice_in_dim(pair_lengths, z // heads, 1)
    qk_gain = jnp.stack([y_half(q_gain, 0), y_half(k_gain, 0)])

    tokens_wide = gather_wide(tokens, 0, "gather_tokens")
    high_weight = lax.all_gather(after(down_half[:, split:], tokens_wide), "row", axis=1, tiled=True)
    qkv = matmul(tokens_wide, qkv_weight)
    units, inverse = front(qkv, cosine, sine_signed, qk_gain, width, 2 * heads, 2)
    q_unit, k_unit, v_unit = (units[:, i].reshape(slots, HEAD_DIM) for i in range(3))
    attn_unit, attn_exact, log_total = attend(unit_length, q_unit, k_unit, v_unit)
    attn_low = turn(attn_unit, True, tok_rows, heads, 3, "turn_attn")
    branch = scatter_wide(matmul(attn_low, out_weight).astype(bf16), 4, "scatter_branch")
    branch_inv = lax.rsqrt(
        feature_total(jnp.sum(branch * branch, axis=1)[None, :], 5, "total_branch")[0] / width
        + norm_eps
    )[:, None]
    resid = tokens.astype(f32) + branch * branch_inv * attn_gain
    resid_wide = gather_wide(resid.astype(bf16), 6, "gather_resid")
    gate = matmul(resid_wide, gate_weight)
    upper = matmul(resid_wide, up_weight)
    sigma = jax.nn.sigmoid(gate)
    hidden = (gate * sigma * upper).astype(bf16)
    mixed_low = scatter_wide(matmul(hidden, low_weight).astype(bf16), 7, "scatter_mixed_low")
    high_weight = after(high_weight, mixed_low)
    incoming = cotangent.astype(f32) * valid
    factor = 1.0 / math.sqrt(slots * data_count)
    block_output, mlp_gain_raw, d_high, d_low_wide = mixed_junction(
        matmul(hidden, high_weight).astype(bf16),
        mixed_low,
        incoming,
        resid,
        valid.T,
        mlp_gain[None, :],
        width,
        17,
    )
    low_raw = (contract_first(hidden, d_low_wide) * factor).astype(bf16)
    d_high_wide = gather_wide(after(d_high, low_raw), 18, "gather_d_mixed_high")
    high_raw = (contract_first(hidden, d_high_wide) * factor).astype(bf16)

    def cut(values, index, count, axis):
        size = values.shape[axis] // count
        return lax.dynamic_slice_in_dim(values, index * size, size, axis)

    def over_dp(piece):
        if data_count > 2:
            groups = [list(range(s, data_count, 2)) for s in (0, 1)]
            piece = lax.psum(piece, "dp", axis_index_groups=groups)
        return piece

    def two_sides(piece, other, bit, axis):
        low = jnp.where(bit == 0, piece, other)
        high = jnp.where(bit == 0, other, piece)
        return jnp.concatenate([low, high], axis=axis)

    def from_twin(piece):
        return lax.ppermute(piece, "dp", pairs)

    def reduce_rows(raw, axis):
        return lax.psum_scatter(raw, "row", scatter_dimension=axis, tiled=True)

    d_hidden = contract_last(d_low_wide, low_weight) + contract_last(d_high_wide, high_weight)
    d_gate = (d_hidden * upper * sigma * (1.0 + gate * (1.0 - sigma))).astype(bf16)
    d_upper = (d_hidden * gate * sigma).astype(bf16)
    gate_raw = (contract_first(resid_wide, d_gate) * factor).astype(bf16)
    up_raw = (contract_first(resid_wide, d_upper) * factor).astype(bf16)
    d_resid_wide = (
        contract_last(d_gate, gate_weight) + contract_last(d_upper, up_weight)
    ).astype(bf16)
    d_resid_wide, low_piece = lax.optimization_barrier(
        (after(d_resid_wide, high_raw, gate_raw, up_raw), reduce_rows(low_raw, 1))
    )
    down_piece = jnp.concatenate([low_piece, reduce_rows(high_raw, 1)], axis=1)
    gate_piece, up_piece = reduce_rows(gate_raw, 0), reduce_rows(up_raw, 0)
    d_resid, attn_gain_raw, d_branch_wide = d_resid_junction(
        d_resid_wide, incoming, branch, branch_inv.T, attn_gain[None, :], width, 10
    )
    down_piece = over_dp(down_piece)
    d_branch_wide, down_piece = lax.optimization_barrier((d_branch_wide, down_piece))
    d_attn = contract_last(d_branch_wide, out_weight).astype(bf16)
    other_down = from_twin(down_piece)
    d_attn_unit, other_down = lax.optimization_barrier(
        (turn(d_attn, False, tok_rows, heads, 13, "turn_d_attn"), other_down)
    )
    out_raw = (contract_first(attn_low, after(d_branch_wide, d_attn_unit)) * factor).astype(bf16)
    d_attn_unit = after(d_attn_unit, out_raw)
    out_piece = reduce_rows(out_raw, 1)
    d_units = attend_back(unit_length, q_unit, k_unit, v_unit, d_attn_unit, attn_exact, log_total)
    d_units, gate_piece = lax.optimization_barrier((d_units, over_dp(gate_piece)))
    other_gate = from_twin(gate_piece)
    d_qkv, gain_sums = rear(d_units, qkv, cosine, sine_signed, qk_gain, inverse, width, 14)
    d_qkv, gain_sums, other_gate, up_piece = lax.optimization_barrier(
        (d_qkv, gain_sums, other_gate, over_dp(up_piece))
    )
    other_up = from_twin(up_piece)
    qkv_raw = (contract_first(tokens_wide, d_qkv) * factor).astype(bf16)
    projected = contract_last(after(d_qkv, qkv_raw), qkv_weight).astype(bf16)
    qkv_piece = over_dp(reduce_rows(qkv_raw, 0))
    scattered, out_piece, gain_sums = lax.optimization_barrier(
        (scatter_wide(projected, 16, "scatter_projected"), over_dp(out_piece), gain_sums)
    )
    other_out = from_twin(out_piece)
    input_grad = d_resid + scattered

    def spread(half):
        return lax.dynamic_update_slice_in_dim(jnp.zeros((feat_part,), f32), half, y * half_feat, 0)

    gains = over_dp(
        gain_total(
            jnp.stack([spread(gain_sums[0]), spread(gain_sums[1]), attn_gain_raw[0], mlp_gain_raw[0]])
            * factor,
            15,
        )
    )

    gains, qkv_piece, other_down, other_gate, other_up = lax.optimization_barrier(
        (gains, qkv_piece, other_down, other_gate, other_up)
    )

    def whole(piece, other, axis):
        return two_sides(piece, other, y, axis).astype(f32)

    qkv_other = from_twin(qkv_piece)
    q_grad, k_grad, v_grad = (
        two_sides(cut(qkv_piece, i, 3, 1), cut(qkv_other, i, 3, 1), y, 1).astype(f32)
        for i in range(3)
    )
    return (
        block_output,
        input_grad,
        q_grad,
        k_grad,
        v_grad,
        whole(out_piece, other_out, 0),
        whole(gate_piece, other_gate, 1),
        whole(up_piece, other_up, 1),
        whole(down_piece, other_down, 0),
        gains[0],
        gains[1],
        gains[2],
        gains[3],
    )


def solution(mesh):
    tok, row_col, col_row, gain = P(("dp", "row"), "col"), P("row", "col"), P("col", "row"), P("col")
    weights = (row_col, row_col, row_col, col_row, row_col, row_col, col_row)
    gains = (gain, gain, gain, gain)
    return jax.shard_map(
        per_device,
        mesh=mesh,
        in_specs=(tok, P("dp")) + weights + gains + (tok,),
        out_specs=(tok, tok) + weights + gains,
        check_vma=False,
    )
```

```python
import functools
import math

import jax
import jax.numpy as jnp
from jax import lax
from jax.experimental import pallas as pl
from jax.experimental.pallas import tpu as pltpu
from jax.sharding import PartitionSpec as P

HEAD_DIM = 128
rope_base = 500000.0
norm_eps = 1e-06
masked_score = -1e30

MESH = pl.DeviceIdType.MESH
bf16 = jnp.bfloat16
f32 = jnp.float32
COST = pl.CostEstimate(flops=0, bytes_accessed=1000, transcendentals=0)


def rope_tables(positions, head_dim):
    half = head_dim // 2
    freq = 1.0 / rope_base ** (jnp.arange(half, dtype=f32) / half)
    angle = positions.astype(f32)[:, None] * freq[None, :]
    angle = jnp.concatenate([angle, angle], axis=1)
    return (jnp.cos(angle), jnp.sin(angle))


def matmul(left, right):
    return jnp.dot(left, right, preferred_element_type=f32)


def contract_first(left, right):
    return lax.dot_general(left, right, (((0,), (0,)), ((), ())), preferred_element_type=f32)


def contract_last(left, right):
    return lax.dot_general(left, right, (((1,), (1,)), ((), ())), preferred_element_type=f32)


def flip(axis, bit):
    return lax.axis_index(axis) ^ bit


def side(axis):
    return lax.axis_index(axis) & 1


def greet(peers):
    barrier = pltpu.get_barrier_semaphore()
    for peer in peers:
        pl.semaphore_signal(barrier, inc=1, device_id=peer, device_id_type=MESH)
    pl.semaphore_wait(barrier, len(peers))


def sender(send_sem, recv_sem, started):
    def send(src, dst, number, peer):
        copy = pltpu.make_async_remote_copy(
            src_ref=src,
            dst_ref=dst,
            send_sem=send_sem.at[number],
            recv_sem=recv_sem.at[number],
            device_id=peer,
            device_id_type=MESH,
        )
        copy.start()
        started.append(copy)
        return copy

    return send


def neighbours():
    return {"col": flip("col", 2)}, {"dp": flip("dp", 1)}, {"col": flip("col", 1)}


def gather_flow(x_ref, out_ref, local_sem, send, base, meanwhile=None):
    rows, width = x_ref.shape
    half = rows // 2
    y, b = side("dp"), lax.axis_index("col")
    to_x, to_y, to_c = neighbours()

    def slot(yy, h, bb, n=half):
        return out_ref.at[
            pl.ds(pl.multiple_of(yy * rows + h * half, half), n),
            pl.ds(pl.multiple_of(bb * width, width), width),
        ]

    low, high = x_ref.at[pl.ds(0, half)], x_ref.at[pl.ds(half, half)]
    own = pltpu.make_async_copy(x_ref, slot(y, 0, b, rows), local_sem)
    xa = send(low, slot(y, 0, b), base + 0, to_x)
    ya = send(high, slot(y, 1, b), base + 1, to_y)
    core = [send(low, slot(y, 0, b), base + 6, to_c)]
    yb = send(low, slot(y, 0, b), base + 2, to_y)
    xb = send(high, slot(y, 1, b), base + 3, to_x)
    core.append(send(high, slot(y, 1, b), base + 7, to_c))
    own.start()
    if meanwhile is not None:
        meanwhile()
    xa.wait_recv()
    piece = slot(y, 0, b ^ 2)
    yc = send(piece, piece, base + 4, to_y)
    core.append(send(piece, piece, base + 8, to_c))
    ya.wait_recv()
    piece = slot(y ^ 1, 1, b)
    xc = send(piece, piece, base + 5, to_x)
    core.append(send(piece, piece, base + 9, to_c))
    yb.wait_recv()
    piece = slot(y ^ 1, 0, b)
    core.append(send(piece, piece, base + 10, to_c))
    xb.wait_recv()
    piece = slot(y, 1, b ^ 2)
    core.append(send(piece, piece, base + 11, to_c))
    yc.wait_recv()
    piece = slot(y ^ 1, 0, b ^ 2)
    core.append(send(piece, piece, base + 12, to_c))
    xc.wait_recv()
    piece = slot(y ^ 1, 1, b ^ 2)
    core.append(send(piece, piece, base + 13, to_c))
    for copy in core:
        copy.wait_recv()
    own.wait()


def gather_kernel(x_ref, out_ref, local_sem, send_sem, recv_sem):
    greet(neighbours())
    started = []
    gather_flow(x_ref, out_ref, local_sem, sender(send_sem, recv_sem, started), 0)
    for copy in started:
        copy.wait_send()


def gather_wide(values, number, name):
    rows, width = values.shape
    return pl.pallas_call(
        gather_kernel,
        name=name,
        out_shape=jax.ShapeDtypeStruct((2 * rows, 4 * width), values.dtype),
        in_specs=[pl.BlockSpec(memory_space=pltpu.VMEM)],
        out_specs=pl.BlockSpec(memory_space=pl.ANY),
        scratch_shapes=[
            pltpu.SemaphoreType.DMA,
            pltpu.SemaphoreType.DMA((14,)),
            pltpu.SemaphoreType.DMA((14,)),
        ],
        compiler_params=pltpu.CompilerParams(collective_id=number, has_side_effects=True),
        cost_estimate=COST,
    )(values)


def scatter_flow(p_ref, buffers, send):
    rc, s1, ry, rx, s2, fy, fx = buffers
    rows, width = p_ref.shape[0] // 2, p_ref.shape[1] // 4
    half = rows // 2
    y, b = side("dp"), lax.axis_index("col")
    x, c = b >> 1, b & 1
    to_x, to_y, to_c = neighbours()

    def place(yy, h):
        return pl.ds(pl.multiple_of(yy * rows + h * half, half), half)

    def column(bb):
        return pl.ds(pl.multiple_of(bb * width, width), width)

    order = [(0, y ^ 1, 0), (1, y ^ 1, 0), (x ^ 1, 0, 1), (x ^ 1, 1, 1)]
    order += [(0, y, 0), (1, y, 0), (x, 0, 1), (x, 1, 1)]
    core = [
        send(
            p_ref.at[place(yy, h), column(2 * xx + (c ^ 1))],
            rc.at[xx, place(yy, h)],
            number,
            to_c,
        )
        for number, (xx, yy, h) in enumerate(order)
    ]

    def settle(*numbers):
        for number in numbers:
            core[number].wait_recv()
            xx, yy, h = order[number]
            s1[xx, place(yy, h), :] = (
                p_ref[place(yy, h), column(2 * xx + c)].astype(f32)
                + rc[xx, place(yy, h), :].astype(f32)
            ).astype(s1.dtype)

    settle(0, 1, 2, 3)
    ya, xa = [], []
    for i in range(2):
        ya.append(send(s1.at[i, place(y ^ 1, 0), :], ry.at[i], 8 + i, to_y))
        xa.append(send(s1.at[x ^ 1, pl.ds(i * rows + half, half), :], rx.at[i], 10 + i, to_x))
    settle(4, 5, 6, 7)
    for copy in ya:
        copy.wait_recv()
    s2[0] = (s1[x ^ 1, place(y, 0), :].astype(f32) + ry[x ^ 1].astype(f32)).astype(s2.dtype)
    xb = send(s2.at[0], fx, 12, to_x)
    for copy in xa:
        copy.wait_recv()
    s2[1] = (s1[x, place(y ^ 1, 1), :].astype(f32) + rx[y ^ 1].astype(f32)).astype(s2.dtype)
    yb = send(s2.at[1], fy, 13, to_y)
    keep = s1[x, place(y, 0), :].astype(f32) + ry[x].astype(f32)
    xb.wait_recv()
    low = keep + fx[...].astype(f32)
    keep = s1[x, place(y, 1), :].astype(f32) + rx[y].astype(f32)
    yb.wait_recv()
    return low, keep + fy[...].astype(f32)


def scatter_buffers(rows, width):
    half = rows // 2
    return [
        pltpu.VMEM((2, 2 * rows, width), bf16),
        pltpu.VMEM((2, 2 * rows, width), bf16),
        pltpu.VMEM((2, half, width), bf16),
        pltpu.VMEM((2, half, width), bf16),
        pltpu.VMEM((2, half, width), bf16),
        pltpu.VMEM((half, width), bf16),
        pltpu.VMEM((half, width), bf16),
    ]


def scatter_kernel(p_ref, out_ref, *refs):
    buffers, (send_sem, recv_sem) = refs[:7], refs[7:]
    half = out_ref.shape[0] // 2
    greet(neighbours())
    started = []
    low, high = scatter_flow(p_ref, buffers, sender(send_sem, recv_sem, started))
    out_ref[:half, :] = low
    out_ref[half:, :] = high
    for copy in started:
        copy.wait_send()


def scatter_wide(partial, number, name):
    rows, width = partial.shape[0] // 2, partial.shape[1] // 4
    return pl.pallas_call(
        scatter_kernel,
        name=name,
        out_shape=jax.ShapeDtypeStruct((rows, width), f32),
        in_specs=[pl.BlockSpec(memory_space=pltpu.VMEM)],
        out_specs=pl.BlockSpec(memory_space=pltpu.VMEM),
        scratch_shapes=scatter_buffers(rows, width)
        + [pltpu.SemaphoreType.DMA((14,)), pltpu.SemaphoreType.DMA((14,))],
        compiler_params=pltpu.CompilerParams(
            collective_id=number, has_side_effects=True, vmem_limit_bytes=48 * 2**20
        ),
        cost_estimate=COST,
    )(partial)


def exchange(stat, slots, send, base):
    me = lax.axis_index("col")
    copies = [send(stat, slots.at[me], base + d, peer) for d, peer in enumerate(feature_peers(False))]
    slots[me] = stat[...]
    return copies


def column_total(slots, copies):
    for copy in copies:
        copy.wait_recv()
    return (slots[0] + slots[1]) + (slots[2] + slots[3])


def junction_peers():
    to_x, to_y, to_c = neighbours()
    return [to_x, to_y, to_c, {"col": flip("col", 3)}]


def mixed_kernel(
    width,
    p_ref,
    low_ref,
    incoming_ref,
    resid_ref,
    valid_ref,
    gain_ref,
    block_ref,
    raw_ref,
    rest_ref,
    wide_ref,
    mixed,
    x_ref,
    stat,
    slots,
    *refs,
):
    buffers, (local_sem, send_sem, recv_sem) = refs[:7], refs[7:]
    rows, split = low_ref.shape
    half = rows // 2
    greet(junction_peers())
    started = []
    send = sender(send_sem, recv_sem, started)
    mixed[:, :split] = low_ref[...]
    low, high = scatter_flow(p_ref, buffers, send)
    mixed[:half, split:] = low
    mixed[half:, split:] = high
    stat[0:1, :] = jnp.sum(mixed[...] * mixed[...], axis=1, keepdims=True).T
    stat[1:2, :] = jnp.sum(incoming_ref[...] * gain_ref[...] * mixed[...], axis=1, keepdims=True).T
    total = column_total(slots, exchange(stat, slots, send, 14)) / width
    inverse = lax.rsqrt(total[0:1, :] + norm_eps)
    first = inverse.T
    second = (inverse * inverse * inverse * total[1:2, :]).T

    def slope(cols):
        return (
            first * (incoming_ref[:, cols] * gain_ref[:, cols]) - mixed[:, cols] * second
        ).astype(bf16)

    x_ref[...] = slope(slice(0, split))

    def meanwhile():
        rest_ref[...] = slope(slice(split, 2 * split))
        normed = mixed[...] * first
        block_ref[...] = ((resid_ref[...] + normed * gain_ref[...]) * valid_ref[...].T).astype(bf16)
        raw_ref[...] = jnp.sum(incoming_ref[...] * normed, axis=0, keepdims=True)

    gather_flow(x_ref, wide_ref, local_sem, send, 17, meanwhile)
    for copy in started:
        copy.wait_send()


def mixed_junction(partial, mixed_low, incoming, resid, valid, gain, width, number):
    rows, part = incoming.shape
    split = mixed_low.shape[1]
    vmem = pl.BlockSpec(memory_space=pltpu.VMEM)
    return pl.pallas_call(
        functools.partial(mixed_kernel, width),
        name="mixed_junction",
        out_shape=(
            jax.ShapeDtypeStruct((rows, part), bf16),
            jax.ShapeDtypeStruct((1, part), f32),
            jax.ShapeDtypeStruct((rows, part - split), bf16),
            jax.ShapeDtypeStruct((2 * rows, 4 * split), bf16),
        ),
        in_specs=[vmem] * 6,
        out_specs=(vmem, vmem, vmem, pl.BlockSpec(memory_space=pl.ANY)),
        scratch_shapes=[
            pltpu.VMEM((rows, part), f32),
            pltpu.VMEM((rows, split), bf16),
            pltpu.VMEM((2, rows), f32),
            pltpu.VMEM((4, 2, rows), f32),
        ]
        + scatter_buffers(rows, split)
        + [
            pltpu.SemaphoreType.DMA,
            pltpu.SemaphoreType.DMA((31,)),
            pltpu.SemaphoreType.DMA((31,)),
        ],
        compiler_params=pltpu.CompilerParams(
            collective_id=number, has_side_effects=True, vmem_limit_bytes=48 * 2**20
        ),
        cost_estimate=COST,
    )(partial, mixed_low, incoming, resid, valid, gain)


def d_resid_kernel(
    width,
    p_ref,
    incoming_ref,
    branch_ref,
    inv_ref,
    gain_ref,
    resid_ref,
    raw_ref,
    wide_ref,
    x_ref,
    stat,
    slots,
    *refs,
):
    buffers, (local_sem, send_sem, recv_sem) = refs[:7], refs[7:]
    half = x_ref.shape[0] // 2
    greet(junction_peers())
    started = []
    send = sender(send_sem, recv_sem, started)
    low, high = scatter_flow(p_ref, buffers, send)
    resid_ref[:half, :] = low + incoming_ref[:half, :]
    resid_ref[half:, :] = high + incoming_ref[half:, :]
    stat[...] = jnp.sum(resid_ref[...] * gain_ref[...] * branch_ref[...], axis=1, keepdims=True).T
    inner = column_total(slots, exchange(stat, slots, send, 14)) / width
    inverse = inv_ref[...]
    first = inverse.T
    second = (inverse * inverse * inverse * inner).T
    x_ref[...] = (first * (resid_ref[...] * gain_ref[...]) - branch_ref[...] * second).astype(bf16)

    def meanwhile():
        raw_ref[...] = jnp.sum(resid_ref[...] * branch_ref[...] * first, axis=0, keepdims=True)

    gather_flow(x_ref, wide_ref, local_sem, send, 17, meanwhile)
    for copy in started:
        copy.wait_send()


def d_resid_junction(partial, incoming, branch, inverse, gain, width, number):
    rows, part = incoming.shape
    vmem = pl.BlockSpec(memory_space=pltpu.VMEM)
    return pl.pallas_call(
        functools.partial(d_resid_kernel, width),
        name="d_resid_junction",
        out_shape=(
            jax.ShapeDtypeStruct((rows, part), f32),
            jax.ShapeDtypeStruct((1, part), f32),
            jax.ShapeDtypeStruct((2 * rows, 4 * part), bf16),
        ),
        in_specs=[vmem] * 5,
        out_specs=(vmem, vmem, pl.BlockSpec(memory_space=pl.ANY)),
        scratch_shapes=[
            pltpu.VMEM((rows, part), bf16),
            pltpu.VMEM((1, rows), f32),
            pltpu.VMEM((4, 1, rows), f32),
        ]
        + scatter_buffers(rows, part)
        + [
            pltpu.SemaphoreType.DMA,
            pltpu.SemaphoreType.DMA((31,)),
            pltpu.SemaphoreType.DMA((31,)),
        ],
        compiler_params=pltpu.CompilerParams(
            collective_id=number, has_side_effects=True, vmem_limit_bytes=48 * 2**20
        ),
        cost_estimate=COST,
    )(partial, incoming, branch, inverse, gain)


def feature_peers(wide):
    peers = []
    for d in range(1, 8 if wide else 4):
        peer = {"col": flip("col", d & 3)}
        if d >> 2:
            peer["dp"] = flip("dp", 1)
        peers.append(peer)
    return peers


def total_kernel(v_ref, out_ref, slots, send_sem, recv_sem):
    me = lax.axis_index("col")
    peers = feature_peers(False)
    greet(peers)
    started = []
    send = sender(send_sem, recv_sem, started)
    for d, peer in enumerate(peers):
        send(v_ref, slots.at[me], d, peer)
    slots[me] = v_ref[...]
    for copy in started:
        copy.wait_recv()
    total = slots[0]
    for i in range(1, 4):
        total = total + slots[i]
    out_ref[...] = total
    for copy in started:
        copy.wait_send()


def feature_total(values, number, name):
    k, t = values.shape
    flat = values.reshape(k * t // 128, 128)
    total = pl.pallas_call(
        total_kernel,
        name=name,
        out_shape=jax.ShapeDtypeStruct(flat.shape, f32),
        in_specs=[pl.BlockSpec(memory_space=pltpu.VMEM)],
        out_specs=pl.BlockSpec(memory_space=pltpu.VMEM),
        scratch_shapes=[
            pltpu.VMEM((4,) + flat.shape, f32),
            pltpu.SemaphoreType.DMA((3,)),
            pltpu.SemaphoreType.DMA((3,)),
        ],
        compiler_params=pltpu.CompilerParams(collective_id=number, has_side_effects=True),
    )(flat)
    return total.reshape(k, t)


def gain_peers():
    peers = []
    for d in range(1, 8):
        peers.append({"row": flip("row", d & 3), "dp": flip("dp", d >> 2)})
    return peers


def last_kernel(p_ref, gains_ref, out_ref, total_ref, slots, *refs):
    buffers, (send_sem, recv_sem) = refs[:7], refs[7:]
    half = out_ref.shape[0] // 2
    me = side("dp") * 4 + lax.axis_index("row")
    to_x, _, to_c = neighbours()
    peers = gain_peers()
    greet([to_x, to_c] + peers)
    started = []
    send = sender(send_sem, recv_sem, started)
    copies = [send(gains_ref, slots.at[me], 14 + d, peer) for d, peer in enumerate(peers)]
    slots[me] = gains_ref[...]
    low, high = scatter_flow(p_ref, buffers, send)
    out_ref[:half, :] = low
    out_ref[half:, :] = high
    for copy in copies:
        copy.wait_recv()
    total = slots[0]
    for i in range(1, 8):
        total = total + slots[i]
    total_ref[...] = total
    for copy in started:
        copy.wait_send()


def last_scatter(partial, gains, number):
    rows, width = partial.shape[0] // 2, partial.shape[1] // 4
    flat = gains.reshape(-1, 128)
    vmem = pl.BlockSpec(memory_space=pltpu.VMEM)
    out, total = pl.pallas_call(
        last_kernel,
        name="scatter_projected",
        out_shape=(
            jax.ShapeDtypeStruct((rows, width), f32),
            jax.ShapeDtypeStruct(flat.shape, f32),
        ),
        in_specs=[vmem, vmem],
        out_specs=(vmem, vmem),
        scratch_shapes=[pltpu.VMEM((8,) + flat.shape, f32)]
        + scatter_buffers(rows, width)
        + [pltpu.SemaphoreType.DMA((21,)), pltpu.SemaphoreType.DMA((21,))],
        compiler_params=pltpu.CompilerParams(
            collective_id=number, has_side_effects=True, vmem_limit_bytes=48 * 2**20
        ),
        cost_estimate=COST,
    )(partial, flat)
    return out, total.reshape(gains.shape)


def row_peers():
    return [(d, {"row": flip("row", d)}) for d in (3, 2, 1)]


def unit_view(ref, unit, tok, heads):
    rows = pl.ds(pl.multiple_of((unit // heads) * tok, tok), tok)
    cols = pl.ds(pl.multiple_of((unit % heads) * HEAD_DIM, HEAD_DIM), HEAD_DIM)
    return ref.at[rows, cols]


def turn_kernel(back, tok, heads, x_ref, out_ref, local_sem, send_sem, recv_sem):
    z = lax.axis_index("row")
    greet([peer for _, peer in row_peers()])
    started = []
    send = sender(send_sem, recv_sem, started)

    def line(ref, i):
        return ref.at[pl.ds(pl.multiple_of(i * tok, tok), tok)]

    def ends(i):
        if back:
            return line(x_ref, i), unit_view(out_ref, z, tok, heads)
        return unit_view(x_ref, i, tok, heads), line(out_ref, z)

    for d, peer in row_peers():
        send(*ends(z ^ d), d - 1, peer)
    own = pltpu.make_async_copy(*ends(z), local_sem)
    own.start()
    for copy in started:
        copy.wait()
    own.wait()


def turn(values, back, tok, heads, number, name):
    shape = (2 * tok, heads * HEAD_DIM) if back else (2 * heads * tok, HEAD_DIM)
    return pl.pallas_call(
        functools.partial(turn_kernel, back, tok, heads),
        name=name,
        out_shape=jax.ShapeDtypeStruct(shape, values.dtype),
        in_specs=[pl.BlockSpec(memory_space=pltpu.VMEM)],
        out_specs=pl.BlockSpec(memory_space=pl.ANY),
        scratch_shapes=[
            pltpu.SemaphoreType.DMA,
            pltpu.SemaphoreType.DMA((3,)),
            pltpu.SemaphoreType.DMA((3,)),
        ],
        compiler_params=pltpu.CompilerParams(collective_id=number, has_side_effects=True),
        cost_estimate=COST,
    )(values)


def totals(stat, slots, started):
    for copy in started:
        copy.wait_recv()
    total = slots[0]
    for i in range(1, 8):
        total = total + slots[i]
    return total


def front_kernel(
    width,
    qkv_ref,
    cos_ref,
    sin_ref,
    gain_ref,
    out_ref,
    inv_ref,
    turned,
    packed,
    stat,
    slots,
    local_sem,
    stat_send,
    stat_recv,
    send_sem,
    recv_sem,
):
    count, tok = qkv_ref.shape[0], cos_ref.shape[0]
    part = qkv_ref.shape[1] // 3
    heads = part // HEAD_DIM
    z = lax.axis_index("row")
    me = side("dp") * 4 + lax.axis_index("col")
    peers = feature_peers(True)
    greet(peers + [peer for _, peer in row_peers()])
    for i in range(2):
        values = qkv_ref[:, i * part : (i + 1) * part]
        stat[i : i + 1, :] = jnp.sum(values * values, axis=1, keepdims=True).T
    started, moved, local = [], [], []
    send = sender(stat_send, stat_recv, started)
    for d, peer in enumerate(peers):
        send(stat, slots.at[me], d, peer)
    slots[me] = stat[...]
    move = sender(send_sem, recv_sem, moved)

    def ship(i):
        for d, peer in row_peers():
            move(packed.at[z ^ d, i], out_ref.at[z, i], 3 * i + d - 1, peer)
        copy = pltpu.make_async_copy(packed.at[z, i], out_ref.at[z, i], local_sem.at[i])
        copy.start()
        local.append(copy)

    def spots():
        return [(s, h, s * heads + h) for s in range(2) for h in range(heads)]

    for s, h, unit in spots():
        packed[unit, 2] = qkv_ref[
            s * tok : (s + 1) * tok, 2 * part + h * HEAD_DIM : 2 * part + (h + 1) * HEAD_DIM
        ].astype(bf16)
    ship(2)
    for i in (1, 0):
        for s, h, unit in spots():
            values = (
                qkv_ref[s * tok : (s + 1) * tok, i * part + h * HEAD_DIM : i * part + (h + 1) * HEAD_DIM]
                * gain_ref[i : i + 1, h * HEAD_DIM : (h + 1) * HEAD_DIM]
            )
            turned[i, unit] = values * cos_ref[...] + pltpu.roll(values, HEAD_DIM // 2, 1) * sin_ref[...]
    inverse = lax.rsqrt(totals(stat, slots, started) / width + norm_eps)
    inv_ref[...] = inverse
    for i in (1, 0):
        column = inverse[i : i + 1, :].T
        for s, h, unit in spots():
            packed[unit, i] = (turned[i, unit] * column[s * tok : (s + 1) * tok]).astype(bf16)
        ship(i)
    for copy in moved:
        copy.wait()
    for copy in local:
        copy.wait()
    for copy in started:
        copy.wait_send()


def front(qkv, cosine, sine_signed, gains, width, units, number):
    count, tok = qkv.shape[0], cosine.shape[0]
    return pl.pallas_call(
        functools.partial(front_kernel, width),
        name="front",
        out_shape=(
            jax.ShapeDtypeStruct((units, 3, tok, HEAD_DIM), bf16),
            jax.ShapeDtypeStruct((2, count), f32),
        ),
        in_specs=[pl.BlockSpec(memory_space=pltpu.VMEM)] * 4,
        out_specs=(pl.BlockSpec(memory_space=pl.ANY), pl.BlockSpec(memory_space=pltpu.VMEM)),
        scratch_shapes=[
            pltpu.VMEM((2, units, tok, HEAD_DIM), f32),
            pltpu.VMEM((units, 3, tok, HEAD_DIM), bf16),
            pltpu.VMEM((2, count), f32),
            pltpu.VMEM((8, 2, count), f32),
            pltpu.SemaphoreType.DMA((3,)),
            pltpu.SemaphoreType.DMA((7,)),
            pltpu.SemaphoreType.DMA((7,)),
            pltpu.SemaphoreType.DMA((9,)),
            pltpu.SemaphoreType.DMA((9,)),
        ],
        compiler_params=pltpu.CompilerParams(
            collective_id=number, has_side_effects=True, vmem_limit_bytes=40 * 2**20
        ),
        cost_estimate=COST,
    )(qkv, cosine, sine_signed, gains)


def rear_kernel(
    width,
    d_ref,
    qkv_ref,
    cos_ref,
    sin_ref,
    gain_ref,
    inv_ref,
    out_ref,
    sums_ref,
    landed,
    normed,
    stat,
    slots,
    stat_send,
    stat_recv,
    send_sem,
    recv_sem,
):
    count, tok = qkv_ref.shape[0], cos_ref.shape[0]
    part = qkv_ref.shape[1] // 3
    heads = part // HEAD_DIM
    z = lax.axis_index("row")
    me = side("dp") * 4 + lax.axis_index("col")
    peers = feature_peers(True)
    greet(peers + [peer for _, peer in row_peers()])
    started, moved = [], []
    move = sender(send_sem, recv_sem, moved)
    for i in (0, 1):
        for d, peer in row_peers():
            there = pl.ds(pl.multiple_of((z ^ d) * tok, tok), tok)
            move(d_ref.at[i, there], landed.at[z, i], 3 * i + d - 1, peer)
    here = pl.ds(pl.multiple_of(z * tok, tok), tok)
    for i in (0, 1):
        landed[z, i] = d_ref[i, here, :]
    for i in (0, 1):
        for copy in moved[3 * i : 3 * i + 3]:
            copy.wait_recv()
        for h in range(heads):
            cols = slice(i * part + h * HEAD_DIM, i * part + (h + 1) * HEAD_DIM)
            gain = gain_ref[i : i + 1, h * HEAD_DIM : (h + 1) * HEAD_DIM]
            raw = jnp.zeros((1, HEAD_DIM), f32)
            for s in range(2):
                rows = slice(s * tok, (s + 1) * tok)
                values = landed[s * heads + h, i].astype(f32)
                back = values * cos_ref[...] - pltpu.roll(values, HEAD_DIM // 2, 1) * sin_ref[...]
                pre = qkv_ref[rows, cols]
                inverse = inv_ref[i : i + 1, rows].T
                crossed = back * pre
                raw = raw + jnp.sum(crossed * inverse, axis=0, keepdims=True)
                partial = jnp.sum(crossed * gain, axis=1, keepdims=True).T
                if h == 0:
                    stat[i : i + 1, rows] = partial
                else:
                    stat[i : i + 1, rows] = stat[i : i + 1, rows] + partial
                normed[rows, cols] = back * gain
            sums_ref[i : i + 1, h * HEAD_DIM : (h + 1) * HEAD_DIM] = raw
    send = sender(stat_send, stat_recv, started)
    for d, peer in enumerate(peers):
        send(stat, slots.at[me], d, peer)
    slots[me] = stat[...]
    inner = totals(stat, slots, started) / width
    for i in (0, 1):
        inverse = inv_ref[i : i + 1, :]
        first = inverse.T
        second = (inverse * inverse * inverse * inner[i : i + 1, :]).T
        cols = slice(i * part, (i + 1) * part)
        out_ref[:, cols] = (first * normed[:, cols] - qkv_ref[:, cols] * second).astype(bf16)
    for copy in moved + started:
        copy.wait_send()


def rear(d_units, qkv, cosine, sine_signed, gains, inverse, width, number):
    count, tok = qkv.shape[0], cosine.shape[0]
    part = qkv.shape[1] // 3
    units = d_units.shape[1] // tok
    return pl.pallas_call(
        functools.partial(rear_kernel, width),
        name="rear",
        out_shape=(
            jax.ShapeDtypeStruct((count, 2 * part), bf16),
            jax.ShapeDtypeStruct((2, part), f32),
        ),
        in_specs=[pl.BlockSpec(memory_space=pltpu.VMEM)] * 6,
        out_specs=[pl.BlockSpec(memory_space=pltpu.VMEM)] * 2,
        scratch_shapes=[
            pltpu.VMEM((units, 2, tok, HEAD_DIM), bf16),
            pltpu.VMEM((count, 2 * part), f32),
            pltpu.VMEM((2, count), f32),
            pltpu.VMEM((8, 2, count), f32),
            pltpu.SemaphoreType.DMA((7,)),
            pltpu.SemaphoreType.DMA((7,)),
            pltpu.SemaphoreType.DMA((6,)),
            pltpu.SemaphoreType.DMA((6,)),
        ],
        compiler_params=pltpu.CompilerParams(
            collective_id=number, has_side_effects=True, vmem_limit_bytes=40 * 2**20
        ),
        cost_estimate=COST,
    )(d_units, qkv, cosine, sine_signed, gains, inverse)


BLOCK = 512


def attend_kernel(len_ref, q_ref, k_ref, v_ref, o_ref, o32_ref, lse_ref):
    i = pl.program_id(0)
    bq, bk = q_ref.shape[0], BLOCK
    length = len_ref[0]
    scale = HEAD_DIM ** (-0.5)
    q = q_ref[...]
    rows = i * bq + lax.broadcasted_iota(jnp.int32, (bq, bk), 0)
    cols0 = lax.broadcasted_iota(jnp.int32, (bq, bk), 1)

    def step(j, carry, masked):
        top, total, acc = carry
        j0 = pl.multiple_of(j * bk, bk)
        scores = contract_last(q, k_ref[pl.ds(j0, bk), :]) * scale
        if masked:
            cols = j0 + cols0
            scores = jnp.where((cols <= rows) & (cols < length), scores, masked_score)
        new = jnp.maximum(top, jnp.max(scores, axis=1, keepdims=True))
        weights = jnp.exp(scores - new)
        fix = jnp.exp(top - new)
        total = total * fix + jnp.sum(weights, axis=1, keepdims=True)
        acc = acc * fix + matmul(weights.astype(bf16), v_ref[pl.ds(j0, bk), :])
        return new, total, acc

    carry = (
        jnp.full((bq, 1), -jnp.inf, f32),
        jnp.zeros((bq, 1), f32),
        jnp.zeros((bq, HEAD_DIM), f32),
    )
    whole = jnp.minimum(i, length // bk)
    last = jnp.minimum(i + 1, (length + bk - 1) // bk)
    carry = lax.fori_loop(0, whole, lambda j, s: step(j, s, False), carry)
    top, total, acc = lax.fori_loop(whole, last, lambda j, s: step(j, s, True), carry)
    out = acc / total
    o_ref[...] = out.astype(bf16)
    o32_ref[...] = out
    lse_ref[...] = jnp.broadcast_to((top + jnp.log(total)).T, lse_ref.shape)


def attend(length, q, k, v):
    slots = q.shape[0]
    whole = pl.BlockSpec((slots, HEAD_DIM), lambda i: (0, 0))
    part = pl.BlockSpec((BLOCK, HEAD_DIM), lambda i: (i, 0))
    return pl.pallas_call(
        attend_kernel,
        name="attend",
        grid=(slots // BLOCK,),
        out_shape=(
            jax.ShapeDtypeStruct((slots, HEAD_DIM), bf16),
            jax.ShapeDtypeStruct((slots, HEAD_DIM), f32),
            jax.ShapeDtypeStruct((8, slots), f32),
        ),
        in_specs=[pl.BlockSpec(memory_space=pltpu.SMEM), part, whole, whole],
        out_specs=(part, part, pl.BlockSpec((8, BLOCK), lambda i: (0, i))),
        cost_estimate=COST,
    )(length, q, k, v)


def attend_back_kernel(
    len_ref, q_ref, k_ref, v_ref, do_ref, o_ref, lse_ref, out_ref, dv_ref, dq_acc, delta_ref
):
    j = pl.program_id(0)
    bk, bq = k_ref.shape[0], BLOCK
    slots = q_ref.shape[0]
    length = len_ref[0]
    scale = HEAD_DIM ** (-0.5)

    @pl.when(j == 0)
    def _():
        dq_acc[...] = jnp.zeros_like(dq_acc)
        for i in range(slots // bq):
            here = slice(i * bq, (i + 1) * bq)
            product = do_ref[here, :].astype(f32) * o_ref[here, :]
            delta_ref[0:1, here] = jnp.sum(product, axis=1, keepdims=True).T

    k, v = k_ref[...], v_ref[...]
    j0 = j * bk
    cols = j0 + lax.broadcasted_iota(jnp.int32, (bk, bq), 0)
    rows0 = lax.broadcasted_iota(jnp.int32, (bk, bq), 1)

    def step(i, carry, masked):
        dk, dv = carry
        i0 = pl.multiple_of(i * bq, bq)
        here = pl.ds(i0, bq)
        q, do = q_ref[here, :], do_ref[here, :]
        scores = contract_last(k, q) * scale
        if masked:
            scores = jnp.where((cols <= i0 + rows0) & (cols < length), scores, masked_score)
        probs = jnp.exp(scores - lse_ref[0:1, here])
        dv = dv + matmul(probs.astype(bf16), do)
        d_probs = contract_last(v, do)
        d_scores = (probs * (d_probs - delta_ref[0:1, here])).astype(bf16)
        dk = dk + matmul(d_scores, q)
        dq_acc[here, :] += contract_first(d_scores, k)
        return dk, dv

    zero = jnp.zeros((bk, HEAD_DIM), f32)
    top = slots // bq
    first = jnp.where(j0 + bk <= length, j + 1, top)
    first = jnp.where(j0 < length, first, j)
    stop = jnp.where(j0 < length, top, j)
    carry = lax.fori_loop(j, first, lambda i, s: step(i, s, True), (zero, zero))
    dk, dv = lax.fori_loop(first, stop, lambda i, s: step(i, s, False), carry)
    there = pl.ds(pl.multiple_of(j0, bk), bk)
    out_ref[1, there, :] = (dk * scale).astype(bf16)
    dv_ref[...] = dv.astype(bf16)

    @pl.when(j == pl.num_programs(0) - 1)
    def _():
        out_ref[0] = (dq_acc[...] * scale).astype(bf16)


def attend_back(length, q, k, v, do, o, lse):
    slots = q.shape[0]
    whole = pl.BlockSpec((slots, HEAD_DIM), lambda j: (0, 0))
    part = pl.BlockSpec((BLOCK, HEAD_DIM), lambda j: (j, 0))
    line = pl.BlockSpec((8, slots), lambda j: (0, 0))
    return pl.pallas_call(
        attend_back_kernel,
        name="attend_back",
        grid=(slots // BLOCK,),
        out_shape=(
            jax.ShapeDtypeStruct((2, slots, HEAD_DIM), bf16),
            jax.ShapeDtypeStruct((slots, HEAD_DIM), bf16),
        ),
        in_specs=[pl.BlockSpec(memory_space=pltpu.SMEM), whole, part, part, whole, whole, line],
        out_specs=(pl.BlockSpec((2, slots, HEAD_DIM), lambda j: (0, 0, 0)), part),
        scratch_shapes=[pltpu.VMEM((slots, HEAD_DIM), f32), pltpu.VMEM((8, slots), f32)],
        cost_estimate=COST,
    )(length, q, k, v, do, o, lse)


def per_device(
    tokens,
    seq_lengths,
    w_query,
    w_key,
    w_value,
    w_out,
    w_gate,
    w_up,
    w_down,
    q_gain,
    k_gain,
    attn_gain,
    mlp_gain,
    cotangent,
):
    tok_rows, feat_part = tokens.shape
    row_count, data_count = lax.axis_size("row"), lax.axis_size("dp")
    width = feat_part * lax.axis_size("col")
    slots = tok_rows * row_count
    half_feat = feat_part // 2
    y, z = side("dp"), lax.axis_index("row")
    heads = half_feat // HEAD_DIM
    pairs = [(i, i ^ 1) for i in range(data_count)]
    after = lambda values, *done: lax.optimization_barrier((values,) + done)[0]

    def y_half(values, axis):
        size = values.shape[axis] // 2
        return lax.dynamic_slice_in_dim(values, y * size, size, axis)

    qkv_weight = lax.all_gather(
        jnp.concatenate([y_half(w_query, 1), y_half(w_key, 1), y_half(w_value, 1)], axis=1),
        "row",
        axis=0,
        tiled=True,
    )
    out_weight = lax.all_gather(y_half(w_out, 0), "row", axis=1, tiled=True)
    gate_up_weight = lax.all_gather(
        jnp.concatenate([y_half(w_gate, 1), y_half(w_up, 1)], axis=1), "row", axis=0, tiled=True
    )
    hidden_part = gate_up_weight.shape[1] // 2
    gate_weight, up_weight = gate_up_weight[:, :hidden_part], gate_up_weight[:, hidden_part:]
    down_half = y_half(w_down, 0)
    split = down_half.shape[1] // 2
    low_weight = lax.all_gather(down_half[:, :split], "row", axis=1, tiled=True)

    positions = z * tok_rows + jnp.arange(tok_rows)
    length = seq_lengths[0]
    valid = (positions < length).astype(f32)[:, None]
    cosine, sine = rope_tables(positions, HEAD_DIM)
    sine_signed = jnp.where(jnp.arange(HEAD_DIM)[None, :] < HEAD_DIM // 2, -sine, sine)
    other_length = lax.ppermute(seq_lengths, "dp", pairs)
    pair_lengths = jnp.where(
        y == 0,
        jnp.concatenate([seq_lengths, other_length]),
        jnp.concatenate([other_length, seq_lengths]),
    )
    unit_length = lax.dynamic_slice_in_dim(pair_lengths, z // heads, 1)
    qk_gain = jnp.stack([y_half(q_gain, 0), y_half(k_gain, 0)])

    tokens_wide = gather_wide(tokens, 0, "gather_tokens")
    high_weight = lax.all_gather(after(down_half[:, split:], tokens_wide), "row", axis=1, tiled=True)
    qkv = matmul(tokens_wide, qkv_weight)
    units, inverse = front(qkv, cosine, sine_signed, qk_gain, width, 2 * heads, 2)
    q_unit, k_unit, v_unit = (units[:, i].reshape(slots, HEAD_DIM) for i in range(3))
    attn_unit, attn_exact, log_total = attend(unit_length, q_unit, k_unit, v_unit)
    attn_low = turn(attn_unit, True, tok_rows, heads, 3, "turn_attn")
    branch = scatter_wide(matmul(attn_low, out_weight).astype(bf16), 4, "scatter_branch")
    branch_inv = lax.rsqrt(
        feature_total(jnp.sum(branch * branch, axis=1)[None, :], 5, "total_branch")[0] / width
        + norm_eps
    )[:, None]
    resid = tokens.astype(f32) + branch * branch_inv * attn_gain
    resid_wide = gather_wide(resid.astype(bf16), 6, "gather_resid")
    gate = matmul(resid_wide, gate_weight)
    upper = matmul(resid_wide, up_weight)
    sigma = jax.nn.sigmoid(gate)
    hidden = (gate * sigma * upper).astype(bf16)
    mixed_low = scatter_wide(matmul(hidden, low_weight).astype(bf16), 7, "scatter_mixed_low")
    high_weight = after(high_weight, mixed_low)
    incoming = cotangent.astype(f32) * valid
    factor = 1.0 / math.sqrt(slots * data_count)
    block_output, mlp_gain_raw, d_high, d_low_wide = mixed_junction(
        matmul(hidden, high_weight).astype(bf16),
        mixed_low,
        incoming,
        resid,
        valid.T,
        mlp_gain[None, :],
        width,
        17,
    )
    low_raw = (contract_first(hidden, d_low_wide) * factor).astype(bf16)
    d_high_wide = gather_wide(after(d_high, low_raw), 18, "gather_d_mixed_high")
    high_raw = (contract_first(hidden, d_high_wide) * factor).astype(bf16)

    def cut(values, index, count, axis):
        size = values.shape[axis] // count
        return lax.dynamic_slice_in_dim(values, index * size, size, axis)

    def over_dp(piece):
        if data_count > 2:
            groups = [list(range(s, data_count, 2)) for s in (0, 1)]
            piece = lax.psum(piece, "dp", axis_index_groups=groups)
        return piece

    def two_sides(piece, other, bit, axis):
        low = jnp.where(bit == 0, piece, other)
        high = jnp.where(bit == 0, other, piece)
        return jnp.concatenate([low, high], axis=axis)

    def from_twin(piece):
        return lax.ppermute(piece, "dp", pairs)

    def reduce_rows(raw, axis):
        return lax.psum_scatter(raw, "row", scatter_dimension=axis, tiled=True)

    d_hidden = contract_last(d_low_wide, low_weight) + contract_last(d_high_wide, high_weight)
    d_gate = (d_hidden * upper * sigma * (1.0 + gate * (1.0 - sigma))).astype(bf16)
    d_upper = (d_hidden * gate * sigma).astype(bf16)
    gate_raw = (contract_first(resid_wide, d_gate) * factor).astype(bf16)
    up_raw = (contract_first(resid_wide, d_upper) * factor).astype(bf16)
    d_resid_wide = (
        contract_last(d_gate, gate_weight) + contract_last(d_upper, up_weight)
    ).astype(bf16)
    d_resid_wide, low_piece = lax.optimization_barrier(
        (after(d_resid_wide, high_raw, gate_raw, up_raw), reduce_rows(low_raw, 1))
    )
    down_piece = jnp.concatenate([low_piece, reduce_rows(high_raw, 1)], axis=1)
    gate_piece, up_piece = reduce_rows(gate_raw, 0), reduce_rows(up_raw, 0)
    d_resid, attn_gain_raw, d_branch_wide = d_resid_junction(
        d_resid_wide, incoming, branch, branch_inv.T, attn_gain[None, :], width, 10
    )
    down_piece = over_dp(down_piece)
    d_branch_wide, down_piece = lax.optimization_barrier((d_branch_wide, down_piece))
    d_attn = contract_last(d_branch_wide, out_weight).astype(bf16)
    other_down = from_twin(down_piece)
    d_attn_unit, other_down = lax.optimization_barrier(
        (turn(d_attn, False, tok_rows, heads, 13, "turn_d_attn"), other_down)
    )
    out_raw = (contract_first(attn_low, after(d_branch_wide, d_attn_unit)) * factor).astype(bf16)
    d_attn_unit = after(d_attn_unit, out_raw)
    out_piece = reduce_rows(out_raw, 1)
    d_units, d_value_unit = attend_back(
        unit_length, q_unit, k_unit, v_unit, d_attn_unit, attn_exact, log_total
    )
    d_value = turn(d_value_unit, True, tok_rows, heads, 12, "turn_d_value")
    v_raw = (contract_first(tokens_wide, d_value) * factor).astype(bf16)
    v_piece = reduce_rows(v_raw, 0)
    d_units, gate_piece = lax.optimization_barrier((after(d_units, v_raw), over_dp(gate_piece)))
    other_gate = from_twin(gate_piece)
    d_qk, gain_sums = rear(d_units, qkv, cosine, sine_signed, qk_gain, inverse, width, 14)
    d_qk, gain_sums, other_gate, up_piece = lax.optimization_barrier(
        (d_qk, gain_sums, other_gate, over_dp(up_piece))
    )
    other_up = from_twin(up_piece)
    qk_raw = (contract_first(tokens_wide, d_qk) * factor).astype(bf16)
    d_qkv = jnp.concatenate([after(d_qk, qk_raw), d_value], axis=1)
    projected = contract_last(d_qkv, qkv_weight).astype(bf16)
    qk_piece = over_dp(reduce_rows(qk_raw, 0))

    def spread(half):
        return lax.dynamic_update_slice_in_dim(jnp.zeros((feat_part,), f32), half, y * half_feat, 0)

    gains_raw = jnp.stack(
        [spread(gain_sums[0]), spread(gain_sums[1]), attn_gain_raw[0], mlp_gain_raw[0]]
    )
    scattered, gains = last_scatter(projected, gains_raw * factor, 16)
    scattered, gains, out_piece, v_piece = lax.optimization_barrier(
        (scattered, gains, over_dp(out_piece), over_dp(v_piece))
    )
    other_out, other_v = from_twin(out_piece), from_twin(v_piece)
    input_grad = d_resid + scattered
    gains = over_dp(gains)
    input_grad, qk_piece, other_down, other_gate, other_up = lax.optimization_barrier(
        (input_grad, qk_piece, other_down, other_gate, other_up)
    )

    def whole(piece, other, axis):
        return two_sides(piece, other, y, axis).astype(f32)

    qk_other = from_twin(qk_piece)
    q_grad, k_grad = (
        whole(cut(qk_piece, i, 2, 1), cut(qk_other, i, 2, 1), 1) for i in range(2)
    )
    v_grad = whole(v_piece, other_v, 1)
    return (
        block_output,
        input_grad,
        q_grad,
        k_grad,
        v_grad,
        whole(out_piece, other_out, 0),
        whole(gate_piece, other_gate, 1),
        whole(up_piece, other_up, 1),
        whole(down_piece, other_down, 0),
        gains[0],
        gains[1],
        gains[2],
        gains[3],
    )


def solution(mesh):
    tok, row_col, col_row, gain = P(("dp", "row"), "col"), P("row", "col"), P("col", "row"), P("col")
    weights = (row_col, row_col, row_col, col_row, row_col, row_col, col_row)
    gains = (gain, gain, gain, gain)
    return jax.shard_map(
        per_device,
        mesh=mesh,
        in_specs=(tok, P("dp")) + weights + gains + (tok,),
        out_specs=(tok, tok) + weights + gains,
        check_vma=False,
    )
```

```python
import functools
import math

import jax
import jax.numpy as jnp
from jax import lax
from jax.experimental import pallas as pl
from jax.experimental.pallas import tpu as pltpu
from jax.sharding import PartitionSpec as P

HEAD_DIM = 128
rope_base = 500000.0
norm_eps = 1e-06
masked_score = -1e30

MESH = pl.DeviceIdType.MESH
bf16 = jnp.bfloat16
f32 = jnp.float32
COST = pl.CostEstimate(flops=0, bytes_accessed=1000, transcendentals=0)


def rope_tables(positions, head_dim):
    half = head_dim // 2
    freq = 1.0 / rope_base ** (jnp.arange(half, dtype=f32) / half)
    angle = positions.astype(f32)[:, None] * freq[None, :]
    angle = jnp.concatenate([angle, angle], axis=1)
    return (jnp.cos(angle), jnp.sin(angle))


def matmul(left, right):
    return jnp.dot(left, right, preferred_element_type=f32)


def contract_first(left, right):
    return lax.dot_general(left, right, (((0,), (0,)), ((), ())), preferred_element_type=f32)


def contract_last(left, right):
    return lax.dot_general(left, right, (((1,), (1,)), ((), ())), preferred_element_type=f32)


def flip(axis, bit):
    return lax.axis_index(axis) ^ bit


def side(axis):
    return lax.axis_index(axis) & 1


def greet(peers):
    barrier = pltpu.get_barrier_semaphore()
    for peer in peers:
        pl.semaphore_signal(barrier, inc=1, device_id=peer, device_id_type=MESH)
    pl.semaphore_wait(barrier, len(peers))


def sender(send_sem, recv_sem, started):
    def send(src, dst, number, peer):
        copy = pltpu.make_async_remote_copy(
            src_ref=src,
            dst_ref=dst,
            send_sem=send_sem.at[number],
            recv_sem=recv_sem.at[number],
            device_id=peer,
            device_id_type=MESH,
        )
        copy.start()
        started.append(copy)
        return copy

    return send


def neighbours():
    return {"col": flip("col", 2)}, {"dp": flip("dp", 1)}, {"col": flip("col", 1)}


def gather_flow(x_ref, out_ref, local_sem, send, base, meanwhile=None):
    rows, width = x_ref.shape
    half = rows // 2
    y, b = side("dp"), lax.axis_index("col")
    to_x, to_y, to_c = neighbours()

    def slot(yy, h, bb, n=half):
        return out_ref.at[
            pl.ds(pl.multiple_of(yy * rows + h * half, half), n),
            pl.ds(pl.multiple_of(bb * width, width), width),
        ]

    low, high = x_ref.at[pl.ds(0, half)], x_ref.at[pl.ds(half, half)]
    own = pltpu.make_async_copy(x_ref, slot(y, 0, b, rows), local_sem)
    xa = send(low, slot(y, 0, b), base + 0, to_x)
    ya = send(high, slot(y, 1, b), base + 1, to_y)
    core = [send(low, slot(y, 0, b), base + 6, to_c)]
    yb = send(low, slot(y, 0, b), base + 2, to_y)
    xb = send(high, slot(y, 1, b), base + 3, to_x)
    core.append(send(high, slot(y, 1, b), base + 7, to_c))
    own.start()
    if meanwhile is not None:
        meanwhile()
    xa.wait_recv()
    piece = slot(y, 0, b ^ 2)
    yc = send(piece, piece, base + 4, to_y)
    core.append(send(piece, piece, base + 8, to_c))
    ya.wait_recv()
    piece = slot(y ^ 1, 1, b)
    xc = send(piece, piece, base + 5, to_x)
    core.append(send(piece, piece, base + 9, to_c))
    yb.wait_recv()
    piece = slot(y ^ 1, 0, b)
    core.append(send(piece, piece, base + 10, to_c))
    xb.wait_recv()
    piece = slot(y, 1, b ^ 2)
    core.append(send(piece, piece, base + 11, to_c))
    yc.wait_recv()
    piece = slot(y ^ 1, 0, b ^ 2)
    core.append(send(piece, piece, base + 12, to_c))
    xc.wait_recv()
    piece = slot(y ^ 1, 1, b ^ 2)
    core.append(send(piece, piece, base + 13, to_c))
    for copy in core:
        copy.wait_recv()
    own.wait()


def gather_kernel(x_ref, out_ref, local_sem, send_sem, recv_sem):
    greet(neighbours())
    started = []
    gather_flow(x_ref, out_ref, local_sem, sender(send_sem, recv_sem, started), 0)
    for copy in started:
        copy.wait_send()


def gather_wide(values, number, name):
    rows, width = values.shape
    return pl.pallas_call(
        gather_kernel,
        name=name,
        out_shape=jax.ShapeDtypeStruct((2 * rows, 4 * width), values.dtype),
        in_specs=[pl.BlockSpec(memory_space=pltpu.VMEM)],
        out_specs=pl.BlockSpec(memory_space=pl.ANY),
        scratch_shapes=[
            pltpu.SemaphoreType.DMA,
            pltpu.SemaphoreType.DMA((14,)),
            pltpu.SemaphoreType.DMA((14,)),
        ],
        compiler_params=pltpu.CompilerParams(collective_id=number, has_side_effects=True),
        cost_estimate=COST,
    )(values)


def scatter_flow(p_ref, buffers, send):
    rc, s1, ry, rx, s2, fy, fx = buffers
    rows, width = p_ref.shape[0] // 2, p_ref.shape[1] // 4
    half = rows // 2
    y, b = side("dp"), lax.axis_index("col")
    x, c = b >> 1, b & 1
    to_x, to_y, to_c = neighbours()

    def place(yy, h):
        return pl.ds(pl.multiple_of(yy * rows + h * half, half), half)

    def column(bb):
        return pl.ds(pl.multiple_of(bb * width, width), width)

    order = [(0, y ^ 1, 0), (1, y ^ 1, 0), (x ^ 1, 0, 1), (x ^ 1, 1, 1)]
    order += [(0, y, 0), (1, y, 0), (x, 0, 1), (x, 1, 1)]
    core = [
        send(
            p_ref.at[place(yy, h), column(2 * xx + (c ^ 1))],
            rc.at[xx, place(yy, h)],
            number,
            to_c,
        )
        for number, (xx, yy, h) in enumerate(order)
    ]

    def settle(*numbers):
        for number in numbers:
            core[number].wait_recv()
            xx, yy, h = order[number]
            s1[xx, place(yy, h), :] = (
                p_ref[place(yy, h), column(2 * xx + c)].astype(f32)
                + rc[xx, place(yy, h), :].astype(f32)
            ).astype(s1.dtype)

    settle(0, 1, 2, 3)
    ya, xa = [], []
    for i in range(2):
        ya.append(send(s1.at[i, place(y ^ 1, 0), :], ry.at[i], 8 + i, to_y))
        xa.append(send(s1.at[x ^ 1, pl.ds(i * rows + half, half), :], rx.at[i], 10 + i, to_x))
    settle(4, 5, 6, 7)
    for copy in ya:
        copy.wait_recv()
    s2[0] = (s1[x ^ 1, place(y, 0), :].astype(f32) + ry[x ^ 1].astype(f32)).astype(s2.dtype)
    xb = send(s2.at[0], fx, 12, to_x)
    for copy in xa:
        copy.wait_recv()
    s2[1] = (s1[x, place(y ^ 1, 1), :].astype(f32) + rx[y ^ 1].astype(f32)).astype(s2.dtype)
    yb = send(s2.at[1], fy, 13, to_y)
    keep = s1[x, place(y, 0), :].astype(f32) + ry[x].astype(f32)
    xb.wait_recv()
    low = keep + fx[...].astype(f32)
    keep = s1[x, place(y, 1), :].astype(f32) + rx[y].astype(f32)
    yb.wait_recv()
    return low, keep + fy[...].astype(f32)


def scatter_buffers(rows, width):
    half = rows // 2
    return [
        pltpu.VMEM((2, 2 * rows, width), bf16),
        pltpu.VMEM((2, 2 * rows, width), bf16),
        pltpu.VMEM((2, half, width), bf16),
        pltpu.VMEM((2, half, width), bf16),
        pltpu.VMEM((2, half, width), bf16),
        pltpu.VMEM((half, width), bf16),
        pltpu.VMEM((half, width), bf16),
    ]


def scatter_kernel(p_ref, out_ref, *refs):
    buffers, (send_sem, recv_sem) = refs[:7], refs[7:]
    half = out_ref.shape[0] // 2
    greet(neighbours())
    started = []
    low, high = scatter_flow(p_ref, buffers, sender(send_sem, recv_sem, started))
    out_ref[:half, :] = low
    out_ref[half:, :] = high
    for copy in started:
        copy.wait_send()


def scatter_wide(partial, number, name):
    rows, width = partial.shape[0] // 2, partial.shape[1] // 4
    return pl.pallas_call(
        scatter_kernel,
        name=name,
        out_shape=jax.ShapeDtypeStruct((rows, width), f32),
        in_specs=[pl.BlockSpec(memory_space=pltpu.VMEM)],
        out_specs=pl.BlockSpec(memory_space=pltpu.VMEM),
        scratch_shapes=scatter_buffers(rows, width)
        + [pltpu.SemaphoreType.DMA((14,)), pltpu.SemaphoreType.DMA((14,))],
        compiler_params=pltpu.CompilerParams(
            collective_id=number, has_side_effects=True, vmem_limit_bytes=48 * 2**20
        ),
        cost_estimate=COST,
    )(partial)


def exchange(stat, slots, send, base):
    me = lax.axis_index("col")
    copies = [send(stat, slots.at[me], base + d, peer) for d, peer in enumerate(feature_peers(False))]
    slots[me] = stat[...]
    return copies


def column_total(slots, copies):
    for copy in copies:
        copy.wait_recv()
    return (slots[0] + slots[1]) + (slots[2] + slots[3])


def junction_peers():
    to_x, to_y, to_c = neighbours()
    return [to_x, to_y, to_c, {"col": flip("col", 3)}]


def mixed_kernel(
    width,
    p_ref,
    low_ref,
    incoming_ref,
    resid_ref,
    valid_ref,
    gain_ref,
    block_ref,
    raw_ref,
    rest_ref,
    wide_ref,
    mixed,
    x_ref,
    stat,
    slots,
    *refs,
):
    buffers, (local_sem, send_sem, recv_sem) = refs[:7], refs[7:]
    rows, split = low_ref.shape
    half = rows // 2
    greet(junction_peers())
    started = []
    send = sender(send_sem, recv_sem, started)
    mixed[:, :split] = low_ref[...]
    low, high = scatter_flow(p_ref, buffers, send)
    mixed[:half, split:] = low
    mixed[half:, split:] = high
    stat[0:1, :] = jnp.sum(mixed[...] * mixed[...], axis=1, keepdims=True).T
    stat[1:2, :] = jnp.sum(incoming_ref[...] * gain_ref[...] * mixed[...], axis=1, keepdims=True).T
    total = column_total(slots, exchange(stat, slots, send, 14)) / width
    inverse = lax.rsqrt(total[0:1, :] + norm_eps)
    first = inverse.T
    second = (inverse * inverse * inverse * total[1:2, :]).T

    def slope(cols):
        return (
            first * (incoming_ref[:, cols] * gain_ref[:, cols]) - mixed[:, cols] * second
        ).astype(bf16)

    x_ref[...] = slope(slice(0, split))

    def meanwhile():
        rest_ref[...] = slope(slice(split, 2 * split))
        normed = mixed[...] * first
        block_ref[...] = ((resid_ref[...] + normed * gain_ref[...]) * valid_ref[...].T).astype(bf16)
        raw_ref[...] = jnp.sum(incoming_ref[...] * normed, axis=0, keepdims=True)

    gather_flow(x_ref, wide_ref, local_sem, send, 17, meanwhile)
    for copy in started:
        copy.wait_send()


def mixed_junction(partial, mixed_low, incoming, resid, valid, gain, width, number):
    rows, part = incoming.shape
    split = mixed_low.shape[1]
    vmem = pl.BlockSpec(memory_space=pltpu.VMEM)
    return pl.pallas_call(
        functools.partial(mixed_kernel, width),
        name="mixed_junction",
        out_shape=(
            jax.ShapeDtypeStruct((rows, part), bf16),
            jax.ShapeDtypeStruct((1, part), f32),
            jax.ShapeDtypeStruct((rows, part - split), bf16),
            jax.ShapeDtypeStruct((2 * rows, 4 * split), bf16),
        ),
        in_specs=[vmem] * 6,
        out_specs=(vmem, vmem, vmem, pl.BlockSpec(memory_space=pl.ANY)),
        scratch_shapes=[
            pltpu.VMEM((rows, part), f32),
            pltpu.VMEM((rows, split), bf16),
            pltpu.VMEM((2, rows), f32),
            pltpu.VMEM((4, 2, rows), f32),
        ]
        + scatter_buffers(rows, split)
        + [
            pltpu.SemaphoreType.DMA,
            pltpu.SemaphoreType.DMA((31,)),
            pltpu.SemaphoreType.DMA((31,)),
        ],
        compiler_params=pltpu.CompilerParams(
            collective_id=number, has_side_effects=True, vmem_limit_bytes=48 * 2**20
        ),
        cost_estimate=COST,
    )(partial, mixed_low, incoming, resid, valid, gain)


def d_resid_kernel(
    width,
    p_ref,
    incoming_ref,
    branch_ref,
    inv_ref,
    gain_ref,
    resid_ref,
    raw_ref,
    wide_ref,
    x_ref,
    stat,
    slots,
    *refs,
):
    buffers, (local_sem, send_sem, recv_sem) = refs[:7], refs[7:]
    half = x_ref.shape[0] // 2
    greet(junction_peers())
    started = []
    send = sender(send_sem, recv_sem, started)
    low, high = scatter_flow(p_ref, buffers, send)
    resid_ref[:half, :] = low + incoming_ref[:half, :]
    resid_ref[half:, :] = high + incoming_ref[half:, :]
    stat[...] = jnp.sum(resid_ref[...] * gain_ref[...] * branch_ref[...], axis=1, keepdims=True).T
    inner = column_total(slots, exchange(stat, slots, send, 14)) / width
    inverse = inv_ref[...]
    first = inverse.T
    second = (inverse * inverse * inverse * inner).T
    x_ref[...] = (first * (resid_ref[...] * gain_ref[...]) - branch_ref[...] * second).astype(bf16)

    def meanwhile():
        raw_ref[...] = jnp.sum(resid_ref[...] * branch_ref[...] * first, axis=0, keepdims=True)

    gather_flow(x_ref, wide_ref, local_sem, send, 17, meanwhile)
    for copy in started:
        copy.wait_send()


def d_resid_junction(partial, incoming, branch, inverse, gain, width, number):
    rows, part = incoming.shape
    vmem = pl.BlockSpec(memory_space=pltpu.VMEM)
    return pl.pallas_call(
        functools.partial(d_resid_kernel, width),
        name="d_resid_junction",
        out_shape=(
            jax.ShapeDtypeStruct((rows, part), f32),
            jax.ShapeDtypeStruct((1, part), f32),
            jax.ShapeDtypeStruct((2 * rows, 4 * part), bf16),
        ),
        in_specs=[vmem] * 5,
        out_specs=(vmem, vmem, pl.BlockSpec(memory_space=pl.ANY)),
        scratch_shapes=[
            pltpu.VMEM((rows, part), bf16),
            pltpu.VMEM((1, rows), f32),
            pltpu.VMEM((4, 1, rows), f32),
        ]
        + scatter_buffers(rows, part)
        + [
            pltpu.SemaphoreType.DMA,
            pltpu.SemaphoreType.DMA((31,)),
            pltpu.SemaphoreType.DMA((31,)),
        ],
        compiler_params=pltpu.CompilerParams(
            collective_id=number, has_side_effects=True, vmem_limit_bytes=48 * 2**20
        ),
        cost_estimate=COST,
    )(partial, incoming, branch, inverse, gain)


def feature_peers(wide):
    peers = []
    for d in range(1, 8 if wide else 4):
        peer = {"col": flip("col", d & 3)}
        if d >> 2:
            peer["dp"] = flip("dp", 1)
        peers.append(peer)
    return peers


def total_kernel(v_ref, out_ref, slots, send_sem, recv_sem):
    me = lax.axis_index("col")
    peers = feature_peers(False)
    greet(peers)
    started = []
    send = sender(send_sem, recv_sem, started)
    for d, peer in enumerate(peers):
        send(v_ref, slots.at[me], d, peer)
    slots[me] = v_ref[...]
    for copy in started:
        copy.wait_recv()
    total = slots[0]
    for i in range(1, 4):
        total = total + slots[i]
    out_ref[...] = total
    for copy in started:
        copy.wait_send()


def feature_total(values, number, name):
    k, t = values.shape
    flat = values.reshape(k * t // 128, 128)
    total = pl.pallas_call(
        total_kernel,
        name=name,
        out_shape=jax.ShapeDtypeStruct(flat.shape, f32),
        in_specs=[pl.BlockSpec(memory_space=pltpu.VMEM)],
        out_specs=pl.BlockSpec(memory_space=pltpu.VMEM),
        scratch_shapes=[
            pltpu.VMEM((4,) + flat.shape, f32),
            pltpu.SemaphoreType.DMA((3,)),
            pltpu.SemaphoreType.DMA((3,)),
        ],
        compiler_params=pltpu.CompilerParams(collective_id=number, has_side_effects=True),
    )(flat)
    return total.reshape(k, t)


def gain_peers():
    peers = []
    for d in range(1, 8):
        peers.append({"row": flip("row", d & 3), "dp": flip("dp", d >> 2)})
    return peers


def last_kernel(p_ref, gains_ref, out_ref, total_ref, slots, *refs):
    buffers, (send_sem, recv_sem) = refs[:7], refs[7:]
    half = out_ref.shape[0] // 2
    me = side("dp") * 4 + lax.axis_index("row")
    to_x, _, to_c = neighbours()
    peers = gain_peers()
    greet([to_x, to_c] + peers)
    started = []
    send = sender(send_sem, recv_sem, started)
    copies = [send(gains_ref, slots.at[me], 14 + d, peer) for d, peer in enumerate(peers)]
    slots[me] = gains_ref[...]
    low, high = scatter_flow(p_ref, buffers, send)
    out_ref[:half, :] = low
    out_ref[half:, :] = high
    for copy in copies:
        copy.wait_recv()
    total = slots[0]
    for i in range(1, 8):
        total = total + slots[i]
    total_ref[...] = total
    for copy in started:
        copy.wait_send()


def last_scatter(partial, gains, number):
    rows, width = partial.shape[0] // 2, partial.shape[1] // 4
    flat = gains.reshape(-1, 128)
    vmem = pl.BlockSpec(memory_space=pltpu.VMEM)
    out, total = pl.pallas_call(
        last_kernel,
        name="scatter_projected",
        out_shape=(
            jax.ShapeDtypeStruct((rows, width), f32),
            jax.ShapeDtypeStruct(flat.shape, f32),
        ),
        in_specs=[vmem, vmem],
        out_specs=(vmem, vmem),
        scratch_shapes=[pltpu.VMEM((8,) + flat.shape, f32)]
        + scatter_buffers(rows, width)
        + [pltpu.SemaphoreType.DMA((21,)), pltpu.SemaphoreType.DMA((21,))],
        compiler_params=pltpu.CompilerParams(
            collective_id=number, has_side_effects=True, vmem_limit_bytes=48 * 2**20
        ),
        cost_estimate=COST,
    )(partial, flat)
    return out, total.reshape(gains.shape)


def row_peers():
    return [(d, {"row": flip("row", d)}) for d in (3, 2, 1)]


def unit_view(ref, unit, tok, heads):
    rows = pl.ds(pl.multiple_of((unit // heads) * tok, tok), tok)
    cols = pl.ds(pl.multiple_of((unit % heads) * HEAD_DIM, HEAD_DIM), HEAD_DIM)
    return ref.at[rows, cols]


def turn_kernel(back, tok, heads, x_ref, out_ref, local_sem, send_sem, recv_sem):
    z = lax.axis_index("row")
    greet([peer for _, peer in row_peers()])
    started = []
    send = sender(send_sem, recv_sem, started)

    def line(ref, i):
        return ref.at[pl.ds(pl.multiple_of(i * tok, tok), tok)]

    def ends(i):
        if back:
            return line(x_ref, i), unit_view(out_ref, z, tok, heads)
        return unit_view(x_ref, i, tok, heads), line(out_ref, z)

    for d, peer in row_peers():
        send(*ends(z ^ d), d - 1, peer)
    own = pltpu.make_async_copy(*ends(z), local_sem)
    own.start()
    for copy in started:
        copy.wait()
    own.wait()


def turn(values, back, tok, heads, number, name):
    shape = (2 * tok, heads * HEAD_DIM) if back else (2 * heads * tok, HEAD_DIM)
    return pl.pallas_call(
        functools.partial(turn_kernel, back, tok, heads),
        name=name,
        out_shape=jax.ShapeDtypeStruct(shape, values.dtype),
        in_specs=[pl.BlockSpec(memory_space=pltpu.VMEM)],
        out_specs=pl.BlockSpec(memory_space=pl.ANY),
        scratch_shapes=[
            pltpu.SemaphoreType.DMA,
            pltpu.SemaphoreType.DMA((3,)),
            pltpu.SemaphoreType.DMA((3,)),
        ],
        compiler_params=pltpu.CompilerParams(collective_id=number, has_side_effects=True),
        cost_estimate=COST,
    )(values)


def totals(stat, slots, started):
    for copy in started:
        copy.wait_recv()
    total = slots[0]
    for i in range(1, 8):
        total = total + slots[i]
    return total


def front_kernel(
    width,
    qkv_ref,
    cos_ref,
    sin_ref,
    gain_ref,
    out_ref,
    inv_ref,
    turned,
    packed,
    stat,
    slots,
    local_sem,
    stat_send,
    stat_recv,
    send_sem,
    recv_sem,
):
    count, tok = qkv_ref.shape[0], cos_ref.shape[0]
    part = qkv_ref.shape[1] // 3
    heads = part // HEAD_DIM
    z = lax.axis_index("row")
    me = side("dp") * 4 + lax.axis_index("col")
    peers = feature_peers(True)
    greet(peers + [peer for _, peer in row_peers()])
    for i in range(2):
        values = qkv_ref[:, i * part : (i + 1) * part]
        stat[i : i + 1, :] = jnp.sum(values * values, axis=1, keepdims=True).T
    started, moved, local = [], [], []
    send = sender(stat_send, stat_recv, started)
    for d, peer in enumerate(peers):
        send(stat, slots.at[me], d, peer)
    slots[me] = stat[...]
    move = sender(send_sem, recv_sem, moved)

    def ship(i):
        for d, peer in row_peers():
            move(packed.at[z ^ d, i], out_ref.at[z, i], 3 * i + d - 1, peer)
        copy = pltpu.make_async_copy(packed.at[z, i], out_ref.at[z, i], local_sem.at[i])
        copy.start()
        local.append(copy)

    def spots():
        return [(s, h, s * heads + h) for s in range(2) for h in range(heads)]

    for s, h, unit in spots():
        packed[unit, 2] = qkv_ref[
            s * tok : (s + 1) * tok, 2 * part + h * HEAD_DIM : 2 * part + (h + 1) * HEAD_DIM
        ].astype(bf16)
    ship(2)
    for i in (1, 0):
        for s, h, unit in spots():
            values = (
                qkv_ref[s * tok : (s + 1) * tok, i * part + h * HEAD_DIM : i * part + (h + 1) * HEAD_DIM]
                * gain_ref[i : i + 1, h * HEAD_DIM : (h + 1) * HEAD_DIM]
            )
            turned[i, unit] = values * cos_ref[...] + pltpu.roll(values, HEAD_DIM // 2, 1) * sin_ref[...]
    inverse = lax.rsqrt(totals(stat, slots, started) / width + norm_eps)
    inv_ref[...] = inverse
    for i in (1, 0):
        column = inverse[i : i + 1, :].T
        for s, h, unit in spots():
            packed[unit, i] = (turned[i, unit] * column[s * tok : (s + 1) * tok]).astype(bf16)
        ship(i)
    for copy in moved:
        copy.wait()
    for copy in local:
        copy.wait()
    for copy in started:
        copy.wait_send()


def front(qkv, cosine, sine_signed, gains, width, units, number):
    count, tok = qkv.shape[0], cosine.shape[0]
    return pl.pallas_call(
        functools.partial(front_kernel, width),
        name="front",
        out_shape=(
            jax.ShapeDtypeStruct((units, 3, tok, HEAD_DIM), bf16),
            jax.ShapeDtypeStruct((2, count), f32),
        ),
        in_specs=[pl.BlockSpec(memory_space=pltpu.VMEM)] * 4,
        out_specs=(pl.BlockSpec(memory_space=pl.ANY), pl.BlockSpec(memory_space=pltpu.VMEM)),
        scratch_shapes=[
            pltpu.VMEM((2, units, tok, HEAD_DIM), f32),
            pltpu.VMEM((units, 3, tok, HEAD_DIM), bf16),
            pltpu.VMEM((2, count), f32),
            pltpu.VMEM((8, 2, count), f32),
            pltpu.SemaphoreType.DMA((3,)),
            pltpu.SemaphoreType.DMA((7,)),
            pltpu.SemaphoreType.DMA((7,)),
            pltpu.SemaphoreType.DMA((9,)),
            pltpu.SemaphoreType.DMA((9,)),
        ],
        compiler_params=pltpu.CompilerParams(
            collective_id=number, has_side_effects=True, vmem_limit_bytes=40 * 2**20
        ),
        cost_estimate=COST,
    )(qkv, cosine, sine_signed, gains)


def rear_kernel(
    width,
    d_ref,
    qkv_ref,
    cos_ref,
    sin_ref,
    gain_ref,
    inv_ref,
    out_ref,
    sums_ref,
    landed,
    normed,
    stat,
    slots,
    stat_send,
    stat_recv,
    send_sem,
    recv_sem,
):
    count, tok = qkv_ref.shape[0], cos_ref.shape[0]
    part = qkv_ref.shape[1] // 3
    heads = part // HEAD_DIM
    z = lax.axis_index("row")
    me = side("dp") * 4 + lax.axis_index("col")
    peers = feature_peers(True)
    greet(peers + [peer for _, peer in row_peers()])
    started, moved = [], []
    move = sender(send_sem, recv_sem, moved)
    for i in (0, 1, 2):
        for d, peer in row_peers():
            there = pl.ds(pl.multiple_of((z ^ d) * tok, tok), tok)
            move(d_ref.at[i, there], landed.at[z, i], 3 * i + d - 1, peer)
    here = pl.ds(pl.multiple_of(z * tok, tok), tok)
    for i in (0, 1, 2):
        landed[z, i] = d_ref[i, here, :]
    spots = [(s, h, s * heads + h) for s in range(2) for h in range(heads)]
    for i in (0, 1):
        for copy in moved[3 * i : 3 * i + 3]:
            copy.wait_recv()
        for h in range(heads):
            cols = slice(i * part + h * HEAD_DIM, i * part + (h + 1) * HEAD_DIM)
            gain = gain_ref[i : i + 1, h * HEAD_DIM : (h + 1) * HEAD_DIM]
            raw = jnp.zeros((1, HEAD_DIM), f32)
            for s in range(2):
                rows = slice(s * tok, (s + 1) * tok)
                values = landed[s * heads + h, i].astype(f32)
                back = values * cos_ref[...] - pltpu.roll(values, HEAD_DIM // 2, 1) * sin_ref[...]
                pre = qkv_ref[rows, cols]
                inverse = inv_ref[i : i + 1, rows].T
                crossed = back * pre
                raw = raw + jnp.sum(crossed * inverse, axis=0, keepdims=True)
                partial = jnp.sum(crossed * gain, axis=1, keepdims=True).T
                if h == 0:
                    stat[i : i + 1, rows] = partial
                else:
                    stat[i : i + 1, rows] = stat[i : i + 1, rows] + partial
                normed[rows, cols] = back * gain
            sums_ref[i : i + 1, h * HEAD_DIM : (h + 1) * HEAD_DIM] = raw
    send = sender(stat_send, stat_recv, started)
    for d, peer in enumerate(peers):
        send(stat, slots.at[me], d, peer)
    slots[me] = stat[...]
    for copy in moved[6:]:
        copy.wait_recv()
    for s, h, unit in spots:
        cols = slice(2 * part + h * HEAD_DIM, 2 * part + (h + 1) * HEAD_DIM)
        out_ref[s * tok : (s + 1) * tok, cols] = landed[unit, 2]
    inner = totals(stat, slots, started) / width
    for i in (0, 1):
        inverse = inv_ref[i : i + 1, :]
        first = inverse.T
        second = (inverse * inverse * inverse * inner[i : i + 1, :]).T
        cols = slice(i * part, (i + 1) * part)
        out_ref[:, cols] = (first * normed[:, cols] - qkv_ref[:, cols] * second).astype(bf16)
    for copy in moved + started:
        copy.wait_send()


def rear(d_units, qkv, cosine, sine_signed, gains, inverse, width, number):
    count, tok = qkv.shape[0], cosine.shape[0]
    part = qkv.shape[1] // 3
    units = d_units.shape[1] // tok
    return pl.pallas_call(
        functools.partial(rear_kernel, width),
        name="rear",
        out_shape=(
            jax.ShapeDtypeStruct((count, 3 * part), bf16),
            jax.ShapeDtypeStruct((2, part), f32),
        ),
        in_specs=[pl.BlockSpec(memory_space=pltpu.VMEM)] * 6,
        out_specs=[pl.BlockSpec(memory_space=pltpu.VMEM)] * 2,
        scratch_shapes=[
            pltpu.VMEM((units, 3, tok, HEAD_DIM), bf16),
            pltpu.VMEM((count, 2 * part), f32),
            pltpu.VMEM((2, count), f32),
            pltpu.VMEM((8, 2, count), f32),
            pltpu.SemaphoreType.DMA((7,)),
            pltpu.SemaphoreType.DMA((7,)),
            pltpu.SemaphoreType.DMA((9,)),
            pltpu.SemaphoreType.DMA((9,)),
        ],
        compiler_params=pltpu.CompilerParams(
            collective_id=number, has_side_effects=True, vmem_limit_bytes=40 * 2**20
        ),
        cost_estimate=COST,
    )(d_units, qkv, cosine, sine_signed, gains, inverse)


BLOCK = 512


def attend_kernel(len_ref, q_ref, k_ref, v_ref, o_ref, o32_ref, lse_ref):
    i = pl.program_id(0)
    bq, bk = q_ref.shape[0], BLOCK
    length = len_ref[0]
    scale = HEAD_DIM ** (-0.5)
    q = q_ref[...]
    rows = i * bq + lax.broadcasted_iota(jnp.int32, (bq, bk), 0)
    cols0 = lax.broadcasted_iota(jnp.int32, (bq, bk), 1)

    def step(j, carry, masked):
        top, total, acc = carry
        j0 = pl.multiple_of(j * bk, bk)
        scores = contract_last(q, k_ref[pl.ds(j0, bk), :]) * scale
        if masked:
            cols = j0 + cols0
            scores = jnp.where((cols <= rows) & (cols < length), scores, masked_score)
        new = jnp.maximum(top, jnp.max(scores, axis=1, keepdims=True))
        weights = jnp.exp(scores - new)
        fix = jnp.exp(top - new)
        total = total * fix + jnp.sum(weights, axis=1, keepdims=True)
        acc = acc * fix + matmul(weights.astype(bf16), v_ref[pl.ds(j0, bk), :])
        return new, total, acc

    carry = (
        jnp.full((bq, 1), -jnp.inf, f32),
        jnp.zeros((bq, 1), f32),
        jnp.zeros((bq, HEAD_DIM), f32),
    )
    whole = jnp.minimum(i, length // bk)
    last = jnp.minimum(i + 1, (length + bk - 1) // bk)
    carry = lax.fori_loop(0, whole, lambda j, s: step(j, s, False), carry)
    top, total, acc = lax.fori_loop(whole, last, lambda j, s: step(j, s, True), carry)
    out = acc / total
    o_ref[...] = out.astype(bf16)
    o32_ref[...] = out
    lse_ref[...] = jnp.broadcast_to((top + jnp.log(total)).T, lse_ref.shape)


def attend(length, q, k, v):
    slots = q.shape[0]
    whole = pl.BlockSpec((slots, HEAD_DIM), lambda i: (0, 0))
    part = pl.BlockSpec((BLOCK, HEAD_DIM), lambda i: (i, 0))
    return pl.pallas_call(
        attend_kernel,
        name="attend",
        grid=(slots // BLOCK,),
        out_shape=(
            jax.ShapeDtypeStruct((slots, HEAD_DIM), bf16),
            jax.ShapeDtypeStruct((slots, HEAD_DIM), f32),
            jax.ShapeDtypeStruct((8, slots), f32),
        ),
        in_specs=[pl.BlockSpec(memory_space=pltpu.SMEM), part, whole, whole],
        out_specs=(part, part, pl.BlockSpec((8, BLOCK), lambda i: (0, i))),
        cost_estimate=COST,
    )(length, q, k, v)


def attend_back_kernel(
    len_ref, q_ref, k_ref, v_ref, do_ref, o_ref, lse_ref, out_ref, dq_acc, delta_ref
):
    j = pl.program_id(0)
    bk, bq = k_ref.shape[0], BLOCK
    slots = q_ref.shape[0]
    length = len_ref[0]
    scale = HEAD_DIM ** (-0.5)

    @pl.when(j == 0)
    def _():
        dq_acc[...] = jnp.zeros_like(dq_acc)
        for i in range(slots // bq):
            here = slice(i * bq, (i + 1) * bq)
            product = do_ref[here, :].astype(f32) * o_ref[here, :]
            delta_ref[0:1, here] = jnp.sum(product, axis=1, keepdims=True).T

    k, v = k_ref[...], v_ref[...]
    j0 = j * bk
    cols = j0 + lax.broadcasted_iota(jnp.int32, (bk, bq), 0)
    rows0 = lax.broadcasted_iota(jnp.int32, (bk, bq), 1)

    def step(i, carry, masked):
        dk, dv = carry
        i0 = pl.multiple_of(i * bq, bq)
        here = pl.ds(i0, bq)
        q, do = q_ref[here, :], do_ref[here, :]
        scores = contract_last(k, q) * scale
        if masked:
            scores = jnp.where((cols <= i0 + rows0) & (cols < length), scores, masked_score)
        probs = jnp.exp(scores - lse_ref[0:1, here])
        dv = dv + matmul(probs.astype(bf16), do)
        d_probs = contract_last(v, do)
        d_scores = (probs * (d_probs - delta_ref[0:1, here])).astype(bf16)
        dk = dk + matmul(d_scores, q)
        dq_acc[here, :] += contract_first(d_scores, k)
        return dk, dv

    zero = jnp.zeros((bk, HEAD_DIM), f32)
    top = slots // bq
    first = jnp.where(j0 + bk <= length, j + 1, top)
    first = jnp.where(j0 < length, first, j)
    stop = jnp.where(j0 < length, top, j)
    carry = lax.fori_loop(j, first, lambda i, s: step(i, s, True), (zero, zero))
    dk, dv = lax.fori_loop(first, stop, lambda i, s: step(i, s, False), carry)
    there = pl.ds(pl.multiple_of(j0, bk), bk)
    out_ref[1, there, :] = (dk * scale).astype(bf16)
    out_ref[2, there, :] = dv.astype(bf16)

    @pl.when(j == pl.num_programs(0) - 1)
    def _():
        out_ref[0] = (dq_acc[...] * scale).astype(bf16)


def attend_back(length, q, k, v, do, o, lse):
    slots = q.shape[0]
    whole = pl.BlockSpec((slots, HEAD_DIM), lambda j: (0, 0))
    part = pl.BlockSpec((BLOCK, HEAD_DIM), lambda j: (j, 0))
    line = pl.BlockSpec((8, slots), lambda j: (0, 0))
    return pl.pallas_call(
        attend_back_kernel,
        name="attend_back",
        grid=(slots // BLOCK,),
        out_shape=jax.ShapeDtypeStruct((3, slots, HEAD_DIM), bf16),
        in_specs=[pl.BlockSpec(memory_space=pltpu.SMEM), whole, part, part, whole, whole, line],
        out_specs=pl.BlockSpec((3, slots, HEAD_DIM), lambda j: (0, 0, 0)),
        scratch_shapes=[pltpu.VMEM((slots, HEAD_DIM), f32), pltpu.VMEM((8, slots), f32)],
        cost_estimate=COST,
    )(length, q, k, v, do, o, lse)


def per_device(
    tokens,
    seq_lengths,
    w_query,
    w_key,
    w_value,
    w_out,
    w_gate,
    w_up,
    w_down,
    q_gain,
    k_gain,
    attn_gain,
    mlp_gain,
    cotangent,
):
    tok_rows, feat_part = tokens.shape
    row_count, data_count = lax.axis_size("row"), lax.axis_size("dp")
    width = feat_part * lax.axis_size("col")
    slots = tok_rows * row_count
    half_feat = feat_part // 2
    y, z = side("dp"), lax.axis_index("row")
    heads = half_feat // HEAD_DIM
    pairs = [(i, i ^ 1) for i in range(data_count)]
    after = lambda values, *done: lax.optimization_barrier((values,) + done)[0]

    def y_half(values, axis):
        size = values.shape[axis] // 2
        return lax.dynamic_slice_in_dim(values, y * size, size, axis)

    qkv_weight = lax.all_gather(
        jnp.concatenate([y_half(w_query, 1), y_half(w_key, 1), y_half(w_value, 1)], axis=1),
        "row",
        axis=0,
        tiled=True,
    )
    out_weight = lax.all_gather(y_half(w_out, 0), "row", axis=1, tiled=True)
    gate_up_weight = lax.all_gather(
        jnp.concatenate([y_half(w_gate, 1), y_half(w_up, 1)], axis=1), "row", axis=0, tiled=True
    )
    hidden_part = gate_up_weight.shape[1] // 2
    gate_weight, up_weight = gate_up_weight[:, :hidden_part], gate_up_weight[:, hidden_part:]
    down_half = y_half(w_down, 0)
    split = down_half.shape[1] // 2
    low_weight = lax.all_gather(down_half[:, :split], "row", axis=1, tiled=True)

    positions = z * tok_rows + jnp.arange(tok_rows)
    length = seq_lengths[0]
    valid = (positions < length).astype(f32)[:, None]
    cosine, sine = rope_tables(positions, HEAD_DIM)
    sine_signed = jnp.where(jnp.arange(HEAD_DIM)[None, :] < HEAD_DIM // 2, -sine, sine)
    other_length = lax.ppermute(seq_lengths, "dp", pairs)
    pair_lengths = jnp.where(
        y == 0,
        jnp.concatenate([seq_lengths, other_length]),
        jnp.concatenate([other_length, seq_lengths]),
    )
    unit_length = lax.dynamic_slice_in_dim(pair_lengths, z // heads, 1)
    qk_gain = jnp.stack([y_half(q_gain, 0), y_half(k_gain, 0)])

    tokens_wide = gather_wide(tokens, 0, "gather_tokens")
    high_weight = lax.all_gather(after(down_half[:, split:], tokens_wide), "row", axis=1, tiled=True)
    qkv = matmul(tokens_wide, qkv_weight)
    units, inverse = front(qkv, cosine, sine_signed, qk_gain, width, 2 * heads, 2)
    q_unit, k_unit, v_unit = (units[:, i].reshape(slots, HEAD_DIM) for i in range(3))
    attn_unit, attn_exact, log_total = attend(unit_length, q_unit, k_unit, v_unit)
    attn_low = turn(attn_unit, True, tok_rows, heads, 3, "turn_attn")
    branch = scatter_wide(matmul(attn_low, out_weight).astype(bf16), 4, "scatter_branch")
    branch_inv = lax.rsqrt(
        feature_total(jnp.sum(branch * branch, axis=1)[None, :], 5, "total_branch")[0] / width
        + norm_eps
    )[:, None]
    resid = tokens.astype(f32) + branch * branch_inv * attn_gain
    resid_wide = gather_wide(resid.astype(bf16), 6, "gather_resid")
    gate = matmul(resid_wide, gate_weight)
    upper = matmul(resid_wide, up_weight)
    sigma = jax.nn.sigmoid(gate)
    hidden = (gate * sigma * upper).astype(bf16)
    mixed_low = scatter_wide(matmul(hidden, low_weight).astype(bf16), 7, "scatter_mixed_low")
    high_weight = after(high_weight, mixed_low)
    incoming = cotangent.astype(f32) * valid
    factor = 1.0 / math.sqrt(slots * data_count)
    block_output, mlp_gain_raw, d_high, d_low_wide = mixed_junction(
        matmul(hidden, high_weight).astype(bf16),
        mixed_low,
        incoming,
        resid,
        valid.T,
        mlp_gain[None, :],
        width,
        17,
    )
    low_raw = (contract_first(hidden, d_low_wide) * factor).astype(bf16)
    d_high_wide = gather_wide(after(d_high, low_raw), 18, "gather_d_mixed_high")
    high_raw = (contract_first(hidden, d_high_wide) * factor).astype(bf16)

    def cut(values, index, count, axis):
        size = values.shape[axis] // count
        return lax.dynamic_slice_in_dim(values, index * size, size, axis)

    def over_dp(piece):
        if data_count > 2:
            groups = [list(range(s, data_count, 2)) for s in (0, 1)]
            piece = lax.psum(piece, "dp", axis_index_groups=groups)
        return piece

    def two_sides(piece, other, bit, axis):
        low = jnp.where(bit == 0, piece, other)
        high = jnp.where(bit == 0, other, piece)
        return jnp.concatenate([low, high], axis=axis)

    def from_twin(piece):
        return lax.ppermute(piece, "dp", pairs)

    def reduce_rows(raw, axis):
        return lax.psum_scatter(raw, "row", scatter_dimension=axis, tiled=True)

    d_hidden = contract_last(d_low_wide, low_weight) + contract_last(d_high_wide, high_weight)
    d_gate = (d_hidden * upper * sigma * (1.0 + gate * (1.0 - sigma))).astype(bf16)
    d_upper = (d_hidden * gate * sigma).astype(bf16)
    d_gate_up = jnp.concatenate([d_gate, d_upper], axis=1)
    gate_up_raw = (contract_first(resid_wide, d_gate_up) * factor).astype(bf16)
    d_resid_wide = contract_last(d_gate_up, gate_up_weight).astype(bf16)
    d_resid_wide, low_piece = lax.optimization_barrier(
        (after(d_resid_wide, high_raw, gate_up_raw), reduce_rows(low_raw, 1))
    )
    down_piece = jnp.concatenate([low_piece, reduce_rows(high_raw, 1)], axis=1)
    gate_up_piece = reduce_rows(gate_up_raw, 0)
    d_resid, attn_gain_raw, d_branch_wide = d_resid_junction(
        d_resid_wide, incoming, branch, branch_inv.T, attn_gain[None, :], width, 10
    )
    down_piece = over_dp(down_piece)
    d_branch_wide, down_piece = lax.optimization_barrier((d_branch_wide, down_piece))
    d_attn = contract_last(d_branch_wide, out_weight).astype(bf16)
    other_down = from_twin(down_piece)
    d_attn_unit, other_down = lax.optimization_barrier(
        (turn(d_attn, False, tok_rows, heads, 13, "turn_d_attn"), other_down)
    )
    out_raw = (contract_first(attn_low, after(d_branch_wide, d_attn_unit)) * factor).astype(bf16)
    d_attn_unit = after(d_attn_unit, out_raw)
    out_piece = reduce_rows(out_raw, 1)
    d_units = attend_back(unit_length, q_unit, k_unit, v_unit, d_attn_unit, attn_exact, log_total)
    d_units, gate_up_piece = lax.optimization_barrier((d_units, over_dp(gate_up_piece)))
    other_gate_up = from_twin(gate_up_piece)
    d_qkv, gain_sums = rear(d_units, qkv, cosine, sine_signed, qk_gain, inverse, width, 14)
    d_qkv, gain_sums, other_gate_up = lax.optimization_barrier((d_qkv, gain_sums, other_gate_up))
    qkv_raw = (contract_first(tokens_wide, d_qkv) * factor).astype(bf16)
    projected = contract_last(after(d_qkv, qkv_raw), qkv_weight).astype(bf16)
    qkv_piece = over_dp(reduce_rows(qkv_raw, 0))

    def spread(half):
        return lax.dynamic_update_slice_in_dim(jnp.zeros((feat_part,), f32), half, y * half_feat, 0)

    gains_raw = jnp.stack(
        [spread(gain_sums[0]), spread(gain_sums[1]), attn_gain_raw[0], mlp_gain_raw[0]]
    )
    scattered, gains = last_scatter(projected, gains_raw * factor, 16)
    scattered, gains, out_piece = lax.optimization_barrier((scattered, gains, over_dp(out_piece)))
    other_out = from_twin(out_piece)
    input_grad = d_resid + scattered
    gains = over_dp(gains)
    input_grad, qkv_piece, other_down, other_gate_up = lax.optimization_barrier(
        (input_grad, qkv_piece, other_down, other_gate_up)
    )
    (gate_piece, up_piece), (other_gate, other_up) = (
        [cut(values, i, 2, 1) for i in range(2)] for values in (gate_up_piece, other_gate_up)
    )

    def whole(piece, other, axis):
        return two_sides(piece, other, y, axis).astype(f32)

    qkv_other = from_twin(qkv_piece)
    q_grad, k_grad, v_grad = (
        two_sides(cut(qkv_piece, i, 3, 1), cut(qkv_other, i, 3, 1), y, 1).astype(f32)
        for i in range(3)
    )
    return (
        block_output,
        input_grad,
        q_grad,
        k_grad,
        v_grad,
        whole(out_piece, other_out, 0),
        whole(gate_piece, other_gate, 1),
        whole(up_piece, other_up, 1),
        whole(down_piece, other_down, 0),
        gains[0],
        gains[1],
        gains[2],
        gains[3],
    )


def solution(mesh):
    tok, row_col, col_row, gain = P(("dp", "row"), "col"), P("row", "col"), P("col", "row"), P("col")
    weights = (row_col, row_col, row_col, col_row, row_col, row_col, col_row)
    gains = (gain, gain, gain, gain)
    return jax.shard_map(
        per_device,
        mesh=mesh,
        in_specs=(tok, P("dp")) + weights + gains + (tok,),
        out_specs=(tok, tok) + weights + gains,
        check_vma=False,
    )
```

```python
import functools
import math

import jax
import jax.numpy as jnp
from jax import lax
from jax.experimental import pallas as pl
from jax.experimental.pallas import tpu as pltpu
from jax.sharding import PartitionSpec as P

HEAD_DIM = 128
rope_base = 500000.0
norm_eps = 1e-06
masked_score = -1e30

MESH = pl.DeviceIdType.MESH
bf16 = jnp.bfloat16
f32 = jnp.float32
COST = pl.CostEstimate(flops=0, bytes_accessed=1000, transcendentals=0)


def rope_tables(positions, head_dim):
    half = head_dim // 2
    freq = 1.0 / rope_base ** (jnp.arange(half, dtype=f32) / half)
    angle = positions.astype(f32)[:, None] * freq[None, :]
    angle = jnp.concatenate([angle, angle], axis=1)
    return (jnp.cos(angle), jnp.sin(angle))


def matmul(left, right):
    return jnp.dot(left, right, preferred_element_type=f32)


def contract_first(left, right):
    return lax.dot_general(left, right, (((0,), (0,)), ((), ())), preferred_element_type=f32)


def contract_last(left, right):
    return lax.dot_general(left, right, (((1,), (1,)), ((), ())), preferred_element_type=f32)


def flip(axis, bit):
    return lax.axis_index(axis) ^ bit


def side(axis):
    return lax.axis_index(axis) & 1


def greet(peers):
    barrier = pltpu.get_barrier_semaphore()
    for peer in peers:
        pl.semaphore_signal(barrier, inc=1, device_id=peer, device_id_type=MESH)
    pl.semaphore_wait(barrier, len(peers))


def sender(send_sem, recv_sem, started):
    def send(src, dst, number, peer):
        copy = pltpu.make_async_remote_copy(
            src_ref=src,
            dst_ref=dst,
            send_sem=send_sem.at[number],
            recv_sem=recv_sem.at[number],
            device_id=peer,
            device_id_type=MESH,
        )
        copy.start()
        started.append(copy)
        return copy

    return send


def neighbours():
    return {"col": flip("col", 2)}, {"dp": flip("dp", 1)}, {"col": flip("col", 1)}


def gather_flow(x_ref, out_ref, local_sem, send, base, meanwhile=None):
    rows, width = x_ref.shape
    half = rows // 2
    y, b = side("dp"), lax.axis_index("col")
    to_x, to_y, to_c = neighbours()

    def slot(yy, h, bb, n=half):
        return out_ref.at[
            pl.ds(pl.multiple_of(yy * rows + h * half, half), n),
            pl.ds(pl.multiple_of(bb * width, width), width),
        ]

    low, high = x_ref.at[pl.ds(0, half)], x_ref.at[pl.ds(half, half)]
    own = pltpu.make_async_copy(x_ref, slot(y, 0, b, rows), local_sem)
    xa = send(low, slot(y, 0, b), base + 0, to_x)
    ya = send(high, slot(y, 1, b), base + 1, to_y)
    core = [send(low, slot(y, 0, b), base + 6, to_c)]
    yb = send(low, slot(y, 0, b), base + 2, to_y)
    xb = send(high, slot(y, 1, b), base + 3, to_x)
    core.append(send(high, slot(y, 1, b), base + 7, to_c))
    own.start()
    if meanwhile is not None:
        meanwhile()
    xa.wait_recv()
    piece = slot(y, 0, b ^ 2)
    yc = send(piece, piece, base + 4, to_y)
    core.append(send(piece, piece, base + 8, to_c))
    ya.wait_recv()
    piece = slot(y ^ 1, 1, b)
    xc = send(piece, piece, base + 5, to_x)
    core.append(send(piece, piece, base + 9, to_c))
    yb.wait_recv()
    piece = slot(y ^ 1, 0, b)
    core.append(send(piece, piece, base + 10, to_c))
    xb.wait_recv()
    piece = slot(y, 1, b ^ 2)
    core.append(send(piece, piece, base + 11, to_c))
    yc.wait_recv()
    piece = slot(y ^ 1, 0, b ^ 2)
    core.append(send(piece, piece, base + 12, to_c))
    xc.wait_recv()
    piece = slot(y ^ 1, 1, b ^ 2)
    core.append(send(piece, piece, base + 13, to_c))
    for copy in core:
        copy.wait_recv()
    own.wait()


def gather_kernel(x_ref, out_ref, local_sem, send_sem, recv_sem):
    greet(neighbours())
    started = []
    gather_flow(x_ref, out_ref, local_sem, sender(send_sem, recv_sem, started), 0)
    for copy in started:
        copy.wait_send()


def gather_wide(values, number, name):
    rows, width = values.shape
    return pl.pallas_call(
        gather_kernel,
        name=name,
        out_shape=jax.ShapeDtypeStruct((2 * rows, 4 * width), values.dtype),
        in_specs=[pl.BlockSpec(memory_space=pltpu.VMEM)],
        out_specs=pl.BlockSpec(memory_space=pl.ANY),
        scratch_shapes=[
            pltpu.SemaphoreType.DMA,
            pltpu.SemaphoreType.DMA((14,)),
            pltpu.SemaphoreType.DMA((14,)),
        ],
        compiler_params=pltpu.CompilerParams(
            collective_id=number, has_side_effects=True, vmem_limit_bytes=8 * 2**20
        ),
        cost_estimate=COST,
    )(values)


def scatter_flow(p_ref, buffers, send):
    rc, s1, ry, rx, s2, fy, fx = buffers
    rows, width = p_ref.shape[0] // 2, p_ref.shape[1] // 4
    half = rows // 2
    y, b = side("dp"), lax.axis_index("col")
    x, c = b >> 1, b & 1
    to_x, to_y, to_c = neighbours()

    def place(yy, h):
        return pl.ds(pl.multiple_of(yy * rows + h * half, half), half)

    def column(bb):
        return pl.ds(pl.multiple_of(bb * width, width), width)

    order = [(0, y ^ 1, 0), (1, y ^ 1, 0), (x ^ 1, 0, 1), (x ^ 1, 1, 1)]
    order += [(0, y, 0), (1, y, 0), (x, 0, 1), (x, 1, 1)]
    core = [
        send(
            p_ref.at[place(yy, h), column(2 * xx + (c ^ 1))],
            rc.at[xx, place(yy, h)],
            number,
            to_c,
        )
        for number, (xx, yy, h) in enumerate(order)
    ]

    def settle(*numbers):
        for number in numbers:
            core[number].wait_recv()
            xx, yy, h = order[number]
            s1[xx, place(yy, h), :] = (
                p_ref[place(yy, h), column(2 * xx + c)].astype(f32)
                + rc[xx, place(yy, h), :].astype(f32)
            ).astype(s1.dtype)

    settle(0, 1, 2, 3)
    ya, xa = [], []
    for i in range(2):
        ya.append(send(s1.at[i, place(y ^ 1, 0), :], ry.at[i], 8 + i, to_y))
        xa.append(send(s1.at[x ^ 1, pl.ds(i * rows + half, half), :], rx.at[i], 10 + i, to_x))
    settle(4, 5, 6, 7)
    for copy in ya:
        copy.wait_recv()
    s2[0] = (s1[x ^ 1, place(y, 0), :].astype(f32) + ry[x ^ 1].astype(f32)).astype(s2.dtype)
    xb = send(s2.at[0], fx, 12, to_x)
    for copy in xa:
        copy.wait_recv()
    s2[1] = (s1[x, place(y ^ 1, 1), :].astype(f32) + rx[y ^ 1].astype(f32)).astype(s2.dtype)
    yb = send(s2.at[1], fy, 13, to_y)
    keep = s1[x, place(y, 0), :].astype(f32) + ry[x].astype(f32)
    xb.wait_recv()
    low = keep + fx[...].astype(f32)
    keep = s1[x, place(y, 1), :].astype(f32) + rx[y].astype(f32)
    yb.wait_recv()
    return low, keep + fy[...].astype(f32)


def scatter_buffers(rows, width):
    half = rows // 2
    return [
        pltpu.VMEM((2, 2 * rows, width), bf16),
        pltpu.VMEM((2, 2 * rows, width), bf16),
        pltpu.VMEM((2, half, width), bf16),
        pltpu.VMEM((2, half, width), bf16),
        pltpu.VMEM((2, half, width), bf16),
        pltpu.VMEM((half, width), bf16),
        pltpu.VMEM((half, width), bf16),
    ]


def scatter_kernel(p_ref, out_ref, *refs):
    buffers, (send_sem, recv_sem) = refs[:7], refs[7:]
    half = out_ref.shape[0] // 2
    greet(neighbours())
    started = []
    low, high = scatter_flow(p_ref, buffers, sender(send_sem, recv_sem, started))
    out_ref[:half, :] = low
    out_ref[half:, :] = high
    for copy in started:
        copy.wait_send()


def scatter_wide(partial, number, name):
    rows, width = partial.shape[0] // 2, partial.shape[1] // 4
    return pl.pallas_call(
        scatter_kernel,
        name=name,
        out_shape=jax.ShapeDtypeStruct((rows, width), f32),
        in_specs=[pl.BlockSpec(memory_space=pltpu.VMEM)],
        out_specs=pl.BlockSpec(memory_space=pltpu.VMEM),
        scratch_shapes=scatter_buffers(rows, width)
        + [pltpu.SemaphoreType.DMA((14,)), pltpu.SemaphoreType.DMA((14,))],
        compiler_params=pltpu.CompilerParams(
            collective_id=number, has_side_effects=True, vmem_limit_bytes=48 * 2**20
        ),
        cost_estimate=COST,
    )(partial)


def exchange(stat, slots, send, base):
    me = lax.axis_index("col")
    copies = [send(stat, slots.at[me], base + d, peer) for d, peer in enumerate(feature_peers(False))]
    slots[me] = stat[...]
    return copies


def column_total(slots, copies):
    for copy in copies:
        copy.wait_recv()
    return (slots[0] + slots[1]) + (slots[2] + slots[3])


def junction_peers():
    to_x, to_y, to_c = neighbours()
    return [to_x, to_y, to_c, {"col": flip("col", 3)}]


def mixed_kernel(
    width,
    p_ref,
    low_ref,
    incoming_ref,
    resid_ref,
    valid_ref,
    gain_ref,
    block_ref,
    raw_ref,
    rest_ref,
    wide_ref,
    mixed,
    x_ref,
    stat,
    slots,
    *refs,
):
    buffers, (local_sem, send_sem, recv_sem) = refs[:7], refs[7:]
    rows, split = low_ref.shape
    half = rows // 2
    greet(junction_peers())
    started = []
    send = sender(send_sem, recv_sem, started)
    mixed[:, :split] = low_ref[...]
    low, high = scatter_flow(p_ref, buffers, send)
    mixed[:half, split:] = low
    mixed[half:, split:] = high
    stat[0:1, :] = jnp.sum(mixed[...] * mixed[...], axis=1, keepdims=True).T
    stat[1:2, :] = jnp.sum(incoming_ref[...] * gain_ref[...] * mixed[...], axis=1, keepdims=True).T
    total = column_total(slots, exchange(stat, slots, send, 14)) / width
    inverse = lax.rsqrt(total[0:1, :] + norm_eps)
    first = inverse.T
    second = (inverse * inverse * inverse * total[1:2, :]).T

    def slope(cols):
        return (
            first * (incoming_ref[:, cols] * gain_ref[:, cols]) - mixed[:, cols] * second
        ).astype(bf16)

    x_ref[...] = slope(slice(0, split))

    def meanwhile():
        rest_ref[...] = slope(slice(split, 2 * split))
        normed = mixed[...] * first
        block_ref[...] = ((resid_ref[...] + normed * gain_ref[...]) * valid_ref[...].T).astype(bf16)
        raw_ref[...] = jnp.sum(incoming_ref[...] * normed, axis=0, keepdims=True)

    gather_flow(x_ref, wide_ref, local_sem, send, 17, meanwhile)
    for copy in started:
        copy.wait_send()


def mixed_junction(partial, mixed_low, incoming, resid, valid, gain, width, number):
    rows, part = incoming.shape
    split = mixed_low.shape[1]
    vmem = pl.BlockSpec(memory_space=pltpu.VMEM)
    return pl.pallas_call(
        functools.partial(mixed_kernel, width),
        name="mixed_junction",
        out_shape=(
            jax.ShapeDtypeStruct((rows, part), bf16),
            jax.ShapeDtypeStruct((1, part), f32),
            jax.ShapeDtypeStruct((rows, part - split), bf16),
            jax.ShapeDtypeStruct((2 * rows, 4 * split), bf16),
        ),
        in_specs=[vmem] * 6,
        out_specs=(vmem, vmem, vmem, pl.BlockSpec(memory_space=pl.ANY)),
        scratch_shapes=[
            pltpu.VMEM((rows, part), f32),
            pltpu.VMEM((rows, split), bf16),
            pltpu.VMEM((2, rows), f32),
            pltpu.VMEM((4, 2, rows), f32),
        ]
        + scatter_buffers(rows, split)
        + [
            pltpu.SemaphoreType.DMA,
            pltpu.SemaphoreType.DMA((31,)),
            pltpu.SemaphoreType.DMA((31,)),
        ],
        compiler_params=pltpu.CompilerParams(
            collective_id=number, has_side_effects=True, vmem_limit_bytes=48 * 2**20
        ),
        cost_estimate=COST,
    )(partial, mixed_low, incoming, resid, valid, gain)


def d_resid_kernel(
    width,
    p_ref,
    incoming_ref,
    branch_ref,
    inv_ref,
    gain_ref,
    resid_ref,
    raw_ref,
    wide_ref,
    x_ref,
    stat,
    slots,
    *refs,
):
    buffers, (local_sem, send_sem, recv_sem) = refs[:7], refs[7:]
    half = x_ref.shape[0] // 2
    greet(junction_peers())
    started = []
    send = sender(send_sem, recv_sem, started)
    low, high = scatter_flow(p_ref, buffers, send)
    resid_ref[:half, :] = low + incoming_ref[:half, :]
    resid_ref[half:, :] = high + incoming_ref[half:, :]
    stat[...] = jnp.sum(resid_ref[...] * gain_ref[...] * branch_ref[...], axis=1, keepdims=True).T
    inner = column_total(slots, exchange(stat, slots, send, 14)) / width
    inverse = inv_ref[...]
    first = inverse.T
    second = (inverse * inverse * inverse * inner).T
    x_ref[...] = (first * (resid_ref[...] * gain_ref[...]) - branch_ref[...] * second).astype(bf16)

    def meanwhile():
        raw_ref[...] = jnp.sum(resid_ref[...] * branch_ref[...] * first, axis=0, keepdims=True)

    gather_flow(x_ref, wide_ref, local_sem, send, 17, meanwhile)
    for copy in started:
        copy.wait_send()


def d_resid_junction(partial, incoming, branch, inverse, gain, width, number):
    rows, part = incoming.shape
    vmem = pl.BlockSpec(memory_space=pltpu.VMEM)
    return pl.pallas_call(
        functools.partial(d_resid_kernel, width),
        name="d_resid_junction",
        out_shape=(
            jax.ShapeDtypeStruct((rows, part), f32),
            jax.ShapeDtypeStruct((1, part), f32),
            jax.ShapeDtypeStruct((2 * rows, 4 * part), bf16),
        ),
        in_specs=[vmem] * 5,
        out_specs=(vmem, vmem, pl.BlockSpec(memory_space=pl.ANY)),
        scratch_shapes=[
            pltpu.VMEM((rows, part), bf16),
            pltpu.VMEM((1, rows), f32),
            pltpu.VMEM((4, 1, rows), f32),
        ]
        + scatter_buffers(rows, part)
        + [
            pltpu.SemaphoreType.DMA,
            pltpu.SemaphoreType.DMA((31,)),
            pltpu.SemaphoreType.DMA((31,)),
        ],
        compiler_params=pltpu.CompilerParams(
            collective_id=number, has_side_effects=True, vmem_limit_bytes=48 * 2**20
        ),
        cost_estimate=COST,
    )(partial, incoming, branch, inverse, gain)


def feature_peers(wide):
    peers = []
    for d in range(1, 8 if wide else 4):
        peer = {"col": flip("col", d & 3)}
        if d >> 2:
            peer["dp"] = flip("dp", 1)
        peers.append(peer)
    return peers


def total_kernel(v_ref, out_ref, slots, send_sem, recv_sem):
    me = lax.axis_index("col")
    peers = feature_peers(False)
    greet(peers)
    started = []
    send = sender(send_sem, recv_sem, started)
    for d, peer in enumerate(peers):
        send(v_ref, slots.at[me], d, peer)
    slots[me] = v_ref[...]
    for copy in started:
        copy.wait_recv()
    total = slots[0]
    for i in range(1, 4):
        total = total + slots[i]
    out_ref[...] = total
    for copy in started:
        copy.wait_send()


def feature_total(values, number, name):
    k, t = values.shape
    flat = values.reshape(k * t // 128, 128)
    total = pl.pallas_call(
        total_kernel,
        name=name,
        out_shape=jax.ShapeDtypeStruct(flat.shape, f32),
        in_specs=[pl.BlockSpec(memory_space=pltpu.VMEM)],
        out_specs=pl.BlockSpec(memory_space=pltpu.VMEM),
        scratch_shapes=[
            pltpu.VMEM((4,) + flat.shape, f32),
            pltpu.SemaphoreType.DMA((3,)),
            pltpu.SemaphoreType.DMA((3,)),
        ],
        compiler_params=pltpu.CompilerParams(
            collective_id=number, has_side_effects=True, vmem_limit_bytes=8 * 2**20
        ),
    )(flat)
    return total.reshape(k, t)


def gain_peers():
    peers = []
    for d in range(1, 8):
        peers.append({"row": flip("row", d & 3), "dp": flip("dp", d >> 2)})
    return peers


def last_kernel(p_ref, gains_ref, out_ref, total_ref, slots, *refs):
    buffers, (send_sem, recv_sem) = refs[:7], refs[7:]
    half = out_ref.shape[0] // 2
    me = side("dp") * 4 + lax.axis_index("row")
    to_x, _, to_c = neighbours()
    peers = gain_peers()
    greet([to_x, to_c] + peers)
    started = []
    send = sender(send_sem, recv_sem, started)
    copies = [send(gains_ref, slots.at[me], 14 + d, peer) for d, peer in enumerate(peers)]
    slots[me] = gains_ref[...]
    low, high = scatter_flow(p_ref, buffers, send)
    out_ref[:half, :] = low
    out_ref[half:, :] = high
    for copy in copies:
        copy.wait_recv()
    total = slots[0]
    for i in range(1, 8):
        total = total + slots[i]
    total_ref[...] = total
    for copy in started:
        copy.wait_send()


def last_scatter(partial, gains, number):
    rows, width = partial.shape[0] // 2, partial.shape[1] // 4
    flat = gains.reshape(-1, 128)
    vmem = pl.BlockSpec(memory_space=pltpu.VMEM)
    out, total = pl.pallas_call(
        last_kernel,
        name="scatter_projected",
        out_shape=(
            jax.ShapeDtypeStruct((rows, width), f32),
            jax.ShapeDtypeStruct(flat.shape, f32),
        ),
        in_specs=[vmem, vmem],
        out_specs=(vmem, vmem),
        scratch_shapes=[pltpu.VMEM((8,) + flat.shape, f32)]
        + scatter_buffers(rows, width)
        + [pltpu.SemaphoreType.DMA((21,)), pltpu.SemaphoreType.DMA((21,))],
        compiler_params=pltpu.CompilerParams(
            collective_id=number, has_side_effects=True, vmem_limit_bytes=48 * 2**20
        ),
        cost_estimate=COST,
    )(partial, flat)
    return out, total.reshape(gains.shape)


def row_peers():
    return [(d, {"row": flip("row", d)}) for d in (3, 2, 1)]


def unit_view(ref, unit, tok, heads):
    rows = pl.ds(pl.multiple_of((unit // heads) * tok, tok), tok)
    cols = pl.ds(pl.multiple_of((unit % heads) * HEAD_DIM, HEAD_DIM), HEAD_DIM)
    return ref.at[rows, cols]


def turn_kernel(back, tok, heads, x_ref, out_ref, local_sem, send_sem, recv_sem):
    z = lax.axis_index("row")
    greet([peer for _, peer in row_peers()])
    started = []
    send = sender(send_sem, recv_sem, started)

    def line(ref, i):
        return ref.at[pl.ds(pl.multiple_of(i * tok, tok), tok)]

    def ends(i):
        if back:
            return line(x_ref, i), unit_view(out_ref, z, tok, heads)
        return unit_view(x_ref, i, tok, heads), line(out_ref, z)

    for d, peer in row_peers():
        send(*ends(z ^ d), d - 1, peer)
    own = pltpu.make_async_copy(*ends(z), local_sem)
    own.start()
    for copy in started:
        copy.wait()
    own.wait()


def turn(values, back, tok, heads, number, name):
    shape = (2 * tok, heads * HEAD_DIM) if back else (2 * heads * tok, HEAD_DIM)
    return pl.pallas_call(
        functools.partial(turn_kernel, back, tok, heads),
        name=name,
        out_shape=jax.ShapeDtypeStruct(shape, values.dtype),
        in_specs=[pl.BlockSpec(memory_space=pltpu.VMEM)],
        out_specs=pl.BlockSpec(memory_space=pl.ANY),
        scratch_shapes=[
            pltpu.SemaphoreType.DMA,
            pltpu.SemaphoreType.DMA((3,)),
            pltpu.SemaphoreType.DMA((3,)),
        ],
        compiler_params=pltpu.CompilerParams(
            collective_id=number, has_side_effects=True, vmem_limit_bytes=8 * 2**20
        ),
        cost_estimate=COST,
    )(values)


def totals(stat, slots, started):
    for copy in started:
        copy.wait_recv()
    total = slots[0]
    for i in range(1, 8):
        total = total + slots[i]
    return total


def front_kernel(
    width,
    qkv_ref,
    cos_ref,
    sin_ref,
    gain_ref,
    out_ref,
    inv_ref,
    turned,
    packed,
    stat,
    slots,
    local_sem,
    stat_send,
    stat_recv,
    send_sem,
    recv_sem,
):
    count, tok = qkv_ref.shape[0], cos_ref.shape[0]
    part = qkv_ref.shape[1] // 3
    heads = part // HEAD_DIM
    z = lax.axis_index("row")
    me = side("dp") * 4 + lax.axis_index("col")
    peers = feature_peers(True)
    greet(peers + [peer for _, peer in row_peers()])
    for i in range(2):
        values = qkv_ref[:, i * part : (i + 1) * part]
        stat[i : i + 1, :] = jnp.sum(values * values, axis=1, keepdims=True).T
    started, moved, local = [], [], []
    send = sender(stat_send, stat_recv, started)
    for d, peer in enumerate(peers):
        send(stat, slots.at[me], d, peer)
    slots[me] = stat[...]
    move = sender(send_sem, recv_sem, moved)

    def ship(i):
        for d, peer in row_peers():
            move(packed.at[z ^ d, i], out_ref.at[z, i], 3 * i + d - 1, peer)
        copy = pltpu.make_async_copy(packed.at[z, i], out_ref.at[z, i], local_sem.at[i])
        copy.start()
        local.append(copy)

    def spots():
        return [(s, h, s * heads + h) for s in range(2) for h in range(heads)]

    for s, h, unit in spots():
        packed[unit, 2] = qkv_ref[
            s * tok : (s + 1) * tok, 2 * part + h * HEAD_DIM : 2 * part + (h + 1) * HEAD_DIM
        ].astype(bf16)
    ship(2)
    for i in (1, 0):
        for s, h, unit in spots():
            values = (
                qkv_ref[s * tok : (s + 1) * tok, i * part + h * HEAD_DIM : i * part + (h + 1) * HEAD_DIM]
                * gain_ref[i : i + 1, h * HEAD_DIM : (h + 1) * HEAD_DIM]
            )
            turned[i, unit] = values * cos_ref[...] + pltpu.roll(values, HEAD_DIM // 2, 1) * sin_ref[...]
    inverse = lax.rsqrt(totals(stat, slots, started) / width + norm_eps)
    inv_ref[...] = inverse
    for i in (1, 0):
        column = inverse[i : i + 1, :].T
        for s, h, unit in spots():
            packed[unit, i] = (turned[i, unit] * column[s * tok : (s + 1) * tok]).astype(bf16)
        ship(i)
    for copy in moved:
        copy.wait()
    for copy in local:
        copy.wait()
    for copy in started:
        copy.wait_send()


def front(qkv, cosine, sine_signed, gains, width, units, number):
    count, tok = qkv.shape[0], cosine.shape[0]
    return pl.pallas_call(
        functools.partial(front_kernel, width),
        name="front",
        out_shape=(
            jax.ShapeDtypeStruct((units, 3, tok, HEAD_DIM), bf16),
            jax.ShapeDtypeStruct((2, count), f32),
        ),
        in_specs=[pl.BlockSpec(memory_space=pltpu.VMEM)] * 4,
        out_specs=(pl.BlockSpec(memory_space=pl.ANY), pl.BlockSpec(memory_space=pltpu.VMEM)),
        scratch_shapes=[
            pltpu.VMEM((2, units, tok, HEAD_DIM), f32),
            pltpu.VMEM((units, 3, tok, HEAD_DIM), bf16),
            pltpu.VMEM((2, count), f32),
            pltpu.VMEM((8, 2, count), f32),
            pltpu.SemaphoreType.DMA((3,)),
            pltpu.SemaphoreType.DMA((7,)),
            pltpu.SemaphoreType.DMA((7,)),
            pltpu.SemaphoreType.DMA((9,)),
            pltpu.SemaphoreType.DMA((9,)),
        ],
        compiler_params=pltpu.CompilerParams(
            collective_id=number, has_side_effects=True, vmem_limit_bytes=40 * 2**20
        ),
        cost_estimate=COST,
    )(qkv, cosine, sine_signed, gains)


def rear_kernel(
    width,
    d_ref,
    qkv_ref,
    cos_ref,
    sin_ref,
    gain_ref,
    inv_ref,
    out_ref,
    sums_ref,
    landed,
    normed,
    stat,
    slots,
    stat_send,
    stat_recv,
    send_sem,
    recv_sem,
):
    count, tok = qkv_ref.shape[0], cos_ref.shape[0]
    part = qkv_ref.shape[1] // 3
    heads = part // HEAD_DIM
    z = lax.axis_index("row")
    me = side("dp") * 4 + lax.axis_index("col")
    peers = feature_peers(True)
    greet(peers + [peer for _, peer in row_peers()])
    started, moved = [], []
    move = sender(send_sem, recv_sem, moved)
    for i in (0, 1, 2):
        for d, peer in row_peers():
            there = pl.ds(pl.multiple_of((z ^ d) * tok, tok), tok)
            move(d_ref.at[i, there], landed.at[z, i], 3 * i + d - 1, peer)
    here = pl.ds(pl.multiple_of(z * tok, tok), tok)
    for i in (0, 1, 2):
        landed[z, i] = d_ref[i, here, :]
    spots = [(s, h, s * heads + h) for s in range(2) for h in range(heads)]
    for i in (0, 1):
        for copy in moved[3 * i : 3 * i + 3]:
            copy.wait_recv()
        for h in range(heads):
            cols = slice(i * part + h * HEAD_DIM, i * part + (h + 1) * HEAD_DIM)
            gain = gain_ref[i : i + 1, h * HEAD_DIM : (h + 1) * HEAD_DIM]
            raw = jnp.zeros((1, HEAD_DIM), f32)
            for s in range(2):
                rows = slice(s * tok, (s + 1) * tok)
                values = landed[s * heads + h, i].astype(f32)
                back = values * cos_ref[...] - pltpu.roll(values, HEAD_DIM // 2, 1) * sin_ref[...]
                pre = qkv_ref[rows, cols]
                inverse = inv_ref[i : i + 1, rows].T
                crossed = back * pre
                raw = raw + jnp.sum(crossed * inverse, axis=0, keepdims=True)
                partial = jnp.sum(crossed * gain, axis=1, keepdims=True).T
                if h == 0:
                    stat[i : i + 1, rows] = partial
                else:
                    stat[i : i + 1, rows] = stat[i : i + 1, rows] + partial
                normed[rows, cols] = back * gain
            sums_ref[i : i + 1, h * HEAD_DIM : (h + 1) * HEAD_DIM] = raw
    send = sender(stat_send, stat_recv, started)
    for d, peer in enumerate(peers):
        send(stat, slots.at[me], d, peer)
    slots[me] = stat[...]
    for copy in moved[6:]:
        copy.wait_recv()
    for s, h, unit in spots:
        cols = slice(2 * part + h * HEAD_DIM, 2 * part + (h + 1) * HEAD_DIM)
        out_ref[s * tok : (s + 1) * tok, cols] = landed[unit, 2]
    inner = totals(stat, slots, started) / width
    for i in (0, 1):
        inverse = inv_ref[i : i + 1, :]
        first = inverse.T
        second = (inverse * inverse * inverse * inner[i : i + 1, :]).T
        cols = slice(i * part, (i + 1) * part)
        out_ref[:, cols] = (first * normed[:, cols] - qkv_ref[:, cols] * second).astype(bf16)
    for copy in moved + started:
        copy.wait_send()


def rear(d_units, qkv, cosine, sine_signed, gains, inverse, width, number):
    count, tok = qkv.shape[0], cosine.shape[0]
    part = qkv.shape[1] // 3
    units = d_units.shape[1] // tok
    return pl.pallas_call(
        functools.partial(rear_kernel, width),
        name="rear",
        out_shape=(
            jax.ShapeDtypeStruct((count, 3 * part), bf16),
            jax.ShapeDtypeStruct((2, part), f32),
        ),
        in_specs=[pl.BlockSpec(memory_space=pltpu.VMEM)] * 6,
        out_specs=[pl.BlockSpec(memory_space=pltpu.VMEM)] * 2,
        scratch_shapes=[
            pltpu.VMEM((units, 3, tok, HEAD_DIM), bf16),
            pltpu.VMEM((count, 2 * part), f32),
            pltpu.VMEM((2, count), f32),
            pltpu.VMEM((8, 2, count), f32),
            pltpu.SemaphoreType.DMA((7,)),
            pltpu.SemaphoreType.DMA((7,)),
            pltpu.SemaphoreType.DMA((9,)),
            pltpu.SemaphoreType.DMA((9,)),
        ],
        compiler_params=pltpu.CompilerParams(
            collective_id=number, has_side_effects=True, vmem_limit_bytes=40 * 2**20
        ),
        cost_estimate=COST,
    )(d_units, qkv, cosine, sine_signed, gains, inverse)


BLOCK = 512


def attend_kernel(len_ref, q_ref, k_ref, v_ref, o_ref, o32_ref, lse_ref):
    i = pl.program_id(0)
    bq, bk = q_ref.shape[0], BLOCK
    length = len_ref[0]
    scale = HEAD_DIM ** (-0.5)
    q = q_ref[...]
    rows = i * bq + lax.broadcasted_iota(jnp.int32, (bq, bk), 0)
    cols0 = lax.broadcasted_iota(jnp.int32, (bq, bk), 1)

    def step(j, carry, masked):
        top, total, acc = carry
        j0 = pl.multiple_of(j * bk, bk)
        scores = contract_last(q, k_ref[pl.ds(j0, bk), :]) * scale
        if masked:
            cols = j0 + cols0
            scores = jnp.where((cols <= rows) & (cols < length), scores, masked_score)
        new = jnp.maximum(top, jnp.max(scores, axis=1, keepdims=True))
        weights = jnp.exp(scores - new)
        fix = jnp.exp(top - new)
        total = total * fix + jnp.sum(weights, axis=1, keepdims=True)
        acc = acc * fix + matmul(weights.astype(bf16), v_ref[pl.ds(j0, bk), :])
        return new, total, acc

    carry = (
        jnp.full((bq, 1), -jnp.inf, f32),
        jnp.zeros((bq, 1), f32),
        jnp.zeros((bq, HEAD_DIM), f32),
    )
    whole = jnp.minimum(i, length // bk)
    last = jnp.minimum(i + 1, (length + bk - 1) // bk)
    carry = lax.fori_loop(0, whole, lambda j, s: step(j, s, False), carry)
    top, total, acc = lax.fori_loop(whole, last, lambda j, s: step(j, s, True), carry)
    out = acc / total
    o_ref[...] = out.astype(bf16)
    o32_ref[...] = out
    lse_ref[...] = jnp.broadcast_to((top + jnp.log(total)).T, lse_ref.shape)


def attend(length, q, k, v):
    slots = q.shape[0]
    whole = pl.BlockSpec((slots, HEAD_DIM), lambda i: (0, 0))
    part = pl.BlockSpec((BLOCK, HEAD_DIM), lambda i: (i, 0))
    return pl.pallas_call(
        attend_kernel,
        name="attend",
        grid=(slots // BLOCK,),
        out_shape=(
            jax.ShapeDtypeStruct((slots, HEAD_DIM), bf16),
            jax.ShapeDtypeStruct((slots, HEAD_DIM), f32),
            jax.ShapeDtypeStruct((8, slots), f32),
        ),
        in_specs=[pl.BlockSpec(memory_space=pltpu.SMEM), part, whole, whole],
        out_specs=(part, part, pl.BlockSpec((8, BLOCK), lambda i: (0, i))),
        compiler_params=pltpu.CompilerParams(vmem_limit_bytes=24 * 2**20),
        cost_estimate=COST,
    )(length, q, k, v)


def attend_back_kernel(
    len_ref, q_ref, k_ref, v_ref, do_ref, o_ref, lse_ref, out_ref, dq_acc, delta_ref
):
    j = pl.program_id(0)
    bk, bq = k_ref.shape[0], BLOCK
    slots = q_ref.shape[0]
    length = len_ref[0]
    scale = HEAD_DIM ** (-0.5)

    @pl.when(j == 0)
    def _():
        dq_acc[...] = jnp.zeros_like(dq_acc)
        for i in range(slots // bq):
            here = slice(i * bq, (i + 1) * bq)
            product = do_ref[here, :].astype(f32) * o_ref[here, :]
            delta_ref[0:1, here] = jnp.sum(product, axis=1, keepdims=True).T

    k, v = k_ref[...], v_ref[...]
    j0 = j * bk
    cols = j0 + lax.broadcasted_iota(jnp.int32, (bk, bq), 0)
    rows0 = lax.broadcasted_iota(jnp.int32, (bk, bq), 1)

    def step(i, carry, masked):
        dk, dv = carry
        i0 = pl.multiple_of(i * bq, bq)
        here = pl.ds(i0, bq)
        q, do = q_ref[here, :], do_ref[here, :]
        scores = contract_last(k, q) * scale
        if masked:
            scores = jnp.where((cols <= i0 + rows0) & (cols < length), scores, masked_score)
        probs = jnp.exp(scores - lse_ref[0:1, here])
        dv = dv + matmul(probs.astype(bf16), do)
        d_probs = contract_last(v, do)
        d_scores = (probs * (d_probs - delta_ref[0:1, here])).astype(bf16)
        dk = dk + matmul(d_scores, q)
        dq_acc[here, :] += contract_first(d_scores, k)
        return dk, dv

    zero = jnp.zeros((bk, HEAD_DIM), f32)
    top = slots // bq
    first = jnp.where(j0 + bk <= length, j + 1, top)
    first = jnp.where(j0 < length, first, j)
    stop = jnp.where(j0 < length, top, j)
    carry = lax.fori_loop(j, first, lambda i, s: step(i, s, True), (zero, zero))
    dk, dv = lax.fori_loop(first, stop, lambda i, s: step(i, s, False), carry)
    there = pl.ds(pl.multiple_of(j0, bk), bk)
    out_ref[1, there, :] = (dk * scale).astype(bf16)
    out_ref[2, there, :] = dv.astype(bf16)

    @pl.when(j == pl.num_programs(0) - 1)
    def _():
        out_ref[0] = (dq_acc[...] * scale).astype(bf16)


def attend_back(length, q, k, v, do, o, lse):
    slots = q.shape[0]
    whole = pl.BlockSpec((slots, HEAD_DIM), lambda j: (0, 0))
    part = pl.BlockSpec((BLOCK, HEAD_DIM), lambda j: (j, 0))
    line = pl.BlockSpec((8, slots), lambda j: (0, 0))
    return pl.pallas_call(
        attend_back_kernel,
        name="attend_back",
        grid=(slots // BLOCK,),
        out_shape=jax.ShapeDtypeStruct((3, slots, HEAD_DIM), bf16),
        in_specs=[pl.BlockSpec(memory_space=pltpu.SMEM), whole, part, part, whole, whole, line],
        out_specs=pl.BlockSpec((3, slots, HEAD_DIM), lambda j: (0, 0, 0)),
        scratch_shapes=[pltpu.VMEM((slots, HEAD_DIM), f32), pltpu.VMEM((8, slots), f32)],
        compiler_params=pltpu.CompilerParams(vmem_limit_bytes=32 * 2**20),
        cost_estimate=COST,
    )(length, q, k, v, do, o, lse)


def per_device(
    tokens,
    seq_lengths,
    w_query,
    w_key,
    w_value,
    w_out,
    w_gate,
    w_up,
    w_down,
    q_gain,
    k_gain,
    attn_gain,
    mlp_gain,
    cotangent,
):
    tok_rows, feat_part = tokens.shape
    row_count, data_count = lax.axis_size("row"), lax.axis_size("dp")
    width = feat_part * lax.axis_size("col")
    slots = tok_rows * row_count
    half_feat = feat_part // 2
    y, z = side("dp"), lax.axis_index("row")
    heads = half_feat // HEAD_DIM
    pairs = [(i, i ^ 1) for i in range(data_count)]
    after = lambda values, *done: lax.optimization_barrier((values,) + done)[0]

    def y_half(values, axis):
        size = values.shape[axis] // 2
        return lax.dynamic_slice_in_dim(values, y * size, size, axis)

    qkv_weight = lax.all_gather(
        jnp.concatenate([y_half(w_query, 1), y_half(w_key, 1), y_half(w_value, 1)], axis=1),
        "row",
        axis=0,
        tiled=True,
    )
    out_weight = lax.all_gather(y_half(w_out, 0), "row", axis=1, tiled=True)
    gate_up_weight = lax.all_gather(
        jnp.concatenate([y_half(w_gate, 1), y_half(w_up, 1)], axis=1), "row", axis=0, tiled=True
    )
    hidden_part = gate_up_weight.shape[1] // 2
    gate_weight, up_weight = gate_up_weight[:, :hidden_part], gate_up_weight[:, hidden_part:]
    down_half = y_half(w_down, 0)
    split = down_half.shape[1] // 2
    low_weight = lax.all_gather(down_half[:, :split], "row", axis=1, tiled=True)

    positions = z * tok_rows + jnp.arange(tok_rows)
    length = seq_lengths[0]
    valid = (positions < length).astype(f32)[:, None]
    cosine, sine = rope_tables(positions, HEAD_DIM)
    sine_signed = jnp.where(jnp.arange(HEAD_DIM)[None, :] < HEAD_DIM // 2, -sine, sine)
    other_length = lax.ppermute(seq_lengths, "dp", pairs)
    pair_lengths = jnp.where(
        y == 0,
        jnp.concatenate([seq_lengths, other_length]),
        jnp.concatenate([other_length, seq_lengths]),
    )
    unit_length = lax.dynamic_slice_in_dim(pair_lengths, z // heads, 1)
    qk_gain = jnp.stack([y_half(q_gain, 0), y_half(k_gain, 0)])

    tokens_wide = gather_wide(tokens, 0, "gather_tokens")
    high_weight = lax.all_gather(after(down_half[:, split:], tokens_wide), "row", axis=1, tiled=True)
    qkv = matmul(tokens_wide, qkv_weight)
    units, inverse = front(qkv, cosine, sine_signed, qk_gain, width, 2 * heads, 2)
    q_unit, k_unit, v_unit = (units[:, i].reshape(slots, HEAD_DIM) for i in range(3))
    attn_unit, attn_exact, log_total = attend(unit_length, q_unit, k_unit, v_unit)
    attn_low = turn(attn_unit, True, tok_rows, heads, 3, "turn_attn")
    branch = scatter_wide(matmul(attn_low, out_weight).astype(bf16), 4, "scatter_branch")
    branch_inv = lax.rsqrt(
        feature_total(jnp.sum(branch * branch, axis=1)[None, :], 5, "total_branch")[0] / width
        + norm_eps
    )[:, None]
    resid = tokens.astype(f32) + branch * branch_inv * attn_gain
    resid_wide = gather_wide(resid.astype(bf16), 6, "gather_resid")
    gate = matmul(resid_wide, gate_weight)
    upper = matmul(resid_wide, up_weight)
    sigma = jax.nn.sigmoid(gate)
    hidden = (gate * sigma * upper).astype(bf16)
    mixed_low = scatter_wide(matmul(hidden, low_weight).astype(bf16), 7, "scatter_mixed_low")
    high_weight = after(high_weight, mixed_low)
    incoming = cotangent.astype(f32) * valid
    factor = 1.0 / math.sqrt(slots * data_count)
    block_output, mlp_gain_raw, d_high, d_low_wide = mixed_junction(
        matmul(hidden, high_weight).astype(bf16),
        mixed_low,
        incoming,
        resid,
        valid.T,
        mlp_gain[None, :],
        width,
        17,
    )
    low_raw = (contract_first(hidden, d_low_wide) * factor).astype(bf16)
    d_high_wide = gather_wide(after(d_high, low_raw), 18, "gather_d_mixed_high")
    high_raw = (contract_first(hidden, d_high_wide) * factor).astype(bf16)

    def cut(values, index, count, axis):
        size = values.shape[axis] // count
        return lax.dynamic_slice_in_dim(values, index * size, size, axis)

    def over_dp(piece):
        if data_count > 2:
            groups = [list(range(s, data_count, 2)) for s in (0, 1)]
            piece = lax.psum(piece, "dp", axis_index_groups=groups)
        return piece

    def two_sides(piece, other, bit, axis):
        low = jnp.where(bit == 0, piece, other)
        high = jnp.where(bit == 0, other, piece)
        return jnp.concatenate([low, high], axis=axis)

    def from_twin(piece):
        return lax.ppermute(piece, "dp", pairs)

    def reduce_rows(raw, axis):
        return lax.psum_scatter(raw, "row", scatter_dimension=axis, tiled=True)

    d_hidden = contract_last(d_low_wide, low_weight) + contract_last(d_high_wide, high_weight)
    d_gate = (d_hidden * upper * sigma * (1.0 + gate * (1.0 - sigma))).astype(bf16)
    d_upper = (d_hidden * gate * sigma).astype(bf16)
    d_gate_up = jnp.concatenate([d_gate, d_upper], axis=1)
    gate_up_raw = (contract_first(resid_wide, d_gate_up) * factor).astype(bf16)
    d_resid_wide = contract_last(d_gate_up, gate_up_weight).astype(bf16)
    d_resid_wide, low_piece = lax.optimization_barrier(
        (after(d_resid_wide, high_raw, gate_up_raw), reduce_rows(low_raw, 1))
    )
    down_piece = jnp.concatenate([low_piece, reduce_rows(high_raw, 1)], axis=1)
    gate_up_piece = reduce_rows(gate_up_raw, 0)
    d_resid, attn_gain_raw, d_branch_wide = d_resid_junction(
        d_resid_wide, incoming, branch, branch_inv.T, attn_gain[None, :], width, 10
    )
    down_piece = over_dp(down_piece)
    d_branch_wide, down_piece = lax.optimization_barrier((d_branch_wide, down_piece))
    d_attn = contract_last(d_branch_wide, out_weight).astype(bf16)
    other_down = from_twin(down_piece)
    d_attn_unit, other_down = lax.optimization_barrier(
        (turn(d_attn, False, tok_rows, heads, 13, "turn_d_attn"), other_down)
    )
    out_raw = (contract_first(attn_low, after(d_branch_wide, d_attn_unit)) * factor).astype(bf16)
    d_attn_unit = after(d_attn_unit, out_raw)
    out_piece = reduce_rows(out_raw, 1)
    d_units = attend_back(unit_length, q_unit, k_unit, v_unit, d_attn_unit, attn_exact, log_total)
    d_units, gate_up_piece = lax.optimization_barrier((d_units, over_dp(gate_up_piece)))
    other_gate_up = from_twin(gate_up_piece)
    d_qkv, gain_sums = rear(d_units, qkv, cosine, sine_signed, qk_gain, inverse, width, 14)
    d_qkv, gain_sums, other_gate_up = lax.optimization_barrier((d_qkv, gain_sums, other_gate_up))
    qkv_raw = (contract_first(tokens_wide, d_qkv) * factor).astype(bf16)
    projected = contract_last(after(d_qkv, qkv_raw), qkv_weight).astype(bf16)
    qkv_piece = over_dp(reduce_rows(qkv_raw, 0))

    def spread(half):
        return lax.dynamic_update_slice_in_dim(jnp.zeros((feat_part,), f32), half, y * half_feat, 0)

    gains_raw = jnp.stack(
        [spread(gain_sums[0]), spread(gain_sums[1]), attn_gain_raw[0], mlp_gain_raw[0]]
    )
    scattered, gains = last_scatter(projected, gains_raw * factor, 16)
    scattered, gains, out_piece = lax.optimization_barrier((scattered, gains, over_dp(out_piece)))
    other_out = from_twin(out_piece)
    input_grad = d_resid + scattered
    gains = over_dp(gains)
    input_grad, qkv_piece, other_down, other_gate_up = lax.optimization_barrier(
        (input_grad, qkv_piece, other_down, other_gate_up)
    )
    (gate_piece, up_piece), (other_gate, other_up) = (
        [cut(values, i, 2, 1) for i in range(2)] for values in (gate_up_piece, other_gate_up)
    )

    def whole(piece, other, axis):
        return two_sides(piece, other, y, axis).astype(f32)

    qkv_other = from_twin(qkv_piece)
    q_grad, k_grad, v_grad = (
        two_sides(cut(qkv_piece, i, 3, 1), cut(qkv_other, i, 3, 1), y, 1).astype(f32)
        for i in range(3)
    )
    return (
        block_output,
        input_grad,
        q_grad,
        k_grad,
        v_grad,
        whole(out_piece, other_out, 0),
        whole(gate_piece, other_gate, 1),
        whole(up_piece, other_up, 1),
        whole(down_piece, other_down, 0),
        gains[0],
        gains[1],
        gains[2],
        gains[3],
    )


def solution(mesh):
    tok, row_col, col_row, gain = P(("dp", "row"), "col"), P("row", "col"), P("col", "row"), P("col")
    weights = (row_col, row_col, row_col, col_row, row_col, row_col, col_row)
    gains = (gain, gain, gain, gain)
    return jax.shard_map(
        per_device,
        mesh=mesh,
        in_specs=(tok, P("dp")) + weights + gains + (tok,),
        out_specs=(tok, tok) + weights + gains,
        check_vma=False,
    )
```

```python
import functools
import math

import jax
import jax.numpy as jnp
from jax import lax
from jax.experimental import pallas as pl
from jax.experimental.pallas import tpu as pltpu
from jax.sharding import PartitionSpec as P

HEAD_DIM = 128
rope_base = 500000.0
norm_eps = 1e-06
masked_score = -1e30

MESH = pl.DeviceIdType.MESH
bf16 = jnp.bfloat16
f32 = jnp.float32
COST = pl.CostEstimate(flops=0, bytes_accessed=1000, transcendentals=0)


def rope_tables(positions, head_dim):
    half = head_dim // 2
    freq = 1.0 / rope_base ** (jnp.arange(half, dtype=f32) / half)
    angle = positions.astype(f32)[:, None] * freq[None, :]
    angle = jnp.concatenate([angle, angle], axis=1)
    return (jnp.cos(angle), jnp.sin(angle))


def matmul(left, right):
    return jnp.dot(left, right, preferred_element_type=f32)


def contract_first(left, right):
    return lax.dot_general(left, right, (((0,), (0,)), ((), ())), preferred_element_type=f32)


def contract_last(left, right):
    return lax.dot_general(left, right, (((1,), (1,)), ((), ())), preferred_element_type=f32)


def flip(axis, bit):
    return lax.axis_index(axis) ^ bit


def side(axis):
    return lax.axis_index(axis) & 1


def greet(peers):
    barrier = pltpu.get_barrier_semaphore()
    for peer in peers:
        pl.semaphore_signal(barrier, inc=1, device_id=peer, device_id_type=MESH)
    pl.semaphore_wait(barrier, len(peers))


def sender(send_sem, recv_sem, started):
    def send(src, dst, number, peer):
        copy = pltpu.make_async_remote_copy(
            src_ref=src,
            dst_ref=dst,
            send_sem=send_sem.at[number],
            recv_sem=recv_sem.at[number],
            device_id=peer,
            device_id_type=MESH,
        )
        copy.start()
        started.append(copy)
        return copy

    return send


def neighbours():
    return {"col": flip("col", 2)}, {"dp": flip("dp", 1)}, {"col": flip("col", 1)}


def gather_flow(x_ref, out_ref, local_sem, send, base, meanwhile=None):
    rows, width = x_ref.shape
    half = rows // 2
    y, b = side("dp"), lax.axis_index("col")
    to_x, to_y, to_c = neighbours()

    def slot(yy, h, bb, n=half):
        return out_ref.at[
            pl.ds(pl.multiple_of(yy * rows + h * half, half), n),
            pl.ds(pl.multiple_of(bb * width, width), width),
        ]

    low, high = x_ref.at[pl.ds(0, half)], x_ref.at[pl.ds(half, half)]
    own = pltpu.make_async_copy(x_ref, slot(y, 0, b, rows), local_sem)
    xa = send(low, slot(y, 0, b), base + 0, to_x)
    ya = send(high, slot(y, 1, b), base + 1, to_y)
    core = [send(low, slot(y, 0, b), base + 6, to_c)]
    yb = send(low, slot(y, 0, b), base + 2, to_y)
    xb = send(high, slot(y, 1, b), base + 3, to_x)
    core.append(send(high, slot(y, 1, b), base + 7, to_c))
    own.start()
    if meanwhile is not None:
        meanwhile()
    xa.wait_recv()
    piece = slot(y, 0, b ^ 2)
    yc = send(piece, piece, base + 4, to_y)
    core.append(send(piece, piece, base + 8, to_c))
    ya.wait_recv()
    piece = slot(y ^ 1, 1, b)
    xc = send(piece, piece, base + 5, to_x)
    core.append(send(piece, piece, base + 9, to_c))
    yb.wait_recv()
    piece = slot(y ^ 1, 0, b)
    core.append(send(piece, piece, base + 10, to_c))
    xb.wait_recv()
    piece = slot(y, 1, b ^ 2)
    core.append(send(piece, piece, base + 11, to_c))
    yc.wait_recv()
    piece = slot(y ^ 1, 0, b ^ 2)
    core.append(send(piece, piece, base + 12, to_c))
    xc.wait_recv()
    piece = slot(y ^ 1, 1, b ^ 2)
    core.append(send(piece, piece, base + 13, to_c))
    for copy in core:
        copy.wait_recv()
    own.wait()


def gather_kernel(x_ref, out_ref, local_sem, send_sem, recv_sem):
    greet(neighbours())
    started = []
    gather_flow(x_ref, out_ref, local_sem, sender(send_sem, recv_sem, started), 0)
    for copy in started:
        copy.wait_send()


def gather_wide(values, number, name):
    rows, width = values.shape
    return pl.pallas_call(
        gather_kernel,
        name=name,
        out_shape=jax.ShapeDtypeStruct((2 * rows, 4 * width), values.dtype),
        in_specs=[pl.BlockSpec(memory_space=pltpu.VMEM)],
        out_specs=pl.BlockSpec(memory_space=pl.ANY),
        scratch_shapes=[
            pltpu.SemaphoreType.DMA,
            pltpu.SemaphoreType.DMA((14,)),
            pltpu.SemaphoreType.DMA((14,)),
        ],
        compiler_params=pltpu.CompilerParams(collective_id=number, has_side_effects=True),
        cost_estimate=COST,
    )(values)


def scatter_flow(p_ref, buffers, send):
    rc, s1, ry, rx, s2, fy, fx = buffers
    rows, width = p_ref.shape[0] // 2, p_ref.shape[1] // 4
    half = rows // 2
    y, b = side("dp"), lax.axis_index("col")
    x, c = b >> 1, b & 1
    to_x, to_y, to_c = neighbours()

    def place(yy, h):
        return pl.ds(pl.multiple_of(yy * rows + h * half, half), half)

    def column(bb):
        return pl.ds(pl.multiple_of(bb * width, width), width)

    order = [(0, y ^ 1, 0), (1, y ^ 1, 0), (x ^ 1, 0, 1), (x ^ 1, 1, 1)]
    order += [(0, y, 0), (1, y, 0), (x, 0, 1), (x, 1, 1)]
    core = [
        send(
            p_ref.at[place(yy, h), column(2 * xx + (c ^ 1))],
            rc.at[xx, place(yy, h)],
            number,
            to_c,
        )
        for number, (xx, yy, h) in enumerate(order)
    ]

    def settle(*numbers):
        for number in numbers:
            core[number].wait_recv()
            xx, yy, h = order[number]
            s1[xx, place(yy, h), :] = (
                p_ref[place(yy, h), column(2 * xx + c)].astype(f32)
                + rc[xx, place(yy, h), :].astype(f32)
            ).astype(s1.dtype)

    settle(0, 1, 2, 3)
    ya, xa = [], []
    for i in range(2):
        ya.append(send(s1.at[i, place(y ^ 1, 0), :], ry.at[i], 8 + i, to_y))
        xa.append(send(s1.at[x ^ 1, pl.ds(i * rows + half, half), :], rx.at[i], 10 + i, to_x))
    settle(4, 5, 6, 7)
    for copy in ya:
        copy.wait_recv()
    s2[0] = (s1[x ^ 1, place(y, 0), :].astype(f32) + ry[x ^ 1].astype(f32)).astype(s2.dtype)
    xb = send(s2.at[0], fx, 12, to_x)
    for copy in xa:
        copy.wait_recv()
    s2[1] = (s1[x, place(y ^ 1, 1), :].astype(f32) + rx[y ^ 1].astype(f32)).astype(s2.dtype)
    yb = send(s2.at[1], fy, 13, to_y)
    keep = s1[x, place(y, 0), :].astype(f32) + ry[x].astype(f32)
    xb.wait_recv()
    low = keep + fx[...].astype(f32)
    keep = s1[x, place(y, 1), :].astype(f32) + rx[y].astype(f32)
    yb.wait_recv()
    return low, keep + fy[...].astype(f32)


def scatter_buffers(rows, width):
    half = rows // 2
    return [
        pltpu.VMEM((2, 2 * rows, width), bf16),
        pltpu.VMEM((2, 2 * rows, width), bf16),
        pltpu.VMEM((2, half, width), bf16),
        pltpu.VMEM((2, half, width), bf16),
        pltpu.VMEM((2, half, width), bf16),
        pltpu.VMEM((half, width), bf16),
        pltpu.VMEM((half, width), bf16),
    ]


def scatter_kernel(p_ref, out_ref, *refs):
    buffers, (send_sem, recv_sem) = refs[:7], refs[7:]
    half = out_ref.shape[0] // 2
    greet(neighbours())
    started = []
    low, high = scatter_flow(p_ref, buffers, sender(send_sem, recv_sem, started))
    out_ref[:half, :] = low
    out_ref[half:, :] = high
    for copy in started:
        copy.wait_send()


def scatter_wide(partial, number, name):
    rows, width = partial.shape[0] // 2, partial.shape[1] // 4
    return pl.pallas_call(
        scatter_kernel,
        name=name,
        out_shape=jax.ShapeDtypeStruct((rows, width), f32),
        in_specs=[pl.BlockSpec(memory_space=pltpu.VMEM)],
        out_specs=pl.BlockSpec(memory_space=pltpu.VMEM),
        scratch_shapes=scatter_buffers(rows, width)
        + [pltpu.SemaphoreType.DMA((14,)), pltpu.SemaphoreType.DMA((14,))],
        compiler_params=pltpu.CompilerParams(
            collective_id=number, has_side_effects=True, vmem_limit_bytes=48 * 2**20
        ),
        cost_estimate=COST,
    )(partial)


def exchange(stat, slots, send, base):
    me = lax.axis_index("col")
    copies = [send(stat, slots.at[me], base + d, peer) for d, peer in enumerate(feature_peers(False))]
    slots[me] = stat[...]
    return copies


def column_total(slots, copies):
    for copy in copies:
        copy.wait_recv()
    return (slots[0] + slots[1]) + (slots[2] + slots[3])


def junction_peers():
    to_x, to_y, to_c = neighbours()
    return [to_x, to_y, to_c, {"col": flip("col", 3)}]


def mixed_kernel(
    width,
    p_ref,
    low_ref,
    incoming_ref,
    resid_ref,
    valid_ref,
    gain_ref,
    block_ref,
    raw_ref,
    rest_ref,
    wide_ref,
    mixed,
    x_ref,
    stat,
    slots,
    *refs,
):
    buffers, (local_sem, send_sem, recv_sem) = refs[:7], refs[7:]
    rows, split = low_ref.shape
    half = rows // 2
    greet(junction_peers())
    started = []
    send = sender(send_sem, recv_sem, started)
    mixed[:, :split] = low_ref[...]
    low, high = scatter_flow(p_ref, buffers, send)
    mixed[:half, split:] = low
    mixed[half:, split:] = high
    stat[0:1, :] = jnp.sum(mixed[...] * mixed[...], axis=1, keepdims=True).T
    stat[1:2, :] = jnp.sum(incoming_ref[...] * gain_ref[...] * mixed[...], axis=1, keepdims=True).T
    total = column_total(slots, exchange(stat, slots, send, 14)) / width
    inverse = lax.rsqrt(total[0:1, :] + norm_eps)
    first = inverse.T
    second = (inverse * inverse * inverse * total[1:2, :]).T

    def slope(cols):
        return (
            first * (incoming_ref[:, cols] * gain_ref[:, cols]) - mixed[:, cols] * second
        ).astype(bf16)

    x_ref[...] = slope(slice(0, split))

    def meanwhile():
        rest_ref[...] = slope(slice(split, 2 * split))
        normed = mixed[...] * first
        block_ref[...] = ((resid_ref[...] + normed * gain_ref[...]) * valid_ref[...].T).astype(bf16)
        raw_ref[...] = jnp.sum(incoming_ref[...] * normed, axis=0, keepdims=True)

    gather_flow(x_ref, wide_ref, local_sem, send, 17, meanwhile)
    for copy in started:
        copy.wait_send()


def mixed_junction(partial, mixed_low, incoming, resid, valid, gain, width, number):
    rows, part = incoming.shape
    split = mixed_low.shape[1]
    vmem = pl.BlockSpec(memory_space=pltpu.VMEM)
    return pl.pallas_call(
        functools.partial(mixed_kernel, width),
        name="mixed_junction",
        out_shape=(
            jax.ShapeDtypeStruct((rows, part), bf16),
            jax.ShapeDtypeStruct((1, part), f32),
            jax.ShapeDtypeStruct((rows, part - split), bf16),
            jax.ShapeDtypeStruct((2 * rows, 4 * split), bf16),
        ),
        in_specs=[vmem] * 6,
        out_specs=(vmem, vmem, vmem, pl.BlockSpec(memory_space=pl.ANY)),
        scratch_shapes=[
            pltpu.VMEM((rows, part), f32),
            pltpu.VMEM((rows, split), bf16),
            pltpu.VMEM((2, rows), f32),
            pltpu.VMEM((4, 2, rows), f32),
        ]
        + scatter_buffers(rows, split)
        + [
            pltpu.SemaphoreType.DMA,
            pltpu.SemaphoreType.DMA((31,)),
            pltpu.SemaphoreType.DMA((31,)),
        ],
        compiler_params=pltpu.CompilerParams(
            collective_id=number, has_side_effects=True, vmem_limit_bytes=48 * 2**20
        ),
        cost_estimate=COST,
    )(partial, mixed_low, incoming, resid, valid, gain)


def d_resid_kernel(
    width,
    p_ref,
    incoming_ref,
    branch_ref,
    inv_ref,
    gain_ref,
    resid_ref,
    raw_ref,
    wide_ref,
    x_ref,
    stat,
    slots,
    *refs,
):
    buffers, (local_sem, send_sem, recv_sem) = refs[:7], refs[7:]
    half = x_ref.shape[0] // 2
    greet(junction_peers())
    started = []
    send = sender(send_sem, recv_sem, started)
    low, high = scatter_flow(p_ref, buffers, send)
    resid_ref[:half, :] = low + incoming_ref[:half, :]
    resid_ref[half:, :] = high + incoming_ref[half:, :]
    stat[...] = jnp.sum(resid_ref[...] * gain_ref[...] * branch_ref[...], axis=1, keepdims=True).T
    inner = column_total(slots, exchange(stat, slots, send, 14)) / width
    inverse = inv_ref[...]
    first = inverse.T
    second = (inverse * inverse * inverse * inner).T
    x_ref[...] = (first * (resid_ref[...] * gain_ref[...]) - branch_ref[...] * second).astype(bf16)

    def meanwhile():
        raw_ref[...] = jnp.sum(resid_ref[...] * branch_ref[...] * first, axis=0, keepdims=True)

    gather_flow(x_ref, wide_ref, local_sem, send, 17, meanwhile)
    for copy in started:
        copy.wait_send()


def d_resid_junction(partial, incoming, branch, inverse, gain, width, number):
    rows, part = incoming.shape
    vmem = pl.BlockSpec(memory_space=pltpu.VMEM)
    return pl.pallas_call(
        functools.partial(d_resid_kernel, width),
        name="d_resid_junction",
        out_shape=(
            jax.ShapeDtypeStruct((rows, part), f32),
            jax.ShapeDtypeStruct((1, part), f32),
            jax.ShapeDtypeStruct((2 * rows, 4 * part), bf16),
        ),
        in_specs=[vmem] * 5,
        out_specs=(vmem, vmem, pl.BlockSpec(memory_space=pl.ANY)),
        scratch_shapes=[
            pltpu.VMEM((rows, part), bf16),
            pltpu.VMEM((1, rows), f32),
            pltpu.VMEM((4, 1, rows), f32),
        ]
        + scatter_buffers(rows, part)
        + [
            pltpu.SemaphoreType.DMA,
            pltpu.SemaphoreType.DMA((31,)),
            pltpu.SemaphoreType.DMA((31,)),
        ],
        compiler_params=pltpu.CompilerParams(
            collective_id=number, has_side_effects=True, vmem_limit_bytes=48 * 2**20
        ),
        cost_estimate=COST,
    )(partial, incoming, branch, inverse, gain)


def feature_peers(wide):
    peers = []
    for d in range(1, 8 if wide else 4):
        peer = {"col": flip("col", d & 3)}
        if d >> 2:
            peer["dp"] = flip("dp", 1)
        peers.append(peer)
    return peers


def total_kernel(v_ref, out_ref, slots, send_sem, recv_sem):
    me = lax.axis_index("col")
    peers = feature_peers(False)
    greet(peers)
    started = []
    send = sender(send_sem, recv_sem, started)
    for d, peer in enumerate(peers):
        send(v_ref, slots.at[me], d, peer)
    slots[me] = v_ref[...]
    for copy in started:
        copy.wait_recv()
    total = slots[0]
    for i in range(1, 4):
        total = total + slots[i]
    out_ref[...] = total
    for copy in started:
        copy.wait_send()


def feature_total(values, number, name):
    k, t = values.shape
    flat = values.reshape(k * t // 128, 128)
    total = pl.pallas_call(
        total_kernel,
        name=name,
        out_shape=jax.ShapeDtypeStruct(flat.shape, f32),
        in_specs=[pl.BlockSpec(memory_space=pltpu.VMEM)],
        out_specs=pl.BlockSpec(memory_space=pltpu.VMEM),
        scratch_shapes=[
            pltpu.VMEM((4,) + flat.shape, f32),
            pltpu.SemaphoreType.DMA((3,)),
            pltpu.SemaphoreType.DMA((3,)),
        ],
        compiler_params=pltpu.CompilerParams(collective_id=number, has_side_effects=True),
    )(flat)
    return total.reshape(k, t)


def gain_peers():
    peers = []
    for d in range(1, 8):
        peers.append({"row": flip("row", d & 3), "dp": flip("dp", d >> 2)})
    return peers


def last_kernel(p_ref, gains_ref, out_ref, total_ref, slots, *refs):
    buffers, (send_sem, recv_sem) = refs[:7], refs[7:]
    half = out_ref.shape[0] // 2
    me = side("dp") * 4 + lax.axis_index("row")
    to_x, _, to_c = neighbours()
    peers = gain_peers()
    greet([to_x, to_c] + peers)
    started = []
    send = sender(send_sem, recv_sem, started)
    copies = [send(gains_ref, slots.at[me], 14 + d, peer) for d, peer in enumerate(peers)]
    slots[me] = gains_ref[...]
    low, high = scatter_flow(p_ref, buffers, send)
    out_ref[:half, :] = low
    out_ref[half:, :] = high
    for copy in copies:
        copy.wait_recv()
    total = slots[0]
    for i in range(1, 8):
        total = total + slots[i]
    total_ref[...] = total
    for copy in started:
        copy.wait_send()


def last_scatter(partial, gains, number):
    rows, width = partial.shape[0] // 2, partial.shape[1] // 4
    flat = gains.reshape(-1, 128)
    vmem = pl.BlockSpec(memory_space=pltpu.VMEM)
    out, total = pl.pallas_call(
        last_kernel,
        name="scatter_projected",
        out_shape=(
            jax.ShapeDtypeStruct((rows, width), f32),
            jax.ShapeDtypeStruct(flat.shape, f32),
        ),
        in_specs=[vmem, vmem],
        out_specs=(vmem, vmem),
        scratch_shapes=[pltpu.VMEM((8,) + flat.shape, f32)]
        + scatter_buffers(rows, width)
        + [pltpu.SemaphoreType.DMA((21,)), pltpu.SemaphoreType.DMA((21,))],
        compiler_params=pltpu.CompilerParams(
            collective_id=number, has_side_effects=True, vmem_limit_bytes=48 * 2**20
        ),
        cost_estimate=COST,
    )(partial, flat)
    return out, total.reshape(gains.shape)


def row_peers():
    return [(d, {"row": flip("row", d)}) for d in (3, 2, 1)]


def unit_view(ref, unit, tok, heads):
    rows = pl.ds(pl.multiple_of((unit // heads) * tok, tok), tok)
    cols = pl.ds(pl.multiple_of((unit % heads) * HEAD_DIM, HEAD_DIM), HEAD_DIM)
    return ref.at[rows, cols]


def turn_kernel(back, tok, heads, x_ref, out_ref, local_sem, send_sem, recv_sem):
    z = lax.axis_index("row")
    greet([peer for _, peer in row_peers()])
    started = []
    send = sender(send_sem, recv_sem, started)

    def line(ref, i):
        return ref.at[pl.ds(pl.multiple_of(i * tok, tok), tok)]

    def ends(i):
        if back:
            return line(x_ref, i), unit_view(out_ref, z, tok, heads)
        return unit_view(x_ref, i, tok, heads), line(out_ref, z)

    for d, peer in row_peers():
        send(*ends(z ^ d), d - 1, peer)
    own = pltpu.make_async_copy(*ends(z), local_sem)
    own.start()
    for copy in started:
        copy.wait()
    own.wait()


def turn(values, back, tok, heads, number, name):
    shape = (2 * tok, heads * HEAD_DIM) if back else (2 * heads * tok, HEAD_DIM)
    return pl.pallas_call(
        functools.partial(turn_kernel, back, tok, heads),
        name=name,
        out_shape=jax.ShapeDtypeStruct(shape, values.dtype),
        in_specs=[pl.BlockSpec(memory_space=pltpu.VMEM)],
        out_specs=pl.BlockSpec(memory_space=pl.ANY),
        scratch_shapes=[
            pltpu.SemaphoreType.DMA,
            pltpu.SemaphoreType.DMA((3,)),
            pltpu.SemaphoreType.DMA((3,)),
        ],
        compiler_params=pltpu.CompilerParams(collective_id=number, has_side_effects=True),
        cost_estimate=COST,
    )(values)


def totals(stat, slots, started):
    for copy in started:
        copy.wait_recv()
    total = slots[0]
    for i in range(1, 8):
        total = total + slots[i]
    return total


def front_kernel(
    width,
    qkv_ref,
    cos_ref,
    sin_ref,
    gain_ref,
    out_ref,
    inv_ref,
    turned,
    packed,
    stat,
    slots,
    local_sem,
    stat_send,
    stat_recv,
    send_sem,
    recv_sem,
):
    count, tok = qkv_ref.shape[0], cos_ref.shape[0]
    part = qkv_ref.shape[1] // 3
    heads = part // HEAD_DIM
    z = lax.axis_index("row")
    me = side("dp") * 4 + lax.axis_index("col")
    peers = feature_peers(True)
    greet(peers + [peer for _, peer in row_peers()])
    for i in range(2):
        values = qkv_ref[:, i * part : (i + 1) * part]
        stat[i : i + 1, :] = jnp.sum(values * values, axis=1, keepdims=True).T
    started, moved, local = [], [], []
    send = sender(stat_send, stat_recv, started)
    for d, peer in enumerate(peers):
        send(stat, slots.at[me], d, peer)
    slots[me] = stat[...]
    move = sender(send_sem, recv_sem, moved)

    def ship(i):
        for d, peer in row_peers():
            move(packed.at[z ^ d, i], out_ref.at[z, i], 3 * i + d - 1, peer)
        copy = pltpu.make_async_copy(packed.at[z, i], out_ref.at[z, i], local_sem.at[i])
        copy.start()
        local.append(copy)

    def spots():
        return [(s, h, s * heads + h) for s in range(2) for h in range(heads)]

    for s, h, unit in spots():
        packed[unit, 2] = qkv_ref[
            s * tok : (s + 1) * tok, 2 * part + h * HEAD_DIM : 2 * part + (h + 1) * HEAD_DIM
        ].astype(bf16)
    ship(2)
    for i in (1, 0):
        for s, h, unit in spots():
            values = (
                qkv_ref[s * tok : (s + 1) * tok, i * part + h * HEAD_DIM : i * part + (h + 1) * HEAD_DIM]
                * gain_ref[i : i + 1, h * HEAD_DIM : (h + 1) * HEAD_DIM]
            )
            turned[i, unit] = values * cos_ref[...] + pltpu.roll(values, HEAD_DIM // 2, 1) * sin_ref[...]
    inverse = lax.rsqrt(totals(stat, slots, started) / width + norm_eps)
    inv_ref[...] = inverse
    for i in (1, 0):
        column = inverse[i : i + 1, :].T
        for s, h, unit in spots():
            packed[unit, i] = (turned[i, unit] * column[s * tok : (s + 1) * tok]).astype(bf16)
        ship(i)
    for copy in moved:
        copy.wait()
    for copy in local:
        copy.wait()
    for copy in started:
        copy.wait_send()


def front(qkv, cosine, sine_signed, gains, width, units, number):
    count, tok = qkv.shape[0], cosine.shape[0]
    return pl.pallas_call(
        functools.partial(front_kernel, width),
        name="front",
        out_shape=(
            jax.ShapeDtypeStruct((units, 3, tok, HEAD_DIM), bf16),
            jax.ShapeDtypeStruct((2, count), f32),
        ),
        in_specs=[pl.BlockSpec(memory_space=pltpu.VMEM)] * 4,
        out_specs=(pl.BlockSpec(memory_space=pl.ANY), pl.BlockSpec(memory_space=pltpu.VMEM)),
        scratch_shapes=[
            pltpu.VMEM((2, units, tok, HEAD_DIM), f32),
            pltpu.VMEM((units, 3, tok, HEAD_DIM), bf16),
            pltpu.VMEM((2, count), f32),
            pltpu.VMEM((8, 2, count), f32),
            pltpu.SemaphoreType.DMA((3,)),
            pltpu.SemaphoreType.DMA((7,)),
            pltpu.SemaphoreType.DMA((7,)),
            pltpu.SemaphoreType.DMA((9,)),
            pltpu.SemaphoreType.DMA((9,)),
        ],
        compiler_params=pltpu.CompilerParams(
            collective_id=number, has_side_effects=True, vmem_limit_bytes=40 * 2**20
        ),
        cost_estimate=COST,
    )(qkv, cosine, sine_signed, gains)


def rear_kernel(
    width,
    d_ref,
    qkv_ref,
    cos_ref,
    sin_ref,
    gain_ref,
    inv_ref,
    out_ref,
    sums_ref,
    landed,
    normed,
    stat,
    slots,
    stat_send,
    stat_recv,
    send_sem,
    recv_sem,
):
    count, tok = qkv_ref.shape[0], cos_ref.shape[0]
    part = qkv_ref.shape[1] // 3
    heads = part // HEAD_DIM
    z = lax.axis_index("row")
    me = side("dp") * 4 + lax.axis_index("col")
    peers = feature_peers(True)
    greet(peers + [peer for _, peer in row_peers()])
    started, moved = [], []
    move = sender(send_sem, recv_sem, moved)
    for i in (0, 1, 2):
        for d, peer in row_peers():
            there = pl.ds(pl.multiple_of((z ^ d) * tok, tok), tok)
            move(d_ref.at[i, there], landed.at[z, i], 3 * i + d - 1, peer)
    here = pl.ds(pl.multiple_of(z * tok, tok), tok)
    for i in (0, 1, 2):
        landed[z, i] = d_ref[i, here, :]
    spots = [(s, h, s * heads + h) for s in range(2) for h in range(heads)]
    for i in (0, 1):
        for copy in moved[3 * i : 3 * i + 3]:
            copy.wait_recv()
        for h in range(heads):
            cols = slice(i * part + h * HEAD_DIM, i * part + (h + 1) * HEAD_DIM)
            gain = gain_ref[i : i + 1, h * HEAD_DIM : (h + 1) * HEAD_DIM]
            raw = jnp.zeros((1, HEAD_DIM), f32)
            for s in range(2):
                rows = slice(s * tok, (s + 1) * tok)
                values = landed[s * heads + h, i].astype(f32)
                back = values * cos_ref[...] - pltpu.roll(values, HEAD_DIM // 2, 1) * sin_ref[...]
                pre = qkv_ref[rows, cols]
                inverse = inv_ref[i : i + 1, rows].T
                crossed = back * pre
                raw = raw + jnp.sum(crossed * inverse, axis=0, keepdims=True)
                partial = jnp.sum(crossed * gain, axis=1, keepdims=True).T
                if h == 0:
                    stat[i : i + 1, rows] = partial
                else:
                    stat[i : i + 1, rows] = stat[i : i + 1, rows] + partial
                normed[rows, cols] = back * gain
            sums_ref[i : i + 1, h * HEAD_DIM : (h + 1) * HEAD_DIM] = raw
    send = sender(stat_send, stat_recv, started)
    for d, peer in enumerate(peers):
        send(stat, slots.at[me], d, peer)
    slots[me] = stat[...]
    for copy in moved[6:]:
        copy.wait_recv()
    for s, h, unit in spots:
        cols = slice(2 * part + h * HEAD_DIM, 2 * part + (h + 1) * HEAD_DIM)
        out_ref[s * tok : (s + 1) * tok, cols] = landed[unit, 2]
    inner = totals(stat, slots, started) / width
    for i in (0, 1):
        inverse = inv_ref[i : i + 1, :]
        first = inverse.T
        second = (inverse * inverse * inverse * inner[i : i + 1, :]).T
        cols = slice(i * part, (i + 1) * part)
        out_ref[:, cols] = (first * normed[:, cols] - qkv_ref[:, cols] * second).astype(bf16)
    for copy in moved + started:
        copy.wait_send()


def rear(d_units, qkv, cosine, sine_signed, gains, inverse, width, number):
    count, tok = qkv.shape[0], cosine.shape[0]
    part = qkv.shape[1] // 3
    units = d_units.shape[1] // tok
    return pl.pallas_call(
        functools.partial(rear_kernel, width),
        name="rear",
        out_shape=(
            jax.ShapeDtypeStruct((count, 3 * part), bf16),
            jax.ShapeDtypeStruct((2, part), f32),
        ),
        in_specs=[pl.BlockSpec(memory_space=pltpu.VMEM)] * 6,
        out_specs=[pl.BlockSpec(memory_space=pltpu.VMEM)] * 2,
        scratch_shapes=[
            pltpu.VMEM((units, 3, tok, HEAD_DIM), bf16),
            pltpu.VMEM((count, 2 * part), f32),
            pltpu.VMEM((2, count), f32),
            pltpu.VMEM((8, 2, count), f32),
            pltpu.SemaphoreType.DMA((7,)),
            pltpu.SemaphoreType.DMA((7,)),
            pltpu.SemaphoreType.DMA((9,)),
            pltpu.SemaphoreType.DMA((9,)),
        ],
        compiler_params=pltpu.CompilerParams(
            collective_id=number, has_side_effects=True, vmem_limit_bytes=40 * 2**20
        ),
        cost_estimate=COST,
    )(d_units, qkv, cosine, sine_signed, gains, inverse)


BLOCK = 512


def attend_kernel(len_ref, q_ref, k_ref, v_ref, o_ref, o32_ref, lse_ref):
    i = pl.program_id(0)
    bq, bk = q_ref.shape[0], BLOCK
    length = len_ref[0]
    scale = HEAD_DIM ** (-0.5)
    q = q_ref[...]
    rows = i * bq + lax.broadcasted_iota(jnp.int32, (bq, bk), 0)
    cols0 = lax.broadcasted_iota(jnp.int32, (bq, bk), 1)

    def step(j, carry, masked):
        top, total, acc = carry
        j0 = pl.multiple_of(j * bk, bk)
        scores = contract_last(q, k_ref[pl.ds(j0, bk), :]) * scale
        if masked:
            cols = j0 + cols0
            scores = jnp.where((cols <= rows) & (cols < length), scores, masked_score)
        new = jnp.maximum(top, jnp.max(scores, axis=1, keepdims=True))
        weights = jnp.exp(scores - new)
        fix = jnp.exp(top - new)
        total = total * fix + jnp.sum(weights, axis=1, keepdims=True)
        acc = acc * fix + matmul(weights.astype(bf16), v_ref[pl.ds(j0, bk), :])
        return new, total, acc

    carry = (
        jnp.full((bq, 1), -jnp.inf, f32),
        jnp.zeros((bq, 1), f32),
        jnp.zeros((bq, HEAD_DIM), f32),
    )
    whole = jnp.minimum(i, length // bk)
    last = jnp.minimum(i + 1, (length + bk - 1) // bk)
    carry = lax.fori_loop(0, whole, lambda j, s: step(j, s, False), carry)
    top, total, acc = lax.fori_loop(whole, last, lambda j, s: step(j, s, True), carry)
    out = acc / total
    o_ref[...] = out.astype(bf16)
    o32_ref[...] = out
    lse_ref[...] = jnp.broadcast_to((top + jnp.log(total)).T, lse_ref.shape)


def attend(length, q, k, v):
    slots = q.shape[0]
    whole = pl.BlockSpec((slots, HEAD_DIM), lambda i: (0, 0))
    part = pl.BlockSpec((BLOCK, HEAD_DIM), lambda i: (i, 0))
    return pl.pallas_call(
        attend_kernel,
        name="attend",
        grid=(slots // BLOCK,),
        out_shape=(
            jax.ShapeDtypeStruct((slots, HEAD_DIM), bf16),
            jax.ShapeDtypeStruct((slots, HEAD_DIM), f32),
            jax.ShapeDtypeStruct((8, slots), f32),
        ),
        in_specs=[pl.BlockSpec(memory_space=pltpu.SMEM), part, whole, whole],
        out_specs=(part, part, pl.BlockSpec((8, BLOCK), lambda i: (0, i))),
        cost_estimate=COST,
    )(length, q, k, v)


def attend_back_kernel(
    len_ref, q_ref, k_ref, v_ref, do_ref, o_ref, lse_ref, out_ref, dq_acc, delta_ref
):
    j = pl.program_id(0)
    bk, bq = k_ref.shape[0], BLOCK
    slots = q_ref.shape[0]
    length = len_ref[0]
    scale = HEAD_DIM ** (-0.5)

    @pl.when(j == 0)
    def _():
        dq_acc[...] = jnp.zeros_like(dq_acc)
        for i in range(slots // bq):
            here = slice(i * bq, (i + 1) * bq)
            product = do_ref[here, :].astype(f32) * o_ref[here, :]
            delta_ref[0:1, here] = jnp.sum(product, axis=1, keepdims=True).T

    k, v = k_ref[...], v_ref[...]
    j0 = j * bk
    cols = j0 + lax.broadcasted_iota(jnp.int32, (bk, bq), 0)
    rows0 = lax.broadcasted_iota(jnp.int32, (bk, bq), 1)

    def step(i, carry, masked):
        dk, dv = carry
        i0 = pl.multiple_of(i * bq, bq)
        here = pl.ds(i0, bq)
        q, do = q_ref[here, :], do_ref[here, :]
        scores = contract_last(k, q) * scale
        if masked:
            scores = jnp.where((cols <= i0 + rows0) & (cols < length), scores, masked_score)
        probs = jnp.exp(scores - lse_ref[0:1, here])
        dv = dv + matmul(probs.astype(bf16), do)
        d_probs = contract_last(v, do)
        d_scores = (probs * (d_probs - delta_ref[0:1, here])).astype(bf16)
        dk = dk + matmul(d_scores, q)
        dq_acc[here, :] += contract_first(d_scores, k)
        return dk, dv

    zero = jnp.zeros((bk, HEAD_DIM), f32)
    top = slots // bq
    first = jnp.where(j0 + bk <= length, j + 1, top)
    first = jnp.where(j0 < length, first, j)
    stop = jnp.where(j0 < length, top, j)
    carry = lax.fori_loop(j, first, lambda i, s: step(i, s, True), (zero, zero))
    dk, dv = lax.fori_loop(first, stop, lambda i, s: step(i, s, False), carry)
    there = pl.ds(pl.multiple_of(j0, bk), bk)
    out_ref[1, there, :] = (dk * scale).astype(bf16)
    out_ref[2, there, :] = dv.astype(bf16)

    @pl.when(j == pl.num_programs(0) - 1)
    def _():
        out_ref[0] = (dq_acc[...] * scale).astype(bf16)


def attend_back(length, q, k, v, do, o, lse):
    slots = q.shape[0]
    whole = pl.BlockSpec((slots, HEAD_DIM), lambda j: (0, 0))
    part = pl.BlockSpec((BLOCK, HEAD_DIM), lambda j: (j, 0))
    line = pl.BlockSpec((8, slots), lambda j: (0, 0))
    return pl.pallas_call(
        attend_back_kernel,
        name="attend_back",
        grid=(slots // BLOCK,),
        out_shape=jax.ShapeDtypeStruct((3, slots, HEAD_DIM), bf16),
        in_specs=[pl.BlockSpec(memory_space=pltpu.SMEM), whole, part, part, whole, whole, line],
        out_specs=pl.BlockSpec((3, slots, HEAD_DIM), lambda j: (0, 0, 0)),
        scratch_shapes=[pltpu.VMEM((slots, HEAD_DIM), f32), pltpu.VMEM((8, slots), f32)],
        cost_estimate=COST,
    )(length, q, k, v, do, o, lse)


def per_device(
    tokens,
    seq_lengths,
    w_query,
    w_key,
    w_value,
    w_out,
    w_gate,
    w_up,
    w_down,
    q_gain,
    k_gain,
    attn_gain,
    mlp_gain,
    cotangent,
):
    tok_rows, feat_part = tokens.shape
    row_count, data_count = lax.axis_size("row"), lax.axis_size("dp")
    width = feat_part * lax.axis_size("col")
    slots = tok_rows * row_count
    half_feat = feat_part // 2
    y, z = side("dp"), lax.axis_index("row")
    heads = half_feat // HEAD_DIM
    pairs = [(i, i ^ 1) for i in range(data_count)]
    after = lambda values, *done: lax.optimization_barrier((values,) + done)[0]

    def y_half(values, axis):
        size = values.shape[axis] // 2
        return lax.dynamic_slice_in_dim(values, y * size, size, axis)

    qkv_weight = lax.all_gather(
        jnp.concatenate([y_half(w_query, 1), y_half(w_key, 1), y_half(w_value, 1)], axis=1),
        "row",
        axis=0,
        tiled=True,
    )
    out_weight = lax.all_gather(y_half(w_out, 0), "row", axis=1, tiled=True)
    gate_up_weight = lax.all_gather(
        jnp.concatenate([y_half(w_gate, 1), y_half(w_up, 1)], axis=1), "row", axis=0, tiled=True
    )
    hidden_part = gate_up_weight.shape[1] // 2
    gate_weight, up_weight = gate_up_weight[:, :hidden_part], gate_up_weight[:, hidden_part:]
    down_half = y_half(w_down, 0)
    split = down_half.shape[1] // 2
    low_weight = lax.all_gather(down_half[:, :split], "row", axis=1, tiled=True)

    positions = z * tok_rows + jnp.arange(tok_rows)
    length = seq_lengths[0]
    valid = (positions < length).astype(f32)[:, None]
    cosine, sine = rope_tables(positions, HEAD_DIM)
    sine_signed = jnp.where(jnp.arange(HEAD_DIM)[None, :] < HEAD_DIM // 2, -sine, sine)
    other_length = lax.ppermute(seq_lengths, "dp", pairs)
    pair_lengths = jnp.where(
        y == 0,
        jnp.concatenate([seq_lengths, other_length]),
        jnp.concatenate([other_length, seq_lengths]),
    )
    unit_length = lax.dynamic_slice_in_dim(pair_lengths, z // heads, 1)
    qk_gain = jnp.stack([y_half(q_gain, 0), y_half(k_gain, 0)])

    tokens_wide = gather_wide(tokens, 0, "gather_tokens")
    high_weight = lax.all_gather(after(down_half[:, split:], tokens_wide), "row", axis=1, tiled=True)
    qkv = matmul(tokens_wide, qkv_weight)
    units, inverse = front(qkv, cosine, sine_signed, qk_gain, width, 2 * heads, 2)
    q_unit, k_unit, v_unit = (units[:, i].reshape(slots, HEAD_DIM) for i in range(3))
    attn_unit, attn_exact, log_total = attend(unit_length, q_unit, k_unit, v_unit)
    attn_low = turn(attn_unit, True, tok_rows, heads, 3, "turn_attn")
    branch = scatter_wide(matmul(attn_low, out_weight).astype(bf16), 4, "scatter_branch")
    branch_inv = lax.rsqrt(
        feature_total(jnp.sum(branch * branch, axis=1)[None, :], 5, "total_branch")[0] / width
        + norm_eps
    )[:, None]
    resid = tokens.astype(f32) + branch * branch_inv * attn_gain
    resid_wide = gather_wide(resid.astype(bf16), 6, "gather_resid")
    gate = matmul(resid_wide, gate_weight)
    upper = matmul(resid_wide, up_weight)
    sigma = jax.nn.sigmoid(gate)
    hidden = (gate * sigma * upper).astype(bf16)
    mixed_low = scatter_wide(matmul(hidden, low_weight).astype(bf16), 7, "scatter_mixed_low")
    high_weight = after(high_weight, mixed_low)
    incoming = cotangent.astype(f32) * valid
    factor = 1.0 / math.sqrt(slots * data_count)
    block_output, mlp_gain_raw, d_high, d_low_wide = mixed_junction(
        matmul(hidden, high_weight).astype(bf16),
        mixed_low,
        incoming,
        resid,
        valid.T,
        mlp_gain[None, :],
        width,
        17,
    )
    low_raw = (contract_first(hidden, d_low_wide) * factor).astype(bf16)
    d_high_wide = gather_wide(after(d_high, low_raw), 18, "gather_d_mixed_high")
    high_raw = (contract_first(hidden, d_high_wide) * factor).astype(bf16)

    def cut(values, index, count, axis):
        size = values.shape[axis] // count
        return lax.dynamic_slice_in_dim(values, index * size, size, axis)

    def over_dp(piece):
        if data_count > 2:
            groups = [list(range(s, data_count, 2)) for s in (0, 1)]
            piece = lax.psum(piece, "dp", axis_index_groups=groups)
        return piece

    def two_sides(piece, other, bit, axis):
        low = jnp.where(bit == 0, piece, other)
        high = jnp.where(bit == 0, other, piece)
        return jnp.concatenate([low, high], axis=axis)

    def from_twin(piece):
        return lax.ppermute(piece, "dp", pairs)

    def reduce_rows(raw, axis):
        return lax.psum_scatter(raw, "row", scatter_dimension=axis, tiled=True)

    d_hidden = contract_last(d_low_wide, low_weight) + contract_last(d_high_wide, high_weight)
    d_gate = (d_hidden * upper * sigma * (1.0 + gate * (1.0 - sigma))).astype(bf16)
    d_upper = (d_hidden * gate * sigma).astype(bf16)
    d_gate_up = jnp.concatenate([d_gate, d_upper], axis=1)
    gate_up_raw = (contract_first(resid_wide, d_gate_up) * factor).astype(bf16)
    d_resid_wide = contract_last(d_gate_up, gate_up_weight).astype(bf16)
    d_resid_wide, low_piece = lax.optimization_barrier(
        (after(d_resid_wide, high_raw, gate_up_raw), reduce_rows(low_raw, 1))
    )
    down_piece = jnp.concatenate([low_piece, reduce_rows(high_raw, 1)], axis=1)
    gate_up_piece = reduce_rows(gate_up_raw, 0)
    d_resid, attn_gain_raw, d_branch_wide = d_resid_junction(
        d_resid_wide, incoming, branch, branch_inv.T, attn_gain[None, :], width, 10
    )
    down_piece = over_dp(down_piece)
    d_branch_wide, down_piece = lax.optimization_barrier((d_branch_wide, down_piece))
    d_attn = contract_last(d_branch_wide, out_weight).astype(bf16)
    other_down = from_twin(down_piece)
    d_attn_unit, other_down = lax.optimization_barrier(
        (turn(d_attn, False, tok_rows, heads, 13, "turn_d_attn"), other_down)
    )
    out_raw = (contract_first(attn_low, after(d_branch_wide, d_attn_unit)) * factor).astype(bf16)
    d_attn_unit = after(d_attn_unit, out_raw)
    out_piece = reduce_rows(out_raw, 1)
    d_units = attend_back(unit_length, q_unit, k_unit, v_unit, d_attn_unit, attn_exact, log_total)
    d_qkv, gain_sums = rear(d_units, qkv, cosine, sine_signed, qk_gain, inverse, width, 14)
    d_qkv, gate_up_piece = lax.optimization_barrier((d_qkv, over_dp(gate_up_piece)))
    other_gate_up = from_twin(gate_up_piece)
    qkv_raw = (contract_first(tokens_wide, d_qkv) * factor).astype(bf16)
    projected = contract_last(after(d_qkv, qkv_raw), qkv_weight).astype(bf16)
    qkv_piece = over_dp(reduce_rows(qkv_raw, 0))

    def spread(half):
        return lax.dynamic_update_slice_in_dim(jnp.zeros((feat_part,), f32), half, y * half_feat, 0)

    gains_raw = jnp.stack(
        [spread(gain_sums[0]), spread(gain_sums[1]), attn_gain_raw[0], mlp_gain_raw[0]]
    )
    scattered, gains = last_scatter(projected, gains_raw * factor, 16)
    scattered, gains, out_piece = lax.optimization_barrier((scattered, gains, over_dp(out_piece)))
    other_out = from_twin(out_piece)
    input_grad = d_resid + scattered
    gains = over_dp(gains)
    input_grad, qkv_piece, other_down, other_gate_up = lax.optimization_barrier(
        (input_grad, qkv_piece, other_down, other_gate_up)
    )
    (gate_piece, up_piece), (other_gate, other_up) = (
        [cut(values, i, 2, 1) for i in range(2)] for values in (gate_up_piece, other_gate_up)
    )

    def whole(piece, other, axis):
        return two_sides(piece, other, y, axis).astype(f32)

    qkv_other = from_twin(qkv_piece)
    q_grad, k_grad, v_grad = (
        two_sides(cut(qkv_piece, i, 3, 1), cut(qkv_other, i, 3, 1), y, 1).astype(f32)
        for i in range(3)
    )
    return (
        block_output,
        input_grad,
        q_grad,
        k_grad,
        v_grad,
        whole(out_piece, other_out, 0),
        whole(gate_piece, other_gate, 1),
        whole(up_piece, other_up, 1),
        whole(down_piece, other_down, 0),
        gains[0],
        gains[1],
        gains[2],
        gains[3],
    )


def solution(mesh):
    tok, row_col, col_row, gain = P(("dp", "row"), "col"), P("row", "col"), P("col", "row"), P("col")
    weights = (row_col, row_col, row_col, col_row, row_col, row_col, col_row)
    gains = (gain, gain, gain, gain)
    return jax.shard_map(
        per_device,
        mesh=mesh,
        in_specs=(tok, P("dp")) + weights + gains + (tok,),
        out_specs=(tok, tok) + weights + gains,
        check_vma=False,
    )
```
